32 devices in a mesh: dp: 2 (over core), seq: 4 (over z), head: 4 (over y, x).
Axes of the slice: x: 2, y: 2, z: 4, core: 2. Of those that a mesh axis runs over, the one named last changes fastest.
Arguments:
- activations: bfloat16 [2, 1024, 2048], P('dp', 'seq'), may hold values from -6 to 6
- cotangent: bfloat16 [2, 1024, 2048], P('dp', 'seq'), may hold values from -6 to 6
- lengths: int32 [2], replicated, may hold values from 128 to 1024, as said below
- query_weight: float32 [2048, 2048], P(('dp', 'seq'), 'head'), may hold values from -0.125 to 0.125
- key_weight: float32 [2048, 2048], P(('dp', 'seq'), 'head'), may hold values from -0.125 to 0.125
- value_weight: float32 [2048, 4096], P(('dp', 'seq'), 'head'), may hold values from -0.125 to 0.125
- gate_weight: float32 [2048, 4096], P(('dp', 'seq'), 'head'), may hold values from -0.125 to 0.125
- alpha_weight: float32 [2048, 16], P(('dp', 'seq'), 'head'), may hold values from -0.125 to 0.125
- beta_weight: float32 [2048, 16], P(('dp', 'seq'), 'head'), may hold values from -0.125 to 0.125
- out_weight: float32 [2048, 4096], P(('dp', 'seq'), 'head'), may hold values from -0.1875 to 0.1875
- swiglu_gate: float32 [2048, 5504], P(('dp', 'seq'), 'head'), may hold values from -0.125 to 0.125
- swiglu_value: float32 [2048, 5504], P(('dp', 'seq'), 'head'), may hold values from -0.125 to 0.125
- swiglu_down: float32 [2048, 5504], P(('dp', 'seq'), 'head'), may hold values from -0.15625 to 0.15625
- mixer_gain: float32 [2048], replicated, may hold values from 0.1 to 1.9
- feed_gain: float32 [2048], replicated, may hold values from 0.1 to 1.9
- head_gain: float32 [256], replicated, may hold values from 0.1 to 1.9
- decay_rate: float32 [16], replicated, may hold values from 1e-05 to 0.05
- beta_bias: float32 [16], replicated, may hold values from -6 to 0
Outputs:
- outputs: bfloat16 [2, 1024, 2048], P('dp', ('seq', 'head'))
- input_grad: bfloat16 [2, 1024, 2048], P('dp', ('seq', 'head'))
- query_grad: float32 [2048, 2048], P(('dp', 'seq'), 'head')
- key_grad: float32 [2048, 2048], P(('dp', 'seq'), 'head')
- value_grad: float32 [2048, 4096], P(('dp', 'seq'), 'head')
- gate_grad: float32 [2048, 4096], P(('dp', 'seq'), 'head')
- alpha_grad: float32 [2048, 16], P(('dp', 'seq'), 'head')
- beta_grad: float32 [2048, 16], P(('dp', 'seq'), 'head')
- out_grad: float32 [2048, 4096], P(('dp', 'seq'), 'head')
- swiglu_gate_grad: float32 [2048, 5504], P(('dp', 'seq'), 'head')
- swiglu_value_grad: float32 [2048, 5504], P(('dp', 'seq'), 'head')
- swiglu_down_grad: float32 [2048, 5504], P(('dp', 'seq'), 'head')
- mixer_gain_grad: float32 [2048], replicated
- feed_gain_grad: float32 [2048], replicated
- head_gain_grad: float32 [256], replicated
- decay_grad: float32 [16], replicated
- bias_grad: float32 [16], replicated
The draws below stay inside these ranges and needn't reach their ends.
Inputs may be any that keep to these rules, and one draw needn't show every extreme that they name: lengths[0] is 1024; lengths[1] lies between 128 and 256.
All inputs are finite; a program needn't handle non-finite values.
Results may differ from the reference program's by a relative error of at most 0.019.
The reference program's roundings to bfloat16 on the way count: a program that leaves them out, or rounds other values in their place, can miss the bound.
Values may be sent and summed in bfloat16 or wider, within the bound.
No kernel may reach another device: no remote copies, remote signals or barrier semaphores. Data moves between devices by JAX's collectives and lax.ppermute only.
A program may use at most 192 MiB of HBM per device.

```python
import math
import jax
import jax.numpy as jnp
from jax import lax

D = 2048
H = 16
DK = 128
DV = 256
FF = 5504
BLOCK = 64
SEQ = 1024
N_DP = 2


def draw_lengths(key, part):
    shorter = jax.random.randint(key, (), SEQ // 8, SEQ // 4 + 1)
    return jnp.stack([jnp.full((), SEQ, jnp.int32), shorter.astype(jnp.int32)])


def shard_levels(own_key, shape, split, low, largest):
    level, own = 1.0, jax.random.fold_in(own_key, 6)
    for position, shards_of in split:
        draws = jnp.exp(jax.random.uniform(jax.random.fold_in(own, position), (shards_of,), jnp.float32, low / len(split), largest / len(split)))
        level = level * jnp.repeat(draws, shape[position] // shards_of).reshape([-1 if axis == position else 1 for axis in range(len(shape))])
    return level


def normal_values(stream_key, dims, scale, reach, split=(), kind=jnp.bfloat16):
    level = shard_levels(stream_key, dims, split, -0.22, 0.18) if split else 1.0
    values = jax.random.normal(stream_key, dims, jnp.float32) * scale * level
    return jnp.minimum(jnp.maximum(values, -reach), reach).astype(kind)


def setup_inputs(seed: int = 0) -> dict:
    keys = jax.random.split(jax.random.key(seed), 19)
    activations = normal_values(keys[0], (N_DP, SEQ, D), 1.0, 6.0, ((0, 2), (1, 4)))
    cotangent = normal_values(keys[1], (N_DP, SEQ, D), 1.0, 6.0, ((0, 2), (1, 4)))
    lengths = draw_lengths(jax.random.fold_in(keys[18], 71), 0)
    query_weight = normal_values(keys[3], (D, H * DK), D ** -0.5, 0.125, ((0, 8), (1, 4)), jnp.float32)
    key_weight = normal_values(keys[4], (D, H * DK), D ** -0.5, 0.125, ((0, 8), (1, 4)), jnp.float32)
    value_weight = normal_values(keys[5], (D, H * DV), D ** -0.5, 0.125, ((0, 8), (1, 4)), jnp.float32)
    gate_weight = normal_values(keys[6], (D, H * DV), D ** -0.5, 0.125, ((0, 8), (1, 4)), jnp.float32)
    alpha_weight = normal_values(keys[7], (D, H), D ** -0.5, 0.125, ((0, 8), (1, 4)), jnp.float32)
    beta_weight = normal_values(keys[8], (D, H), D ** -0.5, 0.125, ((0, 8), (1, 4)), jnp.float32)
    out_weight = normal_values(keys[9], (D, H * DV), (H * DV // 4) ** -0.5, 0.1875, ((0, 8), (1, 4)), jnp.float32)
    swiglu_gate = normal_values(keys[10], (D, FF), D ** -0.5, 0.125, ((0, 8), (1, 4)), jnp.float32)
    swiglu_value = normal_values(keys[11], (D, FF), D ** -0.5, 0.125, ((0, 8), (1, 4)), jnp.float32)
    swiglu_down = normal_values(keys[12], (D, FF), (FF // 4) ** -0.5, 0.15625, ((0, 8), (1, 4)), jnp.float32)
    mixer_gain = jnp.clip(1.0 + 0.18 * jax.random.normal(keys[13], (D,), jnp.float32), 0.1, 1.9)
    feed_gain = jnp.clip(1.0 + 0.18 * jax.random.normal(keys[14], (D,), jnp.float32), 0.1, 1.9)
    head_gain = jnp.clip(1.0 + 0.18 * jax.random.normal(keys[15], (DV,), jnp.float32), 0.1, 1.9)
    decay_rate = jnp.clip(jnp.exp(jax.random.uniform(keys[16], (H,), jnp.float32, math.log(9.999999747378752e-06), math.log(0.05))), 9.999999747378752e-06, 0.05)
    beta_bias = jnp.clip(jax.random.uniform(keys[17], (H,), jnp.float32, -6.0, 0.0), -6.0, 0.0)
    return {"activations": activations, "cotangent": cotangent, "lengths": lengths, "query_weight": query_weight, "key_weight": key_weight, "value_weight": value_weight, "gate_weight": gate_weight, "alpha_weight": alpha_weight, "beta_weight": beta_weight, "out_weight": out_weight, "swiglu_gate": swiglu_gate, "swiglu_value": swiglu_value, "swiglu_down": swiglu_down, "mixer_gain": mixer_gain, "feed_gain": feed_gain, "head_gain": head_gain, "decay_rate": decay_rate, "beta_bias": beta_bias}


epsilon = 1e-06
highest = lax.Precision.HIGHEST

@jax.custom_vjp
def low(v):
    return lax.optimization_barrier(v.astype(jnp.bfloat16)).astype(jnp.float32)

@jax.custom_vjp
def low_back(v):
    return v

def low_keep(v):
    return (low(v), None)

def low_pass(kept, grad):
    return (grad,)

def back_keep(v):
    return (v, None)

def back_low(kept, grad):
    return (low(grad),)
low.defvjp(low_keep, low_pass)
low_back.defvjp(back_keep, back_low)

def matmul_high(left, right):
    return jnp.matmul(left, right, precision=highest)

def dense(left, right):
    return jnp.dot(left, right, precision=highest, preferred_element_type=jnp.float32)

def rms_scale(values, gain):
    return values * lax.rsqrt(lax.optimization_barrier(jnp.mean(values * values, axis=-1, keepdims=True)) + epsilon) * gain

def unit_rows(values):
    return values * lax.rsqrt(lax.optimization_barrier(jnp.sum(values * values, axis=-1, keepdims=True)) + epsilon)

def inverse_unit(strict_part, identity):
    negated = -strict_part
    result = identity + negated
    power = negated
    for level in range((strict_part.shape[-1] - 1).bit_length() - 1):
        power = matmul_high(power, power)
        result = matmul_high(result, identity + power)
    return result

def block_core(state, key, value, decay, beta):
    size = decay.shape[-1]
    rows = lax.broadcasted_iota(jnp.int32, (size, size), 0)
    cols = lax.broadcasted_iota(jnp.int32, (size, size), 1)
    lower = rows >= cols
    identity = (rows == cols).astype(decay.dtype)
    cumulative = jnp.cumsum(decay, axis=-1)
    spread = cumulative[:, :, None] - cumulative[:, None, :]
    ratio = jnp.where(lower, jnp.exp(jnp.where(lower, spread, 0.0)), 0.0) * beta[:, None, :]
    growth = jnp.exp(cumulative)[:, :, None]
    keys_dot = matmul_high(key, jnp.swapaxes(key, 1, 2))
    solver = inverse_unit(jnp.where(rows > cols, keys_dot * ratio, 0.0), identity)
    update = matmul_high(solver, value - growth * matmul_high(key, state))
    weights = (jnp.exp(cumulative[:, -1:] - cumulative) * beta)[:, :, None]
    carried = jnp.exp(cumulative[:, -1])[:, None, None] * state + matmul_high(jnp.swapaxes(key * weights, 1, 2), update)
    return (carried, ratio, growth, update)

def block_output(state, block):
    query, key, value, decay, beta = block
    carried, ratio, growth, update = block_core(state, key, value, decay, beta)
    scores = matmul_high(query, jnp.swapaxes(key, 1, 2)) * ratio
    output = growth * matmul_high(query, state) + matmul_high(scores, update)
    return (carried, output)

def split_blocks(array):
    shape = (array.shape[0], array.shape[1] // BLOCK, BLOCK) + array.shape[2:]
    return jnp.moveaxis(array.reshape(shape), 1, 0)

def join_blocks(array):
    moved = jnp.moveaxis(array, 0, 1)
    return moved.reshape((moved.shape[0], -1) + moved.shape[3:])

def segment(query, key, value, decay, beta, state):
    blocks = (split_blocks(query), split_blocks(key), split_blocks(value), split_blocks(decay), split_blocks(beta))
    final, outs = lax.scan(jax.checkpoint(block_output), state, blocks)
    return (join_blocks(outs), final)

def layer(mask, rows_x, query_weight, key_weight, value_weight, gate_weight, alpha_weight, beta_weight, out_weight, swiglu_gate, swiglu_value, swiglu_down, mixer_gain, feed_gain, head_gain, decay_rate, beta_bias):
    query_weight = low(query_weight)
    key_weight = low(key_weight)
    value_weight = low(value_weight)
    gate_weight = low(gate_weight)
    alpha_weight = low(alpha_weight)
    beta_weight = low(beta_weight)
    out_weight = low(out_weight)
    swiglu_gate = low(swiglu_gate)
    swiglu_value = low(swiglu_value)
    swiglu_down = low(swiglu_down)
    length = rows_x.shape[0]
    normed = low(rms_scale(rows_x, mixer_gain))
    query_pre = low_back(dense(normed, query_weight))
    key_pre = low_back(dense(normed, key_weight))
    value_pre = low_back(dense(normed, value_weight))
    gate_pre = low_back(dense(normed, gate_weight))
    alpha_pre = low_back(dense(normed, alpha_weight))
    beta_pre = low_back(dense(normed, beta_weight))
    query = unit_rows(query_pre.reshape(length, H, DK)).transpose(1, 0, 2)
    key = unit_rows(key_pre.reshape(length, H, DK)).transpose(1, 0, 2)
    value = value_pre.reshape(length, H, DV).transpose(1, 0, 2)
    decay = (-decay_rate * jax.nn.softplus(alpha_pre)).T
    beta = jax.nn.sigmoid(beta_pre + beta_bias).T
    outs, final = segment(query, key, value, decay, beta, jnp.zeros((H, DK, DV), jnp.float32))
    outs = outs.transpose(1, 0, 2)
    gated = low((rms_scale(outs, head_gain) * jax.nn.silu(gate_pre.reshape(length, H, DV))).reshape(length, H * DV))
    mixed = low_back(dense(gated, out_weight.T))
    hidden = rows_x + mixed
    normed2 = low(rms_scale(hidden, feed_gain))
    gate_in = low_back(dense(normed2, swiglu_gate))
    up_in = low_back(dense(normed2, swiglu_value))
    active = low(jax.nn.silu(gate_in) * up_in)
    return mask[:, None] * (hidden + dense(active, swiglu_down.T))

def reference(activations, cotangent, lengths, query_weight, key_weight, value_weight, gate_weight, alpha_weight, beta_weight, out_weight, swiglu_gate, swiglu_value, swiglu_down, mixer_gain, feed_gain, head_gain, decay_rate, beta_bias):
    params = (query_weight, key_weight, value_weight, gate_weight, alpha_weight, beta_weight, out_weight, swiglu_gate, swiglu_value, swiglu_down, mixer_gain, feed_gain, head_gain, decay_rate, beta_bias)
    positions = lax.broadcasted_iota(jnp.int32, (SEQ,), 0)
    results = []
    input_grads = []
    totals = None
    for replica in range(N_DP):
        rows_x = activations[replica].astype(jnp.float32)
        mask = (positions < lengths[replica].astype(jnp.int32)).astype(jnp.float32)

        def apply(rows_in, *weights):
            return layer(mask, rows_in, *weights)
        result, back = jax.vjp(apply, rows_x, *params)
        grads = back(cotangent[replica].astype(jnp.float32))
        results.append(result.astype(jnp.bfloat16))
        input_grads.append(grads[0].astype(jnp.bfloat16))
        if totals is None:
            totals = list(grads[1:])
        else:
            totals = [left + right for left, right in zip(totals, grads[1:])]
    return (jnp.stack(results), jnp.stack(input_grads), totals[0], totals[1], totals[2], totals[3], totals[4], totals[5], totals[6], totals[7], totals[8], totals[9], totals[10], totals[11], totals[12], totals[13], totals[14])
```

```python
import jax
import jax.numpy as jnp
from jax import lax
from jax.sharding import PartitionSpec as P

BLOCK = 64


epsilon = 1e-06
highest = lax.Precision.HIGHEST


def from_behind(block, axis, distance):
    devices = range(lax.axis_size(axis))
    route = [(i - distance, i) for i in devices if i - distance in devices]
    return lax.ppermute(block, axis, route)


def matmul_high(left, right):
    return jnp.matmul(left, right, precision=highest)


def contract_rows(left, right):
    return lax.dot_general(
        left, right, (((0,), (0,)), ((), ())), preferred_element_type=jnp.float32
    )


def contract_cols(left, right):
    return lax.dot_general(
        left, right, (((1,), (1,)), ((), ())), preferred_element_type=jnp.float32
    )


def rms_scale(values, gain):
    return values * lax.rsqrt(jnp.mean(values * values, axis=-1, keepdims=True) + epsilon) * gain


def unit_rows(values):
    return values * lax.rsqrt(jnp.sum(values * values, axis=-1, keepdims=True) + epsilon)


def swiglu(gate_in, up_in):
    return jax.nn.silu(gate_in) * up_in


def inverse_unit(strict_part, identity):
    negated = -strict_part
    result = identity + negated
    power = negated
    for level in range((strict_part.shape[-1] - 1).bit_length() - 1):
        power = matmul_high(power, power)
        result = matmul_high(result, identity + power)
    return result


def block_solver(key, decay, beta):
    size = decay.shape[-1]
    rows = lax.broadcasted_iota(jnp.int32, (size, size), 0)
    cols = lax.broadcasted_iota(jnp.int32, (size, size), 1)
    lower = rows >= cols
    identity = (rows == cols).astype(decay.dtype)
    cumulative = matmul_high(decay, (rows <= cols).astype(decay.dtype))
    spread = cumulative[:, :, None] - cumulative[:, None, :]
    ratio = jnp.where(lower, jnp.exp(jnp.where(lower, spread, 0.0)), 0.0) * beta[:, None, :]
    growth = jnp.exp(cumulative)[:, :, None]
    keys_dot = matmul_high(key, jnp.swapaxes(key, 1, 2))
    solver = inverse_unit(jnp.where(rows > cols, keys_dot * ratio, 0.0), identity)
    weights = (jnp.exp(cumulative[:, -1:] - cumulative) * beta)[:, :, None]
    return (cumulative, ratio, growth, solver, weights)


def block_core(state, key, value, decay, beta):
    cumulative, ratio, growth, solver, weights = block_solver(key, decay, beta)
    update = matmul_high(solver, value - growth * matmul_high(key, state))
    carried = jnp.exp(cumulative[:, -1])[:, None, None] * state + matmul_high(
        jnp.swapaxes(key * weights, 1, 2), update
    )
    return (carried, ratio, growth, update)


def block_output(state, block):
    query, key, value, decay, beta = block
    carried, ratio, growth, update = block_core(state, key, value, decay, beta)
    scores = matmul_high(query, jnp.swapaxes(key, 1, 2)) * ratio
    output = growth * matmul_high(query, state) + matmul_high(scores, update)
    return (carried, output)


def block_state(state, block):
    key, value, decay, beta = block
    return (block_core(state, key, value, decay, beta)[0], None)


def block_adjoint(later, block):
    query, key, decay, beta, out_grad = block
    cumulative, ratio, growth, solver, weights = block_solver(key, decay, beta)
    scores = matmul_high(query, jnp.swapaxes(key, 1, 2)) * ratio
    update_grad = matmul_high(jnp.swapaxes(scores, 1, 2), out_grad) + matmul_high(
        key * weights, later
    )
    solved = matmul_high(jnp.swapaxes(solver, 1, 2), update_grad)
    earlier = jnp.exp(cumulative[:, -1])[:, None, None] * later
    earlier = earlier + matmul_high(jnp.swapaxes(growth * query, 1, 2), out_grad)
    earlier = earlier - matmul_high(jnp.swapaxes(growth * key, 1, 2), solved)
    return (earlier, None)


def split_blocks(array):
    shape = (array.shape[0], array.shape[1] // BLOCK, BLOCK) + array.shape[2:]
    return jnp.moveaxis(array.reshape(shape), 1, 0)


def join_blocks(array):
    moved = jnp.moveaxis(array, 0, 1)
    return moved.reshape((moved.shape[0], -1) + moved.shape[3:])


def segment(query, key, value, decay, beta, state):
    blocks = (
        split_blocks(query),
        split_blocks(key),
        split_blocks(value),
        split_blocks(decay),
        split_blocks(beta),
    )
    final, outs = lax.scan(jax.checkpoint(block_output), state, blocks)
    return (join_blocks(outs), final)


def entering_grad(query, key, decay, beta, outs_grad, start):
    blocks = (
        split_blocks(query),
        split_blocks(key),
        split_blocks(decay),
        split_blocks(beta),
        split_blocks(outs_grad),
    )
    result, unused = lax.scan(block_adjoint, start, blocks, reverse=True)
    return result


def transition(key, value, decay, beta):
    heads, rows_here, key_size = key.shape
    value_size = value.shape[2]
    widened = jnp.concatenate(
        [jnp.zeros((heads, rows_here, key_size), jnp.float32), value], axis=-1
    )
    identity = jnp.broadcast_to(jnp.eye(key_size, dtype=jnp.float32), (heads, key_size, key_size))
    begin = jnp.concatenate(
        [identity, jnp.zeros((heads, key_size, value_size), jnp.float32)], axis=-1
    )
    blocks = (split_blocks(key), split_blocks(widened), split_blocks(decay), split_blocks(beta))
    final, unused = lax.scan(block_state, begin, blocks)
    return (final[:, :, :key_size], final[:, :, key_size:])


def prepare(query_pre, key_pre, value_pre, alpha_pre, beta_pre, rates, biases):
    rows_here = query_pre.shape[0]
    heads = rates.shape[0]
    query = unit_rows(query_pre.reshape(rows_here, heads, -1)).transpose(1, 0, 2)
    key = unit_rows(key_pre.reshape(rows_here, heads, -1)).transpose(1, 0, 2)
    value = value_pre.reshape(rows_here, heads, -1).transpose(1, 0, 2)
    decay = (-rates * jax.nn.softplus(alpha_pre)).T
    beta = jax.nn.sigmoid(beta_pre + biases).T
    return (query, key, value, decay, beta)


def finish(outs, gate_pre, gain):
    turned = outs.transpose(1, 0, 2)
    gated = rms_scale(turned, gain) * jax.nn.silu(gate_pre.reshape(turned.shape))
    return gated.reshape(turned.shape[0], -1)


def on_device(
    activations,
    cotangent,
    lengths,
    query_weight,
    key_weight,
    value_weight,
    gate_weight,
    alpha_weight,
    beta_weight,
    out_weight,
    swiglu_gate,
    swiglu_value,
    swiglu_down,
    mixer_gain,
    feed_gain,
    head_gain,
    decay_rate,
    beta_bias,
):
    query_low = query_weight.astype(jnp.bfloat16)
    key_low = key_weight.astype(jnp.bfloat16)
    value_low = value_weight.astype(jnp.bfloat16)
    gate_low = gate_weight.astype(jnp.bfloat16)
    alpha_low = alpha_weight.astype(jnp.bfloat16)
    beta_low = beta_weight.astype(jnp.bfloat16)
    out_low = out_weight.astype(jnp.bfloat16)
    feed_gate_low = swiglu_gate.astype(jnp.bfloat16)
    feed_value_low = swiglu_value.astype(jnp.bfloat16)
    feed_down_low = swiglu_down.astype(jnp.bfloat16)
    spans = ("dp", "seq")
    joined = jnp.concatenate([query_low, key_low, value_low, alpha_low, beta_low], axis=1)
    joined_full = lax.all_gather(joined, spans, axis=0, tiled=True)
    qk_cols = query_low.shape[1]
    v_cols = value_low.shape[1]
    ab_cols = alpha_low.shape[1]
    query_full = joined_full[:, :qk_cols]
    key_full = joined_full[:, qk_cols : 2 * qk_cols]
    value_full = joined_full[:, 2 * qk_cols : 2 * qk_cols + v_cols]
    tail = 2 * qk_cols + v_cols
    alpha_full = joined_full[:, tail : tail + ab_cols]
    beta_full = joined_full[:, tail + ab_cols : tail + 2 * ab_cols]
    gate_full = lax.all_gather(gate_low, spans, axis=0, tiled=True)
    out_full = lax.all_gather(out_low, spans, axis=0, tiled=True)
    gate_ffn = lax.all_gather(feed_gate_low, spans, axis=0, tiled=True)
    value_ffn = lax.all_gather(feed_value_low, spans, axis=0, tiled=True)
    down_ffn = lax.all_gather(feed_down_low, spans, axis=0, tiled=True)

    def everyone(part):
        return lax.all_gather(part, spans, axis=0, tiled=True)

    def own_columns(rows):
        return lax.all_to_all(rows, spans, split_axis=1, concat_axis=0, tiled=True)

    replica = lax.axis_index("dp")
    seq_rank = lax.axis_index("seq")
    head_rank = lax.axis_index("head")
    parts = lax.axis_size("head")
    rows_seg = activations.shape[1]
    slab = rows_seg // parts
    start_row = head_rank * slab
    heads_here = alpha_full.shape[1]
    positions = seq_rank * rows_seg + lax.broadcasted_iota(jnp.int32, (rows_seg,), 0)
    mask = (positions < lengths[replica]).astype(jnp.float32)
    inputs = activations[0].astype(jnp.float32)
    own_rows = lax.dynamic_slice_in_dim(inputs, start_row, slab, 0)
    own_mask = lax.dynamic_slice_in_dim(mask, start_row, slab, 0)
    normed = rms_scale(inputs, mixer_gain).astype(jnp.bfloat16)
    query_pre = jnp.dot(normed, query_full, preferred_element_type=jnp.float32)
    key_pre = jnp.dot(normed, key_full, preferred_element_type=jnp.float32)
    value_pre = jnp.dot(normed, value_full, preferred_element_type=jnp.float32)
    gate_pre = jnp.dot(normed, gate_full, preferred_element_type=jnp.float32)
    alpha_pre = jnp.dot(normed, alpha_full, preferred_element_type=jnp.float32)
    beta_pre = jnp.dot(normed, beta_full, preferred_element_type=jnp.float32)
    rates = lax.dynamic_slice_in_dim(decay_rate, head_rank * heads_here, heads_here)
    biases = lax.dynamic_slice_in_dim(beta_bias, head_rank * heads_here, heads_here)
    prepared, prepare_back = jax.vjp(
        prepare, query_pre, key_pre, value_pre, alpha_pre, beta_pre, rates, biases
    )
    query, key, value, decay, beta = prepared
    mats, offsets = transition(key, value, decay, beta)
    blank = jnp.zeros(offsets.shape, jnp.float32)

    def relay_forward(step, carry):
        return from_behind(matmul_high(mats, carry) + offsets, "seq", 1)

    state_in = lax.fori_loop(0, lax.axis_size("seq") - 1, relay_forward, blank)
    (outs, state_end), delta_back = jax.vjp(segment, query, key, value, decay, beta, state_in)
    gated, finish_back = jax.vjp(finish, outs, gate_pre, head_gain)
    gated_low = gated.astype(jnp.bfloat16)
    piece = gated_low
    mixed = lax.psum_scatter(
        contract_cols(piece, out_full), "head", scatter_dimension=0, tiled=True
    )
    hidden = own_rows + mixed
    normed2, norm2_back = jax.vjp(rms_scale, hidden, feed_gain)
    feed_in = lax.all_gather(normed2.astype(jnp.bfloat16), "head", axis=0, tiled=True)
    gate_in = jnp.dot(feed_in, gate_ffn, preferred_element_type=jnp.float32)
    up_in = jnp.dot(feed_in, value_ffn, preferred_element_type=jnp.float32)
    active, swiglu_back = jax.vjp(swiglu, gate_in, up_in)
    active_low = active.astype(jnp.bfloat16)
    piece = active_low
    feed = lax.psum_scatter(
        contract_cols(piece, down_ffn).astype(jnp.bfloat16), "head", scatter_dimension=0, tiled=True
    ).astype(jnp.float32)
    outputs = (own_mask[:, None] * (hidden + feed)).astype(jnp.bfloat16)[None]
    masked = (cotangent[0].astype(jnp.float32) * mask[:, None]).astype(jnp.bfloat16)
    down_grad = contract_rows(own_columns(masked), everyone(active_low))
    active_grad = jnp.dot(masked, down_ffn, preferred_element_type=jnp.float32)
    gate_in_grad, up_in_grad = swiglu_back(active_grad)
    gate_in_low = gate_in_grad.astype(jnp.bfloat16)
    up_in_low = up_in_grad.astype(jnp.bfloat16)
    feed_cols = own_columns(feed_in)
    feed_gate_grad = contract_rows(feed_cols, everyone(gate_in_low))
    feed_value_grad = contract_rows(feed_cols, everyone(up_in_low))
    normed2_grad = lax.psum_scatter(
        (
            contract_cols(gate_in_low, gate_ffn) + contract_cols(up_in_low, value_ffn)
        ).astype(jnp.bfloat16),
        "head",
        scatter_dimension=0,
        tiled=True,
    ).astype(jnp.float32)
    hidden_back, feed_gain_grad = norm2_back(normed2_grad)
    hidden_grad = (
        lax.dynamic_slice_in_dim(masked, start_row, slab, 0).astype(jnp.float32) + hidden_back
    )
    mixed_in = lax.all_gather(hidden_grad.astype(jnp.bfloat16), "head", axis=0, tiled=True)
    out_grad = contract_rows(own_columns(mixed_in), everyone(gated_low))
    gated_grad = jnp.dot(mixed_in, out_full, preferred_element_type=jnp.float32)
    outs_grad, gate_pre_grad, head_gain_grad = finish_back(gated_grad)
    local_grad = entering_grad(query, key, decay, beta, outs_grad, blank)
    turned = jnp.swapaxes(mats, 1, 2)

    def relay_backward(step, carry):
        return from_behind(matmul_high(turned, carry) + local_grad, "seq", -1)

    state_grad = lax.fori_loop(0, lax.axis_size("seq") - 1, relay_backward, blank)
    recurrence_grads = delta_back((outs_grad, state_grad))
    pre_grads = prepare_back(recurrence_grads[:5])
    (
        query_pre_grad,
        key_pre_grad,
        value_pre_grad,
        alpha_pre_grad,
        beta_pre_grad,
        rates_grad,
        biases_grad,
    ) = pre_grads
    query_pre_low = query_pre_grad.astype(jnp.bfloat16)
    key_pre_low = key_pre_grad.astype(jnp.bfloat16)
    value_pre_low = value_pre_grad.astype(jnp.bfloat16)
    gate_pre_low = gate_pre_grad.astype(jnp.bfloat16)
    alpha_pre_low = alpha_pre_grad.astype(jnp.bfloat16)
    beta_pre_low = beta_pre_grad.astype(jnp.bfloat16)
    normed_cols = own_columns(normed)
    all_pre = everyone(
        jnp.concatenate(
            [query_pre_low, key_pre_low, value_pre_low, alpha_pre_low, beta_pre_low], axis=1
        )
    )
    joined_grad = contract_rows(normed_cols, all_pre)
    query_grad = joined_grad[:, :qk_cols]
    key_grad = joined_grad[:, qk_cols : 2 * qk_cols]
    value_grad = joined_grad[:, 2 * qk_cols : tail]
    alpha_grad = joined_grad[:, tail : tail + ab_cols]
    beta_grad = joined_grad[:, tail + ab_cols :]
    gate_grad = contract_rows(normed_cols, everyone(gate_pre_low))
    total = contract_cols(query_pre_low, query_full)
    total = total + contract_cols(key_pre_low, key_full)
    total = total + contract_cols(value_pre_low, value_full)
    total = total + contract_cols(gate_pre_low, gate_full)
    total = total + contract_cols(alpha_pre_low, alpha_full)
    normed_grad = lax.psum_scatter(
        (total + contract_cols(beta_pre_low, beta_full)).astype(jnp.bfloat16),
        "head",
        scatter_dimension=0,
        tiled=True,
    ).astype(jnp.float32)
    unused_rows, norm1_back = jax.vjp(rms_scale, own_rows, mixer_gain)
    rows_grad, mixer_gain_grad = norm1_back(normed_grad)
    input_grad = (hidden_grad + rows_grad).astype(jnp.bfloat16)[None]
    total_heads = decay_rate.shape[0]
    decay_full = lax.dynamic_update_slice(
        jnp.zeros((total_heads,), jnp.float32), rates_grad, (head_rank * heads_here,)
    )
    bias_full = lax.dynamic_update_slice(
        jnp.zeros((total_heads,), jnp.float32), biases_grad, (head_rank * heads_here,)
    )
    summed = (query_grad, key_grad, value_grad, gate_grad, alpha_grad, beta_grad, out_grad, feed_gate_grad, feed_value_grad, down_grad)
    small = lax.psum(
        (mixer_gain_grad, feed_gain_grad, head_gain_grad, decay_full, bias_full),
        ("dp", "seq", "head"),
    )
    return (
        outputs,
        input_grad,
        summed[0],
        summed[1],
        summed[2],
        summed[3],
        summed[4],
        summed[5],
        summed[6],
        summed[7],
        summed[8],
        summed[9],
        small[0],
        small[1],
        small[2],
        small[3],
        small[4],
    )


def solution(mesh):
    return jax.shard_map(
        on_device,
        mesh=mesh,
        in_specs=(
            P("dp", "seq", None),
            P("dp", "seq", None),
            P(),
            P(("dp", "seq"), "head"),
            P(("dp", "seq"), "head"),
            P(("dp", "seq"), "head"),
            P(("dp", "seq"), "head"),
            P(("dp", "seq"), "head"),
            P(("dp", "seq"), "head"),
            P(("dp", "seq"), "head"),
            P(("dp", "seq"), "head"),
            P(("dp", "seq"), "head"),
            P(("dp", "seq"), "head"),
            P(),
            P(),
            P(),
            P(),
            P(),
        ),
        out_specs=(
            P("dp", ("seq", "head"), None),
            P("dp", ("seq", "head"), None),
            P(("dp", "seq"), "head"),
            P(("dp", "seq"), "head"),
            P(("dp", "seq"), "head"),
            P(("dp", "seq"), "head"),
            P(("dp", "seq"), "head"),
            P(("dp", "seq"), "head"),
            P(("dp", "seq"), "head"),
            P(("dp", "seq"), "head"),
            P(("dp", "seq"), "head"),
            P(("dp", "seq"), "head"),
            P(),
            P(),
            P(),
            P(),
            P(),
        ),
        check_vma=False,
    )
```

```python
import functools

import jax
import jax.numpy as jnp
from jax import lax
from jax.experimental import pallas as pl
from jax.experimental.pallas import tpu as pltpu
from jax.sharding import PartitionSpec as P

BLOCK = 64
epsilon = 1e-06
highest = lax.Precision.HIGHEST
f32 = jnp.float32


def mm(left, right, a=1, b=0):
    return lax.dot_general(
        left, right, (((a,), (b,)), ((), ())), precision=highest, preferred_element_type=f32
    )


def mm_nt(left, right):
    return mm(left, right, 1, 1)


def mm_tn(left, right):
    return mm(left, right, 0, 0)


def each(f, *lists):
    return [f(*items) for items in zip(*lists)]


def square_masks():
    rows = lax.broadcasted_iota(jnp.int32, (BLOCK, BLOCK), 0)
    cols = lax.broadcasted_iota(jnp.int32, (BLOCK, BLOCK), 1)
    return rows >= cols, rows > cols, (rows == cols).astype(f32)


def row_factor(values):
    return lax.rsqrt(jnp.sum(values * values, axis=-1, keepdims=True) + epsilon)


def split(values, count):
    return [values[i * BLOCK : (i + 1) * BLOCK] for i in range(count)]


def decays(col_ref, row_ref, count):
    lower, strict, identity = square_masks()
    out = []
    for i in range(count):
        c_col, b_col = col_ref[0, i, :, 0:1], col_ref[0, i, :, 1:2]
        c_row, b_row = row_ref[0, i, 0:1, :], row_ref[0, i, 1:2, :]
        fade = jnp.where(lower, jnp.exp(jnp.where(lower, c_col - c_row, 0.0)), 0.0)
        last = c_col[BLOCK - 1 : BLOCK, :]
        out.append((fade, fade * b_row, jnp.exp(c_col), jnp.exp(last - c_col), b_col, jnp.exp(last)))
    return [list(items) for items in zip(*out)]


def chains(counts):
    start, out = 0, []
    for count in counts:
        out.append(range(start, start + count))
        start += count
    return out


def solve_kernel(counts, q_ref, k_ref, v_ref, col_ref, row_ref, solver_ref, scores_ref, w_ref, vt_ref, qt_ref, m_ref, b_ref, mseg_ref, bseg_ref):
    count = sum(counts)
    lower, strict, identity = square_masks()
    query = q_ref[...]
    query = split(query * row_factor(query), count)
    key = k_ref[...]
    key = split(key * row_factor(key), count)
    value = split(v_ref[...], count)
    fade, ratio, growth, remain, beta, end = decays(col_ref, row_ref, count)
    power = each(lambda k, p: jnp.where(strict, -mm_nt(k, k) * p, 0.0), key, ratio)
    solver = [identity + p for p in power]
    for _ in range((BLOCK - 1).bit_length() - 1):
        power = each(lambda p: mm(p, p), power)
        solver = each(lambda s, p: s + mm(s, p), solver, power)
    scores = each(lambda q, k, p: mm_nt(q, k) * p, query, key, ratio)
    w = each(lambda s, g, k: mm(s, g * k), solver, growth, key)
    vt = each(mm, solver, value)
    qt = each(lambda g, q, a, x: g * q - mm(a, x), growth, query, scores, w)
    weighted = each(lambda k, r, b: k * (r * b), key, remain, beta)
    size = query[0].shape[1]
    wide = (
        lax.broadcasted_iota(jnp.int32, (size, size), 0)
        == lax.broadcasted_iota(jnp.int32, (size, size), 1)
    ).astype(f32)
    m = each(lambda e, k, x: e * wide - mm_tn(k, x), end, weighted, w)
    b = each(mm_tn, weighted, vt)
    for i in range(count):
        solver_ref[0, i] = solver[i]
        scores_ref[0, i] = scores[i]
        w_ref[0, i] = w[i]
        vt_ref[0, i] = vt[i]
        qt_ref[0, i] = qt[i]
        m_ref[0, i] = m[i]
        b_ref[0, i] = b[i]
    for j, chain in enumerate(chains(counts)):
        mseg_ref[0, j] = m[chain[0]]
        bseg_ref[0, j] = b[chain[0]]
        for i in chain[1:]:
            bseg_ref[0, j] = mm(m_ref[0, i], bseg_ref[0, j]) + b_ref[0, i]
            mseg_ref[0, j] = mm(m_ref[0, i], mseg_ref[0, j])


def output_kernel(counts, state_ref, m_ref, b_ref, qt_ref, scores_ref, vt_ref, gate_ref, gain_ref, states_ref, out_ref, gated_ref):
    count = sum(counts)
    states = [None] * count
    for j, chain in enumerate(chains(counts)):
        state = state_ref[0, j]
        for i in chain:
            states[i] = state
            states_ref[0, i] = state
            if i != chain[-1]:
                state = mm(m_ref[0, i], state) + b_ref[0, i]
    gain = gain_ref[...]
    outs = [mm(qt_ref[0, i], states[i]) + mm(scores_ref[0, i], vt_ref[0, i]) for i in range(count)]
    for i in range(count):
        rows = slice(i * BLOCK, (i + 1) * BLOCK)
        out = outs[i]
        gate = gate_ref[rows, :]
        scale = lax.rsqrt(jnp.mean(out * out, axis=-1, keepdims=True) + epsilon)
        out_ref[rows, :] = out
        gated_ref[rows, :] = (out * scale * gain * (gate * jax.nn.sigmoid(gate))).astype(jnp.bfloat16)


def output_grad_kernel(counts, grad_ref, gate_ref, out_ref, gain_ref, qt_ref, m_ref, out_grad_ref, gate_grad_ref, gain_grad_ref, d_ref, dseg_ref):
    count = sum(counts)
    gain = gain_ref[...]
    gain_grad = jnp.zeros_like(gain)
    grads = []
    for i in range(count):
        rows = slice(i * BLOCK, (i + 1) * BLOCK)
        grad, gate, out = grad_ref[rows, :], gate_ref[rows, :], out_ref[rows, :]
        scale = lax.rsqrt(jnp.mean(out * out, axis=-1, keepdims=True) + epsilon)
        unit = out * scale
        sig = jax.nn.sigmoid(gate)
        normed_grad = grad * (gate * sig)
        gate_grad_ref[rows, :] = (grad * (unit * gain) * (sig * (1.0 + gate * (1.0 - sig)))).astype(jnp.bfloat16)
        gain_grad = gain_grad + jnp.sum(normed_grad * unit, axis=0, keepdims=True)
        inner = normed_grad * gain
        out_grad = scale * (inner - unit * jnp.mean(unit * inner, axis=-1, keepdims=True))
        out_grad_ref[rows, :] = out_grad
        grads.append(out_grad)
    gain_grad_ref[0] = gain_grad
    d = [mm_tn(qt_ref[0, i], grads[i]) for i in range(count)]
    for i in range(count):
        d_ref[0, i] = d[i]
    for j, chain in enumerate(chains(counts)):
        dseg_ref[0, j] = d[chain[-1]]
        for i in list(chain)[-2::-1]:
            dseg_ref[0, j] = mm_tn(m_ref[0, i], dseg_ref[0, j]) + d_ref[0, i]


def unit_back(raw, grad):
    factor = row_factor(raw)
    unit = raw * factor
    return factor * (grad - unit * jnp.sum(unit * grad, axis=-1, keepdims=True))


def grads_kernel(counts, q_ref, k_ref, col_ref, row_ref, solver_ref, scores_ref, w_ref, vt_ref, m_ref, d_ref, states_ref, out_grad_ref, later_ref, q_grad_ref, k_grad_ref, v_grad_ref, col_grad_ref, row_grad_ref):
    count = sum(counts)
    span = range(count)
    lower, strict, identity = square_masks()
    raw_q, raw_k = split(q_ref[...], count), split(k_ref[...], count)
    query = [x * row_factor(x) for x in raw_q]
    key = [x * row_factor(x) for x in raw_k]
    fade, ratio, growth, remain, beta, end = decays(col_ref, row_ref, count)
    out_grad = split(out_grad_ref[...], count)
    later = [None] * count
    for j, chain in enumerate(chains(counts)):
        state = later_ref[0, j]
        for i in list(chain)[::-1]:
            later[i] = state
            if i != chain[0]:
                state = mm_tn(m_ref[0, i], state) + d_ref[0, i]
    states = [states_ref[0, i] for i in span]
    update = [vt_ref[0, i] - mm(w_ref[0, i], states[i]) for i in span]
    update_grad = [
        mm_tn(scores_ref[0, i], out_grad[i]) + mm(key[i] * (remain[i] * beta[i]), later[i]) for i in span
    ]
    solved = [mm_tn(solver_ref[0, i], update_grad[i]) for i in span]
    scores_grad = each(mm_nt, out_grad, update)
    inner_grad = each(lambda y, u: jnp.where(strict, -mm_nt(y, u), 0.0), solved, update)
    query_dot = each(mm_nt, query, key)
    keys_dot = each(mm_nt, key, key)
    from_out = each(mm_nt, out_grad, states)
    from_solved = each(mm_nt, solved, states)
    from_update = each(mm_nt, update, later)
    weighted_scores = each(lambda p, x: p * x, ratio, scores_grad)
    weighted_inner = each(lambda p, x: p * x, ratio, inner_grad)
    q_grad = [growth[i] * from_out[i] + mm(weighted_scores[i], key[i]) for i in span]
    k_grad = [
        mm_tn(weighted_scores[i], query[i])
        + (remain[i] * beta[i]) * from_update[i]
        - growth[i] * from_solved[i]
        + mm(weighted_inner[i], key[i])
        + mm_tn(weighted_inner[i], key[i])
        for i in span
    ]
    last_row = (lax.broadcasted_iota(jnp.int32, (BLOCK, 1), 0) == BLOCK - 1).astype(f32)
    for i in span:
        rows = slice(i * BLOCK, (i + 1) * BLOCK)
        q_grad_ref[rows, :] = unit_back(raw_q[i], q_grad[i]).astype(jnp.bfloat16)
        k_grad_ref[rows, :] = unit_back(raw_k[i], k_grad[i]).astype(jnp.bfloat16)
        v_grad_ref[rows, :] = solved[i].astype(jnp.bfloat16)
        faded = fade[i] * (scores_grad[i] * query_dot[i] + inner_grad[i] * keys_dot[i])
        b_row = row_ref[0, i, 1:2, :]
        growth_grad = jnp.sum(query[i] * from_out[i] - key[i] * from_solved[i], axis=-1, keepdims=True)
        weight_grad = jnp.sum(key[i] * from_update[i], axis=-1, keepdims=True)
        pulled = remain[i] * beta[i] * weight_grad
        tail = jnp.sum(pulled, axis=0, keepdims=True) + end[i] * jnp.sum(
            jnp.sum(later[i] * states[i], axis=-1, keepdims=True), axis=0, keepdims=True
        )
        c_grad = jnp.sum(faded * b_row, axis=-1, keepdims=True) + growth[i] * growth_grad - pulled + last_row * tail
        col_grad_ref[0, i, :, 0:1] = c_grad
        col_grad_ref[0, i, :, 1:2] = remain[i] * weight_grad
        row_grad_ref[0, i] = jnp.sum(faded, axis=0, keepdims=True)


def whole(shape):
    return pl.BlockSpec((1,) + tuple(shape[1:]), lambda j: (j,) + (0,) * (len(shape) - 1))


def columns(rows, width, first=0):
    return pl.BlockSpec((rows, width), lambda j: (0, j + first))


def shaped(shape, dtype=f32):
    return jax.ShapeDtypeStruct(shape, dtype)


def call(kernel, counts, heads, inputs, outputs, flops):
    moved = sum(x.size * x.dtype.itemsize for x, _ in inputs) + sum(
        x.size * x.dtype.itemsize for x, _ in outputs
    )
    return pl.pallas_call(
        functools.partial(kernel, counts),
        grid=(heads,),
        in_specs=[s for _, s in inputs],
        out_specs=[s for _, s in outputs],
        out_shape=[x for x, _ in outputs],
        compiler_params=pltpu.CompilerParams(vmem_limit_bytes=48 << 20),
        cost_estimate=pl.CostEstimate(flops=flops, bytes_accessed=moved, transcendentals=0),
    )(*[x for x, _ in inputs])


def per_head(heads, *shape, dtype=f32):
    s = (heads,) + shape
    return shaped(s, dtype), whole(s)


def flat(array, width, first=0):
    return array, columns(array.shape[0], width, first)


def stacked(array):
    return array, whole(array.shape)


def solve(counts, heads, proj, col, row):
    n, dk, dv = sum(counts), 128, 256
    return call(
        solve_kernel, counts, heads,
        [flat(proj, dk), flat(proj, dk, heads), flat(proj, dv, heads), stacked(col), stacked(row)],
        [per_head(heads, n, BLOCK, BLOCK), per_head(heads, n, BLOCK, BLOCK), per_head(heads, n, BLOCK, dk),
         per_head(heads, n, BLOCK, dv), per_head(heads, n, BLOCK, dk), per_head(heads, n, dk, dk),
         per_head(heads, n, dk, dv), per_head(heads, len(counts), dk, dk), per_head(heads, len(counts), dk, dv)],
        heads * n * 100_000_000,
    )


def outputs_of(counts, heads, state, m, b, qt, scores, vt, gate_pre, gain):
    n, dk, dv = sum(counts), 128, 256
    rows = gate_pre.shape[0]
    cols = columns(rows, dv)
    return call(
        output_kernel, counts, heads,
        [stacked(state), stacked(m), stacked(b), stacked(qt), stacked(scores), stacked(vt), flat(gate_pre, dv),
         (gain, pl.BlockSpec((1, dv), lambda j: (0, 0)))],
        [per_head(heads, n, dk, dv), (shaped((rows, heads * dv)), cols), (shaped((rows, heads * dv), jnp.bfloat16), cols)],
        heads * n * 50_000_000,
    )


def output_grads_of(counts, heads, grad, gate_pre, outs, gain, qt, m):
    n, dk, dv = sum(counts), 128, 256
    rows = gate_pre.shape[0]
    cols = columns(rows, dv)
    return call(
        output_grad_kernel, counts, heads,
        [flat(grad, dv), flat(gate_pre, dv), flat(outs, dv), (gain, pl.BlockSpec((1, dv), lambda j: (0, 0))), stacked(qt), stacked(m)],
        [(shaped((rows, heads * dv)), cols), (shaped((rows, heads * dv), jnp.bfloat16), cols),
         per_head(heads, 1, dv), per_head(heads, n, dk, dv), per_head(heads, len(counts), dk, dv)],
        heads * n * 50_000_000,
    )


def input_grads_of(counts, heads, proj, col, row, solver, scores, w, vt, m, d, states, out_grad, later):
    n, dk, dv = sum(counts), 128, 256
    rows = proj.shape[0]
    return call(
        grads_kernel, counts, heads,
        [flat(proj, dk), flat(proj, dk, heads), stacked(col), stacked(row), stacked(solver), stacked(scores), stacked(w),
         stacked(vt), stacked(m), stacked(d), stacked(states), flat(out_grad, dv), stacked(later)],
        [(shaped((rows, heads * dk), jnp.bfloat16), columns(rows, dk)), (shaped((rows, heads * dk), jnp.bfloat16), columns(rows, dk)),
         (shaped((rows, heads * dv), jnp.bfloat16), columns(rows, dv)), per_head(heads, n, BLOCK, 2), per_head(heads, n, 1, BLOCK)],
        heads * n * 150_000_000,
    )


QUARTERS = 4


def swap(array):
    return lax.ppermute(array, "dp", [(0, 1), (1, 0)])


def from_behind(block, axis, distance):
    devices = range(lax.axis_size(axis))
    route = [(i - distance, i) for i in devices if i - distance in devices]
    return lax.ppermute(block, axis, route)


def relay(mats, offsets, distance):
    carry = from_behind(offsets, "seq", distance)
    for _ in range(lax.axis_size("seq") - 2):
        carry = from_behind(jnp.matmul(mats, carry, precision=highest) + offsets, "seq", distance)
    return carry


def everyone(part):
    return lax.all_gather(part, ("dp", "seq"), axis=0, tiled=True)


def share(rows):
    wide = jnp.broadcast_to(rows[None], (lax.axis_size("head"),) + rows.shape)
    return lax.all_to_all(wide, "head", split_axis=0, concat_axis=0, tiled=True)


def add_parts(parts):
    got = lax.all_to_all(parts.astype(jnp.bfloat16), "head", split_axis=0, concat_axis=0, tiled=True)
    return jnp.sum(got.astype(f32), axis=0)


def add_everywhere(vector):
    for axis in ("dp", "seq", "head"):
        size, step = lax.axis_size(axis), 1
        while step < size:
            vector = vector + lax.ppermute(vector, axis, [(i, i ^ step) for i in range(size)])
            step *= 2
    return vector


def contract_rows(left, right):
    return lax.dot_general(left, right, (((0,), (0,)), ((), ())), preferred_element_type=f32)


def contract_cols(left, right):
    return lax.dot_general(left, right, (((1,), (1,)), ((), ())), preferred_element_type=f32)


def product(left, right):
    return jnp.dot(left, right, preferred_element_type=f32)


def rms_scale(values, gain):
    return values * lax.rsqrt(jnp.mean(values * values, axis=-1, keepdims=True) + epsilon) * gain


def swiglu(gate_in, up_in):
    return jax.nn.silu(gate_in) * up_in


def on_device(
    activations,
    cotangent,
    lengths,
    query_weight,
    key_weight,
    value_weight,
    gate_weight,
    alpha_weight,
    beta_weight,
    out_weight,
    swiglu_gate,
    swiglu_value,
    swiglu_down,
    mixer_gain,
    feed_gain,
    head_gain,
    decay_rate,
    beta_bias,
):
    bf16 = jnp.bfloat16
    core, stage, group = lax.axis_index("dp"), lax.axis_index("seq"), lax.axis_index("head")
    stages, groups = lax.axis_size("seq"), lax.axis_size("head")
    width = activations.shape[2]
    rows0 = activations.shape[1]
    rows1 = rows0 // QUARTERS
    own0, own1 = rows0 // (2 * groups), rows1 // (2 * groups)
    own = own0 + own1
    heads = alpha_weight.shape[1] // 2
    counts = (rows0 // BLOCK, rows1 // BLOCK)
    assert groups == QUARTERS and stages % QUARTERS == 0 and rows1 % BLOCK == 0
    first = core == 0

    def part(array, size, axis, offset=0):
        return lax.dynamic_slice_in_dim(array, offset + core * size, size, axis)

    dk, dv = query_weight.shape[1] // 2, value_weight.shape[1] // 2
    slim = 2 * dk + dv
    mixer_cols = []
    for c in range(2):
        mixer_cols += [
            query_weight[:, c * dk : (c + 1) * dk],
            key_weight[:, c * dk : (c + 1) * dk],
            value_weight[:, c * dv : (c + 1) * dv],
        ]
    mixer_cols += [alpha_weight, beta_weight]
    mixer_full = everyone(jnp.concatenate(mixer_cols, axis=1).astype(bf16))
    gates_full = everyone(jnp.concatenate([gate_weight, out_weight], axis=1).astype(bf16))
    hidden_units = swiglu_gate.shape[1]
    padded = -(-hidden_units // 128) * 128
    spare = ((0, 0), (0, padded - hidden_units))
    feed_full = everyone(
        jnp.concatenate([jnp.pad(w, spare) for w in (swiglu_gate, swiglu_value, swiglu_down)], axis=1).astype(bf16)
    )
    mixer_w = part(mixer_full, slim, 1)
    rates_w = mixer_full[:, 2 * slim :]
    gate_w = part(gates_full, dv, 1)
    out_w = part(gates_full, dv, 1, 2 * dv)
    gate_ffn = feed_full[:, :padded]
    value_ffn = feed_full[:, padded : 2 * padded]
    down_ffn = feed_full[:, 2 * padded :]

    both = jnp.concatenate([activations[0], cotangent[0]], axis=1)
    arrived = jnp.zeros((rows1, 2 * width), bf16)
    for b in range(QUARTERS):
        route = [(stages + a, stages + QUARTERS * a + b) for a in range(stages // QUARTERS)]
        arrived = arrived + lax.ppermute(both[b * rows1 : (b + 1) * rows1], ("dp", "seq"), route)
    near0 = lax.ppermute(both, "dp", [(0, 1)])
    near1 = lax.ppermute(arrived, "dp", [(1, 0)])
    chip = jnp.concatenate([jnp.where(first, both, near0), jnp.where(first, near1, arrived)], axis=0)
    spots0 = stage * rows0 + lax.broadcasted_iota(jnp.int32, (rows0, 1), 0)
    spots1 = stage * rows1 + lax.broadcasted_iota(jnp.int32, (rows1, 1), 0)
    mask = jnp.concatenate([spots0 < lengths[0], spots1 < lengths[1]], axis=0).astype(f32)
    inputs = chip[:, :width].astype(f32)
    masked = (chip[:, width:].astype(f32) * mask).astype(bf16)

    def by_owner(rows):
        wide = rows.shape[1]
        r0 = rows[:rows0].reshape(groups, 2, own0, wide)
        r1 = rows[rows0:].reshape(groups, 2, own1, wide)
        return jnp.concatenate([r0, r1], axis=2).swapaxes(0, 1)

    def in_time(owned):
        wide = owned.shape[3]
        turned = owned.swapaxes(0, 1)
        return jnp.concatenate(
            [turned[:, :, :own0].reshape(rows0, wide), turned[:, :, own0:].reshape(rows1, wide)], axis=0
        )

    def of_core(owned, which):
        return lax.dynamic_index_in_dim(owned, which, 0, keepdims=False)

    def of_group(rows):
        return lax.dynamic_index_in_dim(rows, group, 0, keepdims=False)

    def add_rows(partial):
        owned = by_owner(partial)
        return add_parts(of_core(owned, core) + swap(of_core(owned, 1 - core)))

    def seq_columns(rows):
        half = part(rows, width // 2, 1)
        return lax.all_to_all(half, "seq", split_axis=1, concat_axis=0, tiled=True)

    def all_columns(rows):
        return lax.all_to_all(rows, ("dp", "seq"), split_axis=1, concat_axis=0, tiled=True)

    own_rows = of_group(of_core(by_owner(inputs), core))
    own_mask = of_group(of_core(by_owner(mask), core))
    tokens_masked = of_core(by_owner(masked), core)
    own_masked = of_group(tokens_masked).astype(f32)
    tokens_masked = tokens_masked.reshape(groups * own, width)
    masked_cols = all_columns(tokens_masked)

    normed = rms_scale(inputs, mixer_gain).astype(bf16)
    normed_cols = seq_columns(normed)
    proj = product(normed, mixer_w)
    small_pre = product(normed, rates_w)
    gate_pre = product(normed, gate_w)
    alpha_pre = part(small_pre, heads, 1)
    beta_pre = part(small_pre, heads, 1, 2 * heads)
    head0 = (2 * group + core) * heads
    rates = lax.dynamic_slice_in_dim(decay_rate, head0, heads)
    biases = lax.dynamic_slice_in_dim(beta_bias, head0, heads)
    blocks = sum(counts)

    def to_blocks(array):
        return array.T.reshape(heads, blocks, BLOCK)

    def from_blocks(array):
        return array.reshape(heads, blocks * BLOCK).T

    soft = jax.nn.softplus(alpha_pre)
    beta = jax.nn.sigmoid(beta_pre + biases)
    beta_b = to_blocks(beta)
    upto = (
        lax.broadcasted_iota(jnp.int32, (BLOCK, BLOCK), 0) <= lax.broadcasted_iota(jnp.int32, (BLOCK, BLOCK), 1)
    ).astype(f32)
    sums = jnp.matmul(to_blocks(-rates * soft), upto, precision=highest)
    col = jnp.stack([sums, beta_b], axis=-1)
    row = jnp.stack([sums, beta_b], axis=-2)
    solver, scores, w, vt, qt, m, b, mseg, bseg = solve(counts, heads, proj, col, row)
    state_in = relay(mseg, bseg, 1)
    gain_row = head_gain[None]
    states, outs, gated = outputs_of(counts, heads, state_in, m, b, qt, scores, vt, gate_pre, gain_row)
    mixed = add_rows(contract_cols(gated, out_w))
    hidden = own_rows + mixed

    normed2, norm2_back = jax.vjp(rms_scale, hidden, feed_gain)
    feed_in = share(normed2.astype(bf16)).reshape(groups * own, width)
    feed_cols = all_columns(feed_in)
    gate_in = product(feed_in, gate_ffn)
    up_in = product(feed_in, value_ffn)
    active, swiglu_back = jax.vjp(swiglu, gate_in, up_in)
    active_low = active.astype(bf16)
    feed = add_parts(contract_cols(active_low, down_ffn).reshape(groups, own, width))
    outputs_own = (own_mask * (hidden + feed)).astype(bf16)

    active_grad = product(tokens_masked, down_ffn)
    gate_in_grad, up_in_grad = swiglu_back(active_grad)
    gate_in_low, up_in_low = gate_in_grad.astype(bf16), up_in_grad.astype(bf16)
    partial = contract_cols(gate_in_low, gate_ffn) + contract_cols(up_in_low, value_ffn)
    normed2_grad = add_parts(partial.reshape(groups, own, width))
    hidden_back, feed_gain_grad = norm2_back(normed2_grad)
    hidden_grad = own_masked + hidden_back
    mixed_half = share(hidden_grad.astype(bf16))
    other_half = swap(mixed_half)
    mixed_in = in_time(
        jnp.stack([jnp.where(first, mixed_half, other_half), jnp.where(first, other_half, mixed_half)])
    )
    mixed_cols = seq_columns(mixed_in)

    gated_grad = product(mixed_in, out_w)
    outs_grad, gate_pre_low, gain_grads, d, dseg = output_grads_of(
        counts, heads, gated_grad, gate_pre, outs, gain_row, qt, m
    )
    later = relay(jnp.swapaxes(mseg, 2, 3), dseg, -1)
    query_low, key_low, value_low, col_grad, row_grad = input_grads_of(
        counts, heads, proj, col, row, solver, scores, w, vt, m, d, states, outs_grad, later
    )
    sums_grad = col_grad[..., 0] - row_grad[:, :, 0] * beta_b
    decay_back = from_blocks(jnp.matmul(sums_grad, upto.T, precision=highest))
    beta_back = beta * (1.0 - beta) * from_blocks(col_grad[..., 1] + row_grad[:, :, 0])
    rates_grad = -jnp.sum(soft * decay_back, axis=0)
    biases_grad = jnp.sum(beta_back, axis=0)
    alpha_back = -rates * jax.nn.sigmoid(alpha_pre) * decay_back
    small_low = jnp.concatenate([alpha_back, beta_back], axis=1).astype(bf16)
    slim_low = jnp.concatenate([query_low, key_low, value_low], axis=1)
    slim_all = everyone(jnp.concatenate([slim_low, small_low], axis=1))
    blank = jnp.zeros((rows0 + rows1, 4 * heads), bf16)
    spread = lax.dynamic_update_slice(blank, small_low[:, :heads], (0, core * heads))
    spread = lax.dynamic_update_slice(spread, small_low[:, heads:], (0, (2 + core) * heads))
    total = contract_cols(slim_low, mixer_w) + contract_cols(gate_pre_low, gate_w)
    normed_grad = add_rows(total + contract_cols(spread, rates_w))
    unused_rows, norm1_back = jax.vjp(rms_scale, own_rows, mixer_gain)
    rows_grad, mixer_gain_grad = norm1_back(normed_grad)
    input_own = (hidden_grad + rows_grad).astype(bf16)

    active_all = everyone(active_low)
    feed_all = everyone(jnp.concatenate([gate_in_low, up_in_low], axis=1))
    gates_all = everyone(jnp.concatenate([gate_pre_low, gated], axis=1))
    down_grad = contract_rows(masked_cols, active_all)[:, :hidden_units]
    feed_gate_grad = contract_rows(feed_cols, feed_all[:, :padded])[:, :hidden_units]
    feed_value_grad = contract_rows(feed_cols, feed_all[:, padded:])[:, :hidden_units]
    half = stages * (rows0 + rows1)
    slim_halves = [contract_rows(normed_cols, slim_all[:half]), contract_rows(normed_cols, slim_all[half:])]
    gate_grad = jnp.concatenate(
        [contract_rows(normed_cols, gates_all[:half, :dv]), contract_rows(normed_cols, gates_all[half:, :dv])], axis=1
    )
    out_grad = jnp.concatenate(
        [contract_rows(mixed_cols, gates_all[:half, dv:]), contract_rows(mixed_cols, gates_all[half:, dv:])], axis=1
    )

    def pick(start, size):
        return jnp.concatenate([g[:, start : start + size] for g in slim_halves], axis=1)

    total_heads = decay_rate.shape[0]
    none = jnp.zeros((total_heads,), f32)
    small = add_everywhere(
        jnp.concatenate(
            [
                mixer_gain_grad,
                feed_gain_grad,
                jnp.sum(gain_grads, axis=(0, 1)),
                lax.dynamic_update_slice(none, rates_grad, (head0,)),
                lax.dynamic_update_slice(none, biases_grad, (head0,)),
            ]
        )
    )
    edges = [width, 2 * width, 2 * width + head_gain.shape[0], 2 * width + head_gain.shape[0] + total_heads]

    def place(rows):
        r0, r1 = rows[:own0], rows[own0:]
        out0 = jnp.concatenate([r0, lax.ppermute(r0, "dp", [(1, 0)])], axis=0)
        pair = jnp.concatenate([lax.ppermute(r1, "dp", [(0, 1)]), r1], axis=0)
        gathered = share(pair).reshape(rows1, width)
        route = [
            ((stages + QUARTERS * a + b) * groups + b, (stages + a) * groups + b)
            for a in range(stages // QUARTERS)
            for b in range(QUARTERS)
        ]
        out1 = lax.ppermute(gathered, ("dp", "seq", "head"), route)
        return jnp.where(first, out0, out1)[None]

    return (
        place(outputs_own),
        place(input_own),
        pick(0, dk),
        pick(dk, dk),
        pick(2 * dk, dv),
        gate_grad,
        pick(slim, heads),
        pick(slim + heads, heads),
        out_grad,
        feed_gate_grad,
        feed_value_grad,
        down_grad,
        small[: edges[0]],
        small[edges[0] : edges[1]],
        small[edges[1] : edges[2]],
        small[edges[2] : edges[3]],
        small[edges[3] :],
    )


def solution(mesh):
    return jax.shard_map(
        on_device,
        mesh=mesh,
        in_specs=(
            P("dp", "seq", None),
            P("dp", "seq", None),
            P(),
            P(("dp", "seq"), "head"),
            P(("dp", "seq"), "head"),
            P(("dp", "seq"), "head"),
            P(("dp", "seq"), "head"),
            P(("dp", "seq"), "head"),
            P(("dp", "seq"), "head"),
            P(("dp", "seq"), "head"),
            P(("dp", "seq"), "head"),
            P(("dp", "seq"), "head"),
            P(("dp", "seq"), "head"),
            P(),
            P(),
            P(),
            P(),
            P(),
        ),
        out_specs=(
            P("dp", ("seq", "head"), None),
            P("dp", ("seq", "head"), None),
            P(("dp", "seq"), "head"),
            P(("dp", "seq"), "head"),
            P(("dp", "seq"), "head"),
            P(("dp", "seq"), "head"),
            P(("dp", "seq"), "head"),
            P(("dp", "seq"), "head"),
            P(("dp", "seq"), "head"),
            P(("dp", "seq"), "head"),
            P(("dp", "seq"), "head"),
            P(("dp", "seq"), "head"),
            P(),
            P(),
            P(),
            P(),
            P(),
        ),
        check_vma=False,
    )
```

```python
import functools

import jax
import jax.numpy as jnp
from jax import lax
from jax.experimental import pallas as pl
from jax.experimental.pallas import tpu as pltpu
from jax.sharding import PartitionSpec as P

BLOCK = 64
epsilon = 1e-06
highest = lax.Precision.HIGHEST
f32 = jnp.float32


def mm(left, right, a=1, b=0):
    return lax.dot_general(
        left, right, (((a,), (b,)), ((), ())), precision=highest, preferred_element_type=f32
    )


def mm_nt(left, right):
    return mm(left, right, 1, 1)


def mm_tn(left, right):
    return mm(left, right, 0, 0)


def each(f, *lists):
    return [f(*items) for items in zip(*lists)]


def square_masks():
    rows = lax.broadcasted_iota(jnp.int32, (BLOCK, BLOCK), 0)
    cols = lax.broadcasted_iota(jnp.int32, (BLOCK, BLOCK), 1)
    return rows >= cols, rows > cols, (rows == cols).astype(f32)


def row_factor(values):
    return lax.rsqrt(jnp.sum(values * values, axis=-1, keepdims=True) + epsilon)


def split(values, count):
    return [values[i * BLOCK : (i + 1) * BLOCK] for i in range(count)]


def decays(col_ref, row_ref, count):
    lower, strict, identity = square_masks()
    out = []
    for i in range(count):
        c_col, b_col = col_ref[0, i, :, 0:1], col_ref[0, i, :, 1:2]
        c_row, b_row = row_ref[0, i, 0:1, :], row_ref[0, i, 1:2, :]
        fade = jnp.where(lower, jnp.exp(jnp.where(lower, c_col - c_row, 0.0)), 0.0)
        last = c_col[BLOCK - 1 : BLOCK, :]
        out.append((fade, fade * b_row, jnp.exp(c_col), jnp.exp(last - c_col), b_col, jnp.exp(last)))
    return [list(items) for items in zip(*out)]


def chains(counts):
    start, out = 0, []
    for count in counts:
        out.append(range(start, start + count))
        start += count
    return out


def solve_kernel(counts, q_ref, k_ref, v_ref, col_ref, row_ref, solver_ref, scores_ref, w_ref, vt_ref, qt_ref, m_ref, b_ref, mseg_ref, bseg_ref):
    count = sum(counts)
    lower, strict, identity = square_masks()
    query = q_ref[...]
    query = split(query * row_factor(query), count)
    key = k_ref[...]
    key = split(key * row_factor(key), count)
    value = split(v_ref[...], count)
    fade, ratio, growth, remain, beta, end = decays(col_ref, row_ref, count)
    power = each(lambda k, p: jnp.where(strict, -mm_nt(k, k) * p, 0.0), key, ratio)
    solver = [identity + p for p in power]
    for _ in range((BLOCK - 1).bit_length() - 1):
        power = each(lambda p: mm(p, p), power)
        solver = each(lambda s, p: s + mm(s, p), solver, power)
    scores = each(lambda q, k, p: mm_nt(q, k) * p, query, key, ratio)
    w = each(lambda s, g, k: mm(s, g * k), solver, growth, key)
    vt = each(mm, solver, value)
    qt = each(lambda g, q, a, x: g * q - mm(a, x), growth, query, scores, w)
    weighted = each(lambda k, r, b: k * (r * b), key, remain, beta)
    size = query[0].shape[1]
    wide = (
        lax.broadcasted_iota(jnp.int32, (size, size), 0)
        == lax.broadcasted_iota(jnp.int32, (size, size), 1)
    ).astype(f32)
    m = each(lambda e, k, x: e * wide - mm_tn(k, x), end, weighted, w)
    b = each(mm_tn, weighted, vt)
    for i in range(count):
        solver_ref[0, i] = solver[i]
        scores_ref[0, i] = scores[i]
        w_ref[0, i] = w[i]
        vt_ref[0, i] = vt[i]
        qt_ref[0, i] = qt[i]
        m_ref[0, i] = m[i]
        b_ref[0, i] = b[i]
    for j, chain in enumerate(chains(counts)):
        mseg_ref[0, j] = m[chain[0]]
        bseg_ref[0, j] = b[chain[0]]
        for i in chain[1:]:
            bseg_ref[0, j] = mm(m_ref[0, i], bseg_ref[0, j]) + b_ref[0, i]
            mseg_ref[0, j] = mm(m_ref[0, i], mseg_ref[0, j])


def output_kernel(counts, state_ref, m_ref, b_ref, qt_ref, scores_ref, vt_ref, gate_ref, gain_ref, states_ref, out_ref, gated_ref):
    count = sum(counts)
    states = [None] * count
    for j, chain in enumerate(chains(counts)):
        state = state_ref[0, j]
        for i in chain:
            states[i] = state
            states_ref[0, i] = state
            if i != chain[-1]:
                state = mm(m_ref[0, i], state) + b_ref[0, i]
    gain = gain_ref[...]
    outs = [mm(qt_ref[0, i], states[i]) + mm(scores_ref[0, i], vt_ref[0, i]) for i in range(count)]
    for i in range(count):
        rows = slice(i * BLOCK, (i + 1) * BLOCK)
        out = outs[i]
        gate = gate_ref[rows, :]
        scale = lax.rsqrt(jnp.mean(out * out, axis=-1, keepdims=True) + epsilon)
        out_ref[rows, :] = out
        gated_ref[rows, :] = (out * scale * gain * (gate * jax.nn.sigmoid(gate))).astype(jnp.bfloat16)


def output_grad_kernel(counts, grad_ref, gate_ref, out_ref, gain_ref, qt_ref, m_ref, out_grad_ref, gate_grad_ref, gain_grad_ref, d_ref, dseg_ref):
    count = sum(counts)
    gain = gain_ref[...]
    gain_grad = jnp.zeros_like(gain)
    grads = []
    for i in range(count):
        rows = slice(i * BLOCK, (i + 1) * BLOCK)
        grad, gate, out = grad_ref[rows, :], gate_ref[rows, :], out_ref[rows, :]
        scale = lax.rsqrt(jnp.mean(out * out, axis=-1, keepdims=True) + epsilon)
        unit = out * scale
        sig = jax.nn.sigmoid(gate)
        normed_grad = grad * (gate * sig)
        gate_grad_ref[rows, :] = (grad * (unit * gain) * (sig * (1.0 + gate * (1.0 - sig)))).astype(jnp.bfloat16)
        gain_grad = gain_grad + jnp.sum(normed_grad * unit, axis=0, keepdims=True)
        inner = normed_grad * gain
        out_grad = scale * (inner - unit * jnp.mean(unit * inner, axis=-1, keepdims=True))
        out_grad_ref[rows, :] = out_grad
        grads.append(out_grad)
    gain_grad_ref[0] = gain_grad
    d = [mm_tn(qt_ref[0, i], grads[i]) for i in range(count)]
    for i in range(count):
        d_ref[0, i] = d[i]
    for j, chain in enumerate(chains(counts)):
        dseg_ref[0, j] = d[chain[-1]]
        for i in list(chain)[-2::-1]:
            dseg_ref[0, j] = mm_tn(m_ref[0, i], dseg_ref[0, j]) + d_ref[0, i]


def unit_back(raw, grad):
    factor = row_factor(raw)
    unit = raw * factor
    return factor * (grad - unit * jnp.sum(unit * grad, axis=-1, keepdims=True))


def grads_kernel(counts, q_ref, k_ref, col_ref, row_ref, solver_ref, scores_ref, w_ref, vt_ref, m_ref, d_ref, states_ref, out_grad_ref, later_ref, q_grad_ref, k_grad_ref, v_grad_ref, col_grad_ref, row_grad_ref):
    count = sum(counts)
    span = range(count)
    lower, strict, identity = square_masks()
    raw_q, raw_k = split(q_ref[...], count), split(k_ref[...], count)
    query = [x * row_factor(x) for x in raw_q]
    key = [x * row_factor(x) for x in raw_k]
    fade, ratio, growth, remain, beta, end = decays(col_ref, row_ref, count)
    out_grad = split(out_grad_ref[...], count)
    later = [None] * count
    for j, chain in enumerate(chains(counts)):
        state = later_ref[0, j]
        for i in list(chain)[::-1]:
            later[i] = state
            if i != chain[0]:
                state = mm_tn(m_ref[0, i], state) + d_ref[0, i]
    states = [states_ref[0, i] for i in span]
    update = [vt_ref[0, i] - mm(w_ref[0, i], states[i]) for i in span]
    update_grad = [
        mm_tn(scores_ref[0, i], out_grad[i]) + mm(key[i] * (remain[i] * beta[i]), later[i]) for i in span
    ]
    solved = [mm_tn(solver_ref[0, i], update_grad[i]) for i in span]
    scores_grad = each(mm_nt, out_grad, update)
    inner_grad = each(lambda y, u: jnp.where(strict, -mm_nt(y, u), 0.0), solved, update)
    query_dot = each(mm_nt, query, key)
    keys_dot = each(mm_nt, key, key)
    from_out = each(mm_nt, out_grad, states)
    from_solved = each(mm_nt, solved, states)
    from_update = each(mm_nt, update, later)
    weighted_scores = each(lambda p, x: p * x, ratio, scores_grad)
    weighted_inner = each(lambda p, x: p * x, ratio, inner_grad)
    q_grad = [growth[i] * from_out[i] + mm(weighted_scores[i], key[i]) for i in span]
    k_grad = [
        mm_tn(weighted_scores[i], query[i])
        + (remain[i] * beta[i]) * from_update[i]
        - growth[i] * from_solved[i]
        + mm(weighted_inner[i], key[i])
        + mm_tn(weighted_inner[i], key[i])
        for i in span
    ]
    last_row = (lax.broadcasted_iota(jnp.int32, (BLOCK, 1), 0) == BLOCK - 1).astype(f32)
    for i in span:
        rows = slice(i * BLOCK, (i + 1) * BLOCK)
        q_grad_ref[rows, :] = unit_back(raw_q[i], q_grad[i]).astype(jnp.bfloat16)
        k_grad_ref[rows, :] = unit_back(raw_k[i], k_grad[i]).astype(jnp.bfloat16)
        v_grad_ref[rows, :] = solved[i].astype(jnp.bfloat16)
        faded = fade[i] * (scores_grad[i] * query_dot[i] + inner_grad[i] * keys_dot[i])
        b_row = row_ref[0, i, 1:2, :]
        growth_grad = jnp.sum(query[i] * from_out[i] - key[i] * from_solved[i], axis=-1, keepdims=True)
        weight_grad = jnp.sum(key[i] * from_update[i], axis=-1, keepdims=True)
        pulled = remain[i] * beta[i] * weight_grad
        tail = jnp.sum(pulled, axis=0, keepdims=True) + end[i] * jnp.sum(
            jnp.sum(later[i] * states[i], axis=-1, keepdims=True), axis=0, keepdims=True
        )
        c_grad = jnp.sum(faded * b_row, axis=-1, keepdims=True) + growth[i] * growth_grad - pulled + last_row * tail
        col_grad_ref[0, i, :, 0:1] = c_grad
        col_grad_ref[0, i, :, 1:2] = remain[i] * weight_grad
        row_grad_ref[0, i] = jnp.sum(faded, axis=0, keepdims=True)


def whole(shape):
    return pl.BlockSpec((1,) + tuple(shape[1:]), lambda j: (j,) + (0,) * (len(shape) - 1))


def columns(rows, width, first=0):
    return pl.BlockSpec((rows, width), lambda j: (0, j + first))


def shaped(shape, dtype=f32):
    return jax.ShapeDtypeStruct(shape, dtype)


def call(kernel, counts, heads, inputs, outputs, flops):
    moved = sum(x.size * x.dtype.itemsize for x, _ in inputs) + sum(
        x.size * x.dtype.itemsize for x, _ in outputs
    )
    return pl.pallas_call(
        functools.partial(kernel, counts),
        grid=(heads,),
        in_specs=[s for _, s in inputs],
        out_specs=[s for _, s in outputs],
        out_shape=[x for x, _ in outputs],
        compiler_params=pltpu.CompilerParams(vmem_limit_bytes=48 << 20),
        cost_estimate=pl.CostEstimate(flops=flops, bytes_accessed=moved, transcendentals=0),
    )(*[x for x, _ in inputs])


def per_head(heads, *shape, dtype=f32):
    s = (heads,) + shape
    return shaped(s, dtype), whole(s)


def flat(array, width, first=0):
    return array, columns(array.shape[0], width, first)


def stacked(array):
    return array, whole(array.shape)


def solve(counts, heads, proj, col, row):
    n, dk, dv = sum(counts), 128, 256
    return call(
        solve_kernel, counts, heads,
        [flat(proj, dk), flat(proj, dk, heads), flat(proj, dv, heads), stacked(col), stacked(row)],
        [per_head(heads, n, BLOCK, BLOCK), per_head(heads, n, BLOCK, BLOCK), per_head(heads, n, BLOCK, dk),
         per_head(heads, n, BLOCK, dv), per_head(heads, n, BLOCK, dk), per_head(heads, n, dk, dk),
         per_head(heads, n, dk, dv), per_head(heads, len(counts), dk, dk), per_head(heads, len(counts), dk, dv)],
        heads * n * 100_000_000,
    )


def outputs_of(counts, heads, state, m, b, qt, scores, vt, gate_pre, gain):
    n, dk, dv = sum(counts), 128, 256
    rows = gate_pre.shape[0]
    cols = columns(rows, dv)
    return call(
        output_kernel, counts, heads,
        [stacked(state), stacked(m), stacked(b), stacked(qt), stacked(scores), stacked(vt), flat(gate_pre, dv),
         (gain, pl.BlockSpec((1, dv), lambda j: (0, 0)))],
        [per_head(heads, n, dk, dv), (shaped((rows, heads * dv)), cols), (shaped((rows, heads * dv), jnp.bfloat16), cols)],
        heads * n * 50_000_000,
    )


def output_grads_of(counts, heads, grad, gate_pre, outs, gain, qt, m):
    n, dk, dv = sum(counts), 128, 256
    rows = gate_pre.shape[0]
    cols = columns(rows, dv)
    return call(
        output_grad_kernel, counts, heads,
        [flat(grad, dv), flat(gate_pre, dv), flat(outs, dv), (gain, pl.BlockSpec((1, dv), lambda j: (0, 0))), stacked(qt), stacked(m)],
        [(shaped((rows, heads * dv)), cols), (shaped((rows, heads * dv), jnp.bfloat16), cols),
         per_head(heads, 1, dv), per_head(heads, n, dk, dv), per_head(heads, len(counts), dk, dv)],
        heads * n * 50_000_000,
    )


def input_grads_of(counts, heads, proj, col, row, solver, scores, w, vt, m, d, states, out_grad, later):
    n, dk, dv = sum(counts), 128, 256
    rows = proj.shape[0]
    return call(
        grads_kernel, counts, heads,
        [flat(proj, dk), flat(proj, dk, heads), stacked(col), stacked(row), stacked(solver), stacked(scores), stacked(w),
         stacked(vt), stacked(m), stacked(d), stacked(states), flat(out_grad, dv), stacked(later)],
        [(shaped((rows, heads * dk), jnp.bfloat16), columns(rows, dk)), (shaped((rows, heads * dk), jnp.bfloat16), columns(rows, dk)),
         (shaped((rows, heads * dv), jnp.bfloat16), columns(rows, dv)), per_head(heads, n, BLOCK, 2), per_head(heads, n, 1, BLOCK)],
        heads * n * 150_000_000,
    )


QUARTERS = 4


def swap(array):
    return lax.ppermute(array, "dp", [(0, 1), (1, 0)])


def relay(mats, offsets, forward):
    size = lax.axis_size("seq")
    entering = jnp.zeros_like(offsets)
    leaving = offsets
    for step in range(size - 1):
        route = [(step, step + 1)] if forward else [(size - 1 - step, size - 2 - step)]
        got = lax.ppermute(leaving, "seq", route)
        entering = entering + got
        if step < size - 2:
            leaving = jnp.matmul(mats, got, precision=highest) + offsets
    return entering


def everyone(part):
    return lax.all_gather(part, ("dp", "seq"), axis=0, tiled=True)


def share(rows):
    wide = jnp.broadcast_to(rows[None], (lax.axis_size("head"),) + rows.shape)
    return lax.all_to_all(wide, "head", split_axis=0, concat_axis=0, tiled=True)


def add_parts(parts):
    got = lax.all_to_all(parts.astype(jnp.bfloat16), "head", split_axis=0, concat_axis=0, tiled=True)
    return jnp.sum(got.astype(f32), axis=0)


def add_everywhere(vector):
    for axis in ("dp", "seq", "head"):
        size, step = lax.axis_size(axis), 1
        while step < size:
            vector = vector + lax.ppermute(vector, axis, [(i, i ^ step) for i in range(size)])
            step *= 2
    return vector


def contract_rows(left, right):
    return lax.dot_general(left, right, (((0,), (0,)), ((), ())), preferred_element_type=f32)


def contract_cols(left, right):
    return lax.dot_general(left, right, (((1,), (1,)), ((), ())), preferred_element_type=f32)


def product(left, right):
    return jnp.dot(left, right, preferred_element_type=f32)


def rms_scale(values, gain):
    return values * lax.rsqrt(jnp.mean(values * values, axis=-1, keepdims=True) + epsilon) * gain


def swiglu(gate_in, up_in):
    return jax.nn.silu(gate_in) * up_in


def on_device(
    activations,
    cotangent,
    lengths,
    query_weight,
    key_weight,
    value_weight,
    gate_weight,
    alpha_weight,
    beta_weight,
    out_weight,
    swiglu_gate,
    swiglu_value,
    swiglu_down,
    mixer_gain,
    feed_gain,
    head_gain,
    decay_rate,
    beta_bias,
):
    bf16 = jnp.bfloat16
    core, stage, group = lax.axis_index("dp"), lax.axis_index("seq"), lax.axis_index("head")
    stages, groups = lax.axis_size("seq"), lax.axis_size("head")
    width = activations.shape[2]
    rows0 = activations.shape[1]
    rows1 = rows0 // QUARTERS
    own0, own1 = rows0 // (2 * groups), rows1 // (2 * groups)
    own = own0 + own1
    quota = width // (2 * stages)
    heads = alpha_weight.shape[1] // 2
    counts = (rows0 // BLOCK, rows1 // BLOCK)
    assert groups == QUARTERS and stages % QUARTERS == 0 and rows1 % BLOCK == 0
    first = core == 0

    def part(array, size, axis, offset=0):
        return lax.dynamic_slice_in_dim(array, offset + core * size, size, axis)

    dk, dv = query_weight.shape[1] // 2, value_weight.shape[1] // 2
    slim = 2 * dk + dv
    mixer_cols = []
    for c in range(2):
        mixer_cols += [
            query_weight[:, c * dk : (c + 1) * dk],
            key_weight[:, c * dk : (c + 1) * dk],
            value_weight[:, c * dv : (c + 1) * dv],
        ]
    mixer_cols += [alpha_weight, beta_weight]
    mixer_full = everyone(jnp.concatenate(mixer_cols, axis=1).astype(bf16))
    gates_full = everyone(jnp.concatenate([gate_weight, out_weight], axis=1).astype(bf16))
    hidden_units = swiglu_gate.shape[1]
    padded = -(-hidden_units // 128) * 128
    spare = ((0, 0), (0, padded - hidden_units))
    feed_w = jnp.concatenate([jnp.pad(w, spare) for w in (swiglu_gate, swiglu_value, swiglu_down)], axis=1)
    feed_full = everyone(feed_w.astype(bf16))
    mixer_w = part(mixer_full, slim, 1)
    rates_w = mixer_full[:, 2 * slim :]
    gate_w = part(gates_full, dv, 1)
    out_w = part(gates_full, dv, 1, 2 * dv)
    gate_ffn = feed_full[:, :padded]
    value_ffn = feed_full[:, padded : 2 * padded]
    down_ffn = feed_full[:, 2 * padded :]

    both = jnp.concatenate([activations[0], cotangent[0]], axis=1)
    arrived = jnp.zeros((rows1, 2 * width), bf16)
    for b in range(QUARTERS):
        route = [(stages + a, stages + QUARTERS * a + b) for a in range(stages // QUARTERS)]
        arrived = arrived + lax.ppermute(both[b * rows1 : (b + 1) * rows1], ("dp", "seq"), route)
    near0 = lax.ppermute(both, "dp", [(0, 1)])
    near1 = lax.ppermute(arrived, "dp", [(1, 0)])
    chip = jnp.concatenate([jnp.where(first, both, near0), jnp.where(first, near1, arrived)], axis=0)
    spots0 = stage * rows0 + lax.broadcasted_iota(jnp.int32, (rows0, 1), 0)
    spots1 = stage * rows1 + lax.broadcasted_iota(jnp.int32, (rows1, 1), 0)
    mask = jnp.concatenate([spots0 < lengths[0], spots1 < lengths[1]], axis=0).astype(f32)
    inputs = chip[:, :width].astype(f32)
    masked = (chip[:, width:].astype(f32) * mask).astype(bf16)

    def by_owner(rows):
        wide = rows.shape[1]
        r0 = rows[:rows0].reshape(groups, 2, own0, wide)
        r1 = rows[rows0:].reshape(groups, 2, own1, wide)
        return jnp.concatenate([r0, r1], axis=2).swapaxes(0, 1)

    def in_time(owned):
        wide = owned.shape[3]
        turned = owned.swapaxes(0, 1)
        return jnp.concatenate(
            [turned[:, :, :own0].reshape(rows0, wide), turned[:, :, own0:].reshape(rows1, wide)], axis=0
        )

    def of_core(owned, which):
        return lax.dynamic_index_in_dim(owned, which, 0, keepdims=False)

    def of_group(rows):
        return lax.dynamic_index_in_dim(rows, group, 0, keepdims=False)

    def add_rows(partial):
        owned = by_owner(partial)
        return add_parts(of_core(owned, core) + swap(of_core(owned, 1 - core)))

    def seq_columns(rows):
        half = part(rows, width // 2, 1)
        return lax.all_to_all(half, "seq", split_axis=1, concat_axis=0, tiled=True)

    def here(rows):
        return lax.dynamic_slice_in_dim(rows, stage * (groups * own), groups * own, 0)

    def from_stages(rows):
        wide = jnp.broadcast_to(rows[None], (stages,) + rows.shape)
        met = lax.all_to_all(wide, "seq", split_axis=0, concat_axis=0, tiled=True)
        met = met.reshape(stages * rows.shape[0], rows.shape[1])
        return share(met).swapaxes(0, 1).reshape(met.shape[0], width)

    def own_grad(rows, grads):
        def chosen(which):
            left = lax.dynamic_slice_in_dim(rows, (which * stages + stage) * quota, quota, 1)
            return contract_rows(left, grads)

        return chosen(core) + swap(chosen(1 - core))

    own_rows = of_group(of_core(by_owner(inputs), core))
    own_mask = of_group(of_core(by_owner(mask), core))
    tokens_masked = of_core(by_owner(masked), core)
    own_masked = of_group(tokens_masked).astype(f32)
    quarter = width // groups
    masked_all = from_stages(
        lax.dynamic_slice_in_dim(tokens_masked.reshape(groups * own, width), group * quarter, quarter, 1)
    )

    normed = rms_scale(inputs, mixer_gain).astype(bf16)
    normed_cols = seq_columns(normed)
    proj = product(normed, mixer_w)
    small_pre = product(normed, rates_w)
    gate_pre = product(normed, gate_w)
    alpha_pre = part(small_pre, heads, 1)
    beta_pre = part(small_pre, heads, 1, 2 * heads)
    head0 = (2 * group + core) * heads
    rates = lax.dynamic_slice_in_dim(decay_rate, head0, heads)
    biases = lax.dynamic_slice_in_dim(beta_bias, head0, heads)
    blocks = sum(counts)

    def to_blocks(array):
        return array.T.reshape(heads, blocks, BLOCK)

    def from_blocks(array):
        return array.reshape(heads, blocks * BLOCK).T

    soft = jax.nn.softplus(alpha_pre)
    beta = jax.nn.sigmoid(beta_pre + biases)
    beta_b = to_blocks(beta)
    upto = (
        lax.broadcasted_iota(jnp.int32, (BLOCK, BLOCK), 0) <= lax.broadcasted_iota(jnp.int32, (BLOCK, BLOCK), 1)
    ).astype(f32)
    sums = jnp.matmul(to_blocks(-rates * soft), upto, precision=highest)
    col = jnp.stack([sums, beta_b], axis=-1)
    row = jnp.stack([sums, beta_b], axis=-2)
    solver, scores, w, vt, qt, m, b, mseg, bseg = solve(counts, heads, proj, col, row)
    state_in = relay(mseg, bseg, True)
    gain_row = head_gain[None]
    states, outs, gated = outputs_of(counts, heads, state_in, m, b, qt, scores, vt, gate_pre, gain_row)
    mixed = add_rows(contract_cols(gated, out_w))
    hidden = own_rows + mixed

    normed2, norm2_back = jax.vjp(rms_scale, hidden, feed_gain)
    feed_in = from_stages(
        lax.all_to_all(normed2.astype(bf16), "head", split_axis=1, concat_axis=0, tiled=True)
    )
    gate_in = product(feed_in, gate_ffn)
    up_in = product(feed_in, value_ffn)
    active, swiglu_back = jax.vjp(swiglu, gate_in, up_in)
    active_low = active.astype(bf16)
    feed = add_parts(contract_cols(here(active_low), down_ffn).reshape(groups, own, width))
    outputs_own = (own_mask * (hidden + feed)).astype(bf16)

    active_grad = product(masked_all, down_ffn)
    gate_in_grad, up_in_grad = swiglu_back(active_grad)
    gate_in_low, up_in_low = gate_in_grad.astype(bf16), up_in_grad.astype(bf16)
    partial = contract_cols(here(gate_in_low), gate_ffn) + contract_cols(here(up_in_low), value_ffn)
    normed2_grad = add_parts(partial.reshape(groups, own, width))
    hidden_back, feed_gain_grad = norm2_back(normed2_grad)
    hidden_grad = own_masked + hidden_back
    mixed_half = share(hidden_grad.astype(bf16))
    other_half = swap(mixed_half)
    mixed_in = in_time(
        jnp.stack([jnp.where(first, mixed_half, other_half), jnp.where(first, other_half, mixed_half)])
    )
    mixed_cols = seq_columns(mixed_in)

    gated_grad = product(mixed_in, out_w)
    outs_grad, gate_pre_low, gain_grads, d, dseg = output_grads_of(
        counts, heads, gated_grad, gate_pre, outs, gain_row, qt, m
    )
    later = relay(jnp.swapaxes(mseg, 2, 3), dseg, False)
    query_low, key_low, value_low, col_grad, row_grad = input_grads_of(
        counts, heads, proj, col, row, solver, scores, w, vt, m, d, states, outs_grad, later
    )
    sums_grad = col_grad[..., 0] - row_grad[:, :, 0] * beta_b
    decay_back = from_blocks(jnp.matmul(sums_grad, upto.T, precision=highest))
    beta_back = beta * (1.0 - beta) * from_blocks(col_grad[..., 1] + row_grad[:, :, 0])
    rates_grad = -jnp.sum(soft * decay_back, axis=0)
    biases_grad = jnp.sum(beta_back, axis=0)
    alpha_back = -rates * jax.nn.sigmoid(alpha_pre) * decay_back
    small_low = jnp.concatenate([alpha_back, beta_back], axis=1).astype(bf16)
    slim_low = jnp.concatenate([query_low, key_low, value_low], axis=1)
    blank = jnp.zeros((rows0 + rows1, 4 * heads), bf16)
    spread = lax.dynamic_update_slice(blank, small_low[:, :heads], (0, core * heads))
    spread = lax.dynamic_update_slice(spread, small_low[:, heads:], (0, (2 + core) * heads))
    total = contract_cols(slim_low, mixer_w) + contract_cols(gate_pre_low, gate_w)
    normed_grad = add_rows(total + contract_cols(spread, rates_w))
    unused_rows, norm1_back = jax.vjp(rms_scale, own_rows, mixer_gain)
    rows_grad, mixer_gain_grad = norm1_back(normed_grad)
    input_own = (hidden_grad + rows_grad).astype(bf16)

    gates_all = everyone(jnp.concatenate([gate_pre_low, gated], axis=1))
    slim_all = everyone(jnp.concatenate([slim_low, small_low], axis=1))
    down_grad = own_grad(masked_all, active_low)[:, :hidden_units]
    feed_gate_grad = own_grad(feed_in, gate_in_low)[:, :hidden_units]
    feed_value_grad = own_grad(feed_in, up_in_low)[:, :hidden_units]
    half = stages * (rows0 + rows1)
    slim_halves = [contract_rows(normed_cols, slim_all[:half]), contract_rows(normed_cols, slim_all[half:])]
    gate_grad = jnp.concatenate(
        [contract_rows(normed_cols, gates_all[:half, :dv]), contract_rows(normed_cols, gates_all[half:, :dv])], axis=1
    )
    out_grad = jnp.concatenate(
        [contract_rows(mixed_cols, gates_all[:half, dv:]), contract_rows(mixed_cols, gates_all[half:, dv:])], axis=1
    )

    def pick(start, size):
        return jnp.concatenate([g[:, start : start + size] for g in slim_halves], axis=1)

    total_heads = decay_rate.shape[0]
    none = jnp.zeros((total_heads,), f32)
    small = add_everywhere(
        jnp.concatenate(
            [
                mixer_gain_grad,
                feed_gain_grad,
                jnp.sum(gain_grads, axis=(0, 1)),
                lax.dynamic_update_slice(none, rates_grad, (head0,)),
                lax.dynamic_update_slice(none, biases_grad, (head0,)),
            ]
        )
    )
    edges = [width, 2 * width, 2 * width + head_gain.shape[0], 2 * width + head_gain.shape[0] + total_heads]

    def place(rows):
        r0, r1 = rows[:own0], rows[own0:]
        out0 = jnp.concatenate([r0, lax.ppermute(r0, "dp", [(1, 0)])], axis=0)
        pair = jnp.concatenate([lax.ppermute(r1, "dp", [(0, 1)]), r1], axis=0)
        gathered = share(pair).reshape(rows1, width)
        route = [
            ((stages + QUARTERS * a + b) * groups + b, (stages + a) * groups + b)
            for a in range(stages // QUARTERS)
            for b in range(QUARTERS)
        ]
        out1 = lax.ppermute(gathered, ("dp", "seq", "head"), route)
        return jnp.where(first, out0, out1)[None]

    return (
        place(outputs_own),
        place(input_own),
        pick(0, dk),
        pick(dk, dk),
        pick(2 * dk, dv),
        gate_grad,
        pick(slim, heads),
        pick(slim + heads, heads),
        out_grad,
        feed_gate_grad,
        feed_value_grad,
        down_grad,
        small[: edges[0]],
        small[edges[0] : edges[1]],
        small[edges[1] : edges[2]],
        small[edges[2] : edges[3]],
        small[edges[3] :],
    )


def solution(mesh):
    return jax.shard_map(
        on_device,
        mesh=mesh,
        in_specs=(
            P("dp", "seq", None),
            P("dp", "seq", None),
            P(),
            P(("dp", "seq"), "head"),
            P(("dp", "seq"), "head"),
            P(("dp", "seq"), "head"),
            P(("dp", "seq"), "head"),
            P(("dp", "seq"), "head"),
            P(("dp", "seq"), "head"),
            P(("dp", "seq"), "head"),
            P(("dp", "seq"), "head"),
            P(("dp", "seq"), "head"),
            P(("dp", "seq"), "head"),
            P(),
            P(),
            P(),
            P(),
            P(),
        ),
        out_specs=(
            P("dp", ("seq", "head"), None),
            P("dp", ("seq", "head"), None),
            P(("dp", "seq"), "head"),
            P(("dp", "seq"), "head"),
            P(("dp", "seq"), "head"),
            P(("dp", "seq"), "head"),
            P(("dp", "seq"), "head"),
            P(("dp", "seq"), "head"),
            P(("dp", "seq"), "head"),
            P(("dp", "seq"), "head"),
            P(("dp", "seq"), "head"),
            P(("dp", "seq"), "head"),
            P(),
            P(),
            P(),
            P(),
            P(),
        ),
        check_vma=False,
    )
```

```python
import functools

import jax
import jax.numpy as jnp
from jax import lax
from jax.experimental import pallas as pl
from jax.experimental.pallas import tpu as pltpu
from jax.sharding import PartitionSpec as P

BLOCK = 64
epsilon = 1e-06
highest = lax.Precision.HIGHEST
f32 = jnp.float32


def mm(left, right, a=1, b=0):
    return lax.dot_general(
        left, right, (((a,), (b,)), ((), ())), precision=highest, preferred_element_type=f32
    )


def mm_nt(left, right):
    return mm(left, right, 1, 1)


def mm_tn(left, right):
    return mm(left, right, 0, 0)


def each(f, *lists):
    return [f(*items) for items in zip(*lists)]


def square_masks():
    rows = lax.broadcasted_iota(jnp.int32, (BLOCK, BLOCK), 0)
    cols = lax.broadcasted_iota(jnp.int32, (BLOCK, BLOCK), 1)
    return rows >= cols, rows > cols, (rows == cols).astype(f32)


def row_factor(values):
    return lax.rsqrt(jnp.sum(values * values, axis=-1, keepdims=True) + epsilon)


def split(values, count):
    return [values[i * BLOCK : (i + 1) * BLOCK] for i in range(count)]


def decays(col_ref, row_ref, count):
    lower, strict, identity = square_masks()
    out = []
    for i in range(count):
        c_col, b_col = col_ref[0, i, :, 0:1], col_ref[0, i, :, 1:2]
        c_row, b_row = row_ref[0, i, 0:1, :], row_ref[0, i, 1:2, :]
        fade = jnp.where(lower, jnp.exp(jnp.where(lower, c_col - c_row, 0.0)), 0.0)
        last = c_col[BLOCK - 1 : BLOCK, :]
        out.append((fade, fade * b_row, jnp.exp(c_col), jnp.exp(last - c_col), b_col, jnp.exp(last)))
    return [list(items) for items in zip(*out)]


def chains(counts):
    start, out = 0, []
    for count in counts:
        out.append(range(start, start + count))
        start += count
    return out


def solve_kernel(counts, q_ref, k_ref, v_ref, col_ref, row_ref, solver_ref, scores_ref, w_ref, vt_ref, qt_ref, m_ref, b_ref, mseg_ref, bseg_ref):
    count = sum(counts)
    lower, strict, identity = square_masks()
    query = q_ref[...]
    query = split(query * row_factor(query), count)
    key = k_ref[...]
    key = split(key * row_factor(key), count)
    value = split(v_ref[...], count)
    fade, ratio, growth, remain, beta, end = decays(col_ref, row_ref, count)
    power = each(lambda k, p: jnp.where(strict, -mm_nt(k, k) * p, 0.0), key, ratio)
    solver = [identity + p for p in power]
    for _ in range((BLOCK - 1).bit_length() - 1):
        power = each(lambda p: mm(p, p), power)
        solver = each(lambda s, p: s + mm(s, p), solver, power)
    scores = each(lambda q, k, p: mm_nt(q, k) * p, query, key, ratio)
    w = each(lambda s, g, k: mm(s, g * k), solver, growth, key)
    vt = each(mm, solver, value)
    qt = each(lambda g, q, a, x: g * q - mm(a, x), growth, query, scores, w)
    weighted = each(lambda k, r, b: k * (r * b), key, remain, beta)
    size = query[0].shape[1]
    wide = (
        lax.broadcasted_iota(jnp.int32, (size, size), 0)
        == lax.broadcasted_iota(jnp.int32, (size, size), 1)
    ).astype(f32)
    m = each(lambda e, k, x: e * wide - mm_tn(k, x), end, weighted, w)
    b = each(mm_tn, weighted, vt)
    for i in range(count):
        solver_ref[0, i] = solver[i]
        scores_ref[0, i] = scores[i]
        w_ref[0, i] = w[i]
        vt_ref[0, i] = vt[i]
        qt_ref[0, i] = qt[i]
        m_ref[0, i] = m[i]
        b_ref[0, i] = b[i]
    for j, chain in enumerate(chains(counts)):
        mseg_ref[0, j] = m[chain[0]]
        bseg_ref[0, j] = b[chain[0]]
        for i in chain[1:]:
            bseg_ref[0, j] = mm(m_ref[0, i], bseg_ref[0, j]) + b_ref[0, i]
            mseg_ref[0, j] = mm(m_ref[0, i], mseg_ref[0, j])


def output_kernel(counts, state_ref, m_ref, b_ref, qt_ref, scores_ref, vt_ref, gate_ref, gain_ref, states_ref, out_ref, gated_ref):
    count = sum(counts)
    states = [None] * count
    for j, chain in enumerate(chains(counts)):
        state = state_ref[0, j]
        for i in chain:
            states[i] = state
            states_ref[0, i] = state
            if i != chain[-1]:
                state = mm(m_ref[0, i], state) + b_ref[0, i]
    gain = gain_ref[...]
    outs = [mm(qt_ref[0, i], states[i]) + mm(scores_ref[0, i], vt_ref[0, i]) for i in range(count)]
    for i in range(count):
        rows = slice(i * BLOCK, (i + 1) * BLOCK)
        out = outs[i]
        gate = gate_ref[rows, :]
        scale = lax.rsqrt(jnp.mean(out * out, axis=-1, keepdims=True) + epsilon)
        out_ref[rows, :] = out
        gated_ref[rows, :] = (out * scale * gain * (gate * jax.nn.sigmoid(gate))).astype(jnp.bfloat16)


def output_grad_kernel(counts, grad_ref, gate_ref, out_ref, gain_ref, qt_ref, m_ref, out_grad_ref, gate_grad_ref, gain_grad_ref, d_ref, dseg_ref):
    count = sum(counts)
    gain = gain_ref[...]
    gain_grad = jnp.zeros_like(gain)
    grads = []
    for i in range(count):
        rows = slice(i * BLOCK, (i + 1) * BLOCK)
        grad, gate, out = grad_ref[rows, :], gate_ref[rows, :], out_ref[rows, :]
        scale = lax.rsqrt(jnp.mean(out * out, axis=-1, keepdims=True) + epsilon)
        unit = out * scale
        sig = jax.nn.sigmoid(gate)
        normed_grad = grad * (gate * sig)
        gate_grad_ref[rows, :] = (grad * (unit * gain) * (sig * (1.0 + gate * (1.0 - sig)))).astype(jnp.bfloat16)
        gain_grad = gain_grad + jnp.sum(normed_grad * unit, axis=0, keepdims=True)
        inner = normed_grad * gain
        out_grad = scale * (inner - unit * jnp.mean(unit * inner, axis=-1, keepdims=True))
        out_grad_ref[rows, :] = out_grad
        grads.append(out_grad)
    gain_grad_ref[0] = gain_grad
    d = [mm_tn(qt_ref[0, i], grads[i]) for i in range(count)]
    for i in range(count):
        d_ref[0, i] = d[i]
    for j, chain in enumerate(chains(counts)):
        dseg_ref[0, j] = d[chain[-1]]
        for i in list(chain)[-2::-1]:
            dseg_ref[0, j] = mm_tn(m_ref[0, i], dseg_ref[0, j]) + d_ref[0, i]


def unit_back(raw, grad):
    factor = row_factor(raw)
    unit = raw * factor
    return factor * (grad - unit * jnp.sum(unit * grad, axis=-1, keepdims=True))


def grads_kernel(counts, q_ref, k_ref, col_ref, row_ref, solver_ref, scores_ref, w_ref, vt_ref, m_ref, d_ref, states_ref, out_grad_ref, later_ref, q_grad_ref, k_grad_ref, v_grad_ref, col_grad_ref, row_grad_ref):
    count = sum(counts)
    span = range(count)
    lower, strict, identity = square_masks()
    raw_q, raw_k = split(q_ref[...], count), split(k_ref[...], count)
    query = [x * row_factor(x) for x in raw_q]
    key = [x * row_factor(x) for x in raw_k]
    fade, ratio, growth, remain, beta, end = decays(col_ref, row_ref, count)
    out_grad = split(out_grad_ref[...], count)
    later = [None] * count
    for j, chain in enumerate(chains(counts)):
        state = later_ref[0, j]
        for i in list(chain)[::-1]:
            later[i] = state
            if i != chain[0]:
                state = mm_tn(m_ref[0, i], state) + d_ref[0, i]
    states = [states_ref[0, i] for i in span]
    update = [vt_ref[0, i] - mm(w_ref[0, i], states[i]) for i in span]
    update_grad = [
        mm_tn(scores_ref[0, i], out_grad[i]) + mm(key[i] * (remain[i] * beta[i]), later[i]) for i in span
    ]
    solved = [mm_tn(solver_ref[0, i], update_grad[i]) for i in span]
    scores_grad = each(mm_nt, out_grad, update)
    inner_grad = each(lambda y, u: jnp.where(strict, -mm_nt(y, u), 0.0), solved, update)
    query_dot = each(mm_nt, query, key)
    keys_dot = each(mm_nt, key, key)
    from_out = each(mm_nt, out_grad, states)
    from_solved = each(mm_nt, solved, states)
    from_update = each(mm_nt, update, later)
    weighted_scores = each(lambda p, x: p * x, ratio, scores_grad)
    weighted_inner = each(lambda p, x: p * x, ratio, inner_grad)
    q_grad = [growth[i] * from_out[i] + mm(weighted_scores[i], key[i]) for i in span]
    k_grad = [
        mm_tn(weighted_scores[i], query[i])
        + (remain[i] * beta[i]) * from_update[i]
        - growth[i] * from_solved[i]
        + mm(weighted_inner[i], key[i])
        + mm_tn(weighted_inner[i], key[i])
        for i in span
    ]
    last_row = (lax.broadcasted_iota(jnp.int32, (BLOCK, 1), 0) == BLOCK - 1).astype(f32)
    for i in span:
        rows = slice(i * BLOCK, (i + 1) * BLOCK)
        q_grad_ref[rows, :] = unit_back(raw_q[i], q_grad[i]).astype(jnp.bfloat16)
        k_grad_ref[rows, :] = unit_back(raw_k[i], k_grad[i]).astype(jnp.bfloat16)
        v_grad_ref[rows, :] = solved[i].astype(jnp.bfloat16)
        faded = fade[i] * (scores_grad[i] * query_dot[i] + inner_grad[i] * keys_dot[i])
        b_row = row_ref[0, i, 1:2, :]
        growth_grad = jnp.sum(query[i] * from_out[i] - key[i] * from_solved[i], axis=-1, keepdims=True)
        weight_grad = jnp.sum(key[i] * from_update[i], axis=-1, keepdims=True)
        pulled = remain[i] * beta[i] * weight_grad
        tail = jnp.sum(pulled, axis=0, keepdims=True) + end[i] * jnp.sum(
            jnp.sum(later[i] * states[i], axis=-1, keepdims=True), axis=0, keepdims=True
        )
        c_grad = jnp.sum(faded * b_row, axis=-1, keepdims=True) + growth[i] * growth_grad - pulled + last_row * tail
        col_grad_ref[0, i, :, 0:1] = c_grad
        col_grad_ref[0, i, :, 1:2] = remain[i] * weight_grad
        row_grad_ref[0, i] = jnp.sum(faded, axis=0, keepdims=True)


def whole(shape):
    return pl.BlockSpec((1,) + tuple(shape[1:]), lambda j: (j,) + (0,) * (len(shape) - 1))


def columns(rows, width, first=0):
    return pl.BlockSpec((rows, width), lambda j: (0, j + first))


def shaped(shape, dtype=f32):
    return jax.ShapeDtypeStruct(shape, dtype)


def call(kernel, counts, heads, inputs, outputs, flops):
    moved = sum(x.size * x.dtype.itemsize for x, _ in inputs) + sum(
        x.size * x.dtype.itemsize for x, _ in outputs
    )
    return pl.pallas_call(
        functools.partial(kernel, counts),
        grid=(heads,),
        in_specs=[s for _, s in inputs],
        out_specs=[s for _, s in outputs],
        out_shape=[x for x, _ in outputs],
        compiler_params=pltpu.CompilerParams(vmem_limit_bytes=48 << 20),
        cost_estimate=pl.CostEstimate(flops=flops, bytes_accessed=moved, transcendentals=0),
    )(*[x for x, _ in inputs])


def per_head(heads, *shape, dtype=f32):
    s = (heads,) + shape
    return shaped(s, dtype), whole(s)


def flat(array, width, first=0):
    return array, columns(array.shape[0], width, first)


def stacked(array):
    return array, whole(array.shape)


def solve(counts, heads, proj, col, row):
    n, dk, dv = sum(counts), 128, 256
    return call(
        solve_kernel, counts, heads,
        [flat(proj, dk), flat(proj, dk, heads), flat(proj, dv, heads), stacked(col), stacked(row)],
        [per_head(heads, n, BLOCK, BLOCK), per_head(heads, n, BLOCK, BLOCK), per_head(heads, n, BLOCK, dk),
         per_head(heads, n, BLOCK, dv), per_head(heads, n, BLOCK, dk), per_head(heads, n, dk, dk),
         per_head(heads, n, dk, dv), per_head(heads, len(counts), dk, dk), per_head(heads, len(counts), dk, dv)],
        heads * n * 100_000_000,
    )


def outputs_of(counts, heads, state, m, b, qt, scores, vt, gate_pre, gain):
    n, dk, dv = sum(counts), 128, 256
    rows = gate_pre.shape[0]
    cols = columns(rows, dv)
    return call(
        output_kernel, counts, heads,
        [stacked(state), stacked(m), stacked(b), stacked(qt), stacked(scores), stacked(vt), flat(gate_pre, dv),
         (gain, pl.BlockSpec((1, dv), lambda j: (0, 0)))],
        [per_head(heads, n, dk, dv), (shaped((rows, heads * dv)), cols), (shaped((rows, heads * dv), jnp.bfloat16), cols)],
        heads * n * 50_000_000,
    )


def output_grads_of(counts, heads, grad, gate_pre, outs, gain, qt, m):
    n, dk, dv = sum(counts), 128, 256
    rows = gate_pre.shape[0]
    cols = columns(rows, dv)
    return call(
        output_grad_kernel, counts, heads,
        [flat(grad, dv), flat(gate_pre, dv), flat(outs, dv), (gain, pl.BlockSpec((1, dv), lambda j: (0, 0))), stacked(qt), stacked(m)],
        [(shaped((rows, heads * dv)), cols), (shaped((rows, heads * dv), jnp.bfloat16), cols),
         per_head(heads, 1, dv), per_head(heads, n, dk, dv), per_head(heads, len(counts), dk, dv)],
        heads * n * 50_000_000,
    )


def input_grads_of(counts, heads, proj, col, row, solver, scores, w, vt, m, d, states, out_grad, later):
    n, dk, dv = sum(counts), 128, 256
    rows = proj.shape[0]
    return call(
        grads_kernel, counts, heads,
        [flat(proj, dk), flat(proj, dk, heads), stacked(col), stacked(row), stacked(solver), stacked(scores), stacked(w),
         stacked(vt), stacked(m), stacked(d), stacked(states), flat(out_grad, dv), stacked(later)],
        [(shaped((rows, heads * dk), jnp.bfloat16), columns(rows, dk)), (shaped((rows, heads * dk), jnp.bfloat16), columns(rows, dk)),
         (shaped((rows, heads * dv), jnp.bfloat16), columns(rows, dv)), per_head(heads, n, BLOCK, 2), per_head(heads, n, 1, BLOCK)],
        heads * n * 150_000_000,
    )


def feed_kernel(stage_ref, x_ref, k_ref, xs_ref, ks_ref, w1_ref, w3_ref, w2_ref, t1_ref, t3_ref, t2_ref, feed_ref, back_ref, main_ref, tail_ref, active_s, gate_s, up_s):
    step, chunk = pl.program_id(0), pl.program_id(1)
    own = feed_ref.shape[0]
    near = x_ref.shape[0] // own
    stage = stage_ref[0]
    here = pl.ds(pl.multiple_of(lax.rem(stage, near) * own, own), own)

    @pl.when((step == 0) & (chunk == 0))
    def _():
        feed_ref[...] = jnp.zeros_like(feed_ref)
        back_ref[...] = jnp.zeros_like(back_ref)

    def work(w1, w3, w2, out_ref):
        wide = w1.shape[1]
        gate = jnp.dot(x_ref[...], w1[...], preferred_element_type=f32)
        up = jnp.dot(x_ref[...], w3[...], preferred_element_type=f32)
        grad = jnp.dot(k_ref[...], w2[...], preferred_element_type=f32)
        sig = jax.nn.sigmoid(gate)
        silu = gate * sig
        active = (silu * up).astype(jnp.bfloat16)
        gate_grad = (grad * up * (sig * (1.0 + gate * (1.0 - sig)))).astype(jnp.bfloat16)
        up_grad = (grad * silu).astype(jnp.bfloat16)
        active_s[:, :wide] = active
        gate_s[:, :wide] = gate_grad
        up_s[:, :wide] = up_grad

        @pl.when(chunk == stage // near)
        def _():
            feed_ref[...] += contract_cols(active_s[here, :wide], w2[...])
            back_ref[...] += contract_cols(gate_s[here, :wide], w1[...])
            back_ref[...] += contract_cols(up_s[here, :wide], w3[...])

        parts = (
            jnp.dot(xs_ref[...], gate_grad, preferred_element_type=f32),
            jnp.dot(xs_ref[...], up_grad, preferred_element_type=f32),
            jnp.dot(ks_ref[...], active, preferred_element_type=f32),
        )
        for i, p in enumerate(parts):
            place = slice(i * wide, (i + 1) * wide)

            @pl.when(chunk == 0)
            def _():
                out_ref[:, place] = p

            @pl.when(chunk > 0)
            def _():
                out_ref[:, place] += p

    work(w1_ref, w3_ref, w2_ref, main_ref)

    @pl.when(step == pl.num_programs(0) - 1)
    def _():
        work(t1_ref, t3_ref, t2_ref, tail_ref)


def feed_forward(stage, rows, grads, row_cols, grad_cols, weights, own):
    positions, width = rows.shape
    picked = row_cols.shape[0]
    tile, rest = 256, 128
    steps = (weights.shape[1] - 3 * rest) // (3 * tile)
    chunk = min(positions, 4 * own)
    first_tail = 3 * steps * tile // rest
    grid = (steps, positions // chunk)
    tokens = pl.BlockSpec((chunk, width), lambda i, t, s: (t, 0))
    columns_of = pl.BlockSpec((picked, chunk), lambda i, t, s: (0, t))

    def main_of(n):
        return pl.BlockSpec((width, tile), lambda i, t, s: (0, n * steps + i))

    def tail_of(n):
        return pl.BlockSpec((width, rest), lambda i, t, s: (0, first_tail + n))

    def fixed(*shape):
        return pl.BlockSpec(shape, lambda i, t, s: (0, 0))

    flops = 2 * positions * width * weights.shape[1] + 2 * own * width * weights.shape[1] + 2 * positions * picked * weights.shape[1]
    return pl.pallas_call(
        feed_kernel,
        grid_spec=pltpu.PrefetchScalarGridSpec(
            num_scalar_prefetch=1,
            grid=grid,
            in_specs=[tokens, tokens, columns_of, columns_of, main_of(0), main_of(1), main_of(2), tail_of(0), tail_of(1), tail_of(2)],
            out_specs=[
                fixed(own, width),
                fixed(own, width),
                pl.BlockSpec((picked, 3 * tile), lambda i, t, s: (0, i)),
                fixed(picked, 3 * rest),
            ],
            scratch_shapes=[pltpu.VMEM((chunk, tile), jnp.bfloat16)] * 3,
        ),
        out_shape=[
            shaped((own, width)),
            shaped((own, width)),
            shaped((picked, 3 * tile * steps)),
            shaped((picked, 3 * rest)),
        ],
        compiler_params=pltpu.CompilerParams(
            dimension_semantics=("arbitrary", "arbitrary"), vmem_limit_bytes=56 << 20
        ),
        cost_estimate=pl.CostEstimate(
            flops=flops, bytes_accessed=2 * weights.size + 8 * positions * width, transcendentals=0
        ),
    )(stage, rows, grads, row_cols, grad_cols, weights, weights, weights, weights, weights, weights)


QUARTERS = 4


def swap(array):
    return lax.ppermute(array, "dp", [(0, 1), (1, 0)])


def relay(mats, offsets, forward):
    size = lax.axis_size("seq")
    entering = jnp.zeros_like(offsets)
    leaving = offsets
    for step in range(size - 1):
        route = [(step, step + 1)] if forward else [(size - 1 - step, size - 2 - step)]
        got = lax.ppermute(leaving, "seq", route)
        entering = entering + got
        if step < size - 2:
            leaving = jnp.matmul(mats, got, precision=highest) + offsets
    return entering, leaving


def together(*arrays):
    return lax.optimization_barrier(arrays)


def everyone(part):
    return lax.all_gather(part, ("dp", "seq"), axis=0, tiled=True)


def share(rows):
    wide = jnp.broadcast_to(rows[None], (lax.axis_size("head"),) + rows.shape)
    return lax.all_to_all(wide, "head", split_axis=0, concat_axis=0, tiled=True)


def add_parts(parts):
    got = lax.all_to_all(parts.astype(jnp.bfloat16), "head", split_axis=0, concat_axis=0, tiled=True)
    return jnp.sum(got.astype(f32), axis=0)


def add_everywhere(vector):
    for axis in ("dp", "seq", "head"):
        size, step = lax.axis_size(axis), 1
        while step < size:
            vector = vector + lax.ppermute(vector, axis, [(i, i ^ step) for i in range(size)])
            step *= 2
    return vector


def contract_rows(left, right):
    return lax.dot_general(left, right, (((0,), (0,)), ((), ())), preferred_element_type=f32)


def contract_cols(left, right):
    return lax.dot_general(left, right, (((1,), (1,)), ((), ())), preferred_element_type=f32)


def product(left, right):
    return jnp.dot(left, right, preferred_element_type=f32)


def rms_scale(values, gain):
    return values * lax.rsqrt(jnp.mean(values * values, axis=-1, keepdims=True) + epsilon) * gain


def swiglu(gate_in, up_in):
    return jax.nn.silu(gate_in) * up_in


def on_device(
    activations,
    cotangent,
    lengths,
    query_weight,
    key_weight,
    value_weight,
    gate_weight,
    alpha_weight,
    beta_weight,
    out_weight,
    swiglu_gate,
    swiglu_value,
    swiglu_down,
    mixer_gain,
    feed_gain,
    head_gain,
    decay_rate,
    beta_bias,
):
    bf16 = jnp.bfloat16
    core, stage, group = lax.axis_index("dp"), lax.axis_index("seq"), lax.axis_index("head")
    stages, groups = lax.axis_size("seq"), lax.axis_size("head")
    width = activations.shape[2]
    rows0 = activations.shape[1]
    rows1 = rows0 // QUARTERS
    own0, own1 = rows0 // (2 * groups), rows1 // (2 * groups)
    own = own0 + own1
    quota = width // (2 * stages)
    heads = alpha_weight.shape[1] // 2
    counts = (rows0 // BLOCK, rows1 // BLOCK)
    assert groups == QUARTERS and stages % QUARTERS == 0 and rows1 % BLOCK == 0
    first = core == 0

    def part(array, size, axis, offset=0):
        return lax.dynamic_slice_in_dim(array, offset + core * size, size, axis)

    dk, dv = query_weight.shape[1] // 2, value_weight.shape[1] // 2
    slim = 2 * dk + dv
    mixer_cols = []
    for c in range(2):
        mixer_cols += [
            query_weight[:, c * dk : (c + 1) * dk],
            key_weight[:, c * dk : (c + 1) * dk],
            value_weight[:, c * dv : (c + 1) * dv],
        ]
    mixer_cols += [gate_weight, out_weight, alpha_weight, beta_weight]
    mixer_full = everyone(jnp.concatenate(mixer_cols, axis=1).astype(bf16))
    hidden_units = swiglu_gate.shape[1]
    even = hidden_units // 256 * 256
    odd = hidden_units - even
    assert 0 < odd <= 128
    three = (swiglu_gate, swiglu_value, swiglu_down)
    spare = ((0, 0), (0, 128 - odd))
    feed_full = everyone(
        jnp.concatenate([w[:, :even] for w in three] + [jnp.pad(w[:, even:], spare) for w in three], axis=1).astype(bf16)
    )

    both = jnp.concatenate([activations[0], cotangent[0]], axis=1)
    arrived = jnp.zeros((rows1, 2 * width), bf16)
    for b in range(QUARTERS):
        route = [(stages + a, stages + QUARTERS * a + b) for a in range(stages // QUARTERS)]
        arrived = arrived + lax.ppermute(both[b * rows1 : (b + 1) * rows1], ("dp", "seq"), route)
    near0 = lax.ppermute(both, "dp", [(0, 1)])
    near1 = lax.ppermute(arrived, "dp", [(1, 0)])
    chip = jnp.concatenate([jnp.where(first, both, near0), jnp.where(first, near1, arrived)], axis=0)
    spots0 = stage * rows0 + lax.broadcasted_iota(jnp.int32, (rows0, 1), 0)
    spots1 = stage * rows1 + lax.broadcasted_iota(jnp.int32, (rows1, 1), 0)
    mask = jnp.concatenate([spots0 < lengths[0], spots1 < lengths[1]], axis=0).astype(f32)
    inputs = chip[:, :width].astype(f32)
    masked = (chip[:, width:].astype(f32) * mask).astype(bf16)

    def by_owner(rows):
        wide = rows.shape[1]
        r0 = rows[:rows0].reshape(groups, 2, own0, wide)
        r1 = rows[rows0:].reshape(groups, 2, own1, wide)
        return jnp.concatenate([r0, r1], axis=2).swapaxes(0, 1)

    def in_time(owned):
        wide = owned.shape[3]
        turned = owned.swapaxes(0, 1)
        return jnp.concatenate(
            [turned[:, :, :own0].reshape(rows0, wide), turned[:, :, own0:].reshape(rows1, wide)], axis=0
        )

    def of_core(owned, which):
        return lax.dynamic_index_in_dim(owned, which, 0, keepdims=False)

    def of_group(rows):
        return lax.dynamic_index_in_dim(rows, group, 0, keepdims=False)

    def add_rows(partial):
        owned = by_owner(partial)
        return add_parts(of_core(owned, core) + swap(of_core(owned, 1 - core)))

    def seq_columns(rows):
        half = part(rows, width // 2, 1)
        return lax.all_to_all(half, "seq", split_axis=1, concat_axis=0, tiled=True)

    def from_stages(rows):
        wide = jnp.broadcast_to(rows[None], (stages,) + rows.shape)
        met = lax.all_to_all(wide, "seq", split_axis=0, concat_axis=0, tiled=True)
        met = met.reshape(stages * rows.shape[0], rows.shape[1])
        return share(met).swapaxes(0, 1).reshape(met.shape[0], width)

    def own_columns(rows):
        both = [
            lax.dynamic_slice_in_dim(rows, (which * stages + stage) * quota, quota, 1) for which in (core, 1 - core)
        ]
        return jnp.concatenate(both, axis=1).T

    own_rows = of_group(of_core(by_owner(inputs), core))
    own_mask = of_group(of_core(by_owner(mask), core))
    tokens_masked = of_core(by_owner(masked), core)
    own_masked = of_group(tokens_masked).astype(f32)
    quarter = width // groups
    masked_all = from_stages(
        lax.dynamic_slice_in_dim(tokens_masked.reshape(groups * own, width), group * quarter, quarter, 1)
    )

    factor1 = lax.rsqrt(jnp.mean(inputs * inputs, axis=-1, keepdims=True) + epsilon)
    unit1 = inputs * factor1
    normed = rms_scale(inputs, mixer_gain).astype(bf16)
    normed_cols = seq_columns(normed)
    mixer_full, masked_all, normed_cols = together(mixer_full, masked_all, normed_cols)
    mixer_w = part(mixer_full, slim, 1)
    gate_w = part(mixer_full, dv, 1, 2 * slim)
    out_w = part(mixer_full, dv, 1, 2 * slim + 2 * dv)
    rates_w = mixer_full[:, 2 * slim + 4 * dv :]
    proj = product(normed, mixer_w)
    small_pre = product(normed, rates_w)
    gate_pre = product(normed, gate_w)
    alpha_pre = part(small_pre, heads, 1)
    beta_pre = part(small_pre, heads, 1, 2 * heads)
    head0 = (2 * group + core) * heads
    rates = lax.dynamic_slice_in_dim(decay_rate, head0, heads)
    biases = lax.dynamic_slice_in_dim(beta_bias, head0, heads)
    blocks = sum(counts)

    def to_blocks(array):
        return array.T.reshape(heads, blocks, BLOCK)

    def from_blocks(array):
        return array.reshape(heads, blocks * BLOCK).T

    soft = jax.nn.softplus(alpha_pre)
    beta = jax.nn.sigmoid(beta_pre + biases)
    beta_b = to_blocks(beta)
    upto = (
        lax.broadcasted_iota(jnp.int32, (BLOCK, BLOCK), 0) <= lax.broadcasted_iota(jnp.int32, (BLOCK, BLOCK), 1)
    ).astype(f32)
    sums = jnp.matmul(to_blocks(-rates * soft), upto, precision=highest)
    col = jnp.stack([sums, beta_b], axis=-1)
    row = jnp.stack([sums, beta_b], axis=-2)
    solver, scores, w, vt, qt, m, b, mseg, bseg = solve(counts, heads, proj, col, row)
    state_in, unused_carry = relay(mseg, bseg, True)
    gain_row = head_gain[None]
    states, outs, gated = outputs_of(counts, heads, state_in, m, b, qt, scores, vt, gate_pre, gain_row)
    mixed = add_rows(contract_cols(gated, out_w))
    hidden = own_rows + mixed

    normed2, norm2_back = jax.vjp(rms_scale, hidden, feed_gain)
    feed_in = from_stages(
        lax.all_to_all(normed2.astype(bf16), "head", split_axis=1, concat_axis=0, tiled=True)
    )
    feed_part, back_part, main_grads, tail_grads = feed_forward(
        stage[None], feed_in, masked_all, own_columns(feed_in), own_columns(masked_all), feed_full, groups * own
    )
    normed2_grad = add_parts(back_part.reshape(groups, own, width))
    feed = add_parts(feed_part.reshape(groups, own, width))
    outputs_own = (own_mask * (hidden + feed)).astype(bf16)
    hidden_back, feed_gain_grad = norm2_back(normed2_grad)
    hidden_grad = own_masked + hidden_back
    mixed_half = share(hidden_grad.astype(bf16))
    other_half = swap(mixed_half)
    mixed_in = in_time(
        jnp.stack([jnp.where(first, mixed_half, other_half), jnp.where(first, other_half, mixed_half)])
    )

    gated_all = everyone(gated)
    gated_grad = product(mixed_in, out_w)
    gated_grad, gated_all = together(gated_grad, gated_all)
    outs_grad, gate_pre_low, gain_grads, d, dseg = output_grads_of(
        counts, heads, gated_grad, gate_pre, outs, gain_row, qt, m
    )
    gate_pre_all = everyone(gate_pre_low)
    later, carry = relay(jnp.swapaxes(mseg, 2, 3), dseg, False)

    half = stages * (rows0 + rows1)
    mixed_late, main_late, tail_late, unused_carry = together(mixed_in, main_grads, tail_grads, carry)
    mixed_cols = seq_columns(mixed_late)
    main_own = main_late[:quota] + swap(main_late[quota:])
    tail_own = tail_late[:quota] + swap(tail_late[quota:])

    def feed_grad(n):
        pieces = [main_own[:, (3 * i + n) * 256 : (3 * i + n + 1) * 256] for i in range(even // 256)]
        return jnp.concatenate(pieces + [tail_own[:, n * 128 : n * 128 + odd]], axis=1)

    feed_gate_grad, feed_value_grad, down_grad = feed_grad(0), feed_grad(1), feed_grad(2)
    out_grad = jnp.concatenate(
        [contract_rows(mixed_cols, gated_all[:half]), contract_rows(mixed_cols, gated_all[half:])], axis=1
    )
    gate_back = contract_cols(gate_pre_low, gate_w)
    later, feed_gate_grad, feed_value_grad, down_grad, out_grad, gate_back = together(
        later, feed_gate_grad, feed_value_grad, down_grad, out_grad, gate_back
    )
    query_low, key_low, value_low, col_grad, row_grad = input_grads_of(
        counts, heads, proj, col, row, solver, scores, w, vt, m, d, states, outs_grad, later
    )
    sums_grad = col_grad[..., 0] - row_grad[:, :, 0] * beta_b
    decay_back = from_blocks(jnp.matmul(sums_grad, upto.T, precision=highest))
    beta_back = beta * (1.0 - beta) * from_blocks(col_grad[..., 1] + row_grad[:, :, 0])
    rates_grad = -jnp.sum(soft * decay_back, axis=0)
    biases_grad = jnp.sum(beta_back, axis=0)
    alpha_back = -rates * jax.nn.sigmoid(alpha_pre) * decay_back
    small_low = jnp.concatenate([alpha_back, beta_back], axis=1).astype(bf16)
    slim_low = jnp.concatenate([query_low, key_low, value_low], axis=1)
    slim_all = everyone(slim_low)
    blank = jnp.zeros((rows0 + rows1, 4 * heads), bf16)
    spread = lax.dynamic_update_slice(blank, small_low[:, :heads], (0, core * heads))
    spread = lax.dynamic_update_slice(spread, small_low[:, heads:], (0, (2 + core) * heads))
    total = gate_back + contract_cols(slim_low, mixer_w) + contract_cols(spread, rates_w)
    normed_grad = add_rows(total)
    mixer_gain_part = jnp.sum(total * unit1, axis=0)
    unused_rows, norm1_back = jax.vjp(lambda v: rms_scale(v, mixer_gain), own_rows)
    input_own = (hidden_grad + norm1_back(normed_grad)[0]).astype(bf16)

    small_rows = contract_rows(small_low, normed)
    small_rows = lax.all_to_all(small_rows, ("dp", "seq"), split_axis=1, concat_axis=0, tiled=True)
    small_rows = jnp.sum(small_rows.reshape(2, stages, 2, heads, quota), axis=1)
    alpha_grad = small_rows[:, 0].reshape(2 * heads, quota).T
    beta_grad = small_rows[:, 1].reshape(2 * heads, quota).T
    slim_halves = [contract_rows(normed_cols, slim_all[:half]), contract_rows(normed_cols, slim_all[half:])]
    gate_grad = jnp.concatenate(
        [contract_rows(normed_cols, gate_pre_all[:half]), contract_rows(normed_cols, gate_pre_all[half:])], axis=1
    )

    def pick(start, size):
        return jnp.concatenate([g[:, start : start + size] for g in slim_halves], axis=1)

    total_heads = decay_rate.shape[0]
    none = jnp.zeros((total_heads,), f32)
    small = add_everywhere(
        jnp.concatenate(
            [
                mixer_gain_part,
                feed_gain_grad,
                jnp.sum(gain_grads, axis=(0, 1)),
                lax.dynamic_update_slice(none, rates_grad, (head0,)),
                lax.dynamic_update_slice(none, biases_grad, (head0,)),
            ]
        )
    )
    edges = [width, 2 * width, 2 * width + head_gain.shape[0], 2 * width + head_gain.shape[0] + total_heads]

    def place(rows):
        r0, r1 = rows[:own0], rows[own0:]
        out0 = jnp.concatenate([r0, lax.ppermute(r0, "dp", [(1, 0)])], axis=0)
        pair = jnp.concatenate([lax.ppermute(r1, "dp", [(0, 1)]), r1], axis=0)
        routes = [
            [
                ((stages + QUARTERS * a + b) * groups + k, (stages + a) * groups + b)
                for a in range(stages // QUARTERS)
                for b in range(QUARTERS)
            ]
            for k in range(groups)
        ]
        out1 = jnp.concatenate([lax.ppermute(pair, ("dp", "seq", "head"), route) for route in routes], axis=0)
        return jnp.where(first, out0, out1)[None]

    return (
        place(outputs_own),
        place(input_own),
        pick(0, dk),
        pick(dk, dk),
        pick(2 * dk, dv),
        gate_grad,
        alpha_grad,
        beta_grad,
        out_grad,
        feed_gate_grad,
        feed_value_grad,
        down_grad,
        small[: edges[0]],
        small[edges[0] : edges[1]],
        small[edges[1] : edges[2]],
        small[edges[2] : edges[3]],
        small[edges[3] :],
    )


def solution(mesh):
    return jax.shard_map(
        on_device,
        mesh=mesh,
        in_specs=(
            P("dp", "seq", None),
            P("dp", "seq", None),
            P(),
            P(("dp", "seq"), "head"),
            P(("dp", "seq"), "head"),
            P(("dp", "seq"), "head"),
            P(("dp", "seq"), "head"),
            P(("dp", "seq"), "head"),
            P(("dp", "seq"), "head"),
            P(("dp", "seq"), "head"),
            P(("dp", "seq"), "head"),
            P(("dp", "seq"), "head"),
            P(("dp", "seq"), "head"),
            P(),
            P(),
            P(),
            P(),
            P(),
        ),
        out_specs=(
            P("dp", ("seq", "head"), None),
            P("dp", ("seq", "head"), None),
            P(("dp", "seq"), "head"),
            P(("dp", "seq"), "head"),
            P(("dp", "seq"), "head"),
            P(("dp", "seq"), "head"),
            P(("dp", "seq"), "head"),
            P(("dp", "seq"), "head"),
            P(("dp", "seq"), "head"),
            P(("dp", "seq"), "head"),
            P(("dp", "seq"), "head"),
            P(("dp", "seq"), "head"),
            P(),
            P(),
            P(),
            P(),
            P(),
        ),
        check_vma=False,
    )
```

```python
import functools

import jax
import jax.numpy as jnp
from jax import lax
from jax.experimental import pallas as pl
from jax.experimental.pallas import tpu as pltpu
from jax.sharding import PartitionSpec as P

BLOCK = 64
epsilon = 1e-06
highest = lax.Precision.HIGHEST
f32 = jnp.float32


def mm(left, right, a=1, b=0):
    return lax.dot_general(
        left, right, (((a,), (b,)), ((), ())), precision=highest, preferred_element_type=f32
    )


def mm_nt(left, right):
    return mm(left, right, 1, 1)


def mm_tn(left, right):
    return mm(left, right, 0, 0)


def each(f, *lists):
    return [f(*items) for items in zip(*lists)]


def square_masks():
    rows = lax.broadcasted_iota(jnp.int32, (BLOCK, BLOCK), 0)
    cols = lax.broadcasted_iota(jnp.int32, (BLOCK, BLOCK), 1)
    return rows >= cols, rows > cols, (rows == cols).astype(f32)


def row_factor(values):
    return lax.rsqrt(jnp.sum(values * values, axis=-1, keepdims=True) + epsilon)


def split(values, count):
    return [values[i * BLOCK : (i + 1) * BLOCK] for i in range(count)]


def decays(col_ref, row_ref, count):
    lower, strict, identity = square_masks()
    out = []
    for i in range(count):
        c_col, b_col = col_ref[0, i, :, 0:1], col_ref[0, i, :, 1:2]
        c_row, b_row = row_ref[0, i, 0:1, :], row_ref[0, i, 1:2, :]
        fade = jnp.where(lower, jnp.exp(jnp.where(lower, c_col - c_row, 0.0)), 0.0)
        last = c_col[BLOCK - 1 : BLOCK, :]
        out.append((fade, fade * b_row, jnp.exp(c_col), jnp.exp(last - c_col), b_col, jnp.exp(last)))
    return [list(items) for items in zip(*out)]


def chains(counts):
    start, out = 0, []
    for count in counts:
        out.append(range(start, start + count))
        start += count
    return out


def solve_kernel(counts, q_ref, k_ref, v_ref, col_ref, row_ref, solver_ref, scores_ref, w_ref, vt_ref, qt_ref, m_ref, b_ref, mseg_ref, bseg_ref):
    count = sum(counts)
    lower, strict, identity = square_masks()
    query = q_ref[...]
    query = split(query * row_factor(query), count)
    key = k_ref[...]
    key = split(key * row_factor(key), count)
    value = split(v_ref[...], count)
    fade, ratio, growth, remain, beta, end = decays(col_ref, row_ref, count)
    power = each(lambda k, p: jnp.where(strict, -mm_nt(k, k) * p, 0.0), key, ratio)
    solver = [identity + p for p in power]
    for _ in range((BLOCK - 1).bit_length() - 1):
        power = each(lambda p: mm(p, p), power)
        solver = each(lambda s, p: s + mm(s, p), solver, power)
    scores = each(lambda q, k, p: mm_nt(q, k) * p, query, key, ratio)
    w = each(lambda s, g, k: mm(s, g * k), solver, growth, key)
    vt = each(mm, solver, value)
    qt = each(lambda g, q, a, x: g * q - mm(a, x), growth, query, scores, w)
    weighted = each(lambda k, r, b: k * (r * b), key, remain, beta)
    size = query[0].shape[1]
    wide = (
        lax.broadcasted_iota(jnp.int32, (size, size), 0)
        == lax.broadcasted_iota(jnp.int32, (size, size), 1)
    ).astype(f32)
    m = each(lambda e, k, x: e * wide - mm_tn(k, x), end, weighted, w)
    b = each(mm_tn, weighted, vt)
    for i in range(count):
        solver_ref[0, i] = solver[i]
        scores_ref[0, i] = scores[i]
        w_ref[0, i] = w[i]
        vt_ref[0, i] = vt[i]
        qt_ref[0, i] = qt[i]
        m_ref[0, i] = m[i]
        b_ref[0, i] = b[i]
    for j, chain in enumerate(chains(counts)):
        mseg_ref[0, j] = m[chain[0]]
        bseg_ref[0, j] = b[chain[0]]
        for i in chain[1:]:
            bseg_ref[0, j] = mm(m_ref[0, i], bseg_ref[0, j]) + b_ref[0, i]
            mseg_ref[0, j] = mm(m_ref[0, i], mseg_ref[0, j])


def output_kernel(counts, state_ref, m_ref, b_ref, qt_ref, scores_ref, vt_ref, gate_ref, gain_ref, states_ref, out_ref, gated_ref):
    count = sum(counts)
    states = [None] * count
    for j, chain in enumerate(chains(counts)):
        state = state_ref[0, j]
        for i in chain:
            states[i] = state
            states_ref[0, i] = state
            if i != chain[-1]:
                state = mm(m_ref[0, i], state) + b_ref[0, i]
    gain = gain_ref[...]
    outs = [mm(qt_ref[0, i], states[i]) + mm(scores_ref[0, i], vt_ref[0, i]) for i in range(count)]
    for i in range(count):
        rows = slice(i * BLOCK, (i + 1) * BLOCK)
        out = outs[i]
        gate = gate_ref[rows, :]
        scale = lax.rsqrt(jnp.mean(out * out, axis=-1, keepdims=True) + epsilon)
        out_ref[rows, :] = out
        gated_ref[rows, :] = (out * scale * gain * (gate * jax.nn.sigmoid(gate))).astype(jnp.bfloat16)


def output_grad_kernel(counts, grad_ref, gate_ref, out_ref, gain_ref, qt_ref, m_ref, out_grad_ref, gate_grad_ref, gain_grad_ref, d_ref, dseg_ref):
    count = sum(counts)
    gain = gain_ref[...]
    gain_grad = jnp.zeros_like(gain)
    grads = []
    for i in range(count):
        rows = slice(i * BLOCK, (i + 1) * BLOCK)
        grad, gate, out = grad_ref[rows, :], gate_ref[rows, :], out_ref[rows, :]
        scale = lax.rsqrt(jnp.mean(out * out, axis=-1, keepdims=True) + epsilon)
        unit = out * scale
        sig = jax.nn.sigmoid(gate)
        normed_grad = grad * (gate * sig)
        gate_grad_ref[rows, :] = (grad * (unit * gain) * (sig * (1.0 + gate * (1.0 - sig)))).astype(jnp.bfloat16)
        gain_grad = gain_grad + jnp.sum(normed_grad * unit, axis=0, keepdims=True)
        inner = normed_grad * gain
        out_grad = scale * (inner - unit * jnp.mean(unit * inner, axis=-1, keepdims=True))
        out_grad_ref[rows, :] = out_grad
        grads.append(out_grad)
    gain_grad_ref[0] = gain_grad
    d = [mm_tn(qt_ref[0, i], grads[i]) for i in range(count)]
    for i in range(count):
        d_ref[0, i] = d[i]
    for j, chain in enumerate(chains(counts)):
        dseg_ref[0, j] = d[chain[-1]]
        for i in list(chain)[-2::-1]:
            dseg_ref[0, j] = mm_tn(m_ref[0, i], dseg_ref[0, j]) + d_ref[0, i]


def unit_back(raw, grad):
    factor = row_factor(raw)
    unit = raw * factor
    return factor * (grad - unit * jnp.sum(unit * grad, axis=-1, keepdims=True))


def grads_kernel(counts, q_ref, k_ref, col_ref, row_ref, solver_ref, scores_ref, w_ref, vt_ref, m_ref, d_ref, states_ref, out_grad_ref, later_ref, q_grad_ref, k_grad_ref, v_grad_ref, col_grad_ref, row_grad_ref):
    count = sum(counts)
    span = range(count)
    lower, strict, identity = square_masks()
    raw_q, raw_k = split(q_ref[...], count), split(k_ref[...], count)
    query = [x * row_factor(x) for x in raw_q]
    key = [x * row_factor(x) for x in raw_k]
    fade, ratio, growth, remain, beta, end = decays(col_ref, row_ref, count)
    out_grad = split(out_grad_ref[...], count)
    later = [None] * count
    for j, chain in enumerate(chains(counts)):
        state = later_ref[0, j]
        for i in list(chain)[::-1]:
            later[i] = state
            if i != chain[0]:
                state = mm_tn(m_ref[0, i], state) + d_ref[0, i]
    states = [states_ref[0, i] for i in span]
    update = [vt_ref[0, i] - mm(w_ref[0, i], states[i]) for i in span]
    update_grad = [
        mm_tn(scores_ref[0, i], out_grad[i]) + mm(key[i] * (remain[i] * beta[i]), later[i]) for i in span
    ]
    solved = [mm_tn(solver_ref[0, i], update_grad[i]) for i in span]
    scores_grad = each(mm_nt, out_grad, update)
    inner_grad = each(lambda y, u: jnp.where(strict, -mm_nt(y, u), 0.0), solved, update)
    query_dot = each(mm_nt, query, key)
    keys_dot = each(mm_nt, key, key)
    from_out = each(mm_nt, out_grad, states)
    from_solved = each(mm_nt, solved, states)
    from_update = each(mm_nt, update, later)
    weighted_scores = each(lambda p, x: p * x, ratio, scores_grad)
    weighted_inner = each(lambda p, x: p * x, ratio, inner_grad)
    q_grad = [growth[i] * from_out[i] + mm(weighted_scores[i], key[i]) for i in span]
    k_grad = [
        mm_tn(weighted_scores[i], query[i])
        + (remain[i] * beta[i]) * from_update[i]
        - growth[i] * from_solved[i]
        + mm(weighted_inner[i], key[i])
        + mm_tn(weighted_inner[i], key[i])
        for i in span
    ]
    last_row = (lax.broadcasted_iota(jnp.int32, (BLOCK, 1), 0) == BLOCK - 1).astype(f32)
    for i in span:
        rows = slice(i * BLOCK, (i + 1) * BLOCK)
        q_grad_ref[rows, :] = unit_back(raw_q[i], q_grad[i]).astype(jnp.bfloat16)
        k_grad_ref[rows, :] = unit_back(raw_k[i], k_grad[i]).astype(jnp.bfloat16)
        v_grad_ref[rows, :] = solved[i].astype(jnp.bfloat16)
        faded = fade[i] * (scores_grad[i] * query_dot[i] + inner_grad[i] * keys_dot[i])
        b_row = row_ref[0, i, 1:2, :]
        growth_grad = jnp.sum(query[i] * from_out[i] - key[i] * from_solved[i], axis=-1, keepdims=True)
        weight_grad = jnp.sum(key[i] * from_update[i], axis=-1, keepdims=True)
        pulled = remain[i] * beta[i] * weight_grad
        tail = jnp.sum(pulled, axis=0, keepdims=True) + end[i] * jnp.sum(
            jnp.sum(later[i] * states[i], axis=-1, keepdims=True), axis=0, keepdims=True
        )
        c_grad = jnp.sum(faded * b_row, axis=-1, keepdims=True) + growth[i] * growth_grad - pulled + last_row * tail
        col_grad_ref[0, i, :, 0:1] = c_grad
        col_grad_ref[0, i, :, 1:2] = remain[i] * weight_grad
        row_grad_ref[0, i] = jnp.sum(faded, axis=0, keepdims=True)


def whole(shape):
    return pl.BlockSpec((1,) + tuple(shape[1:]), lambda j: (j,) + (0,) * (len(shape) - 1))


def columns(rows, width, first=0):
    return pl.BlockSpec((rows, width), lambda j: (0, j + first))


def shaped(shape, dtype=f32):
    return jax.ShapeDtypeStruct(shape, dtype)


def call(kernel, counts, heads, inputs, outputs, flops):
    moved = sum(x.size * x.dtype.itemsize for x, _ in inputs) + sum(
        x.size * x.dtype.itemsize for x, _ in outputs
    )
    return pl.pallas_call(
        functools.partial(kernel, counts),
        grid=(heads,),
        in_specs=[s for _, s in inputs],
        out_specs=[s for _, s in outputs],
        out_shape=[x for x, _ in outputs],
        compiler_params=pltpu.CompilerParams(vmem_limit_bytes=48 << 20),
        cost_estimate=pl.CostEstimate(flops=flops, bytes_accessed=moved, transcendentals=0),
    )(*[x for x, _ in inputs])


def per_head(heads, *shape, dtype=f32):
    s = (heads,) + shape
    return shaped(s, dtype), whole(s)


def flat(array, width, first=0):
    return array, columns(array.shape[0], width, first)


def stacked(array):
    return array, whole(array.shape)


def solve(counts, heads, proj, col, row):
    n, dk, dv = sum(counts), 128, 256
    return call(
        solve_kernel, counts, heads,
        [flat(proj, dk), flat(proj, dk, heads), flat(proj, dv, heads), stacked(col), stacked(row)],
        [per_head(heads, n, BLOCK, BLOCK), per_head(heads, n, BLOCK, BLOCK), per_head(heads, n, BLOCK, dk),
         per_head(heads, n, BLOCK, dv), per_head(heads, n, BLOCK, dk), per_head(heads, n, dk, dk),
         per_head(heads, n, dk, dv), per_head(heads, len(counts), dk, dk), per_head(heads, len(counts), dk, dv)],
        heads * n * 100_000_000,
    )


def outputs_of(counts, heads, state, m, b, qt, scores, vt, gate_pre, gain):
    n, dk, dv = sum(counts), 128, 256
    rows = gate_pre.shape[0]
    cols = columns(rows, dv)
    return call(
        output_kernel, counts, heads,
        [stacked(state), stacked(m), stacked(b), stacked(qt), stacked(scores), stacked(vt), flat(gate_pre, dv),
         (gain, pl.BlockSpec((1, dv), lambda j: (0, 0)))],
        [per_head(heads, n, dk, dv), (shaped((rows, heads * dv)), cols), (shaped((rows, heads * dv), jnp.bfloat16), cols)],
        heads * n * 50_000_000,
    )


def output_grads_of(counts, heads, grad, gate_pre, outs, gain, qt, m):
    n, dk, dv = sum(counts), 128, 256
    rows = gate_pre.shape[0]
    cols = columns(rows, dv)
    return call(
        output_grad_kernel, counts, heads,
        [flat(grad, dv), flat(gate_pre, dv), flat(outs, dv), (gain, pl.BlockSpec((1, dv), lambda j: (0, 0))), stacked(qt), stacked(m)],
        [(shaped((rows, heads * dv)), cols), (shaped((rows, heads * dv), jnp.bfloat16), cols),
         per_head(heads, 1, dv), per_head(heads, n, dk, dv), per_head(heads, len(counts), dk, dv)],
        heads * n * 50_000_000,
    )


def input_grads_of(counts, heads, proj, col, row, solver, scores, w, vt, m, d, states, out_grad, later):
    n, dk, dv = sum(counts), 128, 256
    rows = proj.shape[0]
    return call(
        grads_kernel, counts, heads,
        [flat(proj, dk), flat(proj, dk, heads), stacked(col), stacked(row), stacked(solver), stacked(scores), stacked(w),
         stacked(vt), stacked(m), stacked(d), stacked(states), flat(out_grad, dv), stacked(later)],
        [(shaped((rows, heads * dk), jnp.bfloat16), columns(rows, dk)), (shaped((rows, heads * dk), jnp.bfloat16), columns(rows, dk)),
         (shaped((rows, heads * dv), jnp.bfloat16), columns(rows, dv)), per_head(heads, n, BLOCK, 2), per_head(heads, n, 1, BLOCK)],
        heads * n * 150_000_000,
    )


def feed_kernel(stage_ref, x_ref, k_ref, xs_ref, ks_ref, w1_ref, w3_ref, w2_ref, t1_ref, t3_ref, t2_ref, feed_ref, back_ref, main_ref, main_other_ref, tail_ref, tail_other_ref, active_s, gate_s, up_s):
    step, chunk = pl.program_id(0), pl.program_id(1)
    own = feed_ref.shape[0]
    near, piece = x_ref.shape[1] // own, x_ref.shape[2]
    stage = stage_ref[0]
    here = pl.ds(pl.multiple_of(lax.rem(stage, near) * own, own), own)

    @pl.when((step == 0) & (chunk == 0))
    def _():
        feed_ref[...] = jnp.zeros_like(feed_ref)
        back_ref[...] = jnp.zeros_like(back_ref)

    def work(w1, w3, w2, out_refs):
        wide = w1.shape[1]
        gate, up, grad = (
            sum(
                jnp.dot(rows[i], w[i * piece : (i + 1) * piece, :], preferred_element_type=f32)
                for i in range(rows.shape[0])
            )
            for rows, w in ((x_ref, w1), (x_ref, w3), (k_ref, w2))
        )
        sig = jax.nn.sigmoid(gate)
        silu = gate * sig
        active = (silu * up).astype(jnp.bfloat16)
        gate_grad = (grad * up * (sig * (1.0 + gate * (1.0 - sig)))).astype(jnp.bfloat16)
        up_grad = (grad * silu).astype(jnp.bfloat16)
        active_s[:, :wide] = active
        gate_s[:, :wide] = gate_grad
        up_s[:, :wide] = up_grad

        @pl.when(chunk == stage // near)
        def _():
            feed_ref[...] += contract_cols(active_s[here, :wide], w2[...])
            back_ref[...] += contract_cols(gate_s[here, :wide], w1[...])
            back_ref[...] += contract_cols(up_s[here, :wide], w3[...])

        parts = (
            jnp.dot(xs_ref[...], gate_grad, preferred_element_type=f32),
            jnp.dot(xs_ref[...], up_grad, preferred_element_type=f32),
            jnp.dot(ks_ref[...], active, preferred_element_type=f32),
        )
        for i, p in enumerate(parts):
            place = slice(i * wide, (i + 1) * wide)
            quota = p.shape[0] // 2

            @pl.when(chunk == 0)
            def _():
                out_refs[0][:, place] = p[:quota]
                out_refs[1][:, place] = p[quota:]

            @pl.when(chunk > 0)
            def _():
                out_refs[0][:, place] += p[:quota]
                out_refs[1][:, place] += p[quota:]

    work(w1_ref, w3_ref, w2_ref, (main_ref, main_other_ref))

    @pl.when(step == pl.num_programs(0) - 1)
    def _():
        work(t1_ref, t3_ref, t2_ref, (tail_ref, tail_other_ref))


def feed_forward(stage, rows, grads, row_cols, grad_cols, weights, own):
    pieces, positions, piece = rows.shape
    width = pieces * piece
    picked = row_cols.shape[0]
    tile, rest = 256, 128
    steps = (weights.shape[1] - 3 * rest) // (3 * tile)
    chunk = min(positions, 4 * own)
    first_tail = 3 * steps * tile // rest
    grid = (steps, positions // chunk)
    tokens = pl.BlockSpec((pieces, chunk, piece), lambda i, t, s: (0, t, 0))
    columns_of = pl.BlockSpec((picked, chunk), lambda i, t, s: (0, t))

    def main_of(n):
        return pl.BlockSpec((width, tile), lambda i, t, s: (0, n * steps + i))

    def tail_of(n):
        return pl.BlockSpec((width, rest), lambda i, t, s: (0, first_tail + n))

    def fixed(*shape):
        return pl.BlockSpec(shape, lambda i, t, s: (0, 0))

    flops = 2 * positions * width * weights.shape[1] + 2 * own * width * weights.shape[1] + 2 * positions * picked * weights.shape[1]
    return pl.pallas_call(
        feed_kernel,
        grid_spec=pltpu.PrefetchScalarGridSpec(
            num_scalar_prefetch=1,
            grid=grid,
            in_specs=[tokens, tokens, columns_of, columns_of, main_of(0), main_of(1), main_of(2), tail_of(0), tail_of(1), tail_of(2)],
            out_specs=[
                fixed(own, width),
                fixed(own, width),
                pl.BlockSpec((picked // 2, 3 * tile), lambda i, t, s: (0, i)),
                pl.BlockSpec((picked // 2, 3 * tile), lambda i, t, s: (0, i)),
                fixed(picked // 2, 3 * rest),
                fixed(picked // 2, 3 * rest),
            ],
            scratch_shapes=[pltpu.VMEM((chunk, tile), jnp.bfloat16)] * 3,
        ),
        out_shape=[
            shaped((own, width)),
            shaped((own, width)),
            shaped((picked // 2, 3 * tile * steps)),
            shaped((picked // 2, 3 * tile * steps)),
            shaped((picked // 2, 3 * rest)),
            shaped((picked // 2, 3 * rest)),
        ],
        compiler_params=pltpu.CompilerParams(
            dimension_semantics=("arbitrary", "arbitrary"), vmem_limit_bytes=56 << 20
        ),
        cost_estimate=pl.CostEstimate(
            flops=flops, bytes_accessed=2 * weights.size + 8 * positions * width, transcendentals=0
        ),
    )(stage, rows, grads, row_cols, grad_cols, weights, weights, weights, weights, weights, weights)


QUARTERS = 4


def swap(array):
    return lax.ppermute(array, "dp", [(0, 1), (1, 0)])


def relay(mats, offsets, forward):
    size = lax.axis_size("seq")
    entering = jnp.zeros_like(offsets)
    leaving = offsets
    for step in range(size - 1):
        route = [(step, step + 1)] if forward else [(size - 1 - step, size - 2 - step)]
        got = jnp.stack([lax.ppermute(leaving[i], "seq", route) for i in range(offsets.shape[0])])
        entering = entering + got
        if step < size - 2:
            leaving = jnp.matmul(mats, got, precision=highest) + offsets
    return entering, leaving


def together(*arrays):
    return lax.optimization_barrier(arrays)


def everyone(part):
    return lax.all_gather(part, ("dp", "seq"), axis=0, tiled=True)


def share(rows):
    wide = jnp.broadcast_to(rows[None], (lax.axis_size("head"),) + rows.shape)
    return lax.all_to_all(wide, "head", split_axis=0, concat_axis=0, tiled=True)


def add_parts(parts):
    got = lax.all_to_all(parts.astype(jnp.bfloat16), "head", split_axis=0, concat_axis=0, tiled=True)
    return jnp.sum(got.astype(f32), axis=0)


def add_everywhere(vector):
    for axis in ("dp", "seq", "head"):
        size, step = lax.axis_size(axis), 1
        while step < size:
            vector = vector + lax.ppermute(vector, axis, [(i, i ^ step) for i in range(size)])
            step *= 2
    return vector


def contract_rows(left, right):
    return lax.dot_general(left, right, (((0,), (0,)), ((), ())), preferred_element_type=f32)


def contract_cols(left, right):
    return lax.dot_general(left, right, (((1,), (1,)), ((), ())), preferred_element_type=f32)


def product(left, right):
    return jnp.dot(left, right, preferred_element_type=f32)


def rms_scale(values, gain):
    return values * lax.rsqrt(jnp.mean(values * values, axis=-1, keepdims=True) + epsilon) * gain


def swiglu(gate_in, up_in):
    return jax.nn.silu(gate_in) * up_in


def on_device(
    activations,
    cotangent,
    lengths,
    query_weight,
    key_weight,
    value_weight,
    gate_weight,
    alpha_weight,
    beta_weight,
    out_weight,
    swiglu_gate,
    swiglu_value,
    swiglu_down,
    mixer_gain,
    feed_gain,
    head_gain,
    decay_rate,
    beta_bias,
):
    bf16 = jnp.bfloat16
    core, stage, group = lax.axis_index("dp"), lax.axis_index("seq"), lax.axis_index("head")
    stages, groups = lax.axis_size("seq"), lax.axis_size("head")
    width = activations.shape[2]
    rows0 = activations.shape[1]
    rows1 = rows0 // QUARTERS
    own0, own1 = rows0 // (2 * groups), rows1 // (2 * groups)
    own = own0 + own1
    quota = width // (2 * stages)
    heads = alpha_weight.shape[1] // 2
    counts = (rows0 // BLOCK, rows1 // BLOCK)
    assert groups == QUARTERS and stages % QUARTERS == 0 and rows1 % BLOCK == 0
    first = core == 0

    def part(array, size, axis, offset=0):
        return lax.dynamic_slice_in_dim(array, offset + core * size, size, axis)

    dk, dv = query_weight.shape[1] // 2, value_weight.shape[1] // 2
    slim = 2 * dk + dv
    mixer_cols = []
    for c in range(2):
        mixer_cols += [
            query_weight[:, c * dk : (c + 1) * dk],
            key_weight[:, c * dk : (c + 1) * dk],
            value_weight[:, c * dv : (c + 1) * dv],
        ]
    mixer_cols += [alpha_weight, beta_weight]
    mixer_full = everyone(jnp.concatenate(mixer_cols, axis=1).astype(bf16))
    gates_full = everyone(jnp.concatenate([gate_weight, out_weight], axis=1).astype(bf16))
    hidden_units = swiglu_gate.shape[1]
    even = hidden_units // 256 * 256
    odd = hidden_units - even
    assert 0 < odd <= 128
    three = (swiglu_gate, swiglu_value, swiglu_down)
    spare = ((0, 0), (0, 128 - odd))
    feed_full = everyone(
        jnp.concatenate([w[:, :even] for w in three] + [jnp.pad(w[:, even:], spare) for w in three], axis=1).astype(bf16)
    )

    def chip_rows(rows):
        arrived = jnp.zeros((rows1, width), bf16)
        for b in range(QUARTERS):
            route = [(stages + a, stages + QUARTERS * a + b) for a in range(stages // QUARTERS)]
            arrived = arrived + lax.ppermute(rows[b * rows1 : (b + 1) * rows1], ("dp", "seq"), route)
        near0 = lax.ppermute(rows, "dp", [(0, 1)])
        near1 = lax.ppermute(arrived, "dp", [(1, 0)])
        return jnp.concatenate([jnp.where(first, rows, near0), jnp.where(first, near1, arrived)], axis=0)

    inputs = chip_rows(activations[0])
    inputs, late = together(inputs, cotangent[0])
    inputs = inputs.astype(f32)
    spots0 = stage * rows0 + lax.broadcasted_iota(jnp.int32, (rows0, 1), 0)
    spots1 = stage * rows1 + lax.broadcasted_iota(jnp.int32, (rows1, 1), 0)
    mask = jnp.concatenate([spots0 < lengths[0], spots1 < lengths[1]], axis=0).astype(f32)
    masked = (chip_rows(late).astype(f32) * mask).astype(bf16)

    def by_owner(rows):
        wide = rows.shape[1]
        r0 = rows[:rows0].reshape(groups, 2, own0, wide)
        r1 = rows[rows0:].reshape(groups, 2, own1, wide)
        return jnp.concatenate([r0, r1], axis=2).swapaxes(0, 1)

    def in_time(owned):
        wide = owned.shape[3]
        turned = owned.swapaxes(0, 1)
        return jnp.concatenate(
            [turned[:, :, :own0].reshape(rows0, wide), turned[:, :, own0:].reshape(rows1, wide)], axis=0
        )

    def of_core(owned, which):
        return lax.dynamic_index_in_dim(owned, which, 0, keepdims=False)

    def of_group(rows):
        return lax.dynamic_index_in_dim(rows, group, 0, keepdims=False)

    def add_rows(partial):
        owned = by_owner(partial)
        return add_parts(of_core(owned, core) + swap(of_core(owned, 1 - core)))

    def owned_columns(rows):
        got = lax.all_to_all(rows, ("dp", "seq"), split_axis=1, concat_axis=0, tiled=True)
        got = share(got).reshape(groups, 2, stages, own, quota).transpose(2, 0, 1, 3, 4)
        return jnp.concatenate(
            [got[:, :, :, :own0].reshape(stages, rows0, quota), got[:, :, :, own0:].reshape(stages, rows1, quota)], axis=1
        ).reshape(stages * (rows0 + rows1), quota)

    def across_stages(rows):
        wide = jnp.broadcast_to(rows[None], (stages,) + rows.shape)
        met = lax.all_to_all(wide, "seq", split_axis=0, concat_axis=0, tiled=True)
        return met.reshape(stages * rows.shape[0], rows.shape[1])

    def own_columns(rows):
        pieces, positions, piece = rows.shape
        both = []
        for which in (core, 1 - core):
            start = (which * stages + stage) * quota
            both.append(lax.dynamic_slice(rows, (start // piece, 0, start % piece), (1, positions, quota))[0])
        return jnp.concatenate(both, axis=1).T

    own_rows = of_group(of_core(by_owner(inputs), core))
    own_mask = of_group(of_core(by_owner(mask), core))
    tokens_masked = of_core(by_owner(masked), core)
    own_masked = of_group(tokens_masked).astype(f32)
    quarter = width // groups
    masked_met = across_stages(
        lax.dynamic_slice_in_dim(tokens_masked.reshape(groups * own, width), group * quarter, quarter, 1)
    )

    factor1 = lax.rsqrt(jnp.mean(inputs * inputs, axis=-1, keepdims=True) + epsilon)
    unit1 = inputs * factor1
    normed = rms_scale(inputs, mixer_gain).astype(bf16)
    normed_cols = owned_columns(of_group(of_core(by_owner(normed), core)))
    mixer_full, masked_met, normed_cols = together(mixer_full, masked_met, normed_cols)
    mixer_w = part(mixer_full, slim, 1)
    gate_w = part(gates_full, dv, 1)
    out_w = part(gates_full, dv, 1, 2 * dv)
    rates_w = mixer_full[:, 2 * slim :]
    proj = product(normed, mixer_w)
    small_pre = product(normed, rates_w)
    gate_pre = product(normed, gate_w)
    alpha_pre = part(small_pre, heads, 1)
    beta_pre = part(small_pre, heads, 1, 2 * heads)
    head0 = (2 * group + core) * heads
    rates = lax.dynamic_slice_in_dim(decay_rate, head0, heads)
    biases = lax.dynamic_slice_in_dim(beta_bias, head0, heads)
    blocks = sum(counts)

    def to_blocks(array):
        return array.T.reshape(heads, blocks, BLOCK)

    def from_blocks(array):
        return array.reshape(heads, blocks * BLOCK).T

    soft = jax.nn.softplus(alpha_pre)
    beta = jax.nn.sigmoid(beta_pre + biases)
    beta_b = to_blocks(beta)
    upto = (
        lax.broadcasted_iota(jnp.int32, (BLOCK, BLOCK), 0) <= lax.broadcasted_iota(jnp.int32, (BLOCK, BLOCK), 1)
    ).astype(f32)
    sums = jnp.matmul(to_blocks(-rates * soft), upto, precision=highest)
    col = jnp.stack([sums, beta_b], axis=-1)
    row = jnp.stack([sums, beta_b], axis=-2)
    solver, scores, w, vt, qt, m, b, mseg, bseg = solve(counts, heads, proj, col, row)
    state_in, unused_carry = relay(mseg, bseg, True)
    state_in, masked_all = together(state_in, share(masked_met))
    gain_row = head_gain[None]
    states, outs, gated = outputs_of(counts, heads, state_in, m, b, qt, scores, vt, gate_pre, gain_row)
    mixed = add_rows(contract_cols(gated, out_w))
    hidden = own_rows + mixed

    normed2, norm2_back = jax.vjp(rms_scale, hidden, feed_gain)
    feed_in = share(
        across_stages(lax.all_to_all(normed2.astype(bf16), "head", split_axis=1, concat_axis=0, tiled=True))
    )
    feed_part, back_part, main_own, main_other, tail_own, tail_other = feed_forward(
        stage[None], feed_in, masked_all, own_columns(feed_in), own_columns(masked_all), feed_full, groups * own
    )
    normed2_grad = add_parts(back_part.reshape(groups, own, width))
    hidden_back, feed_gain_grad = norm2_back(normed2_grad)
    hidden_grad = own_masked + hidden_back
    mixed_own = hidden_grad.astype(bf16)
    mixed_half = share(mixed_own)
    other_half = swap(mixed_half)
    mixed_in = in_time(
        jnp.stack([jnp.where(first, mixed_half, other_half), jnp.where(first, other_half, mixed_half)])
    )

    gated_all = everyone(gated)
    gated_grad = product(mixed_in, out_w)
    main_other, tail_other = swap(main_other), swap(tail_other)
    mixed_cols = owned_columns(mixed_own)
    gated_grad, gated_all, main_other, tail_other = together(gated_grad, gated_all, main_other, tail_other)
    outs_grad, gate_pre_low, gain_grads, d, dseg = output_grads_of(
        counts, heads, gated_grad, gate_pre, outs, gain_row, qt, m
    )
    gate_pre_all = everyone(gate_pre_low)
    dseg, mixed_cols = together(dseg, mixed_cols)
    later, carry = relay(jnp.swapaxes(mseg, 2, 3), dseg, False)

    half = stages * (rows0 + rows1)
    main_own, main_other, tail_own, tail_other, mixed_cols, unused_carry = together(
        main_own, main_other, tail_own, tail_other, mixed_cols, carry
    )
    main_own, tail_own = main_own + main_other, tail_own + tail_other

    def feed_grad(n):
        pieces = [main_own[:, (3 * i + n) * 256 : (3 * i + n + 1) * 256].T for i in range(even // 256)]
        return jnp.concatenate(pieces + [tail_own[:, n * 128 : n * 128 + odd].T], axis=0)

    feed_gate_grad, feed_value_grad, down_grad = feed_grad(0), feed_grad(1), feed_grad(2)
    out_grad = jnp.concatenate(
        [contract_rows(mixed_cols, gated_all[:half]), contract_rows(mixed_cols, gated_all[half:])], axis=1
    )
    gate_back = contract_cols(gate_pre_low, gate_w)
    later, feed_gate_grad, feed_value_grad, down_grad, out_grad, gate_back = together(
        later, feed_gate_grad, feed_value_grad, down_grad, out_grad, gate_back
    )
    query_low, key_low, value_low, col_grad, row_grad = input_grads_of(
        counts, heads, proj, col, row, solver, scores, w, vt, m, d, states, outs_grad, later
    )
    query_low, feed_part = together(query_low, feed_part)
    feed = add_parts(feed_part.reshape(groups, own, width))
    outputs_own = (own_mask * (hidden + feed)).astype(bf16)
    sums_grad = col_grad[..., 0] - row_grad[:, :, 0] * beta_b
    decay_back = from_blocks(jnp.matmul(sums_grad, upto.T, precision=highest))
    beta_back = beta * (1.0 - beta) * from_blocks(col_grad[..., 1] + row_grad[:, :, 0])
    rates_grad = -jnp.sum(soft * decay_back, axis=0)
    biases_grad = jnp.sum(beta_back, axis=0)
    alpha_back = -rates * jax.nn.sigmoid(alpha_pre) * decay_back
    small_low = jnp.concatenate([alpha_back, beta_back], axis=1).astype(bf16)
    slim_low = jnp.concatenate([query_low, key_low, value_low], axis=1)
    slim_all = everyone(slim_low)
    blank = jnp.zeros((rows0 + rows1, 4 * heads), bf16)
    spread = lax.dynamic_update_slice(blank, small_low[:, :heads], (0, core * heads))
    spread = lax.dynamic_update_slice(spread, small_low[:, heads:], (0, (2 + core) * heads))
    total = gate_back + contract_cols(slim_low, mixer_w) + contract_cols(spread, rates_w)
    normed_grad = add_rows(total)
    mixer_gain_part = jnp.sum(total * unit1, axis=0)
    unused_rows, norm1_back = jax.vjp(lambda v: rms_scale(v, mixer_gain), own_rows)
    input_own = (hidden_grad + norm1_back(normed_grad)[0]).astype(bf16)

    small_rows = contract_rows(small_low, normed)
    small_rows = lax.all_to_all(small_rows, ("dp", "seq"), split_axis=1, concat_axis=0, tiled=True)
    small_rows = jnp.sum(small_rows.reshape(2, stages, 2, heads, quota), axis=1)
    alpha_grad = small_rows[:, 0].reshape(2 * heads, quota).T
    beta_grad = small_rows[:, 1].reshape(2 * heads, quota).T
    slim_halves = [contract_rows(normed_cols, slim_all[:half]), contract_rows(normed_cols, slim_all[half:])]
    gate_grad = jnp.concatenate(
        [contract_rows(normed_cols, gate_pre_all[:half]), contract_rows(normed_cols, gate_pre_all[half:])], axis=1
    )

    def pick(start, size):
        return jnp.concatenate([g[:, start : start + size] for g in slim_halves], axis=1)

    total_heads = decay_rate.shape[0]
    none = jnp.zeros((total_heads,), f32)
    small = add_everywhere(
        jnp.concatenate(
            [
                mixer_gain_part,
                feed_gain_grad,
                jnp.sum(gain_grads, axis=(0, 1)),
                lax.dynamic_update_slice(none, rates_grad, (head0,)),
                lax.dynamic_update_slice(none, biases_grad, (head0,)),
            ]
        )
    )
    edges = [width, 2 * width, 2 * width + head_gain.shape[0], 2 * width + head_gain.shape[0] + total_heads]

    def place(rows):
        r0, r1 = rows[:own0], rows[own0:]
        out0 = jnp.concatenate([r0, lax.ppermute(r0, "dp", [(1, 0)])], axis=0)
        pair = jnp.concatenate([lax.ppermute(r1, "dp", [(0, 1)]), r1], axis=0)
        routes = [
            [
                ((stages + QUARTERS * a + b) * groups + k, (stages + a) * groups + b)
                for a in range(stages // QUARTERS)
                for b in range(QUARTERS)
            ]
            for k in range(groups)
        ]
        out1 = jnp.concatenate([lax.ppermute(pair, ("dp", "seq", "head"), route) for route in routes], axis=0)
        return jnp.where(first, out0, out1)[None]

    return (
        place(outputs_own),
        place(input_own),
        pick(0, dk),
        pick(dk, dk),
        pick(2 * dk, dv),
        gate_grad,
        alpha_grad,
        beta_grad,
        out_grad,
        feed_gate_grad.T,
        feed_value_grad.T,
        down_grad.T,
        small[: edges[0]],
        small[edges[0] : edges[1]],
        small[edges[1] : edges[2]],
        small[edges[2] : edges[3]],
        small[edges[3] :],
    )


def solution(mesh):
    return jax.shard_map(
        on_device,
        mesh=mesh,
        in_specs=(
            P("dp", "seq", None),
            P("dp", "seq", None),
            P(),
            P(("dp", "seq"), "head"),
            P(("dp", "seq"), "head"),
            P(("dp", "seq"), "head"),
            P(("dp", "seq"), "head"),
            P(("dp", "seq"), "head"),
            P(("dp", "seq"), "head"),
            P(("dp", "seq"), "head"),
            P(("dp", "seq"), "head"),
            P(("dp", "seq"), "head"),
            P(("dp", "seq"), "head"),
            P(),
            P(),
            P(),
            P(),
            P(),
        ),
        out_specs=(
            P("dp", ("seq", "head"), None),
            P("dp", ("seq", "head"), None),
            P(("dp", "seq"), "head"),
            P(("dp", "seq"), "head"),
            P(("dp", "seq"), "head"),
            P(("dp", "seq"), "head"),
            P(("dp", "seq"), "head"),
            P(("dp", "seq"), "head"),
            P(("dp", "seq"), "head"),
            P(("dp", "seq"), "head"),
            P(("dp", "seq"), "head"),
            P(("dp", "seq"), "head"),
            P(),
            P(),
            P(),
            P(),
            P(),
        ),
        check_vma=False,
    )
```

```python
import functools

import jax
import jax.numpy as jnp
from jax import lax
from jax.experimental import pallas as pl
from jax.experimental.layout import Layout, with_layout_constraint
from jax.experimental.pallas import tpu as pltpu
from jax.sharding import PartitionSpec as P

BLOCK = 64
epsilon = 1e-06
highest = lax.Precision.HIGHEST
f32 = jnp.float32


def mm(left, right, a=1, b=0):
    return lax.dot_general(
        left, right, (((a,), (b,)), ((), ())), precision=highest, preferred_element_type=f32
    )


def mm_nt(left, right):
    return mm(left, right, 1, 1)


def mm_tn(left, right):
    return mm(left, right, 0, 0)


def each(f, *lists):
    return [f(*items) for items in zip(*lists)]


def square_masks():
    rows = lax.broadcasted_iota(jnp.int32, (BLOCK, BLOCK), 0)
    cols = lax.broadcasted_iota(jnp.int32, (BLOCK, BLOCK), 1)
    return rows >= cols, rows > cols, (rows == cols).astype(f32)


def row_factor(values):
    return lax.rsqrt(jnp.sum(values * values, axis=-1, keepdims=True) + epsilon)


def split(values, count):
    return [values[i * BLOCK : (i + 1) * BLOCK] for i in range(count)]


def decays(col_ref, row_ref, count):
    lower, strict, identity = square_masks()
    out = []
    for i in range(count):
        c_col, b_col = col_ref[0, i, :, 0:1], col_ref[0, i, :, 1:2]
        c_row, b_row = row_ref[0, i, 0:1, :], row_ref[0, i, 1:2, :]
        fade = jnp.where(lower, jnp.exp(jnp.where(lower, c_col - c_row, 0.0)), 0.0)
        last = c_col[BLOCK - 1 : BLOCK, :]
        out.append((fade, fade * b_row, jnp.exp(c_col), jnp.exp(last - c_col), b_col, jnp.exp(last)))
    return [list(items) for items in zip(*out)]


def chains(counts):
    start, out = 0, []
    for count in counts:
        out.append(range(start, start + count))
        start += count
    return out


def solve_kernel(counts, q_ref, k_ref, v_ref, col_ref, row_ref, solver_ref, scores_ref, w_ref, vt_ref, qt_ref, m_ref, b_ref, mseg_ref, bseg_ref):
    count = sum(counts)
    lower, strict, identity = square_masks()
    query = q_ref[...]
    query = split(query * row_factor(query), count)
    key = k_ref[...]
    key = split(key * row_factor(key), count)
    value = split(v_ref[...], count)
    fade, ratio, growth, remain, beta, end = decays(col_ref, row_ref, count)
    power = each(lambda k, p: jnp.where(strict, -mm_nt(k, k) * p, 0.0), key, ratio)
    solver = [identity + p for p in power]
    for _ in range((BLOCK - 1).bit_length() - 1):
        power = each(lambda p: mm(p, p), power)
        solver = each(lambda s, p: s + mm(s, p), solver, power)
    scores = each(lambda q, k, p: mm_nt(q, k) * p, query, key, ratio)
    w = each(lambda s, g, k: mm(s, g * k), solver, growth, key)
    vt = each(mm, solver, value)
    qt = each(lambda g, q, a, x: g * q - mm(a, x), growth, query, scores, w)
    weighted = each(lambda k, r, b: k * (r * b), key, remain, beta)
    size = query[0].shape[1]
    wide = (
        lax.broadcasted_iota(jnp.int32, (size, size), 0)
        == lax.broadcasted_iota(jnp.int32, (size, size), 1)
    ).astype(f32)
    m = each(lambda e, k, x: e * wide - mm_tn(k, x), end, weighted, w)
    b = each(mm_tn, weighted, vt)
    for i in range(count):
        solver_ref[0, i] = solver[i]
        scores_ref[0, i] = scores[i]
        w_ref[0, i] = w[i]
        vt_ref[0, i] = vt[i]
        qt_ref[0, i] = qt[i]
        m_ref[0, i] = m[i]
        b_ref[0, i] = b[i]
    for j, chain in enumerate(chains(counts)):
        mseg_ref[0, j] = m[chain[0]]
        bseg_ref[0, j] = b[chain[0]]
        for i in chain[1:]:
            bseg_ref[0, j] = mm(m_ref[0, i], bseg_ref[0, j]) + b_ref[0, i]
            mseg_ref[0, j] = mm(m_ref[0, i], mseg_ref[0, j])


def output_kernel(counts, state_ref, m_ref, b_ref, qt_ref, scores_ref, vt_ref, gate_ref, gain_ref, states_ref, out_ref, gated_ref):
    count = sum(counts)
    states = [None] * count
    for j, chain in enumerate(chains(counts)):
        state = state_ref[0, j]
        for i in chain:
            states[i] = state
            states_ref[0, i] = state
            if i != chain[-1]:
                state = mm(m_ref[0, i], state) + b_ref[0, i]
    gain = gain_ref[...]
    outs = [mm(qt_ref[0, i], states[i]) + mm(scores_ref[0, i], vt_ref[0, i]) for i in range(count)]
    for i in range(count):
        rows = slice(i * BLOCK, (i + 1) * BLOCK)
        out = outs[i]
        gate = gate_ref[rows, :]
        scale = lax.rsqrt(jnp.mean(out * out, axis=-1, keepdims=True) + epsilon)
        out_ref[rows, :] = out
        gated_ref[rows, :] = (out * scale * gain * (gate * jax.nn.sigmoid(gate))).astype(jnp.bfloat16)


def output_grad_kernel(counts, grad_ref, gate_ref, out_ref, gain_ref, qt_ref, m_ref, out_grad_ref, gate_grad_ref, gain_grad_ref, d_ref, dseg_ref):
    count = sum(counts)
    gain = gain_ref[...]
    gain_grad = jnp.zeros_like(gain)
    grads = []
    for i in range(count):
        rows = slice(i * BLOCK, (i + 1) * BLOCK)
        grad, gate, out = grad_ref[rows, :], gate_ref[rows, :], out_ref[rows, :]
        scale = lax.rsqrt(jnp.mean(out * out, axis=-1, keepdims=True) + epsilon)
        unit = out * scale
        sig = jax.nn.sigmoid(gate)
        normed_grad = grad * (gate * sig)
        gate_grad_ref[rows, :] = (grad * (unit * gain) * (sig * (1.0 + gate * (1.0 - sig)))).astype(jnp.bfloat16)
        gain_grad = gain_grad + jnp.sum(normed_grad * unit, axis=0, keepdims=True)
        inner = normed_grad * gain
        out_grad = scale * (inner - unit * jnp.mean(unit * inner, axis=-1, keepdims=True))
        out_grad_ref[rows, :] = out_grad
        grads.append(out_grad)
    gain_grad_ref[0] = gain_grad
    d = [mm_tn(qt_ref[0, i], grads[i]) for i in range(count)]
    for i in range(count):
        d_ref[0, i] = d[i]
    for j, chain in enumerate(chains(counts)):
        dseg_ref[0, j] = d[chain[-1]]
        for i in list(chain)[-2::-1]:
            dseg_ref[0, j] = mm_tn(m_ref[0, i], dseg_ref[0, j]) + d_ref[0, i]


def unit_back(raw, grad):
    factor = row_factor(raw)
    unit = raw * factor
    return factor * (grad - unit * jnp.sum(unit * grad, axis=-1, keepdims=True))


def grads_kernel(counts, q_ref, k_ref, col_ref, row_ref, solver_ref, scores_ref, w_ref, vt_ref, m_ref, d_ref, states_ref, out_grad_ref, later_ref, q_grad_ref, k_grad_ref, v_grad_ref, col_grad_ref, row_grad_ref):
    count = sum(counts)
    span = range(count)
    lower, strict, identity = square_masks()
    raw_q, raw_k = split(q_ref[...], count), split(k_ref[...], count)
    query = [x * row_factor(x) for x in raw_q]
    key = [x * row_factor(x) for x in raw_k]
    fade, ratio, growth, remain, beta, end = decays(col_ref, row_ref, count)
    out_grad = split(out_grad_ref[...], count)
    later = [None] * count
    for j, chain in enumerate(chains(counts)):
        state = later_ref[0, j]
        for i in list(chain)[::-1]:
            later[i] = state
            if i != chain[0]:
                state = mm_tn(m_ref[0, i], state) + d_ref[0, i]
    states = [states_ref[0, i] for i in span]
    update = [vt_ref[0, i] - mm(w_ref[0, i], states[i]) for i in span]
    update_grad = [
        mm_tn(scores_ref[0, i], out_grad[i]) + mm(key[i] * (remain[i] * beta[i]), later[i]) for i in span
    ]
    solved = [mm_tn(solver_ref[0, i], update_grad[i]) for i in span]
    scores_grad = each(mm_nt, out_grad, update)
    inner_grad = each(lambda y, u: jnp.where(strict, -mm_nt(y, u), 0.0), solved, update)
    query_dot = each(mm_nt, query, key)
    keys_dot = each(mm_nt, key, key)
    from_out = each(mm_nt, out_grad, states)
    from_solved = each(mm_nt, solved, states)
    from_update = each(mm_nt, update, later)
    weighted_scores = each(lambda p, x: p * x, ratio, scores_grad)
    weighted_inner = each(lambda p, x: p * x, ratio, inner_grad)
    q_grad = [growth[i] * from_out[i] + mm(weighted_scores[i], key[i]) for i in span]
    k_grad = [
        mm_tn(weighted_scores[i], query[i])
        + (remain[i] * beta[i]) * from_update[i]
        - growth[i] * from_solved[i]
        + mm(weighted_inner[i], key[i])
        + mm_tn(weighted_inner[i], key[i])
        for i in span
    ]
    last_row = (lax.broadcasted_iota(jnp.int32, (BLOCK, 1), 0) == BLOCK - 1).astype(f32)
    for i in span:
        rows = slice(i * BLOCK, (i + 1) * BLOCK)
        q_grad_ref[rows, :] = unit_back(raw_q[i], q_grad[i]).astype(jnp.bfloat16)
        k_grad_ref[rows, :] = unit_back(raw_k[i], k_grad[i]).astype(jnp.bfloat16)
        v_grad_ref[rows, :] = solved[i].astype(jnp.bfloat16)
        faded = fade[i] * (scores_grad[i] * query_dot[i] + inner_grad[i] * keys_dot[i])
        b_row = row_ref[0, i, 1:2, :]
        growth_grad = jnp.sum(query[i] * from_out[i] - key[i] * from_solved[i], axis=-1, keepdims=True)
        weight_grad = jnp.sum(key[i] * from_update[i], axis=-1, keepdims=True)
        pulled = remain[i] * beta[i] * weight_grad
        tail = jnp.sum(pulled, axis=0, keepdims=True) + end[i] * jnp.sum(
            jnp.sum(later[i] * states[i], axis=-1, keepdims=True), axis=0, keepdims=True
        )
        c_grad = jnp.sum(faded * b_row, axis=-1, keepdims=True) + growth[i] * growth_grad - pulled + last_row * tail
        col_grad_ref[0, i, :, 0:1] = c_grad
        col_grad_ref[0, i, :, 1:2] = remain[i] * weight_grad
        row_grad_ref[0, i] = jnp.sum(faded, axis=0, keepdims=True)


def whole(shape):
    return pl.BlockSpec((1,) + tuple(shape[1:]), lambda j: (j,) + (0,) * (len(shape) - 1))


def columns(rows, width, first=0):
    return pl.BlockSpec((rows, width), lambda j: (0, j + first))


def shaped(shape, dtype=f32):
    return jax.ShapeDtypeStruct(shape, dtype)


def call(kernel, counts, heads, inputs, outputs, flops):
    moved = sum(x.size * x.dtype.itemsize for x, _ in inputs) + sum(
        x.size * x.dtype.itemsize for x, _ in outputs
    )
    return pl.pallas_call(
        functools.partial(kernel, counts),
        grid=(heads,),
        in_specs=[s for _, s in inputs],
        out_specs=[s for _, s in outputs],
        out_shape=[x for x, _ in outputs],
        compiler_params=pltpu.CompilerParams(vmem_limit_bytes=48 << 20),
        cost_estimate=pl.CostEstimate(flops=flops, bytes_accessed=moved, transcendentals=0),
    )(*[x for x, _ in inputs])


def per_head(heads, *shape, dtype=f32):
    s = (heads,) + shape
    return shaped(s, dtype), whole(s)


def flat(array, width, first=0):
    return array, columns(array.shape[0], width, first)


def stacked(array):
    return array, whole(array.shape)


def solve(counts, heads, proj, col, row):
    n, dk, dv = sum(counts), 128, 256
    return call(
        solve_kernel, counts, heads,
        [flat(proj, dk), flat(proj, dk, heads), flat(proj, dv, heads), stacked(col), stacked(row)],
        [per_head(heads, n, BLOCK, BLOCK), per_head(heads, n, BLOCK, BLOCK), per_head(heads, n, BLOCK, dk),
         per_head(heads, n, BLOCK, dv), per_head(heads, n, BLOCK, dk), per_head(heads, n, dk, dk),
         per_head(heads, n, dk, dv), per_head(heads, len(counts), dk, dk), per_head(heads, len(counts), dk, dv)],
        heads * n * 100_000_000,
    )


def outputs_of(counts, heads, state, m, b, qt, scores, vt, gate_pre, gain):
    n, dk, dv = sum(counts), 128, 256
    rows = gate_pre.shape[0]
    cols = columns(rows, dv)
    return call(
        output_kernel, counts, heads,
        [stacked(state), stacked(m), stacked(b), stacked(qt), stacked(scores), stacked(vt), flat(gate_pre, dv),
         (gain, pl.BlockSpec((1, dv), lambda j: (0, 0)))],
        [per_head(heads, n, dk, dv), (shaped((rows, heads * dv)), cols), (shaped((rows, heads * dv), jnp.bfloat16), cols)],
        heads * n * 50_000_000,
    )


def output_grads_of(counts, heads, grad, gate_pre, outs, gain, qt, m):
    n, dk, dv = sum(counts), 128, 256
    rows = gate_pre.shape[0]
    cols = columns(rows, dv)
    return call(
        output_grad_kernel, counts, heads,
        [flat(grad, dv), flat(gate_pre, dv), flat(outs, dv), (gain, pl.BlockSpec((1, dv), lambda j: (0, 0))), stacked(qt), stacked(m)],
        [(shaped((rows, heads * dv)), cols), (shaped((rows, heads * dv), jnp.bfloat16), cols),
         per_head(heads, 1, dv), per_head(heads, n, dk, dv), per_head(heads, len(counts), dk, dv)],
        heads * n * 50_000_000,
    )


def input_grads_of(counts, heads, proj, col, row, solver, scores, w, vt, m, d, states, out_grad, later):
    n, dk, dv = sum(counts), 128, 256
    rows = proj.shape[0]
    return call(
        grads_kernel, counts, heads,
        [flat(proj, dk), flat(proj, dk, heads), stacked(col), stacked(row), stacked(solver), stacked(scores), stacked(w),
         stacked(vt), stacked(m), stacked(d), stacked(states), flat(out_grad, dv), stacked(later)],
        [(shaped((rows, heads * dk), jnp.bfloat16), columns(rows, dk)), (shaped((rows, heads * dk), jnp.bfloat16), columns(rows, dk)),
         (shaped((rows, heads * dv), jnp.bfloat16), columns(rows, dv)), per_head(heads, n, BLOCK, 2), per_head(heads, n, 1, BLOCK)],
        heads * n * 150_000_000,
    )


def feed_kernel(stage_ref, x_ref, k_ref, xs_ref, ks_ref, w1_ref, w3_ref, w2_ref, t1_ref, t3_ref, t2_ref, feed_ref, back_ref, main_ref, main_other_ref, tail_ref, tail_other_ref, active_s, gate_s, up_s):
    step, chunk = pl.program_id(0), pl.program_id(1)
    own = feed_ref.shape[0]
    near, piece = x_ref.shape[1] // own, x_ref.shape[2]
    stage = stage_ref[0]
    here = pl.ds(pl.multiple_of(lax.rem(stage, near) * own, own), own)

    @pl.when((step == 0) & (chunk == 0))
    def _():
        feed_ref[...] = jnp.zeros_like(feed_ref)
        back_ref[...] = jnp.zeros_like(back_ref)

    def work(w1, w3, w2, out_refs):
        wide = w1.shape[1]
        gate, up, grad = (
            sum(
                jnp.dot(rows[i], w[i * piece : (i + 1) * piece, :], preferred_element_type=f32)
                for i in range(rows.shape[0])
            )
            for rows, w in ((x_ref, w1), (x_ref, w3), (k_ref, w2))
        )
        sig = jax.nn.sigmoid(gate)
        silu = gate * sig
        active = (silu * up).astype(jnp.bfloat16)
        gate_grad = (grad * up * (sig * (1.0 + gate * (1.0 - sig)))).astype(jnp.bfloat16)
        up_grad = (grad * silu).astype(jnp.bfloat16)
        active_s[:, :wide] = active
        gate_s[:, :wide] = gate_grad
        up_s[:, :wide] = up_grad

        @pl.when(chunk == stage // near)
        def _():
            feed_ref[...] += contract_cols(active_s[here, :wide], w2[...])
            back_ref[...] += contract_cols(gate_s[here, :wide], w1[...])
            back_ref[...] += contract_cols(up_s[here, :wide], w3[...])

        parts = (
            jnp.dot(xs_ref[...], gate_grad, preferred_element_type=f32),
            jnp.dot(xs_ref[...], up_grad, preferred_element_type=f32),
            jnp.dot(ks_ref[...], active, preferred_element_type=f32),
        )
        for i, p in enumerate(parts):
            place = slice(i * wide, (i + 1) * wide)
            quota = p.shape[0] // 2

            @pl.when(chunk == 0)
            def _():
                out_refs[0][:, place] = p[:quota]
                out_refs[1][:, place] = p[quota:]

            @pl.when(chunk > 0)
            def _():
                out_refs[0][:, place] += p[:quota]
                out_refs[1][:, place] += p[quota:]

    work(w1_ref, w3_ref, w2_ref, (main_ref, main_other_ref))

    @pl.when(step == pl.num_programs(0) - 1)
    def _():
        work(t1_ref, t3_ref, t2_ref, (tail_ref, tail_other_ref))


def feed_forward(stage, rows, grads, row_cols, grad_cols, weights, own):
    pieces, positions, piece = rows.shape
    width = pieces * piece
    picked = row_cols.shape[0]
    tile, rest = 256, 128
    steps = (weights.shape[1] - 3 * rest) // (3 * tile)
    chunk = min(positions, 4 * own)
    first_tail = 3 * steps * tile // rest
    grid = (steps, positions // chunk)
    tokens = pl.BlockSpec((pieces, chunk, piece), lambda i, t, s: (0, t, 0))
    columns_of = pl.BlockSpec((picked, chunk), lambda i, t, s: (0, t))

    def main_of(n):
        return pl.BlockSpec((width, tile), lambda i, t, s: (0, n * steps + i))

    def tail_of(n):
        return pl.BlockSpec((width, rest), lambda i, t, s: (0, first_tail + n))

    def fixed(*shape):
        return pl.BlockSpec(shape, lambda i, t, s: (0, 0))

    flops = 2 * positions * width * weights.shape[1] + 2 * own * width * weights.shape[1] + 2 * positions * picked * weights.shape[1]
    return pl.pallas_call(
        feed_kernel,
        grid_spec=pltpu.PrefetchScalarGridSpec(
            num_scalar_prefetch=1,
            grid=grid,
            in_specs=[tokens, tokens, columns_of, columns_of, main_of(0), main_of(1), main_of(2), tail_of(0), tail_of(1), tail_of(2)],
            out_specs=[
                fixed(own, width),
                fixed(own, width),
                pl.BlockSpec((picked // 2, 3 * tile), lambda i, t, s: (0, i)),
                pl.BlockSpec((picked // 2, 3 * tile), lambda i, t, s: (0, i)),
                fixed(picked // 2, 3 * rest),
                fixed(picked // 2, 3 * rest),
            ],
            scratch_shapes=[pltpu.VMEM((chunk, tile), jnp.bfloat16)] * 3,
        ),
        out_shape=[
            shaped((own, width)),
            shaped((own, width)),
            shaped((picked // 2, 3 * tile * steps)),
            shaped((picked // 2, 3 * tile * steps)),
            shaped((picked // 2, 3 * rest)),
            shaped((picked // 2, 3 * rest)),
        ],
        compiler_params=pltpu.CompilerParams(
            dimension_semantics=("arbitrary", "arbitrary"), vmem_limit_bytes=56 << 20
        ),
        cost_estimate=pl.CostEstimate(
            flops=flops, bytes_accessed=2 * weights.size + 8 * positions * width, transcendentals=0
        ),
    )(stage, rows, grads, row_cols, grad_cols, weights, weights, weights, weights, weights, weights)


QUARTERS = 4


def swap(array):
    return lax.ppermute(array, "dp", [(0, 1), (1, 0)])


def relay(mats, offsets, forward):
    size = lax.axis_size("seq")
    entering = jnp.zeros_like(offsets)
    leaving = offsets
    for step in range(size - 1):
        route = [(step, step + 1)] if forward else [(size - 1 - step, size - 2 - step)]
        got = jnp.stack([lax.ppermute(leaving[i], "seq", route) for i in range(offsets.shape[0])])
        entering = entering + got
        if step < size - 2:
            leaving = jnp.matmul(mats, got, precision=highest) + offsets
    return entering, leaving


def together(*arrays):
    return lax.optimization_barrier(arrays)


def everyone(part):
    return lax.all_gather(part, ("dp", "seq"), axis=0, tiled=True)


def share(rows):
    wide = jnp.broadcast_to(rows[None], (lax.axis_size("head"),) + rows.shape)
    return lax.all_to_all(wide, "head", split_axis=0, concat_axis=0, tiled=True)


def add_parts(parts):
    got = lax.all_to_all(parts.astype(jnp.bfloat16), "head", split_axis=0, concat_axis=0, tiled=True)
    return jnp.sum(got.astype(f32), axis=0)


def add_everywhere(vector):
    for axis in ("dp", "seq", "head"):
        size, step = lax.axis_size(axis), 1
        while step < size:
            vector = vector + lax.ppermute(vector, axis, [(i, i ^ step) for i in range(size)])
            step *= 2
    return vector


def contract_rows(left, right):
    return lax.dot_general(left, right, (((0,), (0,)), ((), ())), preferred_element_type=f32)


def contract_cols(left, right):
    return lax.dot_general(left, right, (((1,), (1,)), ((), ())), preferred_element_type=f32)


def product(left, right):
    return jnp.dot(left, right, preferred_element_type=f32)


def rms_scale(values, gain):
    return values * lax.rsqrt(jnp.mean(values * values, axis=-1, keepdims=True) + epsilon) * gain


def swiglu(gate_in, up_in):
    return jax.nn.silu(gate_in) * up_in


def on_device(
    activations,
    cotangent,
    lengths,
    query_weight,
    key_weight,
    value_weight,
    gate_weight,
    alpha_weight,
    beta_weight,
    out_weight,
    swiglu_gate,
    swiglu_value,
    swiglu_down,
    mixer_gain,
    feed_gain,
    head_gain,
    decay_rate,
    beta_bias,
):
    bf16 = jnp.bfloat16
    core, stage, group = lax.axis_index("dp"), lax.axis_index("seq"), lax.axis_index("head")
    stages, groups = lax.axis_size("seq"), lax.axis_size("head")
    width = activations.shape[2]
    rows0 = activations.shape[1]
    rows1 = rows0 // QUARTERS
    own0, own1 = rows0 // (2 * groups), rows1 // (2 * groups)
    own = own0 + own1
    quota = width // (2 * stages)
    heads = alpha_weight.shape[1] // 2
    counts = (rows0 // BLOCK, rows1 // BLOCK)
    assert groups == QUARTERS and stages % QUARTERS == 0 and rows1 % BLOCK == 0
    first = core == 0

    def part(array, size, axis, offset=0):
        return lax.dynamic_slice_in_dim(array, offset + core * size, size, axis)

    dk, dv = query_weight.shape[1] // 2, value_weight.shape[1] // 2
    slim = 2 * dk + dv
    mixer_cols = []
    for c in range(2):
        mixer_cols += [
            query_weight[:, c * dk : (c + 1) * dk],
            key_weight[:, c * dk : (c + 1) * dk],
            value_weight[:, c * dv : (c + 1) * dv],
        ]
    mixer_cols += [alpha_weight, beta_weight]
    mixer_full = everyone(jnp.concatenate(mixer_cols, axis=1).astype(bf16))
    gates_full = everyone(jnp.concatenate([gate_weight, out_weight], axis=1).astype(bf16))
    hidden_units = swiglu_gate.shape[1]
    even = hidden_units // 256 * 256
    odd = hidden_units - even
    assert 0 < odd <= 128
    three = (swiglu_gate, swiglu_value, swiglu_down)
    spare = ((0, 0), (0, 128 - odd))
    feed_full = everyone(
        jnp.concatenate([w[:, :even] for w in three] + [jnp.pad(w[:, even:], spare) for w in three], axis=1).astype(bf16)
    )

    def chip_rows(rows):
        arrived = jnp.zeros((rows1, width), bf16)
        for b in range(QUARTERS):
            route = [(stages + a, stages + QUARTERS * a + b) for a in range(stages // QUARTERS)]
            arrived = arrived + lax.ppermute(rows[b * rows1 : (b + 1) * rows1], ("dp", "seq"), route)
        near0 = lax.ppermute(rows, "dp", [(0, 1)])
        near1 = lax.ppermute(arrived, "dp", [(1, 0)])
        return jnp.concatenate([jnp.where(first, rows, near0), jnp.where(first, near1, arrived)], axis=0)

    inputs = chip_rows(activations[0])
    inputs, late = together(inputs, cotangent[0])
    inputs = inputs.astype(f32)
    spots0 = stage * rows0 + lax.broadcasted_iota(jnp.int32, (rows0, 1), 0)
    spots1 = stage * rows1 + lax.broadcasted_iota(jnp.int32, (rows1, 1), 0)
    mask = jnp.concatenate([spots0 < lengths[0], spots1 < lengths[1]], axis=0).astype(f32)
    masked = (chip_rows(late).astype(f32) * mask).astype(bf16)

    def by_owner(rows):
        wide = rows.shape[1]
        r0 = rows[:rows0].reshape(groups, 2, own0, wide)
        r1 = rows[rows0:].reshape(groups, 2, own1, wide)
        return jnp.concatenate([r0, r1], axis=2).swapaxes(0, 1)

    def in_time(owned):
        wide = owned.shape[3]
        turned = owned.swapaxes(0, 1)
        return jnp.concatenate(
            [turned[:, :, :own0].reshape(rows0, wide), turned[:, :, own0:].reshape(rows1, wide)], axis=0
        )

    def of_core(owned, which):
        return lax.dynamic_index_in_dim(owned, which, 0, keepdims=False)

    def of_group(rows):
        return lax.dynamic_index_in_dim(rows, group, 0, keepdims=False)

    def add_rows(partial):
        owned = by_owner(partial)
        return add_parts(of_core(owned, core) + swap(of_core(owned, 1 - core)))

    def owned_columns(rows):
        got = lax.all_to_all(rows, ("dp", "seq"), split_axis=1, concat_axis=0, tiled=True)
        got = share(got).reshape(groups, 2, stages, own, quota).transpose(2, 0, 1, 3, 4)
        return jnp.concatenate(
            [got[:, :, :, :own0].reshape(stages, rows0, quota), got[:, :, :, own0:].reshape(stages, rows1, quota)], axis=1
        ).reshape(stages * (rows0 + rows1), quota)

    def across_stages(rows):
        wide = jnp.broadcast_to(rows[None], (stages,) + rows.shape)
        met = lax.all_to_all(wide, "seq", split_axis=0, concat_axis=0, tiled=True)
        return met.reshape(stages * rows.shape[0], rows.shape[1])

    def own_columns(rows):
        pieces, positions, piece = rows.shape
        both = []
        for which in (core, 1 - core):
            start = (which * stages + stage) * quota
            both.append(lax.dynamic_slice(rows, (start // piece, 0, start % piece), (1, positions, quota))[0])
        return jnp.concatenate(both, axis=1).T

    own_rows = of_group(of_core(by_owner(inputs), core))
    own_mask = of_group(of_core(by_owner(mask), core))
    tokens_masked = of_core(by_owner(masked), core)
    own_masked = of_group(tokens_masked).astype(f32)
    quarter = width // groups
    masked_met = across_stages(
        lax.dynamic_slice_in_dim(tokens_masked.reshape(groups * own, width), group * quarter, quarter, 1)
    )

    factor1 = lax.rsqrt(jnp.mean(inputs * inputs, axis=-1, keepdims=True) + epsilon)
    unit1 = inputs * factor1
    normed = rms_scale(inputs, mixer_gain).astype(bf16)
    normed_cols = owned_columns(of_group(of_core(by_owner(normed), core)))
    mixer_full, masked_met, normed_cols = together(mixer_full, masked_met, normed_cols)
    mixer_w = part(mixer_full, slim, 1)
    gate_w = part(gates_full, dv, 1)
    out_w = part(gates_full, dv, 1, 2 * dv)
    rates_w = mixer_full[:, 2 * slim :]
    proj = product(normed, mixer_w)
    small_pre = product(normed, rates_w)
    gate_pre = product(normed, gate_w)
    alpha_pre = part(small_pre, heads, 1)
    beta_pre = part(small_pre, heads, 1, 2 * heads)
    head0 = (2 * group + core) * heads
    rates = lax.dynamic_slice_in_dim(decay_rate, head0, heads)
    biases = lax.dynamic_slice_in_dim(beta_bias, head0, heads)
    blocks = sum(counts)

    def to_blocks(array):
        return array.T.reshape(heads, blocks, BLOCK)

    def from_blocks(array):
        return array.reshape(heads, blocks * BLOCK).T

    soft = jax.nn.softplus(alpha_pre)
    beta = jax.nn.sigmoid(beta_pre + biases)
    beta_b = to_blocks(beta)
    upto = (
        lax.broadcasted_iota(jnp.int32, (BLOCK, BLOCK), 0) <= lax.broadcasted_iota(jnp.int32, (BLOCK, BLOCK), 1)
    ).astype(f32)
    sums = jnp.matmul(to_blocks(-rates * soft), upto, precision=highest)
    col = jnp.stack([sums, beta_b], axis=-1)
    row = jnp.stack([sums, beta_b], axis=-2)
    solver, scores, w, vt, qt, m, b, mseg, bseg = solve(counts, heads, proj, col, row)
    state_in, unused_carry = relay(mseg, bseg, True)
    state_in, masked_all = together(state_in, share(masked_met))
    gain_row = head_gain[None]
    states, outs, gated = outputs_of(counts, heads, state_in, m, b, qt, scores, vt, gate_pre, gain_row)
    mixed = add_rows(contract_cols(gated, out_w))
    hidden = own_rows + mixed

    normed2, norm2_back = jax.vjp(rms_scale, hidden, feed_gain)
    feed_in = share(
        across_stages(lax.all_to_all(normed2.astype(bf16), "head", split_axis=1, concat_axis=0, tiled=True))
    )
    feed_part, back_part, main_own, main_other, tail_own, tail_other = feed_forward(
        stage[None], feed_in, masked_all, own_columns(feed_in), own_columns(masked_all), feed_full, groups * own
    )
    normed2_grad = add_parts(back_part.reshape(groups, own, width))
    hidden_back, feed_gain_grad = norm2_back(normed2_grad)
    hidden_grad = own_masked + hidden_back
    mixed_own = hidden_grad.astype(bf16)
    mixed_half = share(mixed_own)
    other_half = swap(mixed_half)
    mixed_in = in_time(
        jnp.stack([jnp.where(first, mixed_half, other_half), jnp.where(first, other_half, mixed_half)])
    )

    gated_all = everyone(gated)
    gated_grad = product(mixed_in, out_w)
    main_other, tail_other = swap(main_other), swap(tail_other)
    gated_grad, gated_all, main_other, tail_other = together(gated_grad, gated_all, main_other, tail_other)
    outs_grad, gate_pre_low, gain_grads, d, dseg = output_grads_of(
        counts, heads, gated_grad, gate_pre, outs, gain_row, qt, m
    )
    gate_pre_all = everyone(gate_pre_low)
    mixed_late, unused_grads = together(mixed_own, dseg)
    mixed_cols = owned_columns(mixed_late)
    later, carry = relay(jnp.swapaxes(mseg, 2, 3), dseg, False)

    half = stages * (rows0 + rows1)
    main_own, main_other, tail_own, tail_other, unused_carry = together(
        main_own, main_other, tail_own, tail_other, carry
    )
    main_own, tail_own = main_own + main_other, tail_own + tail_other

    def feed_grad(n):
        pieces = [main_own[:, (3 * i + n) * 256 : (3 * i + n + 1) * 256].T for i in range(even // 256)]
        turned = jnp.concatenate(pieces + [tail_own[:, n * 128 : n * 128 + odd].T], axis=0)
        return with_layout_constraint(turned, Layout((0, 1)))

    feed_gate_grad, feed_value_grad, down_grad = feed_grad(0), feed_grad(1), feed_grad(2)
    gate_back = contract_cols(gate_pre_low, gate_w)
    later, feed_gate_grad, feed_value_grad, down_grad, gate_back = together(
        later, feed_gate_grad, feed_value_grad, down_grad, gate_back
    )
    query_low, key_low, value_low, col_grad, row_grad = input_grads_of(
        counts, heads, proj, col, row, solver, scores, w, vt, m, d, states, outs_grad, later
    )
    sums_grad = col_grad[..., 0] - row_grad[:, :, 0] * beta_b
    decay_back = from_blocks(jnp.matmul(sums_grad, upto.T, precision=highest))
    beta_back = beta * (1.0 - beta) * from_blocks(col_grad[..., 1] + row_grad[:, :, 0])
    rates_grad = -jnp.sum(soft * decay_back, axis=0)
    biases_grad = jnp.sum(beta_back, axis=0)
    alpha_back = -rates * jax.nn.sigmoid(alpha_pre) * decay_back
    small_low = jnp.concatenate([alpha_back, beta_back], axis=1).astype(bf16)
    slim_low = jnp.concatenate([query_low, key_low, value_low], axis=1)
    slim_all = everyone(slim_low)
    blank = jnp.zeros((rows0 + rows1, 4 * heads), bf16)
    spread = lax.dynamic_update_slice(blank, small_low[:, :heads], (0, core * heads))
    spread = lax.dynamic_update_slice(spread, small_low[:, heads:], (0, (2 + core) * heads))
    total = gate_back + contract_cols(slim_low, mixer_w) + contract_cols(spread, rates_w)
    normed_grad = add_rows(total)
    normed_grad, feed_part, small_late = together(normed_grad, feed_part, small_low)
    feed = add_parts(feed_part.reshape(groups, own, width))
    outputs_own = (own_mask * (hidden + feed)).astype(bf16)
    mixer_gain_part = jnp.sum(total * unit1, axis=0)
    unused_rows, norm1_back = jax.vjp(lambda v: rms_scale(v, mixer_gain), own_rows)
    input_own = (hidden_grad + norm1_back(normed_grad)[0]).astype(bf16)

    small_rows = contract_rows(small_late, normed)
    small_rows = lax.all_to_all(small_rows, ("dp", "seq"), split_axis=1, concat_axis=0, tiled=True)
    small_rows = jnp.sum(small_rows.reshape(2, stages, 2, heads, quota), axis=1)
    alpha_grad = small_rows[:, 0].reshape(2 * heads, quota).T
    beta_grad = small_rows[:, 1].reshape(2 * heads, quota).T
    out_grad = jnp.concatenate(
        [contract_rows(mixed_cols, gated_all[:half]), contract_rows(mixed_cols, gated_all[half:])], axis=1
    )
    gate_grad = jnp.concatenate(
        [contract_rows(normed_cols, gate_pre_all[:half]), contract_rows(normed_cols, gate_pre_all[half:])], axis=1
    )
    slim_all, out_grad, gate_grad = together(slim_all, out_grad, gate_grad)
    slim_halves = [contract_rows(normed_cols, slim_all[:half]), contract_rows(normed_cols, slim_all[half:])]

    def pick(start, size):
        return jnp.concatenate([g[:, start : start + size] for g in slim_halves], axis=1)

    total_heads = decay_rate.shape[0]
    none = jnp.zeros((total_heads,), f32)
    small = add_everywhere(
        jnp.concatenate(
            [
                mixer_gain_part,
                feed_gain_grad,
                jnp.sum(gain_grads, axis=(0, 1)),
                lax.dynamic_update_slice(none, rates_grad, (head0,)),
                lax.dynamic_update_slice(none, biases_grad, (head0,)),
            ]
        )
    )
    edges = [width, 2 * width, 2 * width + head_gain.shape[0], 2 * width + head_gain.shape[0] + total_heads]

    def place(rows):
        r0, r1 = rows[:own0], rows[own0:]
        out0 = jnp.concatenate([r0, lax.ppermute(r0, "dp", [(1, 0)])], axis=0)
        pair = jnp.concatenate([lax.ppermute(r1, "dp", [(0, 1)]), r1], axis=0)
        routes = [
            [
                ((stages + QUARTERS * a + b) * groups + k, (stages + a) * groups + b)
                for a in range(stages // QUARTERS)
                for b in range(QUARTERS)
            ]
            for k in range(groups)
        ]
        out1 = jnp.concatenate([lax.ppermute(pair, ("dp", "seq", "head"), route) for route in routes], axis=0)
        return jnp.where(first, out0, out1)[None]

    return (
        place(outputs_own),
        place(input_own),
        pick(0, dk),
        pick(dk, dk),
        pick(2 * dk, dv),
        gate_grad,
        alpha_grad,
        beta_grad,
        out_grad,
        feed_gate_grad.T,
        feed_value_grad.T,
        down_grad.T,
        small[: edges[0]],
        small[edges[0] : edges[1]],
        small[edges[1] : edges[2]],
        small[edges[2] : edges[3]],
        small[edges[3] :],
    )


def solution(mesh):
    return jax.shard_map(
        on_device,
        mesh=mesh,
        in_specs=(
            P("dp", "seq", None),
            P("dp", "seq", None),
            P(),
            P(("dp", "seq"), "head"),
            P(("dp", "seq"), "head"),
            P(("dp", "seq"), "head"),
            P(("dp", "seq"), "head"),
            P(("dp", "seq"), "head"),
            P(("dp", "seq"), "head"),
            P(("dp", "seq"), "head"),
            P(("dp", "seq"), "head"),
            P(("dp", "seq"), "head"),
            P(("dp", "seq"), "head"),
            P(),
            P(),
            P(),
            P(),
            P(),
        ),
        out_specs=(
            P("dp", ("seq", "head"), None),
            P("dp", ("seq", "head"), None),
            P(("dp", "seq"), "head"),
            P(("dp", "seq"), "head"),
            P(("dp", "seq"), "head"),
            P(("dp", "seq"), "head"),
            P(("dp", "seq"), "head"),
            P(("dp", "seq"), "head"),
            P(("dp", "seq"), "head"),
            P(("dp", "seq"), "head"),
            P(("dp", "seq"), "head"),
            P(("dp", "seq"), "head"),
            P(),
            P(),
            P(),
            P(),
            P(),
        ),
        check_vma=False,
    )
```

```python
import functools

import jax
import jax.numpy as jnp
from jax import lax
from jax.experimental import pallas as pl
from jax.experimental.pallas import tpu as pltpu
from jax.sharding import PartitionSpec as P

BLOCK = 64
epsilon = 1e-06
highest = lax.Precision.HIGHEST
f32 = jnp.float32


def mm(left, right, a=1, b=0):
    return lax.dot_general(
        left, right, (((a,), (b,)), ((), ())), precision=highest, preferred_element_type=f32
    )


def mm_nt(left, right):
    return mm(left, right, 1, 1)


def mm_tn(left, right):
    return mm(left, right, 0, 0)


def each(f, *lists):
    return [f(*items) for items in zip(*lists)]


def square_masks():
    rows = lax.broadcasted_iota(jnp.int32, (BLOCK, BLOCK), 0)
    cols = lax.broadcasted_iota(jnp.int32, (BLOCK, BLOCK), 1)
    return rows >= cols, rows > cols, (rows == cols).astype(f32)


def row_factor(values):
    return lax.rsqrt(jnp.sum(values * values, axis=-1, keepdims=True) + epsilon)


def split(values, count):
    return [values[i * BLOCK : (i + 1) * BLOCK] for i in range(count)]


def decays(col_ref, row_ref, count):
    lower, strict, identity = square_masks()
    out = []
    for i in range(count):
        c_col, b_col = col_ref[0, i, :, 0:1], col_ref[0, i, :, 1:2]
        c_row, b_row = row_ref[0, i, 0:1, :], row_ref[0, i, 1:2, :]
        fade = jnp.where(lower, jnp.exp(jnp.where(lower, c_col - c_row, 0.0)), 0.0)
        last = c_col[BLOCK - 1 : BLOCK, :]
        out.append((fade, fade * b_row, jnp.exp(c_col), jnp.exp(last - c_col), b_col, jnp.exp(last)))
    return [list(items) for items in zip(*out)]


def chains(counts):
    start, out = 0, []
    for count in counts:
        out.append(range(start, start + count))
        start += count
    return out


def solve_kernel(counts, q_ref, k_ref, v_ref, col_ref, row_ref, solver_ref, scores_ref, w_ref, vt_ref, qt_ref, m_ref, b_ref, mseg_ref, bseg_ref):
    count = sum(counts)
    lower, strict, identity = square_masks()
    query = q_ref[...]
    query = split(query * row_factor(query), count)
    key = k_ref[...]
    key = split(key * row_factor(key), count)
    value = split(v_ref[...], count)
    fade, ratio, growth, remain, beta, end = decays(col_ref, row_ref, count)
    power = each(lambda k, p: jnp.where(strict, -mm_nt(k, k) * p, 0.0), key, ratio)
    solver = [identity + p for p in power]
    for _ in range((BLOCK - 1).bit_length() - 1):
        power = each(lambda p: mm(p, p), power)
        solver = each(lambda s, p: s + mm(s, p), solver, power)
    scores = each(lambda q, k, p: mm_nt(q, k) * p, query, key, ratio)
    w = each(lambda s, g, k: mm(s, g * k), solver, growth, key)
    vt = each(mm, solver, value)
    qt = each(lambda g, q, a, x: g * q - mm(a, x), growth, query, scores, w)
    weighted = each(lambda k, r, b: k * (r * b), key, remain, beta)
    size = query[0].shape[1]
    wide = (
        lax.broadcasted_iota(jnp.int32, (size, size), 0)
        == lax.broadcasted_iota(jnp.int32, (size, size), 1)
    ).astype(f32)
    m = each(lambda e, k, x: e * wide - mm_tn(k, x), end, weighted, w)
    b = each(mm_tn, weighted, vt)
    for i in range(count):
        solver_ref[0, i] = solver[i]
        scores_ref[0, i] = scores[i]
        w_ref[0, i] = w[i]
        vt_ref[0, i] = vt[i]
        qt_ref[0, i] = qt[i]
        m_ref[0, i] = m[i]
        b_ref[0, i] = b[i]
    for j, chain in enumerate(chains(counts)):
        mseg_ref[0, j] = m[chain[0]]
        bseg_ref[0, j] = b[chain[0]]
        for i in chain[1:]:
            bseg_ref[0, j] = mm(m_ref[0, i], bseg_ref[0, j]) + b_ref[0, i]
            mseg_ref[0, j] = mm(m_ref[0, i], mseg_ref[0, j])


def output_kernel(counts, state_ref, m_ref, b_ref, qt_ref, scores_ref, vt_ref, gate_ref, gain_ref, states_ref, out_ref, gated_ref):
    count = sum(counts)
    states = [None] * count
    for j, chain in enumerate(chains(counts)):
        state = state_ref[0, j]
        for i in chain:
            states[i] = state
            states_ref[0, i] = state
            if i != chain[-1]:
                state = mm(m_ref[0, i], state) + b_ref[0, i]
    gain = gain_ref[...]
    outs = [mm(qt_ref[0, i], states[i]) + mm(scores_ref[0, i], vt_ref[0, i]) for i in range(count)]
    for i in range(count):
        rows = slice(i * BLOCK, (i + 1) * BLOCK)
        out = outs[i]
        gate = gate_ref[rows, :]
        scale = lax.rsqrt(jnp.mean(out * out, axis=-1, keepdims=True) + epsilon)
        out_ref[rows, :] = out
        gated_ref[rows, :] = (out * scale * gain * (gate * jax.nn.sigmoid(gate))).astype(jnp.bfloat16)


def output_grad_kernel(counts, grad_ref, gate_ref, out_ref, gain_ref, qt_ref, m_ref, out_grad_ref, gate_grad_ref, gain_grad_ref, d_ref, dseg_ref):
    count = sum(counts)
    gain = gain_ref[...]
    gain_grad = jnp.zeros_like(gain)
    grads = []
    for i in range(count):
        rows = slice(i * BLOCK, (i + 1) * BLOCK)
        grad, gate, out = grad_ref[rows, :], gate_ref[rows, :], out_ref[rows, :]
        scale = lax.rsqrt(jnp.mean(out * out, axis=-1, keepdims=True) + epsilon)
        unit = out * scale
        sig = jax.nn.sigmoid(gate)
        normed_grad = grad * (gate * sig)
        gate_grad_ref[rows, :] = (grad * (unit * gain) * (sig * (1.0 + gate * (1.0 - sig)))).astype(jnp.bfloat16)
        gain_grad = gain_grad + jnp.sum(normed_grad * unit, axis=0, keepdims=True)
        inner = normed_grad * gain
        out_grad = scale * (inner - unit * jnp.mean(unit * inner, axis=-1, keepdims=True))
        out_grad_ref[rows, :] = out_grad
        grads.append(out_grad)
    gain_grad_ref[0] = gain_grad
    d = [mm_tn(qt_ref[0, i], grads[i]) for i in range(count)]
    for i in range(count):
        d_ref[0, i] = d[i]
    for j, chain in enumerate(chains(counts)):
        dseg_ref[0, j] = d[chain[-1]]
        for i in list(chain)[-2::-1]:
            dseg_ref[0, j] = mm_tn(m_ref[0, i], dseg_ref[0, j]) + d_ref[0, i]


def unit_back(raw, grad):
    factor = row_factor(raw)
    unit = raw * factor
    return factor * (grad - unit * jnp.sum(unit * grad, axis=-1, keepdims=True))


def grads_kernel(counts, q_ref, k_ref, col_ref, row_ref, solver_ref, scores_ref, w_ref, vt_ref, m_ref, d_ref, states_ref, out_grad_ref, later_ref, q_grad_ref, k_grad_ref, v_grad_ref, col_grad_ref, row_grad_ref):
    count = sum(counts)
    span = range(count)
    lower, strict, identity = square_masks()
    raw_q, raw_k = split(q_ref[...], count), split(k_ref[...], count)
    query = [x * row_factor(x) for x in raw_q]
    key = [x * row_factor(x) for x in raw_k]
    fade, ratio, growth, remain, beta, end = decays(col_ref, row_ref, count)
    out_grad = split(out_grad_ref[...], count)
    later = [None] * count
    for j, chain in enumerate(chains(counts)):
        state = later_ref[0, j]
        for i in list(chain)[::-1]:
            later[i] = state
            if i != chain[0]:
                state = mm_tn(m_ref[0, i], state) + d_ref[0, i]
    states = [states_ref[0, i] for i in span]
    update = [vt_ref[0, i] - mm(w_ref[0, i], states[i]) for i in span]
    update_grad = [
        mm_tn(scores_ref[0, i], out_grad[i]) + mm(key[i] * (remain[i] * beta[i]), later[i]) for i in span
    ]
    solved = [mm_tn(solver_ref[0, i], update_grad[i]) for i in span]
    scores_grad = each(mm_nt, out_grad, update)
    inner_grad = each(lambda y, u: jnp.where(strict, -mm_nt(y, u), 0.0), solved, update)
    query_dot = each(mm_nt, query, key)
    keys_dot = each(mm_nt, key, key)
    from_out = each(mm_nt, out_grad, states)
    from_solved = each(mm_nt, solved, states)
    from_update = each(mm_nt, update, later)
    weighted_scores = each(lambda p, x: p * x, ratio, scores_grad)
    weighted_inner = each(lambda p, x: p * x, ratio, inner_grad)
    q_grad = [growth[i] * from_out[i] + mm(weighted_scores[i], key[i]) for i in span]
    k_grad = [
        mm_tn(weighted_scores[i], query[i])
        + (remain[i] * beta[i]) * from_update[i]
        - growth[i] * from_solved[i]
        + mm(weighted_inner[i], key[i])
        + mm_tn(weighted_inner[i], key[i])
        for i in span
    ]
    last_row = (lax.broadcasted_iota(jnp.int32, (BLOCK, 1), 0) == BLOCK - 1).astype(f32)
    for i in span:
        rows = slice(i * BLOCK, (i + 1) * BLOCK)
        q_grad_ref[rows, :] = unit_back(raw_q[i], q_grad[i]).astype(jnp.bfloat16)
        k_grad_ref[rows, :] = unit_back(raw_k[i], k_grad[i]).astype(jnp.bfloat16)
        v_grad_ref[rows, :] = solved[i].astype(jnp.bfloat16)
        faded = fade[i] * (scores_grad[i] * query_dot[i] + inner_grad[i] * keys_dot[i])
        b_row = row_ref[0, i, 1:2, :]
        growth_grad = jnp.sum(query[i] * from_out[i] - key[i] * from_solved[i], axis=-1, keepdims=True)
        weight_grad = jnp.sum(key[i] * from_update[i], axis=-1, keepdims=True)
        pulled = remain[i] * beta[i] * weight_grad
        tail = jnp.sum(pulled, axis=0, keepdims=True) + end[i] * jnp.sum(
            jnp.sum(later[i] * states[i], axis=-1, keepdims=True), axis=0, keepdims=True
        )
        c_grad = jnp.sum(faded * b_row, axis=-1, keepdims=True) + growth[i] * growth_grad - pulled + last_row * tail
        col_grad_ref[0, i, :, 0:1] = c_grad
        col_grad_ref[0, i, :, 1:2] = remain[i] * weight_grad
        row_grad_ref[0, i] = jnp.sum(faded, axis=0, keepdims=True)


def whole(shape):
    return pl.BlockSpec((1,) + tuple(shape[1:]), lambda j: (j,) + (0,) * (len(shape) - 1))


def columns(rows, width, first=0):
    return pl.BlockSpec((rows, width), lambda j: (0, j + first))


def shaped(shape, dtype=f32):
    return jax.ShapeDtypeStruct(shape, dtype)


def call(kernel, counts, heads, inputs, outputs, flops):
    moved = sum(x.size * x.dtype.itemsize for x, _ in inputs) + sum(
        x.size * x.dtype.itemsize for x, _ in outputs
    )
    return pl.pallas_call(
        functools.partial(kernel, counts),
        grid=(heads,),
        in_specs=[s for _, s in inputs],
        out_specs=[s for _, s in outputs],
        out_shape=[x for x, _ in outputs],
        compiler_params=pltpu.CompilerParams(vmem_limit_bytes=48 << 20),
        cost_estimate=pl.CostEstimate(flops=flops, bytes_accessed=moved, transcendentals=0),
    )(*[x for x, _ in inputs])


def per_head(heads, *shape, dtype=f32):
    s = (heads,) + shape
    return shaped(s, dtype), whole(s)


def flat(array, width, first=0):
    return array, columns(array.shape[0], width, first)


def stacked(array):
    return array, whole(array.shape)


def solve(counts, heads, proj, col, row):
    n, dk, dv = sum(counts), 128, 256
    return call(
        solve_kernel, counts, heads,
        [flat(proj, dk), flat(proj, dk, heads), flat(proj, dv, heads), stacked(col), stacked(row)],
        [per_head(heads, n, BLOCK, BLOCK), per_head(heads, n, BLOCK, BLOCK), per_head(heads, n, BLOCK, dk),
         per_head(heads, n, BLOCK, dv), per_head(heads, n, BLOCK, dk), per_head(heads, n, dk, dk),
         per_head(heads, n, dk, dv), per_head(heads, len(counts), dk, dk), per_head(heads, len(counts), dk, dv)],
        heads * n * 100_000_000,
    )


def outputs_of(counts, heads, state, m, b, qt, scores, vt, gate_pre, gain):
    n, dk, dv = sum(counts), 128, 256
    rows = gate_pre.shape[0]
    cols = columns(rows, dv)
    return call(
        output_kernel, counts, heads,
        [stacked(state), stacked(m), stacked(b), stacked(qt), stacked(scores), stacked(vt), flat(gate_pre, dv),
         (gain, pl.BlockSpec((1, dv), lambda j: (0, 0)))],
        [per_head(heads, n, dk, dv), (shaped((rows, heads * dv)), cols), (shaped((rows, heads * dv), jnp.bfloat16), cols)],
        heads * n * 50_000_000,
    )


def output_grads_of(counts, heads, grad, gate_pre, outs, gain, qt, m):
    n, dk, dv = sum(counts), 128, 256
    rows = gate_pre.shape[0]
    cols = columns(rows, dv)
    return call(
        output_grad_kernel, counts, heads,
        [flat(grad, dv), flat(gate_pre, dv), flat(outs, dv), (gain, pl.BlockSpec((1, dv), lambda j: (0, 0))), stacked(qt), stacked(m)],
        [(shaped((rows, heads * dv)), cols), (shaped((rows, heads * dv), jnp.bfloat16), cols),
         per_head(heads, 1, dv), per_head(heads, n, dk, dv), per_head(heads, len(counts), dk, dv)],
        heads * n * 50_000_000,
    )


def input_grads_of(counts, heads, proj, col, row, solver, scores, w, vt, m, d, states, out_grad, later):
    n, dk, dv = sum(counts), 128, 256
    rows = proj.shape[0]
    return call(
        grads_kernel, counts, heads,
        [flat(proj, dk), flat(proj, dk, heads), stacked(col), stacked(row), stacked(solver), stacked(scores), stacked(w),
         stacked(vt), stacked(m), stacked(d), stacked(states), flat(out_grad, dv), stacked(later)],
        [(shaped((rows, heads * dk), jnp.bfloat16), columns(rows, dk)), (shaped((rows, heads * dk), jnp.bfloat16), columns(rows, dk)),
         (shaped((rows, heads * dv), jnp.bfloat16), columns(rows, dv)), per_head(heads, n, BLOCK, 2), per_head(heads, n, 1, BLOCK)],
        heads * n * 150_000_000,
    )


def feed_kernel(stage_ref, x_ref, k_ref, xs_ref, ks_ref, w1_ref, w3_ref, w2_ref, t1_ref, t3_ref, t2_ref, sums_ref, main_ref, main_other_ref, tail_ref, tail_other_ref, active_s, gate_s, up_s):
    step, chunk = pl.program_id(0), pl.program_id(1)
    own, width = sums_ref.shape[0], sums_ref.shape[1] // 2
    near, piece = x_ref.shape[1] // own, x_ref.shape[2]
    stage = stage_ref[0]
    here = pl.ds(pl.multiple_of(lax.rem(stage, near) * own, own), own)

    @pl.when((step == 0) & (chunk == 0))
    def _():
        sums_ref[...] = jnp.zeros_like(sums_ref)

    def work(w1, w3, w2, out_refs):
        wide = w1.shape[1]
        gate, up, grad = (
            sum(
                jnp.dot(rows[i], w[i * piece : (i + 1) * piece, :], preferred_element_type=f32)
                for i in range(rows.shape[0])
            )
            for rows, w in ((x_ref, w1), (x_ref, w3), (k_ref, w2))
        )
        sig = jax.nn.sigmoid(gate)
        silu = gate * sig
        active = (silu * up).astype(jnp.bfloat16)
        gate_grad = (grad * up * (sig * (1.0 + gate * (1.0 - sig)))).astype(jnp.bfloat16)
        up_grad = (grad * silu).astype(jnp.bfloat16)
        active_s[:, :wide] = active
        gate_s[:, :wide] = gate_grad
        up_s[:, :wide] = up_grad

        @pl.when(chunk == stage // near)
        def _():
            sums_ref[:, width:] += contract_cols(active_s[here, :wide], w2[...])
            sums_ref[:, :width] += contract_cols(gate_s[here, :wide], w1[...])
            sums_ref[:, :width] += contract_cols(up_s[here, :wide], w3[...])

        parts = (
            contract_rows(gate_grad, xs_ref[...]),
            contract_rows(up_grad, xs_ref[...]),
            contract_rows(active, ks_ref[...]),
        )
        for i, p in enumerate(parts):
            place = slice(i * wide, (i + 1) * wide)
            quota = p.shape[1] // 2

            @pl.when(chunk == 0)
            def _():
                out_refs[0][place, :] = p[:, :quota]
                out_refs[1][place, :] = p[:, quota:]

            @pl.when(chunk > 0)
            def _():
                out_refs[0][place, :] += p[:, :quota]
                out_refs[1][place, :] += p[:, quota:]

    work(w1_ref, w3_ref, w2_ref, (main_ref, main_other_ref))

    @pl.when(step == pl.num_programs(0) - 1)
    def _():
        work(t1_ref, t3_ref, t2_ref, (tail_ref, tail_other_ref))


def feed_forward(stage, rows, grads, row_cols, grad_cols, weights, own):
    pieces, positions, piece = rows.shape
    width = pieces * piece
    picked = row_cols.shape[1]
    tile, rest = 256, 128
    steps = (weights.shape[1] - 3 * rest) // (3 * tile)
    chunk = min(positions, 4 * own)
    first_tail = 3 * steps * tile // rest
    grid = (steps, positions // chunk)
    tokens = pl.BlockSpec((pieces, chunk, piece), lambda i, t, s: (0, t, 0))
    columns_of = pl.BlockSpec((chunk, picked), lambda i, t, s: (t, 0))

    def main_of(n):
        return pl.BlockSpec((width, tile), lambda i, t, s: (0, n * steps + i))

    def tail_of(n):
        return pl.BlockSpec((width, rest), lambda i, t, s: (0, first_tail + n))

    def fixed(*shape):
        return pl.BlockSpec(shape, lambda i, t, s: (0, 0))

    flops = 2 * positions * width * weights.shape[1] + 2 * own * width * weights.shape[1] + 2 * positions * picked * weights.shape[1]
    return pl.pallas_call(
        feed_kernel,
        grid_spec=pltpu.PrefetchScalarGridSpec(
            num_scalar_prefetch=1,
            grid=grid,
            in_specs=[tokens, tokens, columns_of, columns_of, main_of(0), main_of(1), main_of(2), tail_of(0), tail_of(1), tail_of(2)],
            out_specs=[
                fixed(own, 2 * width),
                pl.BlockSpec((3 * tile, picked // 2), lambda i, t, s: (i, 0)),
                pl.BlockSpec((3 * tile, picked // 2), lambda i, t, s: (i, 0)),
                fixed(3 * rest, picked // 2),
                fixed(3 * rest, picked // 2),
            ],
            scratch_shapes=[pltpu.VMEM((chunk, tile), jnp.bfloat16)] * 3,
        ),
        out_shape=[
            shaped((own, 2 * width)),
            shaped((3 * tile * steps, picked // 2)),
            shaped((3 * tile * steps, picked // 2)),
            shaped((3 * rest, picked // 2)),
            shaped((3 * rest, picked // 2)),
        ],
        compiler_params=pltpu.CompilerParams(
            dimension_semantics=("arbitrary", "arbitrary"), vmem_limit_bytes=56 << 20
        ),
        cost_estimate=pl.CostEstimate(
            flops=flops, bytes_accessed=2 * weights.size + 8 * positions * width, transcendentals=0
        ),
    )(stage, rows, grads, row_cols, grad_cols, weights, weights, weights, weights, weights, weights)


def projection_kernel(cols_ref, slim_ref, gate_ref, q_ref, k_ref, v_ref, g_ref):
    dk = q_ref.shape[1]
    joined = jnp.dot(cols_ref[...], slim_ref[...], preferred_element_type=f32)
    q_ref[...] = joined[:, :dk]
    k_ref[...] = joined[:, dk : 2 * dk]
    v_ref[...] = joined[:, 2 * dk :]
    g_ref[...] = jnp.dot(cols_ref[...], gate_ref[...], preferred_element_type=f32)


def projection_grads(cols, slim_all, gate_all):
    quota, positions = cols.shape
    slim, dv = slim_all.shape[1], gate_all.shape[1]
    dk = (slim - dv) // 2
    sizes = (dk, dk, dv, dv)
    return pl.pallas_call(
        projection_kernel,
        grid=(2,),
        in_specs=[
            pl.BlockSpec((quota, positions), lambda c: (0, 0)),
            pl.BlockSpec((positions, slim), lambda c: (c, 0)),
            pl.BlockSpec((positions, dv), lambda c: (c, 0)),
        ],
        out_specs=[pl.BlockSpec((quota, n), lambda c: (0, c)) for n in sizes],
        out_shape=[shaped((quota, 2 * n)) for n in sizes],
        compiler_params=pltpu.CompilerParams(vmem_limit_bytes=56 << 20),
        cost_estimate=pl.CostEstimate(
            flops=4 * quota * positions * (slim + dv), bytes_accessed=2 * slim_all.size + 2 * gate_all.size, transcendentals=0
        ),
    )(cols, slim_all, gate_all)


QUARTERS = 4


def swap(array):
    return lax.ppermute(array, "dp", [(0, 1), (1, 0)])


def relay(mats, offsets, forward):
    size = lax.axis_size("seq")
    entering = jnp.zeros_like(offsets)
    leaving = offsets
    for step in range(size - 1):
        route = [(step, step + 1)] if forward else [(size - 1 - step, size - 2 - step)]
        got = jnp.stack(
            [jnp.stack([lax.ppermute(part, "seq", route) for part in head]) for head in leaving]
        )
        entering = entering + got
        if step < size - 2:
            leaving = jnp.matmul(mats, got, precision=highest) + offsets
    return entering, leaving


def together(*arrays):
    return lax.optimization_barrier(arrays)


def everyone(part):
    return lax.all_gather(part, ("dp", "seq"), axis=0, tiled=True)


def share(rows):
    wide = jnp.broadcast_to(rows[None], (lax.axis_size("head"),) + rows.shape)
    return lax.all_to_all(wide, "head", split_axis=0, concat_axis=0, tiled=True)


def add_parts(parts):
    got = lax.all_to_all(parts.astype(jnp.bfloat16), "head", split_axis=0, concat_axis=0, tiled=True)
    return jnp.sum(got.astype(f32), axis=0)


def add_everywhere(vector):
    for axis in ("dp", "seq", "head"):
        size, step = lax.axis_size(axis), 1
        while step < size:
            vector = vector + lax.ppermute(vector, axis, [(i, i ^ step) for i in range(size)])
            step *= 2
    return vector


def contract_rows(left, right):
    return lax.dot_general(left, right, (((0,), (0,)), ((), ())), preferred_element_type=f32)


def contract_cols(left, right):
    return lax.dot_general(left, right, (((1,), (1,)), ((), ())), preferred_element_type=f32)


def product(left, right):
    return jnp.dot(left, right, preferred_element_type=f32)


def rms_scale(values, gain):
    return values * lax.rsqrt(jnp.mean(values * values, axis=-1, keepdims=True) + epsilon) * gain


def swiglu(gate_in, up_in):
    return jax.nn.silu(gate_in) * up_in


def on_device(
    activations,
    cotangent,
    lengths,
    query_weight,
    key_weight,
    value_weight,
    gate_weight,
    alpha_weight,
    beta_weight,
    out_weight,
    swiglu_gate,
    swiglu_value,
    swiglu_down,
    mixer_gain,
    feed_gain,
    head_gain,
    decay_rate,
    beta_bias,
):
    bf16 = jnp.bfloat16
    core, stage, group = lax.axis_index("dp"), lax.axis_index("seq"), lax.axis_index("head")
    stages, groups = lax.axis_size("seq"), lax.axis_size("head")
    width = activations.shape[2]
    rows0 = activations.shape[1]
    rows1 = rows0 // QUARTERS
    own0, own1 = rows0 // (2 * groups), rows1 // (2 * groups)
    own = own0 + own1
    quota = width // (2 * stages)
    heads = alpha_weight.shape[1] // 2
    counts = (rows0 // BLOCK, rows1 // BLOCK)
    assert groups == QUARTERS and stages % QUARTERS == 0 and rows1 % BLOCK == 0
    first = core == 0

    def part(array, size, axis, offset=0):
        return lax.dynamic_slice_in_dim(array, offset + core * size, size, axis)

    dk, dv = query_weight.shape[1] // 2, value_weight.shape[1] // 2
    slim = 2 * dk + dv
    mixer_cols = []
    for c in range(2):
        mixer_cols += [
            query_weight[:, c * dk : (c + 1) * dk],
            key_weight[:, c * dk : (c + 1) * dk],
            value_weight[:, c * dv : (c + 1) * dv],
        ]
    mixer_cols += [alpha_weight, beta_weight]
    mixer_full = everyone(jnp.concatenate(mixer_cols, axis=1).astype(bf16))
    gates_full = everyone(jnp.concatenate([gate_weight, out_weight], axis=1).astype(bf16))
    hidden_units = swiglu_gate.shape[1]
    even = hidden_units // 256 * 256
    odd = hidden_units - even
    assert 0 < odd <= 128
    three = (swiglu_gate, swiglu_value, swiglu_down)
    spare = ((0, 0), (0, 128 - odd))
    feed_full = everyone(
        jnp.concatenate([w[:, :even] for w in three] + [jnp.pad(w[:, even:], spare) for w in three], axis=1).astype(bf16)
    )

    def chip_rows(rows):
        arrived = jnp.zeros((rows1, width), bf16)
        for b in range(QUARTERS):
            route = [(stages + a, stages + QUARTERS * a + b) for a in range(stages // QUARTERS)]
            arrived = arrived + lax.ppermute(rows[b * rows1 : (b + 1) * rows1], ("dp", "seq"), route)
        near0 = lax.ppermute(rows, "dp", [(0, 1)])
        near1 = lax.ppermute(arrived, "dp", [(1, 0)])
        return jnp.concatenate([jnp.where(first, rows, near0), jnp.where(first, near1, arrived)], axis=0)

    inputs = chip_rows(activations[0])
    inputs, late = together(inputs, cotangent[0])
    inputs = inputs.astype(f32)
    spots0 = stage * rows0 + lax.broadcasted_iota(jnp.int32, (rows0, 1), 0)
    spots1 = stage * rows1 + lax.broadcasted_iota(jnp.int32, (rows1, 1), 0)
    mask = jnp.concatenate([spots0 < lengths[0], spots1 < lengths[1]], axis=0).astype(f32)
    masked = (chip_rows(late).astype(f32) * mask).astype(bf16)

    def by_owner(rows):
        wide = rows.shape[1]
        r0 = rows[:rows0].reshape(groups, 2, own0, wide)
        r1 = rows[rows0:].reshape(groups, 2, own1, wide)
        return jnp.concatenate([r0, r1], axis=2).swapaxes(0, 1)

    def in_time(owned):
        wide = owned.shape[3]
        turned = owned.swapaxes(0, 1)
        return jnp.concatenate(
            [turned[:, :, :own0].reshape(rows0, wide), turned[:, :, own0:].reshape(rows1, wide)], axis=0
        )

    def of_core(owned, which):
        return lax.dynamic_index_in_dim(owned, which, 0, keepdims=False)

    def of_group(rows):
        return lax.dynamic_index_in_dim(rows, group, 0, keepdims=False)

    def add_rows(partial):
        owned = by_owner(partial)
        return add_parts(of_core(owned, core) + swap(of_core(owned, 1 - core)))

    def meet_columns(rows):
        return lax.all_to_all(rows, ("dp", "seq"), split_axis=1, concat_axis=0, tiled=True)

    def owned_columns(met):
        got = share(met).reshape(groups, 2, stages, own, quota).transpose(2, 0, 1, 3, 4)
        return jnp.concatenate(
            [got[:, :, :, :own0].reshape(stages, rows0, quota), got[:, :, :, own0:].reshape(stages, rows1, quota)], axis=1
        ).reshape(stages * (rows0 + rows1), quota)

    def across_stages(rows):
        wide = jnp.broadcast_to(rows[None], (stages,) + rows.shape)
        met = lax.all_to_all(wide, "seq", split_axis=0, concat_axis=0, tiled=True)
        return met.reshape(stages * rows.shape[0], rows.shape[1])

    def own_columns(rows):
        pieces, positions, piece = rows.shape
        both = []
        for which in (core, 1 - core):
            start = (which * stages + stage) * quota
            both.append(lax.dynamic_slice(rows, (start // piece, 0, start % piece), (1, positions, quota))[0])
        return jnp.concatenate(both, axis=1)

    own_rows = of_group(of_core(by_owner(inputs), core))
    own_mask = of_group(of_core(by_owner(mask), core))
    tokens_masked = of_core(by_owner(masked), core)
    own_masked = of_group(tokens_masked).astype(f32)
    quarter = width // groups
    masked_met = across_stages(
        lax.dynamic_slice_in_dim(tokens_masked.reshape(groups * own, width), group * quarter, quarter, 1)
    )

    factor1 = lax.rsqrt(jnp.mean(inputs * inputs, axis=-1, keepdims=True) + epsilon)
    unit1 = inputs * factor1
    normed = rms_scale(inputs, mixer_gain).astype(bf16)
    normed_cols = owned_columns(meet_columns(of_group(of_core(by_owner(normed), core)))).T
    mixer_full, masked_met, normed_cols = together(mixer_full, masked_met, normed_cols)
    mixer_w = part(mixer_full, slim, 1)
    gate_w = part(gates_full, dv, 1)
    out_w = part(gates_full, dv, 1, 2 * dv)
    rates_w = mixer_full[:, 2 * slim :]
    proj = product(normed, mixer_w)
    small_pre = product(normed, rates_w)
    gate_pre = product(normed, gate_w)
    alpha_pre = part(small_pre, heads, 1)
    beta_pre = part(small_pre, heads, 1, 2 * heads)
    head0 = (2 * group + core) * heads
    rates = lax.dynamic_slice_in_dim(decay_rate, head0, heads)
    biases = lax.dynamic_slice_in_dim(beta_bias, head0, heads)
    blocks = sum(counts)

    def to_blocks(array):
        return array.T.reshape(heads, blocks, BLOCK)

    def from_blocks(array):
        return array.reshape(heads, blocks * BLOCK).T

    soft = jax.nn.softplus(alpha_pre)
    beta = jax.nn.sigmoid(beta_pre + biases)
    beta_b = to_blocks(beta)
    upto = (
        lax.broadcasted_iota(jnp.int32, (BLOCK, BLOCK), 0) <= lax.broadcasted_iota(jnp.int32, (BLOCK, BLOCK), 1)
    ).astype(f32)
    sums = jnp.matmul(to_blocks(-rates * soft), upto, precision=highest)
    col = jnp.stack([sums, beta_b], axis=-1)
    row = jnp.stack([sums, beta_b], axis=-2)
    solver, scores, w, vt, qt, m, b, mseg, bseg = solve(counts, heads, proj, col, row)
    state_in, unused_carry = relay(mseg, bseg, True)
    state_in, masked_all = together(state_in, share(masked_met))
    gain_row = head_gain[None]
    states, outs, gated = outputs_of(counts, heads, state_in, m, b, qt, scores, vt, gate_pre, gain_row)
    mixed = add_rows(contract_cols(gated, out_w))
    hidden = own_rows + mixed

    normed2, norm2_back = jax.vjp(rms_scale, hidden, feed_gain)
    feed_in = share(
        across_stages(lax.all_to_all(normed2.astype(bf16), "head", split_axis=1, concat_axis=0, tiled=True))
    )
    sums, main_own, main_other, tail_own, tail_other = feed_forward(
        stage[None], feed_in, masked_all, own_columns(feed_in), own_columns(masked_all), feed_full, groups * own
    )
    sums = add_parts(sums.reshape(groups, own, 2 * width))
    normed2_grad, feed = sums[:, :width], sums[:, width:]
    hidden_back, feed_gain_grad = norm2_back(normed2_grad)
    hidden_grad = own_masked + hidden_back
    mixed_own = hidden_grad.astype(bf16)
    mixed_half = share(mixed_own)
    other_half = swap(mixed_half)
    mixed_in = in_time(
        jnp.stack([jnp.where(first, mixed_half, other_half), jnp.where(first, other_half, mixed_half)])
    )

    gated_all = everyone(gated)
    gated_grad = product(mixed_in, out_w)
    main_other, tail_other = swap(main_other), swap(tail_other)
    gated_grad, gated_all, main_other, tail_other = together(gated_grad, gated_all, main_other, tail_other)
    outs_grad, gate_pre_low, gain_grads, d, dseg = output_grads_of(
        counts, heads, gated_grad, gate_pre, outs, gain_row, qt, m
    )
    gate_pre_all = everyone(gate_pre_low)
    later, carry = relay(jnp.swapaxes(mseg, 2, 3), dseg, False)

    half = stages * (rows0 + rows1)
    main_own, main_other, tail_own, tail_other, mixed_late, unused_carry = together(
        main_own, main_other, tail_own, tail_other, mixed_own, carry
    )
    mixed_met = meet_columns(mixed_late)
    main_own, tail_own = main_own + main_other, tail_own + tail_other

    def feed_grad(n):
        pieces = [main_own[(3 * i + n) * 256 : (3 * i + n + 1) * 256] for i in range(even // 256)]
        return jnp.concatenate(pieces + [tail_own[n * 128 : n * 128 + odd]], axis=0)

    feed_gate_grad, feed_value_grad, down_grad = feed_grad(0), feed_grad(1), feed_grad(2)
    gate_back = contract_cols(gate_pre_low, gate_w)
    later, feed_gate_grad, feed_value_grad, down_grad, gate_back = together(
        later, feed_gate_grad, feed_value_grad, down_grad, gate_back
    )
    query_low, key_low, value_low, col_grad, row_grad = input_grads_of(
        counts, heads, proj, col, row, solver, scores, w, vt, m, d, states, outs_grad, later
    )
    sums_grad = col_grad[..., 0] - row_grad[:, :, 0] * beta_b
    decay_back = from_blocks(jnp.matmul(sums_grad, upto.T, precision=highest))
    beta_back = beta * (1.0 - beta) * from_blocks(col_grad[..., 1] + row_grad[:, :, 0])
    rates_grad = -jnp.sum(soft * decay_back, axis=0)
    biases_grad = jnp.sum(beta_back, axis=0)
    alpha_back = -rates * jax.nn.sigmoid(alpha_pre) * decay_back
    small_low = jnp.concatenate([alpha_back, beta_back], axis=1).astype(bf16)
    query_low, gate_pre_all = together(query_low, gate_pre_all)
    slim_low = jnp.concatenate([query_low, key_low, value_low], axis=1)
    slim_all = everyone(slim_low)
    blank = jnp.zeros((rows0 + rows1, 4 * heads), bf16)
    spread = lax.dynamic_update_slice(blank, small_low[:, :heads], (0, core * heads))
    spread = lax.dynamic_update_slice(spread, small_low[:, heads:], (0, (2 + core) * heads))
    total = gate_back + contract_cols(slim_low, mixer_w) + contract_cols(spread, rates_w)
    normed_grad = add_rows(total)
    mixer_gain_part = jnp.sum(total * unit1, axis=0)
    normed_grad, small_late, mixed_met, mixer_gain_part = together(normed_grad, small_low, mixed_met, mixer_gain_part)
    outputs_own = (own_mask * (hidden + feed)).astype(bf16)
    mixed_cols = owned_columns(mixed_met)
    unused_rows, norm1_back = jax.vjp(lambda v: rms_scale(v, mixer_gain), own_rows)
    input_own = (hidden_grad + norm1_back(normed_grad)[0]).astype(bf16)

    small_rows = contract_rows(small_late, normed)
    small_rows = lax.all_to_all(small_rows, ("dp", "seq"), split_axis=1, concat_axis=0, tiled=True)
    small_rows = jnp.sum(small_rows.reshape(2, stages, 2, heads, quota), axis=1)
    alpha_grad = small_rows[:, 0].reshape(2 * heads, quota).T
    beta_grad = small_rows[:, 1].reshape(2 * heads, quota).T
    out_grad = jnp.concatenate(
        [contract_rows(mixed_cols, gated_all[:half]), contract_rows(mixed_cols, gated_all[half:])], axis=1
    )
    slim_all, out_grad = together(slim_all, out_grad)
    query_grad, key_grad, value_grad, gate_grad = projection_grads(normed_cols, slim_all, gate_pre_all)

    total_heads = decay_rate.shape[0]
    none = jnp.zeros((total_heads,), f32)
    small = add_everywhere(
        jnp.concatenate(
            [
                mixer_gain_part,
                feed_gain_grad,
                jnp.sum(gain_grads, axis=(0, 1)),
                lax.dynamic_update_slice(none, rates_grad, (head0,)),
                lax.dynamic_update_slice(none, biases_grad, (head0,)),
            ]
        )
    )
    edges = [width, 2 * width, 2 * width + head_gain.shape[0], 2 * width + head_gain.shape[0] + total_heads]

    def place(rows):
        r0, r1 = rows[:own0], rows[own0:]
        out0 = jnp.concatenate([r0, lax.ppermute(r0, "dp", [(1, 0)])], axis=0)
        pair = jnp.concatenate([lax.ppermute(r1, "dp", [(0, 1)]), r1], axis=0)
        routes = [
            [
                ((stages + QUARTERS * a + b) * groups + k, (stages + a) * groups + b)
                for a in range(stages // QUARTERS)
                for b in range(QUARTERS)
            ]
            for k in range(groups)
        ]
        out1 = jnp.concatenate([lax.ppermute(pair, ("dp", "seq", "head"), route) for route in routes], axis=0)
        return jnp.where(first, out0, out1)[None]

    placed = place(jnp.concatenate([outputs_own, input_own], axis=1))
    return (
        placed[:, :, :width],
        placed[:, :, width:],
        query_grad,
        key_grad,
        value_grad,
        gate_grad,
        alpha_grad,
        beta_grad,
        out_grad,
        feed_gate_grad.T,
        feed_value_grad.T,
        down_grad.T,
        small[: edges[0]],
        small[edges[0] : edges[1]],
        small[edges[1] : edges[2]],
        small[edges[2] : edges[3]],
        small[edges[3] :],
    )


def solution(mesh):
    return jax.shard_map(
        on_device,
        mesh=mesh,
        in_specs=(
            P("dp", "seq", None),
            P("dp", "seq", None),
            P(),
            P(("dp", "seq"), "head"),
            P(("dp", "seq"), "head"),
            P(("dp", "seq"), "head"),
            P(("dp", "seq"), "head"),
            P(("dp", "seq"), "head"),
            P(("dp", "seq"), "head"),
            P(("dp", "seq"), "head"),
            P(("dp", "seq"), "head"),
            P(("dp", "seq"), "head"),
            P(("dp", "seq"), "head"),
            P(),
            P(),
            P(),
            P(),
            P(),
        ),
        out_specs=(
            P("dp", ("seq", "head"), None),
            P("dp", ("seq", "head"), None),
            P(("dp", "seq"), "head"),
            P(("dp", "seq"), "head"),
            P(("dp", "seq"), "head"),
            P(("dp", "seq"), "head"),
            P(("dp", "seq"), "head"),
            P(("dp", "seq"), "head"),
            P(("dp", "seq"), "head"),
            P(("dp", "seq"), "head"),
            P(("dp", "seq"), "head"),
            P(("dp", "seq"), "head"),
            P(),
            P(),
            P(),
            P(),
            P(),
        ),
        check_vma=False,
    )
```

```python
import functools

import jax
import jax.numpy as jnp
from jax import lax
from jax.experimental import pallas as pl
from jax.experimental.pallas import tpu as pltpu
from jax.sharding import PartitionSpec as P

BLOCK = 64
epsilon = 1e-06
highest = lax.Precision.HIGHEST
f32 = jnp.float32


def mm(left, right, a=1, b=0):
    return lax.dot_general(
        left, right, (((a,), (b,)), ((), ())), precision=highest, preferred_element_type=f32
    )


def mm_nt(left, right):
    return mm(left, right, 1, 1)


def mm_tn(left, right):
    return mm(left, right, 0, 0)


def each(f, *lists):
    return [f(*items) for items in zip(*lists)]


def square_masks():
    rows = lax.broadcasted_iota(jnp.int32, (BLOCK, BLOCK), 0)
    cols = lax.broadcasted_iota(jnp.int32, (BLOCK, BLOCK), 1)
    return rows >= cols, rows > cols, (rows == cols).astype(f32)


def row_factor(values):
    return lax.rsqrt(jnp.sum(values * values, axis=-1, keepdims=True) + epsilon)


def split(values, count):
    return [values[i * BLOCK : (i + 1) * BLOCK] for i in range(count)]


def decays(col_ref, row_ref, count):
    lower, strict, identity = square_masks()
    out = []
    for i in range(count):
        c_col, b_col = col_ref[0, i, :, 0:1], col_ref[0, i, :, 1:2]
        c_row, b_row = row_ref[0, i, 0:1, :], row_ref[0, i, 1:2, :]
        fade = jnp.where(lower, jnp.exp(jnp.where(lower, c_col - c_row, 0.0)), 0.0)
        last = c_col[BLOCK - 1 : BLOCK, :]
        out.append((fade, fade * b_row, jnp.exp(c_col), jnp.exp(last - c_col), b_col, jnp.exp(last)))
    return [list(items) for items in zip(*out)]


def chains(counts):
    start, out = 0, []
    for count in counts:
        out.append(range(start, start + count))
        start += count
    return out


def solve_kernel(counts, q_ref, k_ref, v_ref, col_ref, row_ref, solver_ref, scores_ref, w_ref, vt_ref, qt_ref, m_ref, b_ref, mseg_ref, bseg_ref):
    count = sum(counts)
    lower, strict, identity = square_masks()
    query = q_ref[...]
    query = split(query * row_factor(query), count)
    key = k_ref[...]
    key = split(key * row_factor(key), count)
    value = split(v_ref[...], count)
    fade, ratio, growth, remain, beta, end = decays(col_ref, row_ref, count)
    power = each(lambda k, p: jnp.where(strict, -mm_nt(k, k) * p, 0.0), key, ratio)
    solver = [identity + p for p in power]
    for _ in range((BLOCK - 1).bit_length() - 1):
        power = each(lambda p: mm(p, p), power)
        solver = each(lambda s, p: s + mm(s, p), solver, power)
    scores = each(lambda q, k, p: mm_nt(q, k) * p, query, key, ratio)
    w = each(lambda s, g, k: mm(s, g * k), solver, growth, key)
    vt = each(mm, solver, value)
    qt = each(lambda g, q, a, x: g * q - mm(a, x), growth, query, scores, w)
    weighted = each(lambda k, r, b: k * (r * b), key, remain, beta)
    size = query[0].shape[1]
    wide = (
        lax.broadcasted_iota(jnp.int32, (size, size), 0)
        == lax.broadcasted_iota(jnp.int32, (size, size), 1)
    ).astype(f32)
    m = each(lambda e, k, x: e * wide - mm_tn(k, x), end, weighted, w)
    b = each(mm_tn, weighted, vt)
    for i in range(count):
        solver_ref[0, i] = solver[i]
        scores_ref[0, i] = scores[i]
        w_ref[0, i] = w[i]
        vt_ref[0, i] = vt[i]
        qt_ref[0, i] = qt[i]
        m_ref[0, i] = m[i]
        b_ref[0, i] = b[i]
    for j, chain in enumerate(chains(counts)):
        mseg_ref[0, j] = m[chain[0]]
        bseg_ref[0, j] = b[chain[0]]
        for i in chain[1:]:
            bseg_ref[0, j] = mm(m_ref[0, i], bseg_ref[0, j]) + b_ref[0, i]
            mseg_ref[0, j] = mm(m_ref[0, i], mseg_ref[0, j])


def output_kernel(counts, state_ref, m_ref, b_ref, qt_ref, scores_ref, vt_ref, gate_ref, gain_ref, states_ref, out_ref, gated_ref):
    count = sum(counts)
    states = [None] * count
    for j, chain in enumerate(chains(counts)):
        state = state_ref[0, j]
        for i in chain:
            states[i] = state
            states_ref[0, i] = state
            if i != chain[-1]:
                state = mm(m_ref[0, i], state) + b_ref[0, i]
    gain = gain_ref[...]
    outs = [mm(qt_ref[0, i], states[i]) + mm(scores_ref[0, i], vt_ref[0, i]) for i in range(count)]
    for i in range(count):
        rows = slice(i * BLOCK, (i + 1) * BLOCK)
        out = outs[i]
        gate = gate_ref[rows, :]
        scale = lax.rsqrt(jnp.mean(out * out, axis=-1, keepdims=True) + epsilon)
        out_ref[rows, :] = out
        gated_ref[rows, :] = (out * scale * gain * (gate * jax.nn.sigmoid(gate))).astype(jnp.bfloat16)


def output_grad_kernel(counts, grad_ref, gate_ref, out_ref, gain_ref, qt_ref, m_ref, out_grad_ref, gate_grad_ref, gain_grad_ref, d_ref, dseg_ref):
    count = sum(counts)
    gain = gain_ref[...]
    gain_grad = jnp.zeros_like(gain)
    grads = []
    for i in range(count):
        rows = slice(i * BLOCK, (i + 1) * BLOCK)
        grad, gate, out = grad_ref[rows, :], gate_ref[rows, :], out_ref[rows, :]
        scale = lax.rsqrt(jnp.mean(out * out, axis=-1, keepdims=True) + epsilon)
        unit = out * scale
        sig = jax.nn.sigmoid(gate)
        normed_grad = grad * (gate * sig)
        gate_grad_ref[rows, :] = (grad * (unit * gain) * (sig * (1.0 + gate * (1.0 - sig)))).astype(jnp.bfloat16)
        gain_grad = gain_grad + jnp.sum(normed_grad * unit, axis=0, keepdims=True)
        inner = normed_grad * gain
        out_grad = scale * (inner - unit * jnp.mean(unit * inner, axis=-1, keepdims=True))
        out_grad_ref[rows, :] = out_grad
        grads.append(out_grad)
    gain_grad_ref[0] = gain_grad
    d = [mm_tn(qt_ref[0, i], grads[i]) for i in range(count)]
    for i in range(count):
        d_ref[0, i] = d[i]
    for j, chain in enumerate(chains(counts)):
        dseg_ref[0, j] = d[chain[-1]]
        for i in list(chain)[-2::-1]:
            dseg_ref[0, j] = mm_tn(m_ref[0, i], dseg_ref[0, j]) + d_ref[0, i]


def unit_back(raw, grad):
    factor = row_factor(raw)
    unit = raw * factor
    return factor * (grad - unit * jnp.sum(unit * grad, axis=-1, keepdims=True))


def grads_kernel(counts, q_ref, k_ref, col_ref, row_ref, solver_ref, scores_ref, w_ref, vt_ref, m_ref, d_ref, states_ref, out_grad_ref, gate_ref, later_ref, slim_ref, joint_ref, col_grad_ref, row_grad_ref):
    count = sum(counts)
    span = range(count)
    lower, strict, identity = square_masks()
    raw_q, raw_k = split(q_ref[...], count), split(k_ref[...], count)
    query = [x * row_factor(x) for x in raw_q]
    key = [x * row_factor(x) for x in raw_k]
    fade, ratio, growth, remain, beta, end = decays(col_ref, row_ref, count)
    out_grad = split(out_grad_ref[...], count)
    later = [None] * count
    for j, chain in enumerate(chains(counts)):
        state = later_ref[0, j]
        for i in list(chain)[::-1]:
            later[i] = state
            if i != chain[0]:
                state = mm_tn(m_ref[0, i], state) + d_ref[0, i]
    states = [states_ref[0, i] for i in span]
    update = [vt_ref[0, i] - mm(w_ref[0, i], states[i]) for i in span]
    update_grad = [
        mm_tn(scores_ref[0, i], out_grad[i]) + mm(key[i] * (remain[i] * beta[i]), later[i]) for i in span
    ]
    solved = [mm_tn(solver_ref[0, i], update_grad[i]) for i in span]
    scores_grad = each(mm_nt, out_grad, update)
    inner_grad = each(lambda y, u: jnp.where(strict, -mm_nt(y, u), 0.0), solved, update)
    query_dot = each(mm_nt, query, key)
    keys_dot = each(mm_nt, key, key)
    from_out = each(mm_nt, out_grad, states)
    from_solved = each(mm_nt, solved, states)
    from_update = each(mm_nt, update, later)
    weighted_scores = each(lambda p, x: p * x, ratio, scores_grad)
    weighted_inner = each(lambda p, x: p * x, ratio, inner_grad)
    q_grad = [growth[i] * from_out[i] + mm(weighted_scores[i], key[i]) for i in span]
    k_grad = [
        mm_tn(weighted_scores[i], query[i])
        + (remain[i] * beta[i]) * from_update[i]
        - growth[i] * from_solved[i]
        + mm(weighted_inner[i], key[i])
        + mm_tn(weighted_inner[i], key[i])
        for i in span
    ]
    last_row = (lax.broadcasted_iota(jnp.int32, (BLOCK, 1), 0) == BLOCK - 1).astype(f32)
    for i in span:
        rows = slice(i * BLOCK, (i + 1) * BLOCK)
        start = 0
        for grad in (unit_back(raw_q[i], q_grad[i]), unit_back(raw_k[i], k_grad[i]), solved[i]):
            place = slice(start, start + grad.shape[1])
            start += grad.shape[1]
            slim_ref[rows, place] = grad.astype(jnp.bfloat16)
            joint_ref[rows, place] = grad.astype(jnp.bfloat16)
        joint_ref[rows, start:] = gate_ref[rows, :]
        faded = fade[i] * (scores_grad[i] * query_dot[i] + inner_grad[i] * keys_dot[i])
        b_row = row_ref[0, i, 1:2, :]
        growth_grad = jnp.sum(query[i] * from_out[i] - key[i] * from_solved[i], axis=-1, keepdims=True)
        weight_grad = jnp.sum(key[i] * from_update[i], axis=-1, keepdims=True)
        pulled = remain[i] * beta[i] * weight_grad
        tail = jnp.sum(pulled, axis=0, keepdims=True) + end[i] * jnp.sum(
            jnp.sum(later[i] * states[i], axis=-1, keepdims=True), axis=0, keepdims=True
        )
        c_grad = jnp.sum(faded * b_row, axis=-1, keepdims=True) + growth[i] * growth_grad - pulled + last_row * tail
        col_grad_ref[0, i, :, 0:1] = c_grad
        col_grad_ref[0, i, :, 1:2] = remain[i] * weight_grad
        row_grad_ref[0, i] = jnp.sum(faded, axis=0, keepdims=True)


def whole(shape):
    return pl.BlockSpec((1,) + tuple(shape[1:]), lambda j: (j,) + (0,) * (len(shape) - 1))


def columns(rows, width, first=0, step=1):
    return pl.BlockSpec((rows, width), lambda j: (0, step * j + first))


def shaped(shape, dtype=f32):
    return jax.ShapeDtypeStruct(shape, dtype)


def call(kernel, counts, heads, inputs, outputs, flops):
    moved = sum(x.size * x.dtype.itemsize for x, _ in inputs) + sum(
        x.size * x.dtype.itemsize for x, _ in outputs
    )
    return pl.pallas_call(
        functools.partial(kernel, counts),
        grid=(heads,),
        in_specs=[s for _, s in inputs],
        out_specs=[s for _, s in outputs],
        out_shape=[x for x, _ in outputs],
        compiler_params=pltpu.CompilerParams(vmem_limit_bytes=48 << 20),
        cost_estimate=pl.CostEstimate(flops=flops, bytes_accessed=moved, transcendentals=0),
    )(*[x for x, _ in inputs])


def per_head(heads, *shape, dtype=f32):
    s = (heads,) + shape
    return shaped(s, dtype), whole(s)


def flat(array, width, first=0, step=1):
    return array, columns(array.shape[0], width, first, step)


def stacked(array):
    return array, whole(array.shape)


def solve(counts, heads, proj, col, row):
    n, dk, dv = sum(counts), 128, 256
    return call(
        solve_kernel, counts, heads,
        [flat(proj, dk, 0, 4), flat(proj, dk, 1, 4), flat(proj, dv, 1, 2), stacked(col), stacked(row)],
        [per_head(heads, n, BLOCK, BLOCK), per_head(heads, n, BLOCK, BLOCK), per_head(heads, n, BLOCK, dk),
         per_head(heads, n, BLOCK, dv), per_head(heads, n, BLOCK, dk), per_head(heads, n, dk, dk),
         per_head(heads, n, dk, dv), per_head(heads, len(counts), dk, dk), per_head(heads, len(counts), dk, dv)],
        heads * n * 100_000_000,
    )


def outputs_of(counts, heads, state, m, b, qt, scores, vt, gate_pre, gain):
    n, dk, dv = sum(counts), 128, 256
    rows = gate_pre.shape[0]
    cols = columns(rows, dv)
    return call(
        output_kernel, counts, heads,
        [stacked(state), stacked(m), stacked(b), stacked(qt), stacked(scores), stacked(vt), flat(gate_pre, dv),
         (gain, pl.BlockSpec((1, dv), lambda j: (0, 0)))],
        [per_head(heads, n, dk, dv), (shaped((rows, heads * dv)), cols), (shaped((rows, heads * dv), jnp.bfloat16), cols)],
        heads * n * 50_000_000,
    )


def output_grads_of(counts, heads, grad, gate_pre, outs, gain, qt, m):
    n, dk, dv = sum(counts), 128, 256
    rows = gate_pre.shape[0]
    cols = columns(rows, dv)
    return call(
        output_grad_kernel, counts, heads,
        [flat(grad, dv), flat(gate_pre, dv), flat(outs, dv), (gain, pl.BlockSpec((1, dv), lambda j: (0, 0))), stacked(qt), stacked(m)],
        [(shaped((rows, heads * dv)), cols), (shaped((rows, heads * dv), jnp.bfloat16), cols),
         per_head(heads, 1, dv), per_head(heads, n, dk, dv), per_head(heads, len(counts), dk, dv)],
        heads * n * 50_000_000,
    )


def input_grads_of(counts, heads, proj, col, row, solver, scores, w, vt, m, d, states, out_grad, gate_grad, later):
    n, dk, dv = sum(counts), 128, 256
    rows = proj.shape[0]
    return call(
        grads_kernel, counts, heads,
        [flat(proj, dk, 0, 4), flat(proj, dk, 1, 4), stacked(col), stacked(row), stacked(solver), stacked(scores), stacked(w),
         stacked(vt), stacked(m), stacked(d), stacked(states), flat(out_grad, dv), flat(gate_grad, dv), stacked(later)],
        [(shaped((rows, heads * (2 * dk + dv)), jnp.bfloat16), columns(rows, 2 * dk + dv)),
         (shaped((rows, heads * (2 * dk + 2 * dv)), jnp.bfloat16), columns(rows, 2 * dk + 2 * dv)),
         per_head(heads, n, BLOCK, 2), per_head(heads, n, 1, BLOCK)],
        heads * n * 150_000_000,
    )


def feed_kernel(stage_ref, x_ref, k_ref, xs_ref, ks_ref, w1_ref, w3_ref, w2_ref, t1_ref, t3_ref, t2_ref, sums_ref, main_ref, main_other_ref, tail_ref, tail_other_ref, active_s, gate_s, up_s):
    step, chunk = pl.program_id(0), pl.program_id(1)
    own, width = sums_ref.shape[0], sums_ref.shape[1] // 2
    near, piece = x_ref.shape[1] // own, x_ref.shape[2]
    stage = stage_ref[0]
    here = pl.ds(pl.multiple_of(lax.rem(stage, near) * own, own), own)

    @pl.when((step == 0) & (chunk == 0))
    def _():
        sums_ref[...] = jnp.zeros_like(sums_ref)

    def work(w1, w3, w2, out_refs):
        wide = w1.shape[1]
        gate, up, grad = (
            sum(
                jnp.dot(rows[i], w[i * piece : (i + 1) * piece, :], preferred_element_type=f32)
                for i in range(rows.shape[0])
            )
            for rows, w in ((x_ref, w1), (x_ref, w3), (k_ref, w2))
        )
        sig = jax.nn.sigmoid(gate)
        silu = gate * sig
        active = (silu * up).astype(jnp.bfloat16)
        gate_grad = (grad * up * (sig * (1.0 + gate * (1.0 - sig)))).astype(jnp.bfloat16)
        up_grad = (grad * silu).astype(jnp.bfloat16)
        active_s[:, :wide] = active
        gate_s[:, :wide] = gate_grad
        up_s[:, :wide] = up_grad

        @pl.when(chunk == stage // near)
        def _():
            sums_ref[:, width:] += contract_cols(active_s[here, :wide], w2[...])
            sums_ref[:, :width] += contract_cols(gate_s[here, :wide], w1[...])
            sums_ref[:, :width] += contract_cols(up_s[here, :wide], w3[...])

        parts = (
            contract_rows(gate_grad, xs_ref[...]),
            contract_rows(up_grad, xs_ref[...]),
            contract_rows(active, ks_ref[...]),
        )
        for i, p in enumerate(parts):
            place = slice(i * wide, (i + 1) * wide)
            quota = p.shape[1] // 2

            @pl.when(chunk == 0)
            def _():
                out_refs[0][place, :] = p[:, :quota]
                out_refs[1][place, :] = p[:, quota:]

            @pl.when(chunk > 0)
            def _():
                out_refs[0][place, :] += p[:, :quota]
                out_refs[1][place, :] += p[:, quota:]

    work(w1_ref, w3_ref, w2_ref, (main_ref, main_other_ref))

    @pl.when(step == pl.num_programs(0) - 1)
    def _():
        work(t1_ref, t3_ref, t2_ref, (tail_ref, tail_other_ref))


def feed_forward(stage, rows, grads, row_cols, grad_cols, weights, own):
    pieces, positions, piece = rows.shape
    width = pieces * piece
    picked = row_cols.shape[1]
    tile, rest = 256, 128
    steps = (weights.shape[1] - 3 * rest) // (3 * tile)
    chunk = min(positions, 4 * own)
    first_tail = 3 * steps * tile // rest
    grid = (steps, positions // chunk)
    tokens = pl.BlockSpec((pieces, chunk, piece), lambda i, t, s: (0, t, 0))
    columns_of = pl.BlockSpec((chunk, picked), lambda i, t, s: (t, 0))

    def main_of(n):
        return pl.BlockSpec((width, tile), lambda i, t, s: (0, n * steps + i))

    def tail_of(n):
        return pl.BlockSpec((width, rest), lambda i, t, s: (0, first_tail + n))

    def fixed(*shape):
        return pl.BlockSpec(shape, lambda i, t, s: (0, 0))

    flops = 2 * positions * width * weights.shape[1] + 2 * own * width * weights.shape[1] + 2 * positions * picked * weights.shape[1]
    return pl.pallas_call(
        feed_kernel,
        grid_spec=pltpu.PrefetchScalarGridSpec(
            num_scalar_prefetch=1,
            grid=grid,
            in_specs=[tokens, tokens, columns_of, columns_of, main_of(0), main_of(1), main_of(2), tail_of(0), tail_of(1), tail_of(2)],
            out_specs=[
                fixed(own, 2 * width),
                pl.BlockSpec((3 * tile, picked // 2), lambda i, t, s: (i, 0)),
                pl.BlockSpec((3 * tile, picked // 2), lambda i, t, s: (i, 0)),
                fixed(3 * rest, picked // 2),
                fixed(3 * rest, picked // 2),
            ],
            scratch_shapes=[pltpu.VMEM((chunk, tile), jnp.bfloat16)] * 3,
        ),
        out_shape=[
            shaped((own, 2 * width)),
            shaped((3 * tile * steps, picked // 2)),
            shaped((3 * tile * steps, picked // 2)),
            shaped((3 * rest, picked // 2)),
            shaped((3 * rest, picked // 2)),
        ],
        compiler_params=pltpu.CompilerParams(
            dimension_semantics=("arbitrary", "arbitrary"), vmem_limit_bytes=56 << 20
        ),
        cost_estimate=pl.CostEstimate(
            flops=flops, bytes_accessed=2 * weights.size + 8 * positions * width, transcendentals=0
        ),
    )(stage, rows, grads, row_cols, grad_cols, weights, weights, weights, weights, weights, weights)


def projection_kernel(heads, cols_ref, joint_ref, q_ref, k_ref, v_ref, g_ref):
    joined = jnp.dot(cols_ref[...], joint_ref[...], preferred_element_type=f32)
    start = 0
    for j in range(heads):
        for ref in (q_ref, k_ref, v_ref, g_ref):
            size = ref.shape[1] // heads
            ref[:, j * size : (j + 1) * size] = joined[:, start : start + size]
            start += size


def projection_grads(cols, joint_all, heads, sizes):
    quota, positions = cols.shape
    wide = joint_all.shape[1]
    return pl.pallas_call(
        functools.partial(projection_kernel, heads),
        grid=(2,),
        in_specs=[
            pl.BlockSpec((quota, positions), lambda c: (0, 0)),
            pl.BlockSpec((positions, wide), lambda c: (c, 0)),
        ],
        out_specs=[pl.BlockSpec((quota, n), lambda c: (0, c)) for n in sizes],
        out_shape=[shaped((quota, 2 * n)) for n in sizes],
        compiler_params=pltpu.CompilerParams(vmem_limit_bytes=56 << 20),
        cost_estimate=pl.CostEstimate(
            flops=4 * quota * positions * wide, bytes_accessed=2 * joint_all.size, transcendentals=0
        ),
    )(cols, joint_all)


QUARTERS = 4


def swap(array):
    return lax.ppermute(array, "dp", [(0, 1), (1, 0)])


def relay(mats, offsets, forward):
    size = lax.axis_size("seq")
    entering = jnp.zeros_like(offsets)
    leaving = offsets
    for step in range(size - 1):
        route = [(step, step + 1)] if forward else [(size - 1 - step, size - 2 - step)]
        got = jnp.stack([lax.ppermute(head, "seq", route) for head in leaving])
        entering = entering + got
        if step < size - 2:
            leaving = jnp.matmul(mats, got, precision=highest) + offsets
    return entering, leaving


def together(*arrays):
    return lax.optimization_barrier(arrays)


def everyone(part):
    return lax.all_gather(part, ("dp", "seq"), axis=0, tiled=True)


def share(rows):
    wide = jnp.broadcast_to(rows[None], (lax.axis_size("head"),) + rows.shape)
    return lax.all_to_all(wide, "head", split_axis=0, concat_axis=0, tiled=True)


def add_parts(parts):
    got = lax.all_to_all(parts.astype(jnp.bfloat16), "head", split_axis=0, concat_axis=0, tiled=True)
    return jnp.sum(got.astype(f32), axis=0)


def contract_rows(left, right):
    return lax.dot_general(left, right, (((0,), (0,)), ((), ())), preferred_element_type=f32)


def contract_cols(left, right):
    return lax.dot_general(left, right, (((1,), (1,)), ((), ())), preferred_element_type=f32)


def product(left, right):
    return jnp.dot(left, right, preferred_element_type=f32)


def rms_scale(values, gain):
    return values * lax.rsqrt(jnp.mean(values * values, axis=-1, keepdims=True) + epsilon) * gain


def swiglu(gate_in, up_in):
    return jax.nn.silu(gate_in) * up_in


def on_device(
    activations,
    cotangent,
    lengths,
    query_weight,
    key_weight,
    value_weight,
    gate_weight,
    alpha_weight,
    beta_weight,
    out_weight,
    swiglu_gate,
    swiglu_value,
    swiglu_down,
    mixer_gain,
    feed_gain,
    head_gain,
    decay_rate,
    beta_bias,
):
    bf16 = jnp.bfloat16
    core, stage, group = lax.axis_index("dp"), lax.axis_index("seq"), lax.axis_index("head")
    stages, groups = lax.axis_size("seq"), lax.axis_size("head")
    width = activations.shape[2]
    rows0 = activations.shape[1]
    rows1 = rows0 // QUARTERS
    own0, own1 = rows0 // (2 * groups), rows1 // (2 * groups)
    own = own0 + own1
    quota = width // (2 * stages)
    heads = alpha_weight.shape[1] // 2
    counts = (rows0 // BLOCK, rows1 // BLOCK)
    assert groups == QUARTERS and stages % QUARTERS == 0 and rows1 % BLOCK == 0
    first = core == 0

    def part(array, size, axis, offset=0):
        return lax.dynamic_slice_in_dim(array, offset + core * size, size, axis)

    dk, dv = query_weight.shape[1] // 2, value_weight.shape[1] // 2
    slim = 2 * dk + dv
    mixer_cols = []
    for c in range(2):
        for j in range(c * heads, (c + 1) * heads):
            mixer_cols += [
                query_weight[:, j * dk // heads : (j + 1) * dk // heads],
                key_weight[:, j * dk // heads : (j + 1) * dk // heads],
                value_weight[:, j * dv // heads : (j + 1) * dv // heads],
            ]
    mixer_cols += [alpha_weight, beta_weight]
    mixer_full = everyone(jnp.concatenate(mixer_cols, axis=1).astype(bf16))
    gates_full = everyone(jnp.concatenate([gate_weight, out_weight], axis=1).astype(bf16))
    hidden_units = swiglu_gate.shape[1]
    even = hidden_units // 256 * 256
    odd = hidden_units - even
    assert 0 < odd <= 128
    three = (swiglu_gate, swiglu_value, swiglu_down)
    spare = ((0, 0), (0, 128 - odd))
    feed_full = everyone(
        jnp.concatenate([w[:, :even] for w in three] + [jnp.pad(w[:, even:], spare) for w in three], axis=1).astype(bf16)
    )

    def chip_rows(rows):
        arrived = jnp.zeros((rows1, width), bf16)
        for b in range(QUARTERS):
            route = [(stages + a, stages + QUARTERS * a + b) for a in range(stages // QUARTERS)]
            arrived = arrived + lax.ppermute(rows[b * rows1 : (b + 1) * rows1], ("dp", "seq"), route)
        near0 = lax.ppermute(rows, "dp", [(0, 1)])
        near1 = lax.ppermute(arrived, "dp", [(1, 0)])
        return jnp.concatenate([jnp.where(first, rows, near0), jnp.where(first, near1, arrived)], axis=0)

    inputs = chip_rows(activations[0])
    inputs, late = together(inputs, cotangent[0])
    inputs = inputs.astype(f32)
    spots0 = stage * rows0 + lax.broadcasted_iota(jnp.int32, (rows0, 1), 0)
    spots1 = stage * rows1 + lax.broadcasted_iota(jnp.int32, (rows1, 1), 0)
    mask = jnp.concatenate([spots0 < lengths[0], spots1 < lengths[1]], axis=0).astype(f32)
    masked = (chip_rows(late).astype(f32) * mask).astype(bf16)

    def by_owner(rows):
        wide = rows.shape[1]
        r0 = rows[:rows0].reshape(groups, 2, own0, wide)
        r1 = rows[rows0:].reshape(groups, 2, own1, wide)
        return jnp.concatenate([r0, r1], axis=2).swapaxes(0, 1)

    def in_time(owned):
        wide = owned.shape[3]
        turned = owned.swapaxes(0, 1)
        return jnp.concatenate(
            [turned[:, :, :own0].reshape(rows0, wide), turned[:, :, own0:].reshape(rows1, wide)], axis=0
        )

    def of_core(owned, which):
        return lax.dynamic_index_in_dim(owned, which, 0, keepdims=False)

    def of_group(rows):
        return lax.dynamic_index_in_dim(rows, group, 0, keepdims=False)

    def add_rows(partial):
        owned = by_owner(partial)
        return add_parts(of_core(owned, core) + swap(of_core(owned, 1 - core)))

    def meet_columns(rows):
        return lax.all_to_all(rows, ("dp", "seq"), split_axis=1, concat_axis=0, tiled=True)

    def owned_columns(met):
        got = share(met).reshape(groups, 2, stages, own, quota).transpose(2, 0, 1, 3, 4)
        return jnp.concatenate(
            [got[:, :, :, :own0].reshape(stages, rows0, quota), got[:, :, :, own0:].reshape(stages, rows1, quota)], axis=1
        ).reshape(stages * (rows0 + rows1), quota)

    def across_stages(rows):
        wide = jnp.broadcast_to(rows[None], (stages,) + rows.shape)
        met = lax.all_to_all(wide, "seq", split_axis=0, concat_axis=0, tiled=True)
        return met.reshape(stages * rows.shape[0], rows.shape[1])

    def own_columns(rows):
        pieces, positions, piece = rows.shape
        both = []
        for which in (core, 1 - core):
            start = (which * stages + stage) * quota
            both.append(lax.dynamic_slice(rows, (start // piece, 0, start % piece), (1, positions, quota))[0])
        return jnp.concatenate(both, axis=1)

    own_rows = of_group(of_core(by_owner(inputs), core))
    own_mask = of_group(of_core(by_owner(mask), core))
    tokens_masked = of_core(by_owner(masked), core)
    own_masked = of_group(tokens_masked).astype(f32)
    quarter = width // groups
    masked_met = across_stages(
        lax.dynamic_slice_in_dim(tokens_masked.reshape(groups * own, width), group * quarter, quarter, 1)
    )

    factor1 = lax.rsqrt(jnp.mean(inputs * inputs, axis=-1, keepdims=True) + epsilon)
    unit1 = inputs * factor1
    normed = rms_scale(inputs, mixer_gain).astype(bf16)
    normed_cols = owned_columns(meet_columns(of_group(of_core(by_owner(normed), core)))).T
    mixer_full, masked_met, normed_cols = together(mixer_full, masked_met, normed_cols)
    mixer_w = part(mixer_full, slim, 1)
    gate_w = part(gates_full, dv, 1)
    out_w = part(gates_full, dv, 1, 2 * dv)
    rates_w = mixer_full[:, 2 * slim :]
    proj = product(normed, mixer_w)
    small_pre = product(normed, rates_w)
    gate_pre = product(normed, gate_w)
    alpha_pre = part(small_pre, heads, 1)
    beta_pre = part(small_pre, heads, 1, 2 * heads)
    head0 = (2 * group + core) * heads
    rates = lax.dynamic_slice_in_dim(decay_rate, head0, heads)
    biases = lax.dynamic_slice_in_dim(beta_bias, head0, heads)
    blocks = sum(counts)

    def to_blocks(array):
        return array.T.reshape(heads, blocks, BLOCK)

    def from_blocks(array):
        return array.reshape(heads, blocks * BLOCK).T

    soft = jax.nn.softplus(alpha_pre)
    beta = jax.nn.sigmoid(beta_pre + biases)
    beta_b = to_blocks(beta)
    upto = (
        lax.broadcasted_iota(jnp.int32, (BLOCK, BLOCK), 0) <= lax.broadcasted_iota(jnp.int32, (BLOCK, BLOCK), 1)
    ).astype(f32)
    sums = jnp.matmul(to_blocks(-rates * soft), upto, precision=highest)
    col = jnp.stack([sums, beta_b], axis=-1)
    row = jnp.stack([sums, beta_b], axis=-2)
    solver, scores, w, vt, qt, m, b, mseg, bseg = solve(counts, heads, proj, col, row)
    state_in, unused_carry = relay(mseg, bseg, True)
    state_in, masked_all = together(state_in, share(masked_met))
    gain_row = head_gain[None]
    states, outs, gated = outputs_of(counts, heads, state_in, m, b, qt, scores, vt, gate_pre, gain_row)
    mixed = add_rows(contract_cols(gated, out_w))
    hidden = own_rows + mixed

    normed2, norm2_back = jax.vjp(rms_scale, hidden, feed_gain)
    feed_in = share(
        across_stages(lax.all_to_all(normed2.astype(bf16), "head", split_axis=1, concat_axis=0, tiled=True))
    )
    sums, main_own, main_other, tail_own, tail_other = feed_forward(
        stage[None], feed_in, masked_all, own_columns(feed_in), own_columns(masked_all), feed_full, groups * own
    )
    sums, main_other, tail_other = together(
        add_parts(sums.reshape(groups, own, 2 * width)), swap(main_other), swap(tail_other)
    )
    normed2_grad, feed = sums[:, :width], sums[:, width:]
    hidden_back, feed_gain_grad = norm2_back(normed2_grad)
    hidden_grad = own_masked + hidden_back
    mixed_own = hidden_grad.astype(bf16)
    mixed_half = share(mixed_own)
    other_half = swap(mixed_half)
    mixed_in = in_time(
        jnp.stack([jnp.where(first, mixed_half, other_half), jnp.where(first, other_half, mixed_half)])
    )

    gated_all = everyone(gated)
    gated_grad = product(mixed_in, out_w)
    mixed_late, unused_rows = together(mixed_own, mixed_in)
    mixed_met = meet_columns(mixed_late)
    gated_grad, gated_all = together(gated_grad, gated_all)
    outs_grad, gate_pre_low, gain_grads, d, dseg = output_grads_of(
        counts, heads, gated_grad, gate_pre, outs, gain_row, qt, m
    )
    dseg, mixed_met = together(dseg, mixed_met)
    later, carry = relay(jnp.swapaxes(mseg, 2, 3), dseg, False)

    half = stages * (rows0 + rows1)
    main_own, main_other, tail_own, tail_other, unused_carry = together(
        main_own, main_other, tail_own, tail_other, carry
    )
    main_own, tail_own = main_own + main_other, tail_own + tail_other

    def feed_grad(n):
        pieces = [main_own[(3 * i + n) * 256 : (3 * i + n + 1) * 256] for i in range(even // 256)]
        return jnp.concatenate(pieces + [tail_own[n * 128 : n * 128 + odd]], axis=0)

    feed_gate_grad, feed_value_grad, down_grad = feed_grad(0), feed_grad(1), feed_grad(2)
    gate_back = contract_cols(gate_pre_low, gate_w)
    later, feed_gate_grad, feed_value_grad, down_grad, gate_back = together(
        later, feed_gate_grad, feed_value_grad, down_grad, gate_back
    )
    slim_low, joint_low, col_grad, row_grad = input_grads_of(
        counts, heads, proj, col, row, solver, scores, w, vt, m, d, states, outs_grad, gate_pre_low, later
    )
    joint_all = everyone(joint_low)
    sums_grad = col_grad[..., 0] - row_grad[:, :, 0] * beta_b
    decay_back = from_blocks(jnp.matmul(sums_grad, upto.T, precision=highest))
    beta_back = beta * (1.0 - beta) * from_blocks(col_grad[..., 1] + row_grad[:, :, 0])
    rates_grad = -jnp.sum(soft * decay_back, axis=0)
    biases_grad = jnp.sum(beta_back, axis=0)
    alpha_back = -rates * jax.nn.sigmoid(alpha_pre) * decay_back
    small_low = jnp.concatenate([alpha_back, beta_back], axis=1).astype(bf16)
    blank = jnp.zeros((rows0 + rows1, 4 * heads), bf16)
    spread = lax.dynamic_update_slice(blank, small_low[:, :heads], (0, core * heads))
    spread = lax.dynamic_update_slice(spread, small_low[:, heads:], (0, (2 + core) * heads))
    total = gate_back + contract_cols(slim_low, mixer_w) + contract_cols(spread, rates_w)
    normed_grad = add_rows(total)
    mixer_gain_part = jnp.sum(total * unit1, axis=0)
    normed_grad, small_late, mixer_gain_part, mixed_met = together(
        normed_grad, small_low, mixer_gain_part, mixed_met
    )
    outputs_own = (own_mask * (hidden + feed)).astype(bf16)
    mixed_cols = owned_columns(mixed_met)
    out_grad = jnp.concatenate(
        [contract_rows(mixed_cols, gated_all[:half]), contract_rows(mixed_cols, gated_all[half:])], axis=1
    )
    unused_rows, norm1_back = jax.vjp(lambda v: rms_scale(v, mixer_gain), own_rows)
    input_own = (hidden_grad + norm1_back(normed_grad)[0]).astype(bf16)

    small_rows = contract_rows(small_late, normed).reshape(2 * heads, 2 * stages, quota).swapaxes(0, 1)
    total_heads = decay_rate.shape[0]
    none = jnp.zeros((total_heads,), f32)
    vector = jnp.concatenate(
        [
            mixer_gain_part,
            feed_gain_grad,
            jnp.sum(gain_grads, axis=(0, 1)),
            lax.dynamic_update_slice(none, rates_grad, (head0,)),
            lax.dynamic_update_slice(none, biases_grad, (head0,)),
        ]
    )
    mail = jnp.concatenate(
        [
            small_rows.reshape(2 * stages, 2 * heads * quota),
            jnp.broadcast_to(vector[None], (2 * stages, vector.shape[0])),
        ],
        axis=1,
    )
    mail = lax.all_to_all(mail, ("dp", "seq"), split_axis=0, concat_axis=0, tiled=True)
    small_rows = jnp.sum(mail[:, : 2 * heads * quota].reshape(2, stages, 2, heads, quota), axis=1)
    alpha_grad = small_rows[:, 0].reshape(2 * heads, quota).T
    beta_grad = small_rows[:, 1].reshape(2 * heads, quota).T
    small = jnp.sum(share(jnp.sum(mail[:, 2 * heads * quota :], axis=0)), axis=0)
    joint_all, out_grad = together(joint_all, out_grad)
    query_grad, key_grad, value_grad, gate_grad = projection_grads(normed_cols, joint_all, heads, (dk, dk, dv, dv))

    edges = [width, 2 * width, 2 * width + head_gain.shape[0], 2 * width + head_gain.shape[0] + total_heads]

    def place(rows):
        r0, r1 = rows[:own0], rows[own0:]
        out0 = jnp.concatenate([r0, lax.ppermute(r0, "dp", [(1, 0)])], axis=0)
        pair = jnp.concatenate([lax.ppermute(r1, "dp", [(0, 1)]), r1], axis=0)
        routes = [
            [
                ((stages + QUARTERS * a + b) * groups + k, (stages + a) * groups + b)
                for a in range(stages // QUARTERS)
                for b in range(QUARTERS)
            ]
            for k in range(groups)
        ]
        out1 = jnp.concatenate([lax.ppermute(pair, ("dp", "seq", "head"), route) for route in routes], axis=0)
        return jnp.where(first, out0, out1)[None]

    placed = place(jnp.concatenate([outputs_own, input_own], axis=1))
    return (
        placed[:, :, :width],
        placed[:, :, width:],
        query_grad,
        key_grad,
        value_grad,
        gate_grad,
        alpha_grad,
        beta_grad,
        out_grad,
        feed_gate_grad.T,
        feed_value_grad.T,
        down_grad.T,
        small[: edges[0]],
        small[edges[0] : edges[1]],
        small[edges[1] : edges[2]],
        small[edges[2] : edges[3]],
        small[edges[3] :],
    )


def solution(mesh):
    return jax.shard_map(
        on_device,
        mesh=mesh,
        in_specs=(
            P("dp", "seq", None),
            P("dp", "seq", None),
            P(),
            P(("dp", "seq"), "head"),
            P(("dp", "seq"), "head"),
            P(("dp", "seq"), "head"),
            P(("dp", "seq"), "head"),
            P(("dp", "seq"), "head"),
            P(("dp", "seq"), "head"),
            P(("dp", "seq"), "head"),
            P(("dp", "seq"), "head"),
            P(("dp", "seq"), "head"),
            P(("dp", "seq"), "head"),
            P(),
            P(),
            P(),
            P(),
            P(),
        ),
        out_specs=(
            P("dp", ("seq", "head"), None),
            P("dp", ("seq", "head"), None),
            P(("dp", "seq"), "head"),
            P(("dp", "seq"), "head"),
            P(("dp", "seq"), "head"),
            P(("dp", "seq"), "head"),
            P(("dp", "seq"), "head"),
            P(("dp", "seq"), "head"),
            P(("dp", "seq"), "head"),
            P(("dp", "seq"), "head"),
            P(("dp", "seq"), "head"),
            P(("dp", "seq"), "head"),
            P(),
            P(),
            P(),
            P(),
            P(),
        ),
        check_vma=False,
    )
```

```python
import functools

import jax
import jax.numpy as jnp
from jax import lax
from jax.experimental import pallas as pl
from jax.experimental.pallas import tpu as pltpu
from jax.sharding import PartitionSpec as P

BLOCK = 64
epsilon = 1e-06
highest = lax.Precision.HIGHEST
f32 = jnp.float32


def mm(left, right, a=1, b=0):
    return lax.dot_general(
        left, right, (((a,), (b,)), ((), ())), precision=highest, preferred_element_type=f32
    )


def mm_nt(left, right):
    return mm(left, right, 1, 1)


def mm_tn(left, right):
    return mm(left, right, 0, 0)


def each(f, *lists):
    return [f(*items) for items in zip(*lists)]


def square_masks():
    rows = lax.broadcasted_iota(jnp.int32, (BLOCK, BLOCK), 0)
    cols = lax.broadcasted_iota(jnp.int32, (BLOCK, BLOCK), 1)
    return rows >= cols, rows > cols, (rows == cols).astype(f32)


def row_factor(values):
    return lax.rsqrt(jnp.sum(values * values, axis=-1, keepdims=True) + epsilon)


def split(values, count):
    return [values[i * BLOCK : (i + 1) * BLOCK] for i in range(count)]


def decays(col_ref, row_ref, count):
    lower, strict, identity = square_masks()
    out = []
    for i in range(count):
        c_col, b_col = col_ref[0, i, :, 0:1], col_ref[0, i, :, 1:2]
        c_row, b_row = row_ref[0, i, 0:1, :], row_ref[0, i, 1:2, :]
        fade = jnp.where(lower, jnp.exp(jnp.where(lower, c_col - c_row, 0.0)), 0.0)
        last = c_col[BLOCK - 1 : BLOCK, :]
        out.append((fade, fade * b_row, jnp.exp(c_col), jnp.exp(last - c_col), b_col, jnp.exp(last)))
    return [list(items) for items in zip(*out)]


def chains(counts):
    start, out = 0, []
    for count in counts:
        out.append(range(start, start + count))
        start += count
    return out


def solve_kernel(counts, q_ref, k_ref, v_ref, col_ref, row_ref, solver_ref, scores_ref, w_ref, vt_ref, qt_ref, m_ref, b_ref, mseg_ref, bseg_ref):
    count = sum(counts)
    lower, strict, identity = square_masks()
    query = q_ref[...]
    query = split(query * row_factor(query), count)
    key = k_ref[...]
    key = split(key * row_factor(key), count)
    value = split(v_ref[...], count)
    fade, ratio, growth, remain, beta, end = decays(col_ref, row_ref, count)
    power = each(lambda k, p: jnp.where(strict, -mm_nt(k, k) * p, 0.0), key, ratio)
    solver = [identity + p for p in power]
    for _ in range((BLOCK - 1).bit_length() - 1):
        power = each(lambda p: mm(p, p), power)
        solver = each(lambda s, p: s + mm(s, p), solver, power)
    scores = each(lambda q, k, p: mm_nt(q, k) * p, query, key, ratio)
    w = each(lambda s, g, k: mm(s, g * k), solver, growth, key)
    vt = each(mm, solver, value)
    qt = each(lambda g, q, a, x: g * q - mm(a, x), growth, query, scores, w)
    weighted = each(lambda k, r, b: k * (r * b), key, remain, beta)
    size = query[0].shape[1]
    wide = (
        lax.broadcasted_iota(jnp.int32, (size, size), 0)
        == lax.broadcasted_iota(jnp.int32, (size, size), 1)
    ).astype(f32)
    m = each(lambda e, k, x: e * wide - mm_tn(k, x), end, weighted, w)
    b = each(mm_tn, weighted, vt)
    for i in range(count):
        solver_ref[0, i] = solver[i]
        scores_ref[0, i] = scores[i]
        w_ref[0, i] = w[i]
        vt_ref[0, i] = vt[i]
        qt_ref[0, i] = qt[i]
        m_ref[0, i] = m[i]
        b_ref[0, i] = b[i]
    for j, chain in enumerate(chains(counts)):
        mseg_ref[0, j] = m[chain[0]]
        bseg_ref[0, j] = b[chain[0]]
        for i in chain[1:]:
            bseg_ref[0, j] = mm(m_ref[0, i], bseg_ref[0, j]) + b_ref[0, i]
            mseg_ref[0, j] = mm(m_ref[0, i], mseg_ref[0, j])


def output_kernel(counts, state_ref, m_ref, b_ref, qt_ref, scores_ref, vt_ref, gate_ref, gain_ref, states_ref, out_ref, gated_ref):
    count = sum(counts)
    states = [None] * count
    for j, chain in enumerate(chains(counts)):
        state = state_ref[0, j]
        for i in chain:
            states[i] = state
            states_ref[0, i] = state
            if i != chain[-1]:
                state = mm(m_ref[0, i], state) + b_ref[0, i]
    gain = gain_ref[...]
    outs = [mm(qt_ref[0, i], states[i]) + mm(scores_ref[0, i], vt_ref[0, i]) for i in range(count)]
    for i in range(count):
        rows = slice(i * BLOCK, (i + 1) * BLOCK)
        out = outs[i]
        gate = gate_ref[rows, :]
        scale = lax.rsqrt(jnp.mean(out * out, axis=-1, keepdims=True) + epsilon)
        out_ref[rows, :] = out
        gated_ref[rows, :] = (out * scale * gain * (gate * jax.nn.sigmoid(gate))).astype(jnp.bfloat16)


def output_grad_kernel(counts, grad_ref, gate_ref, out_ref, gain_ref, qt_ref, m_ref, out_grad_ref, gate_grad_ref, gain_grad_ref, d_ref, dseg_ref):
    count = sum(counts)
    gain = gain_ref[...]
    gain_grad = jnp.zeros_like(gain)
    grads = []
    for i in range(count):
        rows = slice(i * BLOCK, (i + 1) * BLOCK)
        grad, gate, out = grad_ref[rows, :], gate_ref[rows, :], out_ref[rows, :]
        scale = lax.rsqrt(jnp.mean(out * out, axis=-1, keepdims=True) + epsilon)
        unit = out * scale
        sig = jax.nn.sigmoid(gate)
        normed_grad = grad * (gate * sig)
        gate_grad_ref[rows, :] = (grad * (unit * gain) * (sig * (1.0 + gate * (1.0 - sig)))).astype(jnp.bfloat16)
        gain_grad = gain_grad + jnp.sum(normed_grad * unit, axis=0, keepdims=True)
        inner = normed_grad * gain
        out_grad = scale * (inner - unit * jnp.mean(unit * inner, axis=-1, keepdims=True))
        out_grad_ref[rows, :] = out_grad
        grads.append(out_grad)
    gain_grad_ref[0] = gain_grad
    d = [mm_tn(qt_ref[0, i], grads[i]) for i in range(count)]
    for i in range(count):
        d_ref[0, i] = d[i]
    for j, chain in enumerate(chains(counts)):
        dseg_ref[0, j] = d[chain[-1]]
        for i in list(chain)[-2::-1]:
            dseg_ref[0, j] = mm_tn(m_ref[0, i], dseg_ref[0, j]) + d_ref[0, i]


def unit_back(raw, grad):
    factor = row_factor(raw)
    unit = raw * factor
    return factor * (grad - unit * jnp.sum(unit * grad, axis=-1, keepdims=True))


def grads_kernel(counts, q_ref, k_ref, col_ref, row_ref, solver_ref, scores_ref, w_ref, vt_ref, m_ref, d_ref, states_ref, out_grad_ref, later_ref, slim_ref, col_grad_ref, row_grad_ref):
    count = sum(counts)
    span = range(count)
    lower, strict, identity = square_masks()
    raw_q, raw_k = split(q_ref[...], count), split(k_ref[...], count)
    query = [x * row_factor(x) for x in raw_q]
    key = [x * row_factor(x) for x in raw_k]
    fade, ratio, growth, remain, beta, end = decays(col_ref, row_ref, count)
    out_grad = split(out_grad_ref[...], count)
    later = [None] * count
    for j, chain in enumerate(chains(counts)):
        state = later_ref[0, j]
        for i in list(chain)[::-1]:
            later[i] = state
            if i != chain[0]:
                state = mm_tn(m_ref[0, i], state) + d_ref[0, i]
    states = [states_ref[0, i] for i in span]
    update = [vt_ref[0, i] - mm(w_ref[0, i], states[i]) for i in span]
    update_grad = [
        mm_tn(scores_ref[0, i], out_grad[i]) + mm(key[i] * (remain[i] * beta[i]), later[i]) for i in span
    ]
    solved = [mm_tn(solver_ref[0, i], update_grad[i]) for i in span]
    scores_grad = each(mm_nt, out_grad, update)
    inner_grad = each(lambda y, u: jnp.where(strict, -mm_nt(y, u), 0.0), solved, update)
    query_dot = each(mm_nt, query, key)
    keys_dot = each(mm_nt, key, key)
    from_out = each(mm_nt, out_grad, states)
    from_solved = each(mm_nt, solved, states)
    from_update = each(mm_nt, update, later)
    weighted_scores = each(lambda p, x: p * x, ratio, scores_grad)
    weighted_inner = each(lambda p, x: p * x, ratio, inner_grad)
    q_grad = [growth[i] * from_out[i] + mm(weighted_scores[i], key[i]) for i in span]
    k_grad = [
        mm_tn(weighted_scores[i], query[i])
        + (remain[i] * beta[i]) * from_update[i]
        - growth[i] * from_solved[i]
        + mm(weighted_inner[i], key[i])
        + mm_tn(weighted_inner[i], key[i])
        for i in span
    ]
    last_row = (lax.broadcasted_iota(jnp.int32, (BLOCK, 1), 0) == BLOCK - 1).astype(f32)
    for i in span:
        rows = slice(i * BLOCK, (i + 1) * BLOCK)
        start = 0
        for grad in (unit_back(raw_q[i], q_grad[i]), unit_back(raw_k[i], k_grad[i]), solved[i]):
            place = slice(start, start + grad.shape[1])
            start += grad.shape[1]
            slim_ref[rows, place] = grad.astype(jnp.bfloat16)
        faded = fade[i] * (scores_grad[i] * query_dot[i] + inner_grad[i] * keys_dot[i])
        b_row = row_ref[0, i, 1:2, :]
        growth_grad = jnp.sum(query[i] * from_out[i] - key[i] * from_solved[i], axis=-1, keepdims=True)
        weight_grad = jnp.sum(key[i] * from_update[i], axis=-1, keepdims=True)
        pulled = remain[i] * beta[i] * weight_grad
        tail = jnp.sum(pulled, axis=0, keepdims=True) + end[i] * jnp.sum(
            jnp.sum(later[i] * states[i], axis=-1, keepdims=True), axis=0, keepdims=True
        )
        c_grad = jnp.sum(faded * b_row, axis=-1, keepdims=True) + growth[i] * growth_grad - pulled + last_row * tail
        col_grad_ref[0, i, :, 0:1] = c_grad
        col_grad_ref[0, i, :, 1:2] = remain[i] * weight_grad
        row_grad_ref[0, i] = jnp.sum(faded, axis=0, keepdims=True)


def whole(shape):
    return pl.BlockSpec((1,) + tuple(shape[1:]), lambda j: (j,) + (0,) * (len(shape) - 1))


def columns(rows, width, first=0, step=1):
    return pl.BlockSpec((rows, width), lambda j: (0, step * j + first))


def shaped(shape, dtype=f32):
    return jax.ShapeDtypeStruct(shape, dtype)


def call(kernel, counts, heads, inputs, outputs, flops):
    moved = sum(x.size * x.dtype.itemsize for x, _ in inputs) + sum(
        x.size * x.dtype.itemsize for x, _ in outputs
    )
    return pl.pallas_call(
        functools.partial(kernel, counts),
        grid=(heads,),
        in_specs=[s for _, s in inputs],
        out_specs=[s for _, s in outputs],
        out_shape=[x for x, _ in outputs],
        compiler_params=pltpu.CompilerParams(vmem_limit_bytes=48 << 20),
        cost_estimate=pl.CostEstimate(flops=flops, bytes_accessed=moved, transcendentals=0),
    )(*[x for x, _ in inputs])


def per_head(heads, *shape, dtype=f32):
    s = (heads,) + shape
    return shaped(s, dtype), whole(s)


def flat(array, width, first=0, step=1):
    return array, columns(array.shape[0], width, first, step)


def stacked(array):
    return array, whole(array.shape)


def solve(counts, heads, proj, col, row):
    n, dk, dv = sum(counts), 128, 256
    return call(
        solve_kernel, counts, heads,
        [flat(proj, dk, 0, 4), flat(proj, dk, 1, 4), flat(proj, dv, 1, 2), stacked(col), stacked(row)],
        [per_head(heads, n, BLOCK, BLOCK), per_head(heads, n, BLOCK, BLOCK), per_head(heads, n, BLOCK, dk),
         per_head(heads, n, BLOCK, dv), per_head(heads, n, BLOCK, dk), per_head(heads, n, dk, dk),
         per_head(heads, n, dk, dv), per_head(heads, len(counts), dk, dk), per_head(heads, len(counts), dk, dv)],
        heads * n * 100_000_000,
    )


def outputs_of(counts, heads, state, m, b, qt, scores, vt, gate_pre, gain):
    n, dk, dv = sum(counts), 128, 256
    rows = gate_pre.shape[0]
    cols = columns(rows, dv)
    return call(
        output_kernel, counts, heads,
        [stacked(state), stacked(m), stacked(b), stacked(qt), stacked(scores), stacked(vt), flat(gate_pre, dv),
         (gain, pl.BlockSpec((1, dv), lambda j: (0, 0)))],
        [per_head(heads, n, dk, dv), (shaped((rows, heads * dv)), cols), (shaped((rows, heads * dv), jnp.bfloat16), cols)],
        heads * n * 50_000_000,
    )


def output_grads_of(counts, heads, grad, gate_pre, outs, gain, qt, m):
    n, dk, dv = sum(counts), 128, 256
    rows = gate_pre.shape[0]
    cols = columns(rows, dv)
    return call(
        output_grad_kernel, counts, heads,
        [flat(grad, dv), flat(gate_pre, dv), flat(outs, dv), (gain, pl.BlockSpec((1, dv), lambda j: (0, 0))), stacked(qt), stacked(m)],
        [(shaped((rows, heads * dv)), cols), (shaped((rows, heads * dv), jnp.bfloat16), cols),
         per_head(heads, 1, dv), per_head(heads, n, dk, dv), per_head(heads, len(counts), dk, dv)],
        heads * n * 50_000_000,
    )


def input_grads_of(counts, heads, proj, col, row, solver, scores, w, vt, m, d, states, out_grad, later):
    n, dk, dv = sum(counts), 128, 256
    rows = proj.shape[0]
    return call(
        grads_kernel, counts, heads,
        [flat(proj, dk, 0, 4), flat(proj, dk, 1, 4), stacked(col), stacked(row), stacked(solver), stacked(scores), stacked(w),
         stacked(vt), stacked(m), stacked(d), stacked(states), flat(out_grad, dv), stacked(later)],
        [(shaped((rows, heads * (2 * dk + dv)), jnp.bfloat16), columns(rows, 2 * dk + dv)),
         per_head(heads, n, BLOCK, 2), per_head(heads, n, 1, BLOCK)],
        heads * n * 150_000_000,
    )


def feed_kernel(stage_ref, x_ref, k_ref, xs_ref, ks_ref, pair_ref, down_ref, tail_pair_ref, tail_down_ref, sums_ref, main_ref, main_other_ref, tail_ref, tail_other_ref, active_s, pair_s):
    step, chunk = pl.program_id(0), pl.program_id(1)
    own, width = sums_ref.shape[0], sums_ref.shape[1] // 2
    near, piece = x_ref.shape[1] // own, x_ref.shape[2]
    stage = stage_ref[0]
    here = pl.ds(pl.multiple_of(lax.rem(stage, near) * own, own), own)

    @pl.when((step == 0) & (chunk == 0))
    def _():
        sums_ref[...] = jnp.zeros_like(sums_ref)

    def work(pair, down, out_refs):
        wide = down.shape[1]
        both, grad = (
            sum(
                jnp.dot(rows[i], w[i * piece : (i + 1) * piece, :], preferred_element_type=f32)
                for i in range(rows.shape[0])
            )
            for rows, w in ((x_ref, pair), (k_ref, down))
        )
        gate, up = both[:, :wide], both[:, wide:]
        sig = jax.nn.sigmoid(gate)
        silu = gate * sig
        active_s[:, :wide] = (silu * up).astype(jnp.bfloat16)
        pair_s[:, :wide] = (grad * up * (sig * (1.0 + gate * (1.0 - sig)))).astype(jnp.bfloat16)
        pair_s[:, wide : 2 * wide] = (grad * silu).astype(jnp.bfloat16)

        @pl.when(chunk == stage // near)
        def _():
            sums_ref[:, width:] += contract_cols(active_s[here, :wide], down[...])
            sums_ref[:, :width] += contract_cols(pair_s[here, : 2 * wide], pair[...])

        parts = (
            contract_rows(pair_s[:, : 2 * wide], xs_ref[...]),
            contract_rows(active_s[:, :wide], ks_ref[...]),
        )
        for i, p in enumerate(parts):
            place = slice(2 * i * wide, 2 * i * wide + p.shape[0])
            quota = p.shape[1] // 2

            @pl.when(chunk == 0)
            def _():
                out_refs[0][place, :] = p[:, :quota]
                out_refs[1][place, :] = p[:, quota:]

            @pl.when(chunk > 0)
            def _():
                out_refs[0][place, :] += p[:, :quota]
                out_refs[1][place, :] += p[:, quota:]

    work(pair_ref, down_ref, (main_ref, main_other_ref))

    @pl.when(step == pl.num_programs(0) - 1)
    def _():
        work(tail_pair_ref, tail_down_ref, (tail_ref, tail_other_ref))


def feed_forward(stage, rows, grads, row_cols, grad_cols, weights, own):
    pieces, positions, piece = rows.shape
    width = pieces * piece
    picked = row_cols.shape[1]
    tile, rest = 256, 128
    steps = (weights.shape[1] - 3 * rest) // (3 * tile)
    chunk = min(positions, 4 * own)
    grid = (steps, positions // chunk)
    tokens = pl.BlockSpec((pieces, chunk, piece), lambda i, t, s: (0, t, 0))
    columns_of = pl.BlockSpec((chunk, picked), lambda i, t, s: (t, 0))

    def piece_of(columns, first):
        return pl.BlockSpec((width, columns), lambda i, t, s: (0, first // columns + i))

    def rest_of(columns, first):
        return pl.BlockSpec((width, columns), lambda i, t, s: (0, first // columns))

    main = steps * tile
    def fixed(*shape):
        return pl.BlockSpec(shape, lambda i, t, s: (0, 0))

    flops = 2 * positions * width * weights.shape[1] + 2 * own * width * weights.shape[1] + 2 * positions * picked * weights.shape[1]
    return pl.pallas_call(
        feed_kernel,
        grid_spec=pltpu.PrefetchScalarGridSpec(
            num_scalar_prefetch=1,
            grid=grid,
            in_specs=[tokens, tokens, columns_of, columns_of, piece_of(2 * tile, 0), piece_of(tile, 2 * main), rest_of(2 * rest, 3 * main), rest_of(rest, 3 * main + 2 * rest)],
            out_specs=[
                fixed(own, 2 * width),
                pl.BlockSpec((3 * tile, picked // 2), lambda i, t, s: (i, 0)),
                pl.BlockSpec((3 * tile, picked // 2), lambda i, t, s: (i, 0)),
                fixed(3 * rest, picked // 2),
                fixed(3 * rest, picked // 2),
            ],
            scratch_shapes=[pltpu.VMEM((chunk, tile), jnp.bfloat16), pltpu.VMEM((chunk, 2 * tile), jnp.bfloat16)],
        ),
        out_shape=[
            shaped((own, 2 * width)),
            shaped((3 * tile * steps, picked // 2)),
            shaped((3 * tile * steps, picked // 2)),
            shaped((3 * rest, picked // 2)),
            shaped((3 * rest, picked // 2)),
        ],
        compiler_params=pltpu.CompilerParams(
            dimension_semantics=("arbitrary", "arbitrary"), vmem_limit_bytes=56 << 20
        ),
        cost_estimate=pl.CostEstimate(
            flops=flops, bytes_accessed=2 * weights.size + 8 * positions * width, transcendentals=0
        ),
    )(stage, rows, grads, row_cols, grad_cols, weights, weights, weights, weights)


def projection_kernel(heads, cols_ref, slim_ref, gate_ref, q_ref, k_ref, v_ref, g_ref):
    joined = jnp.dot(cols_ref[...], slim_ref[...], preferred_element_type=f32)
    start = 0
    for j in range(heads):
        for ref in (q_ref, k_ref, v_ref):
            size = ref.shape[1] // heads
            ref[:, j * size : (j + 1) * size] = joined[:, start : start + size]
            start += size
    g_ref[...] = jnp.dot(cols_ref[...], gate_ref[...], preferred_element_type=f32)


def projection_grads(cols, slim_all, gate_all, heads, sizes):
    quota, positions = cols.shape
    wides = (slim_all.shape[1], gate_all.shape[1])
    return pl.pallas_call(
        functools.partial(projection_kernel, heads),
        grid=(2,),
        in_specs=[pl.BlockSpec((quota, positions), lambda c: (0, 0))]
        + [pl.BlockSpec((positions, n), lambda c: (c, 0)) for n in wides],
        out_specs=[pl.BlockSpec((quota, n), lambda c: (0, c)) for n in sizes],
        out_shape=[shaped((quota, 2 * n)) for n in sizes],
        compiler_params=pltpu.CompilerParams(vmem_limit_bytes=56 << 20),
        cost_estimate=pl.CostEstimate(
            flops=4 * quota * positions * sum(wides), bytes_accessed=4 * positions * sum(wides), transcendentals=0
        ),
    )(cols, slim_all, gate_all)


QUARTERS = 4


def swap(array):
    return lax.ppermute(array, "dp", [(0, 1), (1, 0)])


def relay(mats, offsets, forward):
    size = lax.axis_size("seq")
    entering = jnp.zeros_like(offsets)
    leaving = offsets
    for step in range(size - 1):
        route = [(step, step + 1)] if forward else [(size - 1 - step, size - 2 - step)]
        got = jnp.stack([lax.ppermute(head, "seq", route) for head in leaving])
        entering = entering + got
        if step < size - 2:
            leaving = jnp.matmul(mats, got, precision=highest) + offsets
    return entering, leaving


def together(*arrays):
    return lax.optimization_barrier(arrays)


def everyone(part):
    return lax.all_gather(part, ("dp", "seq"), axis=0, tiled=True)


def share(rows):
    wide = jnp.broadcast_to(rows[None], (lax.axis_size("head"),) + rows.shape)
    return lax.all_to_all(wide, "head", split_axis=0, concat_axis=0, tiled=True)


def add_parts(parts):
    got = lax.all_to_all(parts.astype(jnp.bfloat16), "head", split_axis=0, concat_axis=0, tiled=True)
    return jnp.sum(got.astype(f32), axis=0)


def contract_rows(left, right):
    return lax.dot_general(left, right, (((0,), (0,)), ((), ())), preferred_element_type=f32)


def contract_cols(left, right):
    return lax.dot_general(left, right, (((1,), (1,)), ((), ())), preferred_element_type=f32)


def product(left, right):
    return jnp.dot(left, right, preferred_element_type=f32)


def rms_scale(values, gain):
    return values * lax.rsqrt(jnp.mean(values * values, axis=-1, keepdims=True) + epsilon) * gain


def swiglu(gate_in, up_in):
    return jax.nn.silu(gate_in) * up_in


def on_device(
    activations,
    cotangent,
    lengths,
    query_weight,
    key_weight,
    value_weight,
    gate_weight,
    alpha_weight,
    beta_weight,
    out_weight,
    swiglu_gate,
    swiglu_value,
    swiglu_down,
    mixer_gain,
    feed_gain,
    head_gain,
    decay_rate,
    beta_bias,
):
    bf16 = jnp.bfloat16
    core, stage, group = lax.axis_index("dp"), lax.axis_index("seq"), lax.axis_index("head")
    stages, groups = lax.axis_size("seq"), lax.axis_size("head")
    width = activations.shape[2]
    rows0 = activations.shape[1]
    rows1 = rows0 // QUARTERS
    own0, own1 = rows0 // (2 * groups), rows1 // (2 * groups)
    own = own0 + own1
    quota = width // (2 * stages)
    heads = alpha_weight.shape[1] // 2
    counts = (rows0 // BLOCK, rows1 // BLOCK)
    assert groups == QUARTERS and stages % QUARTERS == 0 and rows1 % BLOCK == 0
    first = core == 0

    def part(array, size, axis, offset=0):
        return lax.dynamic_slice_in_dim(array, offset + core * size, size, axis)

    dk, dv = query_weight.shape[1] // 2, value_weight.shape[1] // 2
    slim = 2 * dk + dv
    mixer_cols = []
    for c in range(2):
        for j in range(c * heads, (c + 1) * heads):
            mixer_cols += [
                query_weight[:, j * dk // heads : (j + 1) * dk // heads],
                key_weight[:, j * dk // heads : (j + 1) * dk // heads],
                value_weight[:, j * dv // heads : (j + 1) * dv // heads],
            ]
    mixer_cols += [alpha_weight, beta_weight]
    mixer_full = everyone(jnp.concatenate(mixer_cols, axis=1).astype(bf16))
    gates_full = everyone(jnp.concatenate([gate_weight, out_weight], axis=1).astype(bf16))
    hidden_units = swiglu_gate.shape[1]
    even = hidden_units // 256 * 256
    odd = hidden_units - even
    assert 0 < odd <= 128
    spare = ((0, 0), (0, 128 - odd))
    feed_cols = []
    for i in range(0, even, 256):
        feed_cols += [swiglu_gate[:, i : i + 256], swiglu_value[:, i : i + 256]]
    feed_cols.append(swiglu_down[:, :even])
    feed_cols += [jnp.pad(w[:, even:], spare) for w in (swiglu_gate, swiglu_value, swiglu_down)]
    feed_full = everyone(jnp.concatenate(feed_cols, axis=1).astype(bf16))

    def chip_rows(rows):
        arrived = jnp.zeros((rows1, width), bf16)
        for b in range(QUARTERS):
            route = [(stages + a, stages + QUARTERS * a + b) for a in range(stages // QUARTERS)]
            arrived = arrived + lax.ppermute(rows[b * rows1 : (b + 1) * rows1], ("dp", "seq"), route)
        near0 = lax.ppermute(rows, "dp", [(0, 1)])
        near1 = lax.ppermute(arrived, "dp", [(1, 0)])
        return jnp.concatenate([jnp.where(first, rows, near0), jnp.where(first, near1, arrived)], axis=0)

    inputs = chip_rows(activations[0])
    inputs, late = together(inputs, cotangent[0])
    inputs = inputs.astype(f32)
    spots0 = stage * rows0 + lax.broadcasted_iota(jnp.int32, (rows0, 1), 0)
    spots1 = stage * rows1 + lax.broadcasted_iota(jnp.int32, (rows1, 1), 0)
    mask = jnp.concatenate([spots0 < lengths[0], spots1 < lengths[1]], axis=0).astype(f32)
    masked = (chip_rows(late).astype(f32) * mask).astype(bf16)

    def by_owner(rows):
        wide = rows.shape[1]
        r0 = rows[:rows0].reshape(groups, 2, own0, wide)
        r1 = rows[rows0:].reshape(groups, 2, own1, wide)
        return jnp.concatenate([r0, r1], axis=2).swapaxes(0, 1)

    def in_time(owned):
        wide = owned.shape[3]
        turned = owned.swapaxes(0, 1)
        return jnp.concatenate(
            [turned[:, :, :own0].reshape(rows0, wide), turned[:, :, own0:].reshape(rows1, wide)], axis=0
        )

    def of_core(owned, which):
        return lax.dynamic_index_in_dim(owned, which, 0, keepdims=False)

    def of_group(rows):
        return lax.dynamic_index_in_dim(rows, group, 0, keepdims=False)

    def add_rows(partial):
        owned = by_owner(partial)
        return add_parts(of_core(owned, core) + swap(of_core(owned, 1 - core)))

    def meet_columns(rows):
        return lax.all_to_all(rows, ("dp", "seq"), split_axis=1, concat_axis=0, tiled=True)

    def owned_columns(met):
        got = share(met).reshape(groups, 2, stages, own, quota).transpose(2, 0, 1, 3, 4)
        return jnp.concatenate(
            [got[:, :, :, :own0].reshape(stages, rows0, quota), got[:, :, :, own0:].reshape(stages, rows1, quota)], axis=1
        ).reshape(stages * (rows0 + rows1), quota)

    def across_stages(rows):
        wide = jnp.broadcast_to(rows[None], (stages,) + rows.shape)
        met = lax.all_to_all(wide, "seq", split_axis=0, concat_axis=0, tiled=True)
        return met.reshape(stages * rows.shape[0], rows.shape[1])

    def own_columns(rows):
        pieces, positions, piece = rows.shape
        both = []
        for which in (core, 1 - core):
            start = (which * stages + stage) * quota
            both.append(lax.dynamic_slice(rows, (start // piece, 0, start % piece), (1, positions, quota))[0])
        return jnp.concatenate(both, axis=1)

    own_rows = of_group(of_core(by_owner(inputs), core))
    own_mask = of_group(of_core(by_owner(mask), core))
    tokens_masked = of_core(by_owner(masked), core)
    own_masked = of_group(tokens_masked).astype(f32)
    quarter = width // groups
    masked_met = across_stages(
        lax.dynamic_slice_in_dim(tokens_masked.reshape(groups * own, width), group * quarter, quarter, 1)
    )

    factor1 = lax.rsqrt(jnp.mean(inputs * inputs, axis=-1, keepdims=True) + epsilon)
    unit1 = inputs * factor1
    normed = rms_scale(inputs, mixer_gain).astype(bf16)
    normed_cols = owned_columns(meet_columns(of_group(of_core(by_owner(normed), core)))).T
    mixer_full, masked_met, normed_cols = together(mixer_full, masked_met, normed_cols)
    mixer_w = part(mixer_full, slim, 1)
    gate_w = part(gates_full, dv, 1)
    out_w = part(gates_full, dv, 1, 2 * dv)
    rates_w = mixer_full[:, 2 * slim :]
    proj = product(normed, mixer_w)
    small_pre = product(normed, rates_w)
    gate_pre = product(normed, gate_w)
    alpha_pre = part(small_pre, heads, 1)
    beta_pre = part(small_pre, heads, 1, 2 * heads)
    head0 = (2 * group + core) * heads
    rates = lax.dynamic_slice_in_dim(decay_rate, head0, heads)
    biases = lax.dynamic_slice_in_dim(beta_bias, head0, heads)
    blocks = sum(counts)

    def to_blocks(array):
        return array.T.reshape(heads, blocks, BLOCK)

    def from_blocks(array):
        return array.reshape(heads, blocks * BLOCK).T

    soft = jax.nn.softplus(alpha_pre)
    beta = jax.nn.sigmoid(beta_pre + biases)
    beta_b = to_blocks(beta)
    upto = (
        lax.broadcasted_iota(jnp.int32, (BLOCK, BLOCK), 0) <= lax.broadcasted_iota(jnp.int32, (BLOCK, BLOCK), 1)
    ).astype(f32)
    sums = jnp.matmul(to_blocks(-rates * soft), upto, precision=highest)
    col = jnp.stack([sums, beta_b], axis=-1)
    row = jnp.stack([sums, beta_b], axis=-2)
    solver, scores, w, vt, qt, m, b, mseg, bseg = solve(counts, heads, proj, col, row)
    state_in, unused_carry = relay(mseg, bseg, True)
    state_in, masked_all = together(state_in, share(masked_met))
    gain_row = head_gain[None]
    states, outs, gated = outputs_of(counts, heads, state_in, m, b, qt, scores, vt, gate_pre, gain_row)
    mixed = add_rows(contract_cols(gated, out_w))
    hidden = own_rows + mixed

    normed2, norm2_back = jax.vjp(rms_scale, hidden, feed_gain)
    feed_in = share(
        across_stages(lax.all_to_all(normed2.astype(bf16), "head", split_axis=1, concat_axis=0, tiled=True))
    )
    sums, main_own, main_other, tail_own, tail_other = feed_forward(
        stage[None], feed_in, masked_all, own_columns(feed_in), own_columns(masked_all), feed_full, groups * own
    )
    sums, main_other, tail_other = together(
        add_parts(sums.reshape(groups, own, 2 * width)), swap(main_other), swap(tail_other)
    )
    normed2_grad, feed = sums[:, :width], sums[:, width:]
    hidden_back, feed_gain_grad = norm2_back(normed2_grad)
    hidden_grad = own_masked + hidden_back
    mixed_own = hidden_grad.astype(bf16)
    mixed_half = share(mixed_own)
    other_half = swap(mixed_half)
    mixed_in = in_time(
        jnp.stack([jnp.where(first, mixed_half, other_half), jnp.where(first, other_half, mixed_half)])
    )

    gated_all = everyone(gated)
    gated_grad = product(mixed_in, out_w)
    mixed_late, unused_rows = together(mixed_own, mixed_in)
    mixed_met = meet_columns(mixed_late)
    gated_grad, gated_all = together(gated_grad, gated_all)
    outs_grad, gate_pre_low, gain_grads, d, dseg = output_grads_of(
        counts, heads, gated_grad, gate_pre, outs, gain_row, qt, m
    )
    dseg, mixed_met = together(dseg, mixed_met)
    later, carry = relay(jnp.swapaxes(mseg, 2, 3), dseg, False)

    half = stages * (rows0 + rows1)
    main_own, main_other, tail_own, tail_other, gate_late, unused_carry = together(
        main_own, main_other, tail_own, tail_other, gate_pre_low, carry
    )
    gate_pre_all = everyone(gate_late)
    main_own, tail_own = main_own + main_other, tail_own + tail_other

    def feed_grad(n):
        pieces = [main_own[(3 * i + n) * 256 : (3 * i + n + 1) * 256] for i in range(even // 256)]
        return jnp.concatenate(pieces + [tail_own[n * 128 : n * 128 + odd]], axis=0)

    feed_gate_grad, feed_value_grad, down_grad = feed_grad(0), feed_grad(1), feed_grad(2)
    gate_back = contract_cols(gate_pre_low, gate_w)
    later, feed_gate_grad, feed_value_grad, down_grad, gate_back = together(
        later, feed_gate_grad, feed_value_grad, down_grad, gate_back
    )
    slim_low, col_grad, row_grad = input_grads_of(
        counts, heads, proj, col, row, solver, scores, w, vt, m, d, states, outs_grad, later
    )
    slim_all = everyone(slim_low)
    slim_low, mixed_met = together(slim_low, mixed_met)
    mixed_cols = owned_columns(mixed_met)
    sums_grad = col_grad[..., 0] - row_grad[:, :, 0] * beta_b
    decay_back = from_blocks(jnp.matmul(sums_grad, upto.T, precision=highest))
    beta_back = beta * (1.0 - beta) * from_blocks(col_grad[..., 1] + row_grad[:, :, 0])
    rates_grad = -jnp.sum(soft * decay_back, axis=0)
    biases_grad = jnp.sum(beta_back, axis=0)
    alpha_back = -rates * jax.nn.sigmoid(alpha_pre) * decay_back
    small_low = jnp.concatenate([alpha_back, beta_back], axis=1).astype(bf16)
    blank = jnp.zeros((rows0 + rows1, 4 * heads), bf16)
    spread = lax.dynamic_update_slice(blank, small_low[:, :heads], (0, core * heads))
    spread = lax.dynamic_update_slice(spread, small_low[:, heads:], (0, (2 + core) * heads))
    total = gate_back + contract_cols(slim_low, mixer_w) + contract_cols(spread, rates_w)
    normed_grad = add_rows(total)
    mixer_gain_part = jnp.sum(total * unit1, axis=0)
    normed_grad, small_late, mixer_gain_part, gate_pre_all = together(
        normed_grad, small_low, mixer_gain_part, gate_pre_all
    )
    outputs_own = (own_mask * (hidden + feed)).astype(bf16)
    out_grad = jnp.concatenate(
        [contract_rows(mixed_cols, gated_all[:half]), contract_rows(mixed_cols, gated_all[half:])], axis=1
    )
    unused_rows, norm1_back = jax.vjp(lambda v: rms_scale(v, mixer_gain), own_rows)
    input_own = (hidden_grad + norm1_back(normed_grad)[0]).astype(bf16)

    small_rows = contract_rows(small_late, normed).reshape(2 * heads, 2 * stages, quota).swapaxes(0, 1)
    total_heads = decay_rate.shape[0]
    none = jnp.zeros((total_heads,), f32)
    vector = jnp.concatenate(
        [
            mixer_gain_part,
            feed_gain_grad,
            jnp.sum(gain_grads, axis=(0, 1)),
            lax.dynamic_update_slice(none, rates_grad, (head0,)),
            lax.dynamic_update_slice(none, biases_grad, (head0,)),
        ]
    )
    mail = jnp.concatenate(
        [
            small_rows.reshape(2 * stages, 2 * heads * quota),
            jnp.broadcast_to(vector[None], (2 * stages, vector.shape[0])),
        ],
        axis=1,
    )
    mail = lax.all_to_all(mail, ("dp", "seq"), split_axis=0, concat_axis=0, tiled=True)
    mail, out_grad = together(mail, out_grad)
    small_rows = jnp.sum(mail[:, : 2 * heads * quota].reshape(2, stages, 2, heads, quota), axis=1)
    alpha_grad = small_rows[:, 0].reshape(2 * heads, quota).T
    beta_grad = small_rows[:, 1].reshape(2 * heads, quota).T
    small = jnp.sum(share(jnp.sum(mail[:, 2 * heads * quota :], axis=0)), axis=0)
    slim_all, out_grad = together(slim_all, out_grad)
    query_grad, key_grad, value_grad, gate_grad = projection_grads(normed_cols, slim_all, gate_pre_all, heads, (dk, dk, dv, dv))

    edges = [width, 2 * width, 2 * width + head_gain.shape[0], 2 * width + head_gain.shape[0] + total_heads]

    def place(rows):
        r0, r1 = rows[:own0], rows[own0:]
        out0 = jnp.concatenate([r0, lax.ppermute(r0, "dp", [(1, 0)])], axis=0)
        pair = jnp.concatenate([lax.ppermute(r1, "dp", [(0, 1)]), r1], axis=0)
        routes = [
            [
                ((stages + QUARTERS * a + b) * groups + k, (stages + a) * groups + b)
                for a in range(stages // QUARTERS)
                for b in range(QUARTERS)
            ]
            for k in range(groups)
        ]
        out1 = jnp.concatenate([lax.ppermute(pair, ("dp", "seq", "head"), route) for route in routes], axis=0)
        return jnp.where(first, out0, out1)[None]

    placed = place(jnp.concatenate([outputs_own, input_own], axis=1))
    return (
        placed[:, :, :width],
        placed[:, :, width:],
        query_grad,
        key_grad,
        value_grad,
        gate_grad,
        alpha_grad,
        beta_grad,
        out_grad,
        feed_gate_grad.T,
        feed_value_grad.T,
        down_grad.T,
        small[: edges[0]],
        small[edges[0] : edges[1]],
        small[edges[1] : edges[2]],
        small[edges[2] : edges[3]],
        small[edges[3] :],
    )


def solution(mesh):
    return jax.shard_map(
        on_device,
        mesh=mesh,
        in_specs=(
            P("dp", "seq", None),
            P("dp", "seq", None),
            P(),
            P(("dp", "seq"), "head"),
            P(("dp", "seq"), "head"),
            P(("dp", "seq"), "head"),
            P(("dp", "seq"), "head"),
            P(("dp", "seq"), "head"),
            P(("dp", "seq"), "head"),
            P(("dp", "seq"), "head"),
            P(("dp", "seq"), "head"),
            P(("dp", "seq"), "head"),
            P(("dp", "seq"), "head"),
            P(),
            P(),
            P(),
            P(),
            P(),
        ),
        out_specs=(
            P("dp", ("seq", "head"), None),
            P("dp", ("seq", "head"), None),
            P(("dp", "seq"), "head"),
            P(("dp", "seq"), "head"),
            P(("dp", "seq"), "head"),
            P(("dp", "seq"), "head"),
            P(("dp", "seq"), "head"),
            P(("dp", "seq"), "head"),
            P(("dp", "seq"), "head"),
            P(("dp", "seq"), "head"),
            P(("dp", "seq"), "head"),
            P(("dp", "seq"), "head"),
            P(),
            P(),
            P(),
            P(),
            P(),
        ),
        check_vma=False,
    )
```

```python
import functools

import jax
import jax.numpy as jnp
from jax import lax
from jax.experimental import pallas as pl
from jax.experimental.pallas import tpu as pltpu
from jax.sharding import PartitionSpec as P

BLOCK = 64
epsilon = 1e-06
highest = lax.Precision.HIGHEST
f32 = jnp.float32


def mm(left, right, a=1, b=0):
    return lax.dot_general(
        left, right, (((a,), (b,)), ((), ())), precision=highest, preferred_element_type=f32
    )


def mm_nt(left, right):
    return mm(left, right, 1, 1)


def mm_tn(left, right):
    return mm(left, right, 0, 0)


def each(f, *lists):
    return [f(*items) for items in zip(*lists)]


def square_masks():
    rows = lax.broadcasted_iota(jnp.int32, (BLOCK, BLOCK), 0)
    cols = lax.broadcasted_iota(jnp.int32, (BLOCK, BLOCK), 1)
    return rows >= cols, rows > cols, (rows == cols).astype(f32)


def row_factor(values):
    return lax.rsqrt(jnp.sum(values * values, axis=-1, keepdims=True) + epsilon)


def split(values, count):
    return [values[i * BLOCK : (i + 1) * BLOCK] for i in range(count)]


def decays(col_ref, row_ref, count):
    lower, strict, identity = square_masks()
    out = []
    for i in range(count):
        c_col, b_col = col_ref[0, i, :, 0:1], col_ref[0, i, :, 1:2]
        c_row, b_row = row_ref[0, i, 0:1, :], row_ref[0, i, 1:2, :]
        fade = jnp.where(lower, jnp.exp(jnp.where(lower, c_col - c_row, 0.0)), 0.0)
        last = c_col[BLOCK - 1 : BLOCK, :]
        out.append((fade, fade * b_row, jnp.exp(c_col), jnp.exp(last - c_col), b_col, jnp.exp(last)))
    return [list(items) for items in zip(*out)]


def chains(counts):
    start, out = 0, []
    for count in counts:
        out.append(range(start, start + count))
        start += count
    return out


def solve_kernel(counts, q_ref, k_ref, v_ref, col_ref, row_ref, solver_ref, scores_ref, w_ref, vt_ref, qt_ref, m_ref, b_ref, mseg_ref, bseg_ref):
    count = sum(counts)
    lower, strict, identity = square_masks()
    query = q_ref[...]
    query = split(query * row_factor(query), count)
    key = k_ref[...]
    key = split(key * row_factor(key), count)
    value = split(v_ref[...], count)
    fade, ratio, growth, remain, beta, end = decays(col_ref, row_ref, count)
    power = each(lambda k, p: jnp.where(strict, -mm_nt(k, k) * p, 0.0), key, ratio)
    solver = [identity + p for p in power]
    for _ in range((BLOCK - 1).bit_length() - 1):
        power = each(lambda p: mm(p, p), power)
        solver = each(lambda s, p: s + mm(s, p), solver, power)
    scores = each(lambda q, k, p: mm_nt(q, k) * p, query, key, ratio)
    w = each(lambda s, g, k: mm(s, g * k), solver, growth, key)
    vt = each(mm, solver, value)
    qt = each(lambda g, q, a, x: g * q - mm(a, x), growth, query, scores, w)
    weighted = each(lambda k, r, b: k * (r * b), key, remain, beta)
    size = query[0].shape[1]
    wide = (
        lax.broadcasted_iota(jnp.int32, (size, size), 0)
        == lax.broadcasted_iota(jnp.int32, (size, size), 1)
    ).astype(f32)
    m = each(lambda e, k, x: e * wide - mm_tn(k, x), end, weighted, w)
    b = each(mm_tn, weighted, vt)
    for i in range(count):
        solver_ref[0, i] = solver[i]
        scores_ref[0, i] = scores[i]
        w_ref[0, i] = w[i]
        vt_ref[0, i] = vt[i]
        qt_ref[0, i] = qt[i]
        m_ref[0, i] = m[i]
        b_ref[0, i] = b[i]
    for j, chain in enumerate(chains(counts)):
        mseg_ref[0, j] = m[chain[0]]
        bseg_ref[0, j] = b[chain[0]]
        for i in chain[1:]:
            bseg_ref[0, j] = mm(m_ref[0, i], bseg_ref[0, j]) + b_ref[0, i]
            mseg_ref[0, j] = mm(m_ref[0, i], mseg_ref[0, j])


def output_kernel(counts, state_ref, m_ref, b_ref, qt_ref, scores_ref, vt_ref, gate_ref, gain_ref, states_ref, out_ref, gated_ref):
    count = sum(counts)
    states = [None] * count
    for j, chain in enumerate(chains(counts)):
        state = state_ref[0, j]
        for i in chain:
            states[i] = state
            states_ref[0, i] = state
            if i != chain[-1]:
                state = mm(m_ref[0, i], state) + b_ref[0, i]
    gain = gain_ref[...]
    outs = [mm(qt_ref[0, i], states[i]) + mm(scores_ref[0, i], vt_ref[0, i]) for i in range(count)]
    for i in range(count):
        rows = slice(i * BLOCK, (i + 1) * BLOCK)
        out = outs[i]
        gate = gate_ref[rows, :]
        scale = lax.rsqrt(jnp.mean(out * out, axis=-1, keepdims=True) + epsilon)
        out_ref[rows, :] = out
        gated_ref[rows, :] = (out * scale * gain * (gate * jax.nn.sigmoid(gate))).astype(jnp.bfloat16)


def output_grad_kernel(counts, grad_ref, gate_ref, out_ref, gain_ref, qt_ref, m_ref, out_grad_ref, gate_grad_ref, gain_grad_ref, d_ref, dseg_ref):
    count = sum(counts)
    gain = gain_ref[...]
    gain_grad = jnp.zeros_like(gain)
    grads = []
    for i in range(count):
        rows = slice(i * BLOCK, (i + 1) * BLOCK)
        grad, gate, out = grad_ref[rows, :], gate_ref[rows, :], out_ref[rows, :]
        scale = lax.rsqrt(jnp.mean(out * out, axis=-1, keepdims=True) + epsilon)
        unit = out * scale
        sig = jax.nn.sigmoid(gate)
        normed_grad = grad * (gate * sig)
        gate_grad_ref[rows, :] = (grad * (unit * gain) * (sig * (1.0 + gate * (1.0 - sig)))).astype(jnp.bfloat16)
        gain_grad = gain_grad + jnp.sum(normed_grad * unit, axis=0, keepdims=True)
        inner = normed_grad * gain
        out_grad = scale * (inner - unit * jnp.mean(unit * inner, axis=-1, keepdims=True))
        out_grad_ref[rows, :] = out_grad
        grads.append(out_grad)
    gain_grad_ref[0] = gain_grad
    d = [mm_tn(qt_ref[0, i], grads[i]) for i in range(count)]
    for i in range(count):
        d_ref[0, i] = d[i]
    for j, chain in enumerate(chains(counts)):
        dseg_ref[0, j] = d[chain[-1]]
        for i in list(chain)[-2::-1]:
            dseg_ref[0, j] = mm_tn(m_ref[0, i], dseg_ref[0, j]) + d_ref[0, i]


def unit_back(raw, grad):
    factor = row_factor(raw)
    unit = raw * factor
    return factor * (grad - unit * jnp.sum(unit * grad, axis=-1, keepdims=True))


def grads_kernel(counts, q_ref, k_ref, col_ref, row_ref, solver_ref, scores_ref, w_ref, vt_ref, m_ref, d_ref, states_ref, out_grad_ref, gate_ref, later_ref, slim_ref, joint_ref, col_grad_ref, row_grad_ref):
    count = sum(counts)
    span = range(count)
    lower, strict, identity = square_masks()
    raw_q, raw_k = split(q_ref[...], count), split(k_ref[...], count)
    query = [x * row_factor(x) for x in raw_q]
    key = [x * row_factor(x) for x in raw_k]
    fade, ratio, growth, remain, beta, end = decays(col_ref, row_ref, count)
    out_grad = split(out_grad_ref[...], count)
    later = [None] * count
    for j, chain in enumerate(chains(counts)):
        state = later_ref[0, j]
        for i in list(chain)[::-1]:
            later[i] = state
            if i != chain[0]:
                state = mm_tn(m_ref[0, i], state) + d_ref[0, i]
    states = [states_ref[0, i] for i in span]
    update = [vt_ref[0, i] - mm(w_ref[0, i], states[i]) for i in span]
    update_grad = [
        mm_tn(scores_ref[0, i], out_grad[i]) + mm(key[i] * (remain[i] * beta[i]), later[i]) for i in span
    ]
    solved = [mm_tn(solver_ref[0, i], update_grad[i]) for i in span]
    scores_grad = each(mm_nt, out_grad, update)
    inner_grad = each(lambda y, u: jnp.where(strict, -mm_nt(y, u), 0.0), solved, update)
    query_dot = each(mm_nt, query, key)
    keys_dot = each(mm_nt, key, key)
    from_out = each(mm_nt, out_grad, states)
    from_solved = each(mm_nt, solved, states)
    from_update = each(mm_nt, update, later)
    weighted_scores = each(lambda p, x: p * x, ratio, scores_grad)
    weighted_inner = each(lambda p, x: p * x, ratio, inner_grad)
    q_grad = [growth[i] * from_out[i] + mm(weighted_scores[i], key[i]) for i in span]
    k_grad = [
        mm_tn(weighted_scores[i], query[i])
        + (remain[i] * beta[i]) * from_update[i]
        - growth[i] * from_solved[i]
        + mm(weighted_inner[i], key[i])
        + mm_tn(weighted_inner[i], key[i])
        for i in span
    ]
    last_row = (lax.broadcasted_iota(jnp.int32, (BLOCK, 1), 0) == BLOCK - 1).astype(f32)
    for i in span:
        rows = slice(i * BLOCK, (i + 1) * BLOCK)
        start = 0
        for grad in (unit_back(raw_q[i], q_grad[i]), unit_back(raw_k[i], k_grad[i]), solved[i]):
            place = slice(start, start + grad.shape[1])
            start += grad.shape[1]
            slim_ref[rows, place] = grad.astype(jnp.bfloat16)
            joint_ref[rows, place] = grad.astype(jnp.bfloat16)
        joint_ref[rows, start:] = gate_ref[rows, :]
        faded = fade[i] * (scores_grad[i] * query_dot[i] + inner_grad[i] * keys_dot[i])
        b_row = row_ref[0, i, 1:2, :]
        growth_grad = jnp.sum(query[i] * from_out[i] - key[i] * from_solved[i], axis=-1, keepdims=True)
        weight_grad = jnp.sum(key[i] * from_update[i], axis=-1, keepdims=True)
        pulled = remain[i] * beta[i] * weight_grad
        tail = jnp.sum(pulled, axis=0, keepdims=True) + end[i] * jnp.sum(
            jnp.sum(later[i] * states[i], axis=-1, keepdims=True), axis=0, keepdims=True
        )
        c_grad = jnp.sum(faded * b_row, axis=-1, keepdims=True) + growth[i] * growth_grad - pulled + last_row * tail
        col_grad_ref[0, i, :, 0:1] = c_grad
        col_grad_ref[0, i, :, 1:2] = remain[i] * weight_grad
        row_grad_ref[0, i] = jnp.sum(faded, axis=0, keepdims=True)


def whole(shape):
    return pl.BlockSpec((1,) + tuple(shape[1:]), lambda j: (j,) + (0,) * (len(shape) - 1))


def columns(rows, width, first=0, step=1):
    return pl.BlockSpec((rows, width), lambda j: (0, step * j + first))


def shaped(shape, dtype=f32):
    return jax.ShapeDtypeStruct(shape, dtype)


def call(kernel, counts, heads, inputs, outputs, flops):
    moved = sum(x.size * x.dtype.itemsize for x, _ in inputs) + sum(
        x.size * x.dtype.itemsize for x, _ in outputs
    )
    return pl.pallas_call(
        functools.partial(kernel, counts),
        grid=(heads,),
        in_specs=[s for _, s in inputs],
        out_specs=[s for _, s in outputs],
        out_shape=[x for x, _ in outputs],
        compiler_params=pltpu.CompilerParams(vmem_limit_bytes=48 << 20),
        cost_estimate=pl.CostEstimate(flops=flops, bytes_accessed=moved, transcendentals=0),
    )(*[x for x, _ in inputs])


def per_head(heads, *shape, dtype=f32):
    s = (heads,) + shape
    return shaped(s, dtype), whole(s)


def flat(array, width, first=0, step=1):
    return array, columns(array.shape[0], width, first, step)


def stacked(array):
    return array, whole(array.shape)


def solve(counts, heads, proj, col, row):
    n, dk, dv = sum(counts), 128, 256
    return call(
        solve_kernel, counts, heads,
        [flat(proj, dk, 0, 4), flat(proj, dk, 1, 4), flat(proj, dv, 1, 2), stacked(col), stacked(row)],
        [per_head(heads, n, BLOCK, BLOCK), per_head(heads, n, BLOCK, BLOCK), per_head(heads, n, BLOCK, dk),
         per_head(heads, n, BLOCK, dv), per_head(heads, n, BLOCK, dk), per_head(heads, n, dk, dk),
         per_head(heads, n, dk, dv), per_head(heads, len(counts), dk, dk), per_head(heads, len(counts), dk, dv)],
        heads * n * 100_000_000,
    )


def outputs_of(counts, heads, state, m, b, qt, scores, vt, gate_pre, gain):
    n, dk, dv = sum(counts), 128, 256
    rows = gate_pre.shape[0]
    cols = columns(rows, dv)
    return call(
        output_kernel, counts, heads,
        [stacked(state), stacked(m), stacked(b), stacked(qt), stacked(scores), stacked(vt), flat(gate_pre, dv),
         (gain, pl.BlockSpec((1, dv), lambda j: (0, 0)))],
        [per_head(heads, n, dk, dv), (shaped((rows, heads * dv)), cols), (shaped((rows, heads * dv), jnp.bfloat16), cols)],
        heads * n * 50_000_000,
    )


def output_grads_of(counts, heads, grad, gate_pre, outs, gain, qt, m):
    n, dk, dv = sum(counts), 128, 256
    rows = gate_pre.shape[0]
    cols = columns(rows, dv)
    return call(
        output_grad_kernel, counts, heads,
        [flat(grad, dv), flat(gate_pre, dv), flat(outs, dv), (gain, pl.BlockSpec((1, dv), lambda j: (0, 0))), stacked(qt), stacked(m)],
        [(shaped((rows, heads * dv)), cols), (shaped((rows, heads * dv), jnp.bfloat16), cols),
         per_head(heads, 1, dv), per_head(heads, n, dk, dv), per_head(heads, len(counts), dk, dv)],
        heads * n * 50_000_000,
    )


def input_grads_of(counts, heads, proj, col, row, solver, scores, w, vt, m, d, states, out_grad, gate_grad, later):
    n, dk, dv = sum(counts), 128, 256
    rows = proj.shape[0]
    return call(
        grads_kernel, counts, heads,
        [flat(proj, dk, 0, 4), flat(proj, dk, 1, 4), stacked(col), stacked(row), stacked(solver), stacked(scores), stacked(w),
         stacked(vt), stacked(m), stacked(d), stacked(states), flat(out_grad, dv), flat(gate_grad, dv), stacked(later)],
        [(shaped((rows, heads * (2 * dk + dv)), jnp.bfloat16), columns(rows, 2 * dk + dv)),
         (shaped((rows, heads * (2 * dk + 2 * dv)), jnp.bfloat16), columns(rows, 2 * dk + 2 * dv)),
         per_head(heads, n, BLOCK, 2), per_head(heads, n, 1, BLOCK)],
        heads * n * 150_000_000,
    )


def feed_kernel(stage_ref, x_ref, k_ref, xs_ref, ks_ref, w1_ref, w3_ref, w2_ref, t1_ref, t3_ref, t2_ref, sums_ref, main_ref, main_other_ref, tail_ref, tail_other_ref, active_s, gate_s, up_s):
    step, chunk = pl.program_id(0), pl.program_id(1)
    own, width = sums_ref.shape[0], sums_ref.shape[1] // 2
    near, piece = x_ref.shape[1] // own, x_ref.shape[2]
    stage = stage_ref[0]
    here = pl.ds(pl.multiple_of(lax.rem(stage, near) * own, own), own)

    @pl.when((step == 0) & (chunk == 0))
    def _():
        sums_ref[...] = jnp.zeros_like(sums_ref)

    def work(w1, w3, w2, out_refs):
        wide = w1.shape[1]
        gate, up, grad = (
            sum(
                jnp.dot(rows[i], w[i * piece : (i + 1) * piece, :], preferred_element_type=f32)
                for i in range(rows.shape[0])
            )
            for rows, w in ((x_ref, w1), (x_ref, w3), (k_ref, w2))
        )
        sig = jax.nn.sigmoid(gate)
        silu = gate * sig
        active = (silu * up).astype(jnp.bfloat16)
        gate_grad = (grad * up * (sig * (1.0 + gate * (1.0 - sig)))).astype(jnp.bfloat16)
        up_grad = (grad * silu).astype(jnp.bfloat16)
        active_s[:, :wide] = active
        gate_s[:, :wide] = gate_grad
        up_s[:, :wide] = up_grad

        @pl.when(chunk == stage // near)
        def _():
            sums_ref[:, width:] += contract_cols(active_s[here, :wide], w2[...])
            sums_ref[:, :width] += contract_cols(gate_s[here, :wide], w1[...])
            sums_ref[:, :width] += contract_cols(up_s[here, :wide], w3[...])

        parts = (
            contract_rows(gate_grad, xs_ref[...]),
            contract_rows(up_grad, xs_ref[...]),
            contract_rows(active, ks_ref[...]),
        )
        for i, p in enumerate(parts):
            place = slice(i * wide, (i + 1) * wide)
            quota = p.shape[1] // 2

            @pl.when(chunk == 0)
            def _():
                out_refs[0][place, :] = p[:, :quota]
                out_refs[1][place, :] = p[:, quota:]

            @pl.when(chunk > 0)
            def _():
                out_refs[0][place, :] += p[:, :quota]
                out_refs[1][place, :] += p[:, quota:]

    work(w1_ref, w3_ref, w2_ref, (main_ref, main_other_ref))

    @pl.when(step == pl.num_programs(0) - 1)
    def _():
        work(t1_ref, t3_ref, t2_ref, (tail_ref, tail_other_ref))


def feed_forward(stage, rows, grads, row_cols, grad_cols, weights, own):
    pieces, positions, piece = rows.shape
    width = pieces * piece
    picked = row_cols.shape[1]
    tile, rest = 256, 128
    steps = (weights.shape[1] - 3 * rest) // (3 * tile)
    chunk = min(positions, 4 * own)
    first_tail = 3 * steps * tile // rest
    grid = (steps, positions // chunk)
    tokens = pl.BlockSpec((pieces, chunk, piece), lambda i, t, s: (0, t, 0))
    columns_of = pl.BlockSpec((chunk, picked), lambda i, t, s: (t, 0))

    def main_of(n):
        return pl.BlockSpec((width, tile), lambda i, t, s: (0, n * steps + i))

    def tail_of(n):
        return pl.BlockSpec((width, rest), lambda i, t, s: (0, first_tail + n))

    def fixed(*shape):
        return pl.BlockSpec(shape, lambda i, t, s: (0, 0))

    flops = 2 * positions * width * weights.shape[1] + 2 * own * width * weights.shape[1] + 2 * positions * picked * weights.shape[1]
    return pl.pallas_call(
        feed_kernel,
        grid_spec=pltpu.PrefetchScalarGridSpec(
            num_scalar_prefetch=1,
            grid=grid,
            in_specs=[tokens, tokens, columns_of, columns_of, main_of(0), main_of(1), main_of(2), tail_of(0), tail_of(1), tail_of(2)],
            out_specs=[
                fixed(own, 2 * width),
                pl.BlockSpec((3 * tile, picked // 2), lambda i, t, s: (i, 0)),
                pl.BlockSpec((3 * tile, picked // 2), lambda i, t, s: (i, 0)),
                fixed(3 * rest, picked // 2),
                fixed(3 * rest, picked // 2),
            ],
            scratch_shapes=[pltpu.VMEM((chunk, tile), jnp.bfloat16)] * 3,
        ),
        out_shape=[
            shaped((own, 2 * width)),
            shaped((3 * tile * steps, picked // 2)),
            shaped((3 * tile * steps, picked // 2)),
            shaped((3 * rest, picked // 2)),
            shaped((3 * rest, picked // 2)),
        ],
        compiler_params=pltpu.CompilerParams(
            dimension_semantics=("arbitrary", "arbitrary"), vmem_limit_bytes=56 << 20
        ),
        cost_estimate=pl.CostEstimate(
            flops=flops, bytes_accessed=2 * weights.size + 8 * positions * width, transcendentals=0
        ),
    )(stage, rows, grads, row_cols, grad_cols, weights, weights, weights, weights, weights, weights)


def projection_kernel(heads, cols_ref, joint_ref, q_ref, k_ref, v_ref, g_ref):
    joined = jnp.dot(cols_ref[...], joint_ref[...], preferred_element_type=f32)
    start = 0
    for j in range(heads):
        for ref in (q_ref, k_ref, v_ref, g_ref):
            size = ref.shape[1] // heads
            ref[:, j * size : (j + 1) * size] = joined[:, start : start + size]
            start += size


def projection_grads(cols, joint_all, heads, sizes):
    quota, positions = cols.shape
    wide = joint_all.shape[1]
    return pl.pallas_call(
        functools.partial(projection_kernel, heads),
        grid=(2,),
        in_specs=[
            pl.BlockSpec((quota, positions), lambda c: (0, 0)),
            pl.BlockSpec((positions, wide), lambda c: (c, 0)),
        ],
        out_specs=[pl.BlockSpec((quota, n), lambda c: (0, c)) for n in sizes],
        out_shape=[shaped((quota, 2 * n)) for n in sizes],
        compiler_params=pltpu.CompilerParams(vmem_limit_bytes=56 << 20),
        cost_estimate=pl.CostEstimate(
            flops=4 * quota * positions * wide, bytes_accessed=2 * joint_all.size, transcendentals=0
        ),
    )(cols, joint_all)


QUARTERS = 4


def swap(array):
    return lax.ppermute(array, "dp", [(0, 1), (1, 0)])


def relay(mats, offsets, forward):
    size = lax.axis_size("seq")
    entering = jnp.zeros_like(offsets)
    leaving = offsets
    for step in range(size - 1):
        route = [(step, step + 1)] if forward else [(size - 1 - step, size - 2 - step)]
        got = jnp.stack([lax.ppermute(head, "seq", route) for head in leaving])
        entering = entering + got
        if step < size - 2:
            leaving = jnp.matmul(mats, got, precision=highest) + offsets
    return entering, leaving


def together(*arrays):
    return lax.optimization_barrier(arrays)


def everyone(part):
    return lax.all_gather(part, ("dp", "seq"), axis=0, tiled=True)


def share(rows):
    wide = jnp.broadcast_to(rows[None], (lax.axis_size("head"),) + rows.shape)
    return lax.all_to_all(wide, "head", split_axis=0, concat_axis=0, tiled=True)


def add_parts(parts):
    got = lax.all_to_all(parts.astype(jnp.bfloat16), "head", split_axis=0, concat_axis=0, tiled=True)
    return jnp.sum(got.astype(f32), axis=0)


def contract_rows(left, right):
    return lax.dot_general(left, right, (((0,), (0,)), ((), ())), preferred_element_type=f32)


def contract_cols(left, right):
    return lax.dot_general(left, right, (((1,), (1,)), ((), ())), preferred_element_type=f32)


def product(left, right):
    return jnp.dot(left, right, preferred_element_type=f32)


def rms_scale(values, gain):
    return values * lax.rsqrt(jnp.mean(values * values, axis=-1, keepdims=True) + epsilon) * gain


def swiglu(gate_in, up_in):
    return jax.nn.silu(gate_in) * up_in


def on_device(
    activations,
    cotangent,
    lengths,
    query_weight,
    key_weight,
    value_weight,
    gate_weight,
    alpha_weight,
    beta_weight,
    out_weight,
    swiglu_gate,
    swiglu_value,
    swiglu_down,
    mixer_gain,
    feed_gain,
    head_gain,
    decay_rate,
    beta_bias,
):
    bf16 = jnp.bfloat16
    core, stage, group = lax.axis_index("dp"), lax.axis_index("seq"), lax.axis_index("head")
    stages, groups = lax.axis_size("seq"), lax.axis_size("head")
    width = activations.shape[2]
    rows0 = activations.shape[1]
    rows1 = rows0 // QUARTERS
    own0, own1 = rows0 // (2 * groups), rows1 // (2 * groups)
    own = own0 + own1
    quota = width // (2 * stages)
    heads = alpha_weight.shape[1] // 2
    counts = (rows0 // BLOCK, rows1 // BLOCK)
    assert groups == QUARTERS and stages % QUARTERS == 0 and rows1 % BLOCK == 0
    first = core == 0

    def part(array, size, axis, offset=0):
        return lax.dynamic_slice_in_dim(array, offset + core * size, size, axis)

    dk, dv = query_weight.shape[1] // 2, value_weight.shape[1] // 2
    slim = 2 * dk + dv
    mixer_cols = []
    for c in range(2):
        for j in range(c * heads, (c + 1) * heads):
            mixer_cols += [
                query_weight[:, j * dk // heads : (j + 1) * dk // heads],
                key_weight[:, j * dk // heads : (j + 1) * dk // heads],
                value_weight[:, j * dv // heads : (j + 1) * dv // heads],
            ]
    mixer_cols += [alpha_weight, beta_weight]
    mixer_full = everyone(jnp.concatenate(mixer_cols, axis=1).astype(bf16))
    gates_full = everyone(jnp.concatenate([gate_weight, out_weight], axis=1).astype(bf16))
    def chip_rows(rows):
        arrived = jnp.zeros((rows1, width), bf16)
        for b in range(QUARTERS):
            route = [(stages + a, stages + QUARTERS * a + b) for a in range(stages // QUARTERS)]
            arrived = arrived + lax.ppermute(rows[b * rows1 : (b + 1) * rows1], ("dp", "seq"), route)
        near0 = lax.ppermute(rows, "dp", [(0, 1)])
        near1 = lax.ppermute(arrived, "dp", [(1, 0)])
        return jnp.concatenate([jnp.where(first, rows, near0), jnp.where(first, near1, arrived)], axis=0)

    inputs = chip_rows(activations[0])
    inputs, late = together(inputs, cotangent[0])

    inputs = inputs.astype(f32)
    spots0 = stage * rows0 + lax.broadcasted_iota(jnp.int32, (rows0, 1), 0)
    spots1 = stage * rows1 + lax.broadcasted_iota(jnp.int32, (rows1, 1), 0)
    mask = jnp.concatenate([spots0 < lengths[0], spots1 < lengths[1]], axis=0).astype(f32)
    masked = (chip_rows(late).astype(f32) * mask).astype(bf16)

    hidden_units = swiglu_gate.shape[1]
    even = hidden_units // 256 * 256
    odd = hidden_units - even
    assert 0 < odd <= 128
    three = together(swiglu_gate, swiglu_value, swiglu_down, masked)[:3]
    spare = ((0, 0), (0, 128 - odd))
    feed_cols = [w[:, :even] for w in three] + [jnp.pad(w[:, even:], spare) for w in three]
    feed_full = everyone(jnp.concatenate(feed_cols, axis=1).astype(bf16))

    def by_owner(rows):
        wide = rows.shape[1]
        r0 = rows[:rows0].reshape(groups, 2, own0, wide)
        r1 = rows[rows0:].reshape(groups, 2, own1, wide)
        return jnp.concatenate([r0, r1], axis=2).swapaxes(0, 1)

    def in_time(owned):
        wide = owned.shape[3]
        turned = owned.swapaxes(0, 1)
        return jnp.concatenate(
            [turned[:, :, :own0].reshape(rows0, wide), turned[:, :, own0:].reshape(rows1, wide)], axis=0
        )

    def of_core(owned, which):
        return lax.dynamic_index_in_dim(owned, which, 0, keepdims=False)

    def of_group(rows):
        return lax.dynamic_index_in_dim(rows, group, 0, keepdims=False)

    def add_rows(partial):
        owned = by_owner(partial)
        return add_parts(of_core(owned, core) + swap(of_core(owned, 1 - core)))

    def meet_columns(rows):
        return lax.all_to_all(rows, ("dp", "seq"), split_axis=1, concat_axis=0, tiled=True)

    def owned_columns(met):
        got = share(met).reshape(groups, 2, stages, own, quota).transpose(2, 0, 1, 3, 4)
        return jnp.concatenate(
            [got[:, :, :, :own0].reshape(stages, rows0, quota), got[:, :, :, own0:].reshape(stages, rows1, quota)], axis=1
        ).reshape(stages * (rows0 + rows1), quota)

    def across_stages(rows):
        wide = jnp.broadcast_to(rows[None], (stages,) + rows.shape)
        met = lax.all_to_all(wide, "seq", split_axis=0, concat_axis=0, tiled=True)
        return met.reshape(stages * rows.shape[0], rows.shape[1])

    def own_columns(rows):
        pieces, positions, piece = rows.shape
        both = []
        for which in (core, 1 - core):
            start = (which * stages + stage) * quota
            both.append(lax.dynamic_slice(rows, (start // piece, 0, start % piece), (1, positions, quota))[0])
        return jnp.concatenate(both, axis=1)

    own_rows = of_group(of_core(by_owner(inputs), core))
    own_mask = of_group(of_core(by_owner(mask), core))
    tokens_masked = of_core(by_owner(masked), core)
    own_masked = of_group(tokens_masked).astype(f32)
    quarter = width // groups
    masked_met = across_stages(
        lax.dynamic_slice_in_dim(tokens_masked.reshape(groups * own, width), group * quarter, quarter, 1)
    )

    factor1 = lax.rsqrt(jnp.mean(inputs * inputs, axis=-1, keepdims=True) + epsilon)
    unit1 = inputs * factor1
    normed = rms_scale(inputs, mixer_gain).astype(bf16)
    mixer_full, masked_met = together(mixer_full, masked_met)
    mixer_w = part(mixer_full, slim, 1)
    gate_w = part(gates_full, dv, 1)
    out_w = part(gates_full, dv, 1, 2 * dv)
    rates_w = mixer_full[:, 2 * slim :]
    proj = product(normed, mixer_w)
    small_pre = product(normed, rates_w)
    gate_pre = product(normed, gate_w)
    alpha_pre = part(small_pre, heads, 1)
    beta_pre = part(small_pre, heads, 1, 2 * heads)
    head0 = (2 * group + core) * heads
    rates = lax.dynamic_slice_in_dim(decay_rate, head0, heads)
    biases = lax.dynamic_slice_in_dim(beta_bias, head0, heads)
    blocks = sum(counts)

    def to_blocks(array):
        return array.T.reshape(heads, blocks, BLOCK)

    def from_blocks(array):
        return array.reshape(heads, blocks * BLOCK).T

    soft = jax.nn.softplus(alpha_pre)
    beta = jax.nn.sigmoid(beta_pre + biases)
    beta_b = to_blocks(beta)
    upto = (
        lax.broadcasted_iota(jnp.int32, (BLOCK, BLOCK), 0) <= lax.broadcasted_iota(jnp.int32, (BLOCK, BLOCK), 1)
    ).astype(f32)
    sums = jnp.matmul(to_blocks(-rates * soft), upto, precision=highest)
    col = jnp.stack([sums, beta_b], axis=-1)
    row = jnp.stack([sums, beta_b], axis=-2)
    solver, scores, w, vt, qt, m, b, mseg, bseg = solve(counts, heads, proj, col, row)
    state_in, unused_carry = relay(mseg, bseg, True)
    state_in, masked_all = together(state_in, share(masked_met))
    gain_row = head_gain[None]
    states, outs, gated = outputs_of(counts, heads, state_in, m, b, qt, scores, vt, gate_pre, gain_row)
    mixed = add_rows(contract_cols(gated, out_w))
    hidden = own_rows + mixed

    normed2, norm2_back = jax.vjp(rms_scale, hidden, feed_gain)
    feed_in = share(
        across_stages(lax.all_to_all(normed2.astype(bf16), "head", split_axis=1, concat_axis=0, tiled=True))
    )
    normed_own, unused_rows = together(of_group(of_core(by_owner(normed), core)), feed_in)
    normed_cols = owned_columns(meet_columns(normed_own)).T
    feed_full, normed_cols = together(feed_full, normed_cols)
    sums, main_own, main_other, tail_own, tail_other = feed_forward(
        stage[None], feed_in, masked_all, own_columns(feed_in), own_columns(masked_all), feed_full, groups * own
    )
    sums, main_other, tail_other = together(
        add_parts(sums.reshape(groups, own, 2 * width)), swap(main_other), swap(tail_other)
    )
    normed2_grad, feed = sums[:, :width], sums[:, width:]
    hidden_back, feed_gain_grad = norm2_back(normed2_grad)
    hidden_grad = own_masked + hidden_back
    mixed_own = hidden_grad.astype(bf16)
    mixed_half = share(mixed_own)
    other_half = swap(mixed_half)
    mixed_in = in_time(
        jnp.stack([jnp.where(first, mixed_half, other_half), jnp.where(first, other_half, mixed_half)])
    )

    gated_all = everyone(gated)
    gated_grad = product(mixed_in, out_w)
    mixed_late, unused_rows = together(mixed_own, mixed_in)
    mixed_met = meet_columns(mixed_late)
    gated_grad, gated_all = together(gated_grad, gated_all)
    outs_grad, gate_pre_low, gain_grads, d, dseg = output_grads_of(
        counts, heads, gated_grad, gate_pre, outs, gain_row, qt, m
    )
    dseg, mixed_met = together(dseg, mixed_met)
    later, carry = relay(jnp.swapaxes(mseg, 2, 3), dseg, False)

    half = stages * (rows0 + rows1)
    main_own, main_other, tail_own, tail_other, unused_carry = together(
        main_own, main_other, tail_own, tail_other, carry
    )
    main_own, tail_own = main_own + main_other, tail_own + tail_other

    def feed_grad(n):
        pieces = [main_own[(3 * i + n) * 256 : (3 * i + n + 1) * 256] for i in range(even // 256)]
        return jnp.concatenate(pieces + [tail_own[n * 128 : n * 128 + odd]], axis=0)

    feed_gate_grad, feed_value_grad, down_grad = feed_grad(0), feed_grad(1), feed_grad(2)
    gate_back = contract_cols(gate_pre_low, gate_w)
    later, feed_gate_grad, feed_value_grad, down_grad, gate_back = together(
        later, feed_gate_grad, feed_value_grad, down_grad, gate_back
    )
    slim_low, joint_low, col_grad, row_grad = input_grads_of(
        counts, heads, proj, col, row, solver, scores, w, vt, m, d, states, outs_grad, gate_pre_low, later
    )
    joint_all = everyone(joint_low)
    slim_low, mixed_met = together(slim_low, mixed_met)
    mixed_cols = owned_columns(mixed_met)
    sums_grad = col_grad[..., 0] - row_grad[:, :, 0] * beta_b
    decay_back = from_blocks(jnp.matmul(sums_grad, upto.T, precision=highest))
    beta_back = beta * (1.0 - beta) * from_blocks(col_grad[..., 1] + row_grad[:, :, 0])
    rates_grad = -jnp.sum(soft * decay_back, axis=0)
    biases_grad = jnp.sum(beta_back, axis=0)
    alpha_back = -rates * jax.nn.sigmoid(alpha_pre) * decay_back
    small_low = jnp.concatenate([alpha_back, beta_back], axis=1).astype(bf16)
    blank = jnp.zeros((rows0 + rows1, 4 * heads), bf16)
    spread = lax.dynamic_update_slice(blank, small_low[:, :heads], (0, core * heads))
    spread = lax.dynamic_update_slice(spread, small_low[:, heads:], (0, (2 + core) * heads))
    total = gate_back + contract_cols(slim_low, mixer_w) + contract_cols(spread, rates_w)
    normed_grad = add_rows(total)
    mixer_gain_part = jnp.sum(total * unit1, axis=0)
    normed_grad, small_late, mixer_gain_part = together(normed_grad, small_low, mixer_gain_part)
    outputs_own = (own_mask * (hidden + feed)).astype(bf16)
    out_grad = jnp.concatenate(
        [contract_rows(mixed_cols, gated_all[:half]), contract_rows(mixed_cols, gated_all[half:])], axis=1
    )
    unused_rows, norm1_back = jax.vjp(lambda v: rms_scale(v, mixer_gain), own_rows)
    input_own = (hidden_grad + norm1_back(normed_grad)[0]).astype(bf16)

    small_rows = contract_rows(small_late, normed).reshape(2 * heads, 2 * stages, quota).swapaxes(0, 1)
    total_heads = decay_rate.shape[0]
    none = jnp.zeros((total_heads,), f32)
    vector = jnp.concatenate(
        [
            mixer_gain_part,
            feed_gain_grad,
            jnp.sum(gain_grads, axis=(0, 1)),
            lax.dynamic_update_slice(none, rates_grad, (head0,)),
            lax.dynamic_update_slice(none, biases_grad, (head0,)),
        ]
    )
    mail = jnp.concatenate(
        [
            small_rows.reshape(2 * stages, 2 * heads * quota),
            jnp.broadcast_to(vector[None], (2 * stages, vector.shape[0])),
        ],
        axis=1,
    )
    mail = lax.all_to_all(mail, ("dp", "seq"), split_axis=0, concat_axis=0, tiled=True)
    mail, out_grad = together(mail, out_grad)
    small_rows = jnp.sum(mail[:, : 2 * heads * quota].reshape(2, stages, 2, heads, quota), axis=1)
    alpha_grad = small_rows[:, 0].reshape(2 * heads, quota).T
    beta_grad = small_rows[:, 1].reshape(2 * heads, quota).T
    small = jnp.sum(share(jnp.sum(mail[:, 2 * heads * quota :], axis=0)), axis=0)
    joint_all, out_grad = together(joint_all, out_grad)
    query_grad, key_grad, value_grad, gate_grad = projection_grads(normed_cols, joint_all, heads, (dk, dk, dv, dv))

    edges = [width, 2 * width, 2 * width + head_gain.shape[0], 2 * width + head_gain.shape[0] + total_heads]

    def place(rows):
        r0, r1 = rows[:own0], rows[own0:]
        out0 = jnp.concatenate([r0, lax.ppermute(r0, "dp", [(1, 0)])], axis=0)
        pair = jnp.concatenate([lax.ppermute(r1, "dp", [(0, 1)]), r1], axis=0)
        routes = [
            [
                ((stages + QUARTERS * a + b) * groups + k, (stages + a) * groups + b)
                for a in range(stages // QUARTERS)
                for b in range(QUARTERS)
            ]
            for k in range(groups)
        ]
        out1 = jnp.concatenate([lax.ppermute(pair, ("dp", "seq", "head"), route) for route in routes], axis=0)
        return jnp.where(first, out0, out1)[None]

    placed = place(jnp.concatenate([outputs_own, input_own], axis=1))
    return (
        placed[:, :, :width],
        placed[:, :, width:],
        query_grad,
        key_grad,
        value_grad,
        gate_grad,
        alpha_grad,
        beta_grad,
        out_grad,
        feed_gate_grad.T,
        feed_value_grad.T,
        down_grad.T,
        small[: edges[0]],
        small[edges[0] : edges[1]],
        small[edges[1] : edges[2]],
        small[edges[2] : edges[3]],
        small[edges[3] :],
    )


def solution(mesh):
    return jax.shard_map(
        on_device,
        mesh=mesh,
        in_specs=(
            P("dp", "seq", None),
            P("dp", "seq", None),
            P(),
            P(("dp", "seq"), "head"),
            P(("dp", "seq"), "head"),
            P(("dp", "seq"), "head"),
            P(("dp", "seq"), "head"),
            P(("dp", "seq"), "head"),
            P(("dp", "seq"), "head"),
            P(("dp", "seq"), "head"),
            P(("dp", "seq"), "head"),
            P(("dp", "seq"), "head"),
            P(("dp", "seq"), "head"),
            P(),
            P(),
            P(),
            P(),
            P(),
        ),
        out_specs=(
            P("dp", ("seq", "head"), None),
            P("dp", ("seq", "head"), None),
            P(("dp", "seq"), "head"),
            P(("dp", "seq"), "head"),
            P(("dp", "seq"), "head"),
            P(("dp", "seq"), "head"),
            P(("dp", "seq"), "head"),
            P(("dp", "seq"), "head"),
            P(("dp", "seq"), "head"),
            P(("dp", "seq"), "head"),
            P(("dp", "seq"), "head"),
            P(("dp", "seq"), "head"),
            P(),
            P(),
            P(),
            P(),
            P(),
        ),
        check_vma=False,
    )
```

```python
import functools

import jax
import jax.numpy as jnp
from jax import lax
from jax.experimental import pallas as pl
from jax.experimental.pallas import tpu as pltpu
from jax.sharding import PartitionSpec as P

BLOCK = 64
epsilon = 1e-06
highest = lax.Precision.HIGH
f32 = jnp.float32


def mm(left, right, a=1, b=0):
    return lax.dot_general(
        left, right, (((a,), (b,)), ((), ())), precision=highest, preferred_element_type=f32
    )


def mm_nt(left, right):
    return mm(left, right, 1, 1)


def mm_tn(left, right):
    return mm(left, right, 0, 0)


def each(f, *lists):
    return [f(*items) for items in zip(*lists)]


def square_masks():
    rows = lax.broadcasted_iota(jnp.int32, (BLOCK, BLOCK), 0)
    cols = lax.broadcasted_iota(jnp.int32, (BLOCK, BLOCK), 1)
    return rows >= cols, rows > cols, (rows == cols).astype(f32)


def row_factor(values):
    return lax.rsqrt(jnp.sum(values * values, axis=-1, keepdims=True) + epsilon)


def split(values, count):
    return [values[i * BLOCK : (i + 1) * BLOCK] for i in range(count)]


def decays(col_ref, row_ref, count):
    lower, strict, identity = square_masks()
    out = []
    for i in range(count):
        c_col, b_col = col_ref[0, i, :, 0:1], col_ref[0, i, :, 1:2]
        c_row, b_row = row_ref[0, i, 0:1, :], row_ref[0, i, 1:2, :]
        fade = jnp.where(lower, jnp.exp(jnp.where(lower, c_col - c_row, 0.0)), 0.0)
        last = c_col[BLOCK - 1 : BLOCK, :]
        out.append((fade, fade * b_row, jnp.exp(c_col), jnp.exp(last - c_col), b_col, jnp.exp(last)))
    return [list(items) for items in zip(*out)]


def chains(counts):
    start, out = 0, []
    for count in counts:
        out.append(range(start, start + count))
        start += count
    return out


def solve_kernel(counts, q_ref, k_ref, v_ref, col_ref, row_ref, solver_ref, scores_ref, w_ref, vt_ref, qt_ref, m_ref, b_ref, mseg_ref, bseg_ref):
    count = sum(counts)
    lower, strict, identity = square_masks()
    query = q_ref[...]
    query = split(query * row_factor(query), count)
    key = k_ref[...]
    key = split(key * row_factor(key), count)
    value = split(v_ref[...], count)
    fade, ratio, growth, remain, beta, end = decays(col_ref, row_ref, count)
    power = each(lambda k, p: jnp.where(strict, -mm_nt(k, k) * p, 0.0), key, ratio)
    solver = [identity + p for p in power]
    for _ in range((BLOCK - 1).bit_length() - 1):
        power = each(lambda p: mm(p, p), power)
        solver = each(lambda s, p: s + mm(s, p), solver, power)
    scores = each(lambda q, k, p: mm_nt(q, k) * p, query, key, ratio)
    w = each(lambda s, g, k: mm(s, g * k), solver, growth, key)
    vt = each(mm, solver, value)
    qt = each(lambda g, q, a, x: g * q - mm(a, x), growth, query, scores, w)
    weighted = each(lambda k, r, b: k * (r * b), key, remain, beta)
    size = query[0].shape[1]
    wide = (
        lax.broadcasted_iota(jnp.int32, (size, size), 0)
        == lax.broadcasted_iota(jnp.int32, (size, size), 1)
    ).astype(f32)
    m = each(lambda e, k, x: e * wide - mm_tn(k, x), end, weighted, w)
    b = each(mm_tn, weighted, vt)
    for i in range(count):
        solver_ref[0, i] = solver[i]
        scores_ref[0, i] = scores[i]
        w_ref[0, i] = w[i]
        vt_ref[0, i] = vt[i]
        qt_ref[0, i] = qt[i]
        m_ref[0, i] = m[i]
        b_ref[0, i] = b[i]
    for j, chain in enumerate(chains(counts)):
        mseg_ref[0, j] = m[chain[0]]
        bseg_ref[0, j] = b[chain[0]]
        for i in chain[1:]:
            bseg_ref[0, j] = mm(m_ref[0, i], bseg_ref[0, j]) + b_ref[0, i]
            mseg_ref[0, j] = mm(m_ref[0, i], mseg_ref[0, j])


def output_kernel(counts, state_ref, m_ref, b_ref, qt_ref, scores_ref, vt_ref, gate_ref, gain_ref, states_ref, out_ref, gated_ref):
    count = sum(counts)
    states = [None] * count
    for j, chain in enumerate(chains(counts)):
        state = state_ref[0, j]
        for i in chain:
            states[i] = state
            states_ref[0, i] = state
            if i != chain[-1]:
                state = mm(m_ref[0, i], state) + b_ref[0, i]
    gain = gain_ref[...]
    outs = [mm(qt_ref[0, i], states[i]) + mm(scores_ref[0, i], vt_ref[0, i]) for i in range(count)]
    for i in range(count):
        rows = slice(i * BLOCK, (i + 1) * BLOCK)
        out = outs[i]
        gate = gate_ref[rows, :]
        scale = lax.rsqrt(jnp.mean(out * out, axis=-1, keepdims=True) + epsilon)
        out_ref[rows, :] = out
        gated_ref[rows, :] = (out * scale * gain * (gate * jax.nn.sigmoid(gate))).astype(jnp.bfloat16)


def output_grad_kernel(counts, grad_ref, gate_ref, out_ref, gain_ref, qt_ref, m_ref, out_grad_ref, gate_grad_ref, gain_grad_ref, d_ref, dseg_ref):
    count = sum(counts)
    gain = gain_ref[...]
    gain_grad = jnp.zeros_like(gain)
    grads = []
    for i in range(count):
        rows = slice(i * BLOCK, (i + 1) * BLOCK)
        grad, gate, out = grad_ref[rows, :], gate_ref[rows, :], out_ref[rows, :]
        scale = lax.rsqrt(jnp.mean(out * out, axis=-1, keepdims=True) + epsilon)
        unit = out * scale
        sig = jax.nn.sigmoid(gate)
        normed_grad = grad * (gate * sig)
        gate_grad_ref[rows, :] = (grad * (unit * gain) * (sig * (1.0 + gate * (1.0 - sig)))).astype(jnp.bfloat16)
        gain_grad = gain_grad + jnp.sum(normed_grad * unit, axis=0, keepdims=True)
        inner = normed_grad * gain
        out_grad = scale * (inner - unit * jnp.mean(unit * inner, axis=-1, keepdims=True))
        out_grad_ref[rows, :] = out_grad
        grads.append(out_grad)
    gain_grad_ref[0] = gain_grad
    d = [mm_tn(qt_ref[0, i], grads[i]) for i in range(count)]
    for i in range(count):
        d_ref[0, i] = d[i]
    for j, chain in enumerate(chains(counts)):
        dseg_ref[0, j] = d[chain[-1]]
        for i in list(chain)[-2::-1]:
            dseg_ref[0, j] = mm_tn(m_ref[0, i], dseg_ref[0, j]) + d_ref[0, i]


def unit_back(raw, grad):
    factor = row_factor(raw)
    unit = raw * factor
    return factor * (grad - unit * jnp.sum(unit * grad, axis=-1, keepdims=True))


def grads_kernel(counts, q_ref, k_ref, col_ref, row_ref, solver_ref, scores_ref, w_ref, vt_ref, m_ref, d_ref, states_ref, out_grad_ref, gate_ref, later_ref, slim_ref, joint_ref, col_grad_ref, row_grad_ref):
    count = sum(counts)
    span = range(count)
    lower, strict, identity = square_masks()
    raw_q, raw_k = split(q_ref[...], count), split(k_ref[...], count)
    query = [x * row_factor(x) for x in raw_q]
    key = [x * row_factor(x) for x in raw_k]
    fade, ratio, growth, remain, beta, end = decays(col_ref, row_ref, count)
    out_grad = split(out_grad_ref[...], count)
    later = [None] * count
    for j, chain in enumerate(chains(counts)):
        state = later_ref[0, j]
        for i in list(chain)[::-1]:
            later[i] = state
            if i != chain[0]:
                state = mm_tn(m_ref[0, i], state) + d_ref[0, i]
    states = [states_ref[0, i] for i in span]
    update = [vt_ref[0, i] - mm(w_ref[0, i], states[i]) for i in span]
    update_grad = [
        mm_tn(scores_ref[0, i], out_grad[i]) + mm(key[i] * (remain[i] * beta[i]), later[i]) for i in span
    ]
    solved = [mm_tn(solver_ref[0, i], update_grad[i]) for i in span]
    scores_grad = each(mm_nt, out_grad, update)
    inner_grad = each(lambda y, u: jnp.where(strict, -mm_nt(y, u), 0.0), solved, update)
    query_dot = each(mm_nt, query, key)
    keys_dot = each(mm_nt, key, key)
    from_out = each(mm_nt, out_grad, states)
    from_solved = each(mm_nt, solved, states)
    from_update = each(mm_nt, update, later)
    weighted_scores = each(lambda p, x: p * x, ratio, scores_grad)
    weighted_inner = each(lambda p, x: p * x, ratio, inner_grad)
    q_grad = [growth[i] * from_out[i] + mm(weighted_scores[i], key[i]) for i in span]
    k_grad = [
        mm_tn(weighted_scores[i], query[i])
        + (remain[i] * beta[i]) * from_update[i]
        - growth[i] * from_solved[i]
        + mm(weighted_inner[i], key[i])
        + mm_tn(weighted_inner[i], key[i])
        for i in span
    ]
    last_row = (lax.broadcasted_iota(jnp.int32, (BLOCK, 1), 0) == BLOCK - 1).astype(f32)
    for i in span:
        rows = slice(i * BLOCK, (i + 1) * BLOCK)
        start = 0
        for grad in (unit_back(raw_q[i], q_grad[i]), unit_back(raw_k[i], k_grad[i]), solved[i]):
            place = slice(start, start + grad.shape[1])
            start += grad.shape[1]
            slim_ref[rows, place] = grad.astype(jnp.bfloat16)
            joint_ref[rows, place] = grad.astype(jnp.bfloat16)
        joint_ref[rows, start:] = gate_ref[rows, :]
        faded = fade[i] * (scores_grad[i] * query_dot[i] + inner_grad[i] * keys_dot[i])
        b_row = row_ref[0, i, 1:2, :]
        growth_grad = jnp.sum(query[i] * from_out[i] - key[i] * from_solved[i], axis=-1, keepdims=True)
        weight_grad = jnp.sum(key[i] * from_update[i], axis=-1, keepdims=True)
        pulled = remain[i] * beta[i] * weight_grad
        tail = jnp.sum(pulled, axis=0, keepdims=True) + end[i] * jnp.sum(
            jnp.sum(later[i] * states[i], axis=-1, keepdims=True), axis=0, keepdims=True
        )
        c_grad = jnp.sum(faded * b_row, axis=-1, keepdims=True) + growth[i] * growth_grad - pulled + last_row * tail
        col_grad_ref[0, i, :, 0:1] = c_grad
        col_grad_ref[0, i, :, 1:2] = remain[i] * weight_grad
        row_grad_ref[0, i] = jnp.sum(faded, axis=0, keepdims=True)


def whole(shape):
    return pl.BlockSpec((1,) + tuple(shape[1:]), lambda j: (j,) + (0,) * (len(shape) - 1))


def columns(rows, width, first=0, step=1):
    return pl.BlockSpec((rows, width), lambda j: (0, step * j + first))


def shaped(shape, dtype=f32):
    return jax.ShapeDtypeStruct(shape, dtype)


def call(kernel, counts, heads, inputs, outputs, flops):
    moved = sum(x.size * x.dtype.itemsize for x, _ in inputs) + sum(
        x.size * x.dtype.itemsize for x, _ in outputs
    )
    return pl.pallas_call(
        functools.partial(kernel, counts),
        grid=(heads,),
        in_specs=[s for _, s in inputs],
        out_specs=[s for _, s in outputs],
        out_shape=[x for x, _ in outputs],
        compiler_params=pltpu.CompilerParams(vmem_limit_bytes=48 << 20),
        cost_estimate=pl.CostEstimate(flops=flops, bytes_accessed=moved, transcendentals=0),
    )(*[x for x, _ in inputs])


def per_head(heads, *shape, dtype=f32):
    s = (heads,) + shape
    return shaped(s, dtype), whole(s)


def flat(array, width, first=0, step=1):
    return array, columns(array.shape[0], width, first, step)


def stacked(array):
    return array, whole(array.shape)


def solve(counts, heads, proj, col, row):
    n, dk, dv = sum(counts), 128, 256
    return call(
        solve_kernel, counts, heads,
        [flat(proj, dk, 0, 4), flat(proj, dk, 1, 4), flat(proj, dv, 1, 2), stacked(col), stacked(row)],
        [per_head(heads, n, BLOCK, BLOCK), per_head(heads, n, BLOCK, BLOCK), per_head(heads, n, BLOCK, dk),
         per_head(heads, n, BLOCK, dv), per_head(heads, n, BLOCK, dk), per_head(heads, n, dk, dk),
         per_head(heads, n, dk, dv), per_head(heads, len(counts), dk, dk), per_head(heads, len(counts), dk, dv)],
        heads * n * 100_000_000,
    )


def outputs_of(counts, heads, state, m, b, qt, scores, vt, gate_pre, gain):
    n, dk, dv = sum(counts), 128, 256
    rows = gate_pre.shape[0]
    cols = columns(rows, dv)
    return call(
        output_kernel, counts, heads,
        [stacked(state), stacked(m), stacked(b), stacked(qt), stacked(scores), stacked(vt), flat(gate_pre, dv),
         (gain, pl.BlockSpec((1, dv), lambda j: (0, 0)))],
        [per_head(heads, n, dk, dv), (shaped((rows, heads * dv)), cols), (shaped((rows, heads * dv), jnp.bfloat16), cols)],
        heads * n * 50_000_000,
    )


def output_grads_of(counts, heads, grad, gate_pre, outs, gain, qt, m):
    n, dk, dv = sum(counts), 128, 256
    rows = gate_pre.shape[0]
    cols = columns(rows, dv)
    return call(
        output_grad_kernel, counts, heads,
        [flat(grad, dv), flat(gate_pre, dv), flat(outs, dv), (gain, pl.BlockSpec((1, dv), lambda j: (0, 0))), stacked(qt), stacked(m)],
        [(shaped((rows, heads * dv)), cols), (shaped((rows, heads * dv), jnp.bfloat16), cols),
         per_head(heads, 1, dv), per_head(heads, n, dk, dv), per_head(heads, len(counts), dk, dv)],
        heads * n * 50_000_000,
    )


def input_grads_of(counts, heads, proj, col, row, solver, scores, w, vt, m, d, states, out_grad, gate_grad, later):
    n, dk, dv = sum(counts), 128, 256
    rows = proj.shape[0]
    return call(
        grads_kernel, counts, heads,
        [flat(proj, dk, 0, 4), flat(proj, dk, 1, 4), stacked(col), stacked(row), stacked(solver), stacked(scores), stacked(w),
         stacked(vt), stacked(m), stacked(d), stacked(states), flat(out_grad, dv), flat(gate_grad, dv), stacked(later)],
        [(shaped((rows, heads * (2 * dk + dv)), jnp.bfloat16), columns(rows, 2 * dk + dv)),
         (shaped((rows, heads * (2 * dk + 2 * dv)), jnp.bfloat16), columns(rows, 2 * dk + 2 * dv)),
         per_head(heads, n, BLOCK, 2), per_head(heads, n, 1, BLOCK)],
        heads * n * 150_000_000,
    )


def feed_kernel(stage_ref, x_ref, k_ref, xs_ref, ks_ref, w1_ref, w3_ref, w2_ref, t1_ref, t3_ref, t2_ref, sums_ref, main_ref, main_other_ref, tail_ref, tail_other_ref, active_s, gate_s, up_s):
    step, chunk = pl.program_id(0), pl.program_id(1)
    own, width = sums_ref.shape[0], sums_ref.shape[1] // 2
    near, piece = x_ref.shape[1] // own, x_ref.shape[2]
    stage = stage_ref[0]
    here = pl.ds(pl.multiple_of(lax.rem(stage, near) * own, own), own)

    @pl.when((step == 0) & (chunk == 0))
    def _():
        sums_ref[...] = jnp.zeros_like(sums_ref)

    def work(w1, w3, w2, out_refs):
        wide = w1.shape[1]
        gate, up, grad = (
            sum(
                jnp.dot(rows[i], w[i * piece : (i + 1) * piece, :], preferred_element_type=f32)
                for i in range(rows.shape[0])
            )
            for rows, w in ((x_ref, w1), (x_ref, w3), (k_ref, w2))
        )
        sig = jax.nn.sigmoid(gate)
        silu = gate * sig
        active = (silu * up).astype(jnp.bfloat16)
        gate_grad = (grad * up * (sig * (1.0 + gate * (1.0 - sig)))).astype(jnp.bfloat16)
        up_grad = (grad * silu).astype(jnp.bfloat16)
        active_s[:, :wide] = active
        gate_s[:, :wide] = gate_grad
        up_s[:, :wide] = up_grad

        @pl.when(chunk == stage // near)
        def _():
            sums_ref[:, width:] += contract_cols(active_s[here, :wide], w2[...])
            sums_ref[:, :width] += contract_cols(gate_s[here, :wide], w1[...])
            sums_ref[:, :width] += contract_cols(up_s[here, :wide], w3[...])

        parts = (
            contract_rows(gate_grad, xs_ref[...]),
            contract_rows(up_grad, xs_ref[...]),
            contract_rows(active, ks_ref[...]),
        )
        for i, p in enumerate(parts):
            place = slice(i * wide, (i + 1) * wide)
            quota = p.shape[1] // 2

            @pl.when(chunk == 0)
            def _():
                out_refs[0][place, :] = p[:, :quota]
                out_refs[1][place, :] = p[:, quota:]

            @pl.when(chunk > 0)
            def _():
                out_refs[0][place, :] += p[:, :quota]
                out_refs[1][place, :] += p[:, quota:]

    work(w1_ref, w3_ref, w2_ref, (main_ref, main_other_ref))

    @pl.when(step == pl.num_programs(0) - 1)
    def _():
        work(t1_ref, t3_ref, t2_ref, (tail_ref, tail_other_ref))


def feed_forward(stage, rows, grads, row_cols, grad_cols, weights, own):
    pieces, positions, piece = rows.shape
    width = pieces * piece
    picked = row_cols.shape[1]
    tile, rest = 256, 128
    steps = (weights.shape[1] - 3 * rest) // (3 * tile)
    chunk = min(positions, 4 * own)
    first_tail = 3 * steps * tile // rest
    grid = (steps, positions // chunk)
    tokens = pl.BlockSpec((pieces, chunk, piece), lambda i, t, s: (0, t, 0))
    columns_of = pl.BlockSpec((chunk, picked), lambda i, t, s: (t, 0))

    def main_of(n):
        return pl.BlockSpec((width, tile), lambda i, t, s: (0, n * steps + i))

    def tail_of(n):
        return pl.BlockSpec((width, rest), lambda i, t, s: (0, first_tail + n))

    def fixed(*shape):
        return pl.BlockSpec(shape, lambda i, t, s: (0, 0))

    flops = 2 * positions * width * weights.shape[1] + 2 * own * width * weights.shape[1] + 2 * positions * picked * weights.shape[1]
    return pl.pallas_call(
        feed_kernel,
        grid_spec=pltpu.PrefetchScalarGridSpec(
            num_scalar_prefetch=1,
            grid=grid,
            in_specs=[tokens, tokens, columns_of, columns_of, main_of(0), main_of(1), main_of(2), tail_of(0), tail_of(1), tail_of(2)],
            out_specs=[
                fixed(own, 2 * width),
                pl.BlockSpec((3 * tile, picked // 2), lambda i, t, s: (i, 0)),
                pl.BlockSpec((3 * tile, picked // 2), lambda i, t, s: (i, 0)),
                fixed(3 * rest, picked // 2),
                fixed(3 * rest, picked // 2),
            ],
            scratch_shapes=[pltpu.VMEM((chunk, tile), jnp.bfloat16)] * 3,
        ),
        out_shape=[
            shaped((own, 2 * width)),
            shaped((3 * tile * steps, picked // 2)),
            shaped((3 * tile * steps, picked // 2)),
            shaped((3 * rest, picked // 2)),
            shaped((3 * rest, picked // 2)),
        ],
        compiler_params=pltpu.CompilerParams(
            dimension_semantics=("arbitrary", "arbitrary"), vmem_limit_bytes=56 << 20
        ),
        cost_estimate=pl.CostEstimate(
            flops=flops, bytes_accessed=2 * weights.size + 8 * positions * width, transcendentals=0
        ),
    )(stage, rows, grads, row_cols, grad_cols, weights, weights, weights, weights, weights, weights)


def projection_kernel(heads, cols_ref, joint_ref, q_ref, k_ref, v_ref, g_ref):
    joined = jnp.dot(cols_ref[...], joint_ref[...], preferred_element_type=f32)
    start = 0
    for j in range(heads):
        for ref in (q_ref, k_ref, v_ref, g_ref):
            size = ref.shape[1] // heads
            ref[:, j * size : (j + 1) * size] = joined[:, start : start + size]
            start += size


def projection_grads(cols, joint_all, heads, sizes):
    quota, positions = cols.shape
    wide = joint_all.shape[1]
    return pl.pallas_call(
        functools.partial(projection_kernel, heads),
        grid=(2,),
        in_specs=[
            pl.BlockSpec((quota, positions), lambda c: (0, 0)),
            pl.BlockSpec((positions, wide), lambda c: (c, 0)),
        ],
        out_specs=[pl.BlockSpec((quota, n), lambda c: (0, c)) for n in sizes],
        out_shape=[shaped((quota, 2 * n)) for n in sizes],
        compiler_params=pltpu.CompilerParams(vmem_limit_bytes=56 << 20),
        cost_estimate=pl.CostEstimate(
            flops=4 * quota * positions * wide, bytes_accessed=2 * joint_all.size, transcendentals=0
        ),
    )(cols, joint_all)


QUARTERS = 4


def swap(array):
    return lax.ppermute(array, "dp", [(0, 1), (1, 0)])


def relay(mats, offsets, forward):
    size = lax.axis_size("seq")
    entering = jnp.zeros_like(offsets)
    leaving = offsets
    for step in range(size - 1):
        route = [(step, step + 1)] if forward else [(size - 1 - step, size - 2 - step)]
        got = jnp.stack([lax.ppermute(head, "seq", route) for head in leaving])
        entering = entering + got
        if step < size - 2:
            leaving = jnp.matmul(mats, got, precision=highest) + offsets
    return entering, leaving


def together(*arrays):
    return lax.optimization_barrier(arrays)


def everyone(part):
    return lax.all_gather(part, ("dp", "seq"), axis=0, tiled=True)


def share(rows):
    wide = jnp.broadcast_to(rows[None], (lax.axis_size("head"),) + rows.shape)
    return lax.all_to_all(wide, "head", split_axis=0, concat_axis=0, tiled=True)


def from_others(piece):
    size = lax.axis_size("head")
    return [lax.ppermute(piece(k), "head", [(i, i ^ k) for i in range(size)]) for k in range(1, size)]


def in_group_order(pieces):
    group = lax.axis_index("head")
    stacked = jnp.stack(pieces)
    return jnp.stack(
        [lax.dynamic_index_in_dim(stacked, g ^ group, 0, keepdims=False) for g in range(lax.axis_size("head"))]
    )


def add_by_permutes(vector):
    near, far, across = from_others(lambda k: vector)
    return (vector + near) + (far + across)


def add_parts_by_permutes(parts):
    group = lax.axis_index("head")

    def piece(k):
        return lax.dynamic_index_in_dim(parts, group ^ k, 0, keepdims=False).astype(jnp.bfloat16)

    near, far, across = [got.astype(f32) for got in from_others(piece)]
    return (piece(0).astype(f32) + near) + (far + across)


def add_parts(parts):
    got = lax.all_to_all(parts.astype(jnp.bfloat16), "head", split_axis=0, concat_axis=0, tiled=True)
    return jnp.sum(got.astype(f32), axis=0)


def contract_rows(left, right):
    return lax.dot_general(left, right, (((0,), (0,)), ((), ())), preferred_element_type=f32)


def contract_cols(left, right):
    return lax.dot_general(left, right, (((1,), (1,)), ((), ())), preferred_element_type=f32)


def product(left, right):
    return jnp.dot(left, right, preferred_element_type=f32)


def rms_scale(values, gain):
    return values * lax.rsqrt(jnp.mean(values * values, axis=-1, keepdims=True) + epsilon) * gain


def swiglu(gate_in, up_in):
    return jax.nn.silu(gate_in) * up_in


def on_device(
    activations,
    cotangent,
    lengths,
    query_weight,
    key_weight,
    value_weight,
    gate_weight,
    alpha_weight,
    beta_weight,
    out_weight,
    swiglu_gate,
    swiglu_value,
    swiglu_down,
    mixer_gain,
    feed_gain,
    head_gain,
    decay_rate,
    beta_bias,
):
    bf16 = jnp.bfloat16
    core, stage, group = lax.axis_index("dp"), lax.axis_index("seq"), lax.axis_index("head")
    stages, groups = lax.axis_size("seq"), lax.axis_size("head")
    width = activations.shape[2]
    rows0 = activations.shape[1]
    rows1 = rows0 // QUARTERS
    own0, own1 = rows0 // (2 * groups), rows1 // (2 * groups)
    own = own0 + own1
    quota = width // (2 * stages)
    heads = alpha_weight.shape[1] // 2
    counts = (rows0 // BLOCK, rows1 // BLOCK)
    assert groups == QUARTERS and stages % QUARTERS == 0 and rows1 % BLOCK == 0
    first = core == 0

    def part(array, size, axis, offset=0):
        return lax.dynamic_slice_in_dim(array, offset + core * size, size, axis)

    dk, dv = query_weight.shape[1] // 2, value_weight.shape[1] // 2
    slim = 2 * dk + dv
    mixer_cols = []
    for c in range(2):
        for j in range(c * heads, (c + 1) * heads):
            mixer_cols += [
                query_weight[:, j * dk // heads : (j + 1) * dk // heads],
                key_weight[:, j * dk // heads : (j + 1) * dk // heads],
                value_weight[:, j * dv // heads : (j + 1) * dv // heads],
            ]
    mixer_cols += [alpha_weight, beta_weight]
    mixer_full = everyone(jnp.concatenate(mixer_cols, axis=1).astype(bf16))
    gates_full = everyone(jnp.concatenate([gate_weight, out_weight], axis=1).astype(bf16))
    hidden_units = swiglu_gate.shape[1]
    even = hidden_units // 256 * 256
    odd = hidden_units - even
    assert 0 < odd <= 128
    three = (swiglu_gate, swiglu_value, swiglu_down)
    spare = ((0, 0), (0, 128 - odd))
    feed_full = everyone(
        jnp.concatenate([w[:, :even] for w in three] + [jnp.pad(w[:, even:], spare) for w in three], axis=1).astype(bf16)
    )

    def chip_rows(rows):
        arrived = jnp.zeros((rows1, width), bf16)
        for b in range(QUARTERS):
            route = [(stages + a, stages + QUARTERS * a + b) for a in range(stages // QUARTERS)]
            arrived = arrived + lax.ppermute(rows[b * rows1 : (b + 1) * rows1], ("dp", "seq"), route)
        near0 = lax.ppermute(rows, "dp", [(0, 1)])
        near1 = lax.ppermute(arrived, "dp", [(1, 0)])
        return jnp.concatenate([jnp.where(first, rows, near0), jnp.where(first, near1, arrived)], axis=0)

    inputs = chip_rows(activations[0])
    inputs, late = together(inputs, cotangent[0])
    inputs = inputs.astype(f32)
    spots0 = stage * rows0 + lax.broadcasted_iota(jnp.int32, (rows0, 1), 0)
    spots1 = stage * rows1 + lax.broadcasted_iota(jnp.int32, (rows1, 1), 0)
    mask = jnp.concatenate([spots0 < lengths[0], spots1 < lengths[1]], axis=0).astype(f32)
    masked = (chip_rows(late).astype(f32) * mask).astype(bf16)

    def by_owner(rows):
        wide = rows.shape[1]
        r0 = rows[:rows0].reshape(groups, 2, own0, wide)
        r1 = rows[rows0:].reshape(groups, 2, own1, wide)
        return jnp.concatenate([r0, r1], axis=2).swapaxes(0, 1)

    def in_time(owned):
        wide = owned.shape[3]
        turned = owned.swapaxes(0, 1)
        return jnp.concatenate(
            [turned[:, :, :own0].reshape(rows0, wide), turned[:, :, own0:].reshape(rows1, wide)], axis=0
        )

    def of_core(owned, which):
        return lax.dynamic_index_in_dim(owned, which, 0, keepdims=False)

    def of_group(rows):
        return lax.dynamic_index_in_dim(rows, group, 0, keepdims=False)

    def add_rows(partial):
        owned = by_owner(partial)
        return add_parts_by_permutes(of_core(owned, core) + swap(of_core(owned, 1 - core)))

    def meet_columns(rows):
        return lax.all_to_all(rows, ("dp", "seq"), split_axis=1, concat_axis=0, tiled=True)

    def owned_columns(met, share_rows):
        got = share_rows(met).reshape(groups, 2, stages, own, quota).transpose(2, 0, 1, 3, 4)
        return jnp.concatenate(
            [got[:, :, :, :own0].reshape(stages, rows0, quota), got[:, :, :, own0:].reshape(stages, rows1, quota)], axis=1
        ).reshape(stages * (rows0 + rows1), quota)

    def across_stages(rows):
        wide = jnp.broadcast_to(rows[None], (stages,) + rows.shape)
        met = lax.all_to_all(wide, "seq", split_axis=0, concat_axis=0, tiled=True)
        return met.reshape(stages * rows.shape[0], rows.shape[1])

    def own_columns(rows):
        pieces, positions, piece = rows.shape
        both = []
        for which in (core, 1 - core):
            start = (which * stages + stage) * quota
            both.append(lax.dynamic_slice(rows, (start // piece, 0, start % piece), (1, positions, quota))[0])
        return jnp.concatenate(both, axis=1)

    own_rows = of_group(of_core(by_owner(inputs), core))
    own_mask = of_group(of_core(by_owner(mask), core))
    tokens_masked = of_core(by_owner(masked), core)
    own_masked = of_group(tokens_masked).astype(f32)
    quarter = width // groups
    masked_met = across_stages(
        lax.dynamic_slice_in_dim(tokens_masked.reshape(groups * own, width), group * quarter, quarter, 1)
    )

    factor1 = lax.rsqrt(jnp.mean(inputs * inputs, axis=-1, keepdims=True) + epsilon)
    unit1 = inputs * factor1
    normed = rms_scale(inputs, mixer_gain).astype(bf16)
    normed_cols = owned_columns(meet_columns(of_group(of_core(by_owner(normed), core))), share).T
    mixer_full, masked_met, normed_cols = together(mixer_full, masked_met, normed_cols)
    mixer_w = part(mixer_full, slim, 1)
    gate_w = part(gates_full, dv, 1)
    out_w = part(gates_full, dv, 1, 2 * dv)
    rates_w = mixer_full[:, 2 * slim :]
    proj = product(normed, mixer_w)
    small_pre = product(normed, rates_w)
    gate_pre = product(normed, gate_w)
    alpha_pre = part(small_pre, heads, 1)
    beta_pre = part(small_pre, heads, 1, 2 * heads)
    head0 = (2 * group + core) * heads
    rates = lax.dynamic_slice_in_dim(decay_rate, head0, heads)
    biases = lax.dynamic_slice_in_dim(beta_bias, head0, heads)
    blocks = sum(counts)

    def to_blocks(array):
        return array.T.reshape(heads, blocks, BLOCK)

    def from_blocks(array):
        return array.reshape(heads, blocks * BLOCK).T

    soft = jax.nn.softplus(alpha_pre)
    beta = jax.nn.sigmoid(beta_pre + biases)
    beta_b = to_blocks(beta)
    upto = (
        lax.broadcasted_iota(jnp.int32, (BLOCK, BLOCK), 0) <= lax.broadcasted_iota(jnp.int32, (BLOCK, BLOCK), 1)
    ).astype(f32)
    sums = jnp.matmul(to_blocks(-rates * soft), upto, precision=highest)
    col = jnp.stack([sums, beta_b], axis=-1)
    row = jnp.stack([sums, beta_b], axis=-2)
    solver, scores, w, vt, qt, m, b, mseg, bseg = solve(counts, heads, proj, col, row)
    state_in, unused_carry = relay(mseg, bseg, True)
    state_in, masked_all = together(state_in, share(masked_met))
    gain_row = head_gain[None]
    states, outs, gated = outputs_of(counts, heads, state_in, m, b, qt, scores, vt, gate_pre, gain_row)
    mixed = add_rows(contract_cols(gated, out_w))
    hidden = own_rows + mixed

    normed2, norm2_back = jax.vjp(rms_scale, hidden, feed_gain)
    feed_in = share(
        across_stages(lax.all_to_all(normed2.astype(bf16), "head", split_axis=1, concat_axis=0, tiled=True))
    )
    sums, main_own, main_other, tail_own, tail_other = feed_forward(
        stage[None], feed_in, masked_all, own_columns(feed_in), own_columns(masked_all), feed_full, groups * own
    )
    sums, main_other, tail_other = together(
        add_parts(sums.reshape(groups, own, 2 * width)), swap(main_other), swap(tail_other)
    )
    normed2_grad, feed = sums[:, :width], sums[:, width:]
    hidden_back, feed_gain_grad = norm2_back(normed2_grad)
    hidden_grad = own_masked + hidden_back
    mixed_own = hidden_grad.astype(bf16)
    mixed_half = share(mixed_own)
    other_half = swap(mixed_half)
    mixed_in = in_time(
        jnp.stack([jnp.where(first, mixed_half, other_half), jnp.where(first, other_half, mixed_half)])
    )

    gated_all = everyone(gated)
    gated_grad = product(mixed_in, out_w)
    mixed_late, unused_rows = together(mixed_own, mixed_in)
    mixed_met = meet_columns(mixed_late)
    gated_grad, gated_all = together(gated_grad, gated_all)
    outs_grad, gate_pre_low, gain_grads, d, dseg = output_grads_of(
        counts, heads, gated_grad, gate_pre, outs, gain_row, qt, m
    )
    dseg, mixed_met = together(dseg, mixed_met)
    later, carry = relay(jnp.swapaxes(mseg, 2, 3), dseg, False)

    half = stages * (rows0 + rows1)
    main_own, main_other, tail_own, tail_other, unused_carry = together(
        main_own, main_other, tail_own, tail_other, carry
    )
    main_own, tail_own = main_own + main_other, tail_own + tail_other

    def feed_grad(n):
        pieces = [main_own[(3 * i + n) * 256 : (3 * i + n + 1) * 256] for i in range(even // 256)]
        return jnp.concatenate(pieces + [tail_own[n * 128 : n * 128 + odd]], axis=0)

    feed_gate_grad, feed_value_grad, down_grad = feed_grad(0), feed_grad(1), feed_grad(2)
    gate_back = contract_cols(gate_pre_low, gate_w)
    later, feed_gate_grad, feed_value_grad, down_grad, gate_back = together(
        later, feed_gate_grad, feed_value_grad, down_grad, gate_back
    )
    slim_low, joint_low, col_grad, row_grad = input_grads_of(
        counts, heads, proj, col, row, solver, scores, w, vt, m, d, states, outs_grad, gate_pre_low, later
    )
    joint_all = everyone(joint_low)
    slim_low, mixed_met = together(slim_low, mixed_met)
    mixed_pieces = from_others(lambda k: mixed_met)
    sums_grad = col_grad[..., 0] - row_grad[:, :, 0] * beta_b
    decay_back = from_blocks(jnp.matmul(sums_grad, upto.T, precision=highest))
    beta_back = beta * (1.0 - beta) * from_blocks(col_grad[..., 1] + row_grad[:, :, 0])
    rates_grad = -jnp.sum(soft * decay_back, axis=0)
    biases_grad = jnp.sum(beta_back, axis=0)
    alpha_back = -rates * jax.nn.sigmoid(alpha_pre) * decay_back
    small_low = jnp.concatenate([alpha_back, beta_back], axis=1).astype(bf16)
    blank = jnp.zeros((rows0 + rows1, 4 * heads), bf16)
    spread = lax.dynamic_update_slice(blank, small_low[:, :heads], (0, core * heads))
    spread = lax.dynamic_update_slice(spread, small_low[:, heads:], (0, (2 + core) * heads))
    total = gate_back + contract_cols(slim_low, mixer_w) + contract_cols(spread, rates_w)
    normed_grad = add_rows(total)
    mixer_gain_part = jnp.sum(total * unit1, axis=0)
    normed_grad, small_late, mixer_gain_part, *mixed_pieces = together(
        normed_grad, small_low, mixer_gain_part, mixed_met, *mixed_pieces
    )
    mixed_cols = owned_columns(mixed_met, lambda rows: in_group_order(mixed_pieces))
    outputs_own = (own_mask * (hidden + feed)).astype(bf16)
    out_grad = jnp.concatenate(
        [contract_rows(mixed_cols, gated_all[:half]), contract_rows(mixed_cols, gated_all[half:])], axis=1
    )
    unused_rows, norm1_back = jax.vjp(lambda v: rms_scale(v, mixer_gain), own_rows)
    input_own = (hidden_grad + norm1_back(normed_grad)[0]).astype(bf16)

    small_rows = contract_rows(small_late, normed).reshape(2 * heads, 2 * stages, quota).swapaxes(0, 1)
    total_heads = decay_rate.shape[0]
    none = jnp.zeros((total_heads,), f32)
    vector = jnp.concatenate(
        [
            mixer_gain_part,
            feed_gain_grad,
            jnp.sum(gain_grads, axis=(0, 1)),
            lax.dynamic_update_slice(none, rates_grad, (head0,)),
            lax.dynamic_update_slice(none, biases_grad, (head0,)),
        ]
    )
    mail = jnp.concatenate(
        [
            small_rows.reshape(2 * stages, 2 * heads * quota),
            jnp.broadcast_to(vector[None], (2 * stages, vector.shape[0])),
        ],
        axis=1,
    )
    mail = lax.all_to_all(mail, ("dp", "seq"), split_axis=0, concat_axis=0, tiled=True)
    mail, out_grad = together(mail, out_grad)
    small_rows = jnp.sum(mail[:, : 2 * heads * quota].reshape(2, stages, 2, heads, quota), axis=1)
    alpha_grad = small_rows[:, 0].reshape(2 * heads, quota).T
    beta_grad = small_rows[:, 1].reshape(2 * heads, quota).T
    small = add_by_permutes(jnp.sum(mail[:, 2 * heads * quota :], axis=0))
    joint_all, out_grad = together(joint_all, out_grad)
    query_grad, key_grad, value_grad, gate_grad = projection_grads(normed_cols, joint_all, heads, (dk, dk, dv, dv))

    edges = [width, 2 * width, 2 * width + head_gain.shape[0], 2 * width + head_gain.shape[0] + total_heads]

    def place(rows):
        r0, r1 = rows[:own0], rows[own0:]
        out0 = jnp.concatenate([r0, lax.ppermute(r0, "dp", [(1, 0)])], axis=0)
        pair = jnp.concatenate([lax.ppermute(r1, "dp", [(0, 1)]), r1], axis=0)
        routes = [
            [
                ((stages + QUARTERS * a + b) * groups + k, (stages + a) * groups + b)
                for a in range(stages // QUARTERS)
                for b in range(QUARTERS)
            ]
            for k in range(groups)
        ]
        out1 = jnp.concatenate([lax.ppermute(pair, ("dp", "seq", "head"), route) for route in routes], axis=0)
        return jnp.where(first, out0, out1)[None]

    placed = place(jnp.concatenate([outputs_own, input_own], axis=1))
    return (
        placed[:, :, :width],
        placed[:, :, width:],
        query_grad,
        key_grad,
        value_grad,
        gate_grad,
        alpha_grad,
        beta_grad,
        out_grad,
        feed_gate_grad.T,
        feed_value_grad.T,
        down_grad.T,
        small[: edges[0]],
        small[edges[0] : edges[1]],
        small[edges[1] : edges[2]],
        small[edges[2] : edges[3]],
        small[edges[3] :],
    )


def solution(mesh):
    return jax.shard_map(
        on_device,
        mesh=mesh,
        in_specs=(
            P("dp", "seq", None),
            P("dp", "seq", None),
            P(),
            P(("dp", "seq"), "head"),
            P(("dp", "seq"), "head"),
            P(("dp", "seq"), "head"),
            P(("dp", "seq"), "head"),
            P(("dp", "seq"), "head"),
            P(("dp", "seq"), "head"),
            P(("dp", "seq"), "head"),
            P(("dp", "seq"), "head"),
            P(("dp", "seq"), "head"),
            P(("dp", "seq"), "head"),
            P(),
            P(),
            P(),
            P(),
            P(),
        ),
        out_specs=(
            P("dp", ("seq", "head"), None),
            P("dp", ("seq", "head"), None),
            P(("dp", "seq"), "head"),
            P(("dp", "seq"), "head"),
            P(("dp", "seq"), "head"),
            P(("dp", "seq"), "head"),
            P(("dp", "seq"), "head"),
            P(("dp", "seq"), "head"),
            P(("dp", "seq"), "head"),
            P(("dp", "seq"), "head"),
            P(("dp", "seq"), "head"),
            P(("dp", "seq"), "head"),
            P(),
            P(),
            P(),
            P(),
            P(),
        ),
        check_vma=False,
    )
```

```python
import functools

import jax
import jax.numpy as jnp
from jax import lax
from jax.experimental import pallas as pl
from jax.experimental.pallas import tpu as pltpu
from jax.sharding import PartitionSpec as P

BLOCK = 64
epsilon = 1e-06
highest = lax.Precision.HIGH
f32 = jnp.float32


def mm(left, right, a=1, b=0):
    return lax.dot_general(
        left, right, (((a,), (b,)), ((), ())), precision=highest, preferred_element_type=f32
    )


def mm_nt(left, right):
    return mm(left, right, 1, 1)


def mm_tn(left, right):
    return mm(left, right, 0, 0)


def each(f, *lists):
    return [f(*items) for items in zip(*lists)]


def square_masks():
    rows = lax.broadcasted_iota(jnp.int32, (BLOCK, BLOCK), 0)
    cols = lax.broadcasted_iota(jnp.int32, (BLOCK, BLOCK), 1)
    return rows >= cols, rows > cols, (rows == cols).astype(f32)


def row_factor(values):
    return lax.rsqrt(jnp.sum(values * values, axis=-1, keepdims=True) + epsilon)


def split(values, count):
    return [values[i * BLOCK : (i + 1) * BLOCK] for i in range(count)]


def decays(col_ref, row_ref, count):
    lower, strict, identity = square_masks()
    out = []
    for i in range(count):
        c_col, b_col = col_ref[0, i, :, 0:1], col_ref[0, i, :, 1:2]
        c_row, b_row = row_ref[0, i, 0:1, :], row_ref[0, i, 1:2, :]
        fade = jnp.where(lower, jnp.exp(jnp.where(lower, c_col - c_row, 0.0)), 0.0)
        last = c_col[BLOCK - 1 : BLOCK, :]
        out.append((fade, fade * b_row, jnp.exp(c_col), jnp.exp(last - c_col), b_col, jnp.exp(last)))
    return [list(items) for items in zip(*out)]


def chains(counts):
    start, out = 0, []
    for count in counts:
        out.append(range(start, start + count))
        start += count
    return out


def solve_kernel(counts, q_ref, k_ref, v_ref, col_ref, row_ref, solver_ref, scores_ref, w_ref, vt_ref, qt_ref, m_ref, b_ref, mseg_ref, bseg_ref):
    count = sum(counts)
    lower, strict, identity = square_masks()
    query = q_ref[...]
    query = split(query * row_factor(query), count)
    key = k_ref[...]
    key = split(key * row_factor(key), count)
    value = split(v_ref[...], count)
    fade, ratio, growth, remain, beta, end = decays(col_ref, row_ref, count)
    power = each(lambda k, p: jnp.where(strict, -mm_nt(k, k) * p, 0.0), key, ratio)
    solver = [identity + p for p in power]
    for _ in range((BLOCK - 1).bit_length() - 1):
        power = each(lambda p: mm(p, p), power)
        solver = each(lambda s, p: s + mm(s, p), solver, power)
    scores = each(lambda q, k, p: mm_nt(q, k) * p, query, key, ratio)
    w = each(lambda s, g, k: mm(s, g * k), solver, growth, key)
    vt = each(mm, solver, value)
    qt = each(lambda g, q, a, x: g * q - mm(a, x), growth, query, scores, w)
    weighted = each(lambda k, r, b: k * (r * b), key, remain, beta)
    size = query[0].shape[1]
    wide = (
        lax.broadcasted_iota(jnp.int32, (size, size), 0)
        == lax.broadcasted_iota(jnp.int32, (size, size), 1)
    ).astype(f32)
    m = each(lambda e, k, x: e * wide - mm_tn(k, x), end, weighted, w)
    b = each(mm_tn, weighted, vt)
    for i in range(count):
        solver_ref[0, i] = solver[i]
        scores_ref[0, i] = scores[i]
        w_ref[0, i] = w[i]
        vt_ref[0, i] = vt[i]
        qt_ref[0, i] = qt[i]
        m_ref[0, i] = m[i]
        b_ref[0, i] = b[i]
    for j, chain in enumerate(chains(counts)):
        mseg_ref[0, j] = m[chain[0]]
        bseg_ref[0, j] = b[chain[0]]
        for i in chain[1:]:
            bseg_ref[0, j] = mm(m_ref[0, i], bseg_ref[0, j]) + b_ref[0, i]
            mseg_ref[0, j] = mm(m_ref[0, i], mseg_ref[0, j])


def output_kernel(counts, state_ref, m_ref, b_ref, qt_ref, scores_ref, vt_ref, gate_ref, gain_ref, states_ref, out_ref, gated_ref):
    count = sum(counts)
    states = [None] * count
    for j, chain in enumerate(chains(counts)):
        state = state_ref[0, j]
        for i in chain:
            states[i] = state
            states_ref[0, i] = state
            if i != chain[-1]:
                state = mm(m_ref[0, i], state) + b_ref[0, i]
    gain = gain_ref[...]
    outs = [mm(qt_ref[0, i], states[i]) + mm(scores_ref[0, i], vt_ref[0, i]) for i in range(count)]
    for i in range(count):
        rows = slice(i * BLOCK, (i + 1) * BLOCK)
        out = outs[i]
        gate = gate_ref[rows, :]
        scale = lax.rsqrt(jnp.mean(out * out, axis=-1, keepdims=True) + epsilon)
        out_ref[rows, :] = out
        gated_ref[rows, :] = (out * scale * gain * (gate * jax.nn.sigmoid(gate))).astype(jnp.bfloat16)


def output_grad_kernel(counts, grad_ref, gate_ref, out_ref, gain_ref, qt_ref, m_ref, out_grad_ref, gate_grad_ref, gain_grad_ref, d_ref, dseg_ref):
    count = sum(counts)
    gain = gain_ref[...]
    gain_grad = jnp.zeros_like(gain)
    grads = []
    for i in range(count):
        rows = slice(i * BLOCK, (i + 1) * BLOCK)
        grad, gate, out = grad_ref[rows, :], gate_ref[rows, :], out_ref[rows, :]
        scale = lax.rsqrt(jnp.mean(out * out, axis=-1, keepdims=True) + epsilon)
        unit = out * scale
        sig = jax.nn.sigmoid(gate)
        normed_grad = grad * (gate * sig)
        gate_grad_ref[rows, :] = (grad * (unit * gain) * (sig * (1.0 + gate * (1.0 - sig)))).astype(jnp.bfloat16)
        gain_grad = gain_grad + jnp.sum(normed_grad * unit, axis=0, keepdims=True)
        inner = normed_grad * gain
        out_grad = scale * (inner - unit * jnp.mean(unit * inner, axis=-1, keepdims=True))
        out_grad_ref[rows, :] = out_grad
        grads.append(out_grad)
    gain_grad_ref[0] = gain_grad
    d = [mm_tn(qt_ref[0, i], grads[i]) for i in range(count)]
    for i in range(count):
        d_ref[0, i] = d[i]
    for j, chain in enumerate(chains(counts)):
        dseg_ref[0, j] = d[chain[-1]]
        for i in list(chain)[-2::-1]:
            dseg_ref[0, j] = mm_tn(m_ref[0, i], dseg_ref[0, j]) + d_ref[0, i]


def unit_back(raw, grad):
    factor = row_factor(raw)
    unit = raw * factor
    return factor * (grad - unit * jnp.sum(unit * grad, axis=-1, keepdims=True))


def grads_kernel(counts, q_ref, k_ref, col_ref, row_ref, solver_ref, scores_ref, w_ref, vt_ref, m_ref, d_ref, states_ref, out_grad_ref, gate_ref, later_ref, slim_ref, joint_ref, col_grad_ref, row_grad_ref):
    count = sum(counts)
    span = range(count)
    lower, strict, identity = square_masks()
    raw_q, raw_k = split(q_ref[...], count), split(k_ref[...], count)
    query = [x * row_factor(x) for x in raw_q]
    key = [x * row_factor(x) for x in raw_k]
    fade, ratio, growth, remain, beta, end = decays(col_ref, row_ref, count)
    out_grad = split(out_grad_ref[...], count)
    later = [None] * count
    for j, chain in enumerate(chains(counts)):
        state = later_ref[0, j]
        for i in list(chain)[::-1]:
            later[i] = state
            if i != chain[0]:
                state = mm_tn(m_ref[0, i], state) + d_ref[0, i]
    states = [states_ref[0, i] for i in span]
    update = [vt_ref[0, i] - mm(w_ref[0, i], states[i]) for i in span]
    update_grad = [
        mm_tn(scores_ref[0, i], out_grad[i]) + mm(key[i] * (remain[i] * beta[i]), later[i]) for i in span
    ]
    solved = [mm_tn(solver_ref[0, i], update_grad[i]) for i in span]
    scores_grad = each(mm_nt, out_grad, update)
    inner_grad = each(lambda y, u: jnp.where(strict, -mm_nt(y, u), 0.0), solved, update)
    query_dot = each(mm_nt, query, key)
    keys_dot = each(mm_nt, key, key)
    from_out = each(mm_nt, out_grad, states)
    from_solved = each(mm_nt, solved, states)
    from_update = each(mm_nt, update, later)
    weighted_scores = each(lambda p, x: p * x, ratio, scores_grad)
    weighted_inner = each(lambda p, x: p * x, ratio, inner_grad)
    q_grad = [growth[i] * from_out[i] + mm(weighted_scores[i], key[i]) for i in span]
    k_grad = [
        mm_tn(weighted_scores[i], query[i])
        + (remain[i] * beta[i]) * from_update[i]
        - growth[i] * from_solved[i]
        + mm(weighted_inner[i], key[i])
        + mm_tn(weighted_inner[i], key[i])
        for i in span
    ]
    last_row = (lax.broadcasted_iota(jnp.int32, (BLOCK, 1), 0) == BLOCK - 1).astype(f32)
    for i in span:
        rows = slice(i * BLOCK, (i + 1) * BLOCK)
        start = 0
        for grad in (unit_back(raw_q[i], q_grad[i]), unit_back(raw_k[i], k_grad[i]), solved[i]):
            place = slice(start, start + grad.shape[1])
            start += grad.shape[1]
            slim_ref[rows, place] = grad.astype(jnp.bfloat16)
            joint_ref[rows, place] = grad.astype(jnp.bfloat16)
        joint_ref[rows, start:] = gate_ref[rows, :]
        faded = fade[i] * (scores_grad[i] * query_dot[i] + inner_grad[i] * keys_dot[i])
        b_row = row_ref[0, i, 1:2, :]
        growth_grad = jnp.sum(query[i] * from_out[i] - key[i] * from_solved[i], axis=-1, keepdims=True)
        weight_grad = jnp.sum(key[i] * from_update[i], axis=-1, keepdims=True)
        pulled = remain[i] * beta[i] * weight_grad
        tail = jnp.sum(pulled, axis=0, keepdims=True) + end[i] * jnp.sum(
            jnp.sum(later[i] * states[i], axis=-1, keepdims=True), axis=0, keepdims=True
        )
        c_grad = jnp.sum(faded * b_row, axis=-1, keepdims=True) + growth[i] * growth_grad - pulled + last_row * tail
        col_grad_ref[0, i, :, 0:1] = c_grad
        col_grad_ref[0, i, :, 1:2] = remain[i] * weight_grad
        row_grad_ref[0, i] = jnp.sum(faded, axis=0, keepdims=True)


def whole(shape):
    return pl.BlockSpec((1,) + tuple(shape[1:]), lambda j: (j,) + (0,) * (len(shape) - 1))


def columns(rows, width, first=0, step=1):
    return pl.BlockSpec((rows, width), lambda j: (0, step * j + first))


def shaped(shape, dtype=f32):
    return jax.ShapeDtypeStruct(shape, dtype)


def call(kernel, counts, heads, inputs, outputs, flops):
    moved = sum(x.size * x.dtype.itemsize for x, _ in inputs) + sum(
        x.size * x.dtype.itemsize for x, _ in outputs
    )
    return pl.pallas_call(
        functools.partial(kernel, counts),
        grid=(heads,),
        in_specs=[s for _, s in inputs],
        out_specs=[s for _, s in outputs],
        out_shape=[x for x, _ in outputs],
        compiler_params=pltpu.CompilerParams(vmem_limit_bytes=48 << 20),
        cost_estimate=pl.CostEstimate(flops=flops, bytes_accessed=moved, transcendentals=0),
    )(*[x for x, _ in inputs])


def per_head(heads, *shape, dtype=f32):
    s = (heads,) + shape
    return shaped(s, dtype), whole(s)


def flat(array, width, first=0, step=1):
    return array, columns(array.shape[0], width, first, step)


def stacked(array):
    return array, whole(array.shape)


def solve(counts, heads, proj, col, row):
    n, dk, dv = sum(counts), 128, 256
    return call(
        solve_kernel, counts, heads,
        [flat(proj, dk, 0, 4), flat(proj, dk, 1, 4), flat(proj, dv, 1, 2), stacked(col), stacked(row)],
        [per_head(heads, n, BLOCK, BLOCK), per_head(heads, n, BLOCK, BLOCK), per_head(heads, n, BLOCK, dk),
         per_head(heads, n, BLOCK, dv), per_head(heads, n, BLOCK, dk), per_head(heads, n, dk, dk),
         per_head(heads, n, dk, dv), per_head(heads, len(counts), dk, dk), per_head(heads, len(counts), dk, dv)],
        heads * n * 100_000_000,
    )


def outputs_of(counts, heads, state, m, b, qt, scores, vt, gate_pre, gain):
    n, dk, dv = sum(counts), 128, 256
    rows = gate_pre.shape[0]
    cols = columns(rows, dv)
    return call(
        output_kernel, counts, heads,
        [stacked(state), stacked(m), stacked(b), stacked(qt), stacked(scores), stacked(vt), flat(gate_pre, dv),
         (gain, pl.BlockSpec((1, dv), lambda j: (0, 0)))],
        [per_head(heads, n, dk, dv), (shaped((rows, heads * dv)), cols), (shaped((rows, heads * dv), jnp.bfloat16), cols)],
        heads * n * 50_000_000,
    )


def output_grads_of(counts, heads, grad, gate_pre, outs, gain, qt, m):
    n, dk, dv = sum(counts), 128, 256
    rows = gate_pre.shape[0]
    cols = columns(rows, dv)
    return call(
        output_grad_kernel, counts, heads,
        [flat(grad, dv), flat(gate_pre, dv), flat(outs, dv), (gain, pl.BlockSpec((1, dv), lambda j: (0, 0))), stacked(qt), stacked(m)],
        [(shaped((rows, heads * dv)), cols), (shaped((rows, heads * dv), jnp.bfloat16), cols),
         per_head(heads, 1, dv), per_head(heads, n, dk, dv), per_head(heads, len(counts), dk, dv)],
        heads * n * 50_000_000,
    )


def input_grads_of(counts, heads, proj, col, row, solver, scores, w, vt, m, d, states, out_grad, gate_grad, later):
    n, dk, dv = sum(counts), 128, 256
    rows = proj.shape[0]
    return call(
        grads_kernel, counts, heads,
        [flat(proj, dk, 0, 4), flat(proj, dk, 1, 4), stacked(col), stacked(row), stacked(solver), stacked(scores), stacked(w),
         stacked(vt), stacked(m), stacked(d), stacked(states), flat(out_grad, dv), flat(gate_grad, dv), stacked(later)],
        [(shaped((rows, heads * (2 * dk + dv)), jnp.bfloat16), columns(rows, 2 * dk + dv)),
         (shaped((rows, heads * (2 * dk + 2 * dv)), jnp.bfloat16), columns(rows, 2 * dk + 2 * dv)),
         per_head(heads, n, BLOCK, 2), per_head(heads, n, 1, BLOCK)],
        heads * n * 150_000_000,
    )


def feed_kernel(stage_ref, x_ref, k_ref, xs_ref, ks_ref, w1_ref, w3_ref, w2_ref, t1_ref, t3_ref, t2_ref, back_ref, feed_ref, main_ref, main_other_ref, tail_ref, tail_other_ref, active_s, gate_s, up_s, sums_s):
    step, chunk = pl.program_id(0), pl.program_id(1)
    own, width = sums_s.shape[0], sums_s.shape[1] // 2
    groups, rows_each = back_ref.shape[0], back_ref.shape[1]
    near, piece = x_ref.shape[1] // own, x_ref.shape[2]
    stage = stage_ref[0]
    here = pl.ds(pl.multiple_of(lax.rem(stage, near) * own, own), own)

    @pl.when((step == 0) & (chunk == 0))
    def _():
        sums_s[...] = jnp.zeros_like(sums_s)

    def work(w1, w3, w2, out_refs):
        wide = w1.shape[1]
        gate, up, grad = (
            sum(
                jnp.dot(rows[i], w[i * piece : (i + 1) * piece, :], preferred_element_type=f32)
                for i in range(rows.shape[0])
            )
            for rows, w in ((x_ref, w1), (x_ref, w3), (k_ref, w2))
        )
        sig = jax.nn.sigmoid(gate)
        silu = gate * sig
        active = (silu * up).astype(jnp.bfloat16)
        gate_grad = (grad * up * (sig * (1.0 + gate * (1.0 - sig)))).astype(jnp.bfloat16)
        up_grad = (grad * silu).astype(jnp.bfloat16)
        active_s[:, :wide] = active
        gate_s[:, :wide] = gate_grad
        up_s[:, :wide] = up_grad

        @pl.when(chunk == stage // near)
        def _():
            sums_s[:, width:] += contract_cols(active_s[here, :wide], w2[...])
            sums_s[:, :width] += contract_cols(gate_s[here, :wide], w1[...])
            sums_s[:, :width] += contract_cols(up_s[here, :wide], w3[...])

        parts = (
            contract_rows(gate_grad, xs_ref[...]),
            contract_rows(up_grad, xs_ref[...]),
            contract_rows(active, ks_ref[...]),
        )
        for i, p in enumerate(parts):
            place = slice(i * wide, (i + 1) * wide)
            quota = p.shape[1] // 2

            @pl.when(chunk == 0)
            def _():
                out_refs[0][place, :] = p[:, :quota]
                out_refs[1][place, :] = p[:, quota:]

            @pl.when(chunk > 0)
            def _():
                out_refs[0][place, :] += p[:, :quota]
                out_refs[1][place, :] += p[:, quota:]

    work(w1_ref, w3_ref, w2_ref, (main_ref, main_other_ref))

    @pl.when(step == pl.num_programs(0) - 1)
    def _():
        work(t1_ref, t3_ref, t2_ref, (tail_ref, tail_other_ref))

    @pl.when((step == pl.num_programs(0) - 1) & (chunk == pl.num_programs(1) - 1))
    def _():
        for g in range(groups):
            rows = slice(g * rows_each, (g + 1) * rows_each)
            back_ref[g] = sums_s[rows, :width].astype(jnp.bfloat16)
            feed_ref[g] = sums_s[rows, width:].astype(jnp.bfloat16)


def feed_forward(stage, rows, grads, row_cols, grad_cols, weights, groups, rows_each):
    pieces, positions, piece = rows.shape
    width, own = pieces * piece, groups * rows_each
    picked = row_cols.shape[1]
    tile, rest = 256, 128
    steps = (weights.shape[1] - 3 * rest) // (3 * tile)
    chunk = min(positions, 4 * own)
    first_tail = 3 * steps * tile // rest
    grid = (steps, positions // chunk)
    tokens = pl.BlockSpec((pieces, chunk, piece), lambda i, t, s: (0, t, 0))
    columns_of = pl.BlockSpec((chunk, picked), lambda i, t, s: (t, 0))

    def main_of(n):
        return pl.BlockSpec((width, tile), lambda i, t, s: (0, n * steps + i))

    def tail_of(n):
        return pl.BlockSpec((width, rest), lambda i, t, s: (0, first_tail + n))

    def fixed(*shape):
        return pl.BlockSpec(shape, lambda i, t, s: (0, 0))

    flops = 2 * positions * width * weights.shape[1] + 2 * own * width * weights.shape[1] + 2 * positions * picked * weights.shape[1]
    return pl.pallas_call(
        feed_kernel,
        grid_spec=pltpu.PrefetchScalarGridSpec(
            num_scalar_prefetch=1,
            grid=grid,
            in_specs=[tokens, tokens, columns_of, columns_of, main_of(0), main_of(1), main_of(2), tail_of(0), tail_of(1), tail_of(2)],
            out_specs=[
                pl.BlockSpec((groups, rows_each, width), lambda i, t, s: (0, 0, 0)),
                pl.BlockSpec((groups, rows_each, width), lambda i, t, s: (0, 0, 0)),
                pl.BlockSpec((3 * tile, picked // 2), lambda i, t, s: (i, 0)),
                pl.BlockSpec((3 * tile, picked // 2), lambda i, t, s: (i, 0)),
                fixed(3 * rest, picked // 2),
                fixed(3 * rest, picked // 2),
            ],
            scratch_shapes=[pltpu.VMEM((chunk, tile), jnp.bfloat16)] * 3 + [pltpu.VMEM((own, 2 * width), f32)],
        ),
        out_shape=[
            shaped((groups, rows_each, width), jnp.bfloat16),
            shaped((groups, rows_each, width), jnp.bfloat16),
            shaped((3 * tile * steps, picked // 2)),
            shaped((3 * tile * steps, picked // 2)),
            shaped((3 * rest, picked // 2)),
            shaped((3 * rest, picked // 2)),
        ],
        compiler_params=pltpu.CompilerParams(
            dimension_semantics=("arbitrary", "arbitrary"), vmem_limit_bytes=56 << 20
        ),
        cost_estimate=pl.CostEstimate(
            flops=flops, bytes_accessed=2 * weights.size + 8 * positions * width, transcendentals=0
        ),
    )(stage, rows, grads, row_cols, grad_cols, weights, weights, weights, weights, weights, weights)


def projection_kernel(heads, cols_ref, joint_ref, q_ref, k_ref, v_ref, g_ref):
    joined = jnp.dot(cols_ref[...], joint_ref[...], preferred_element_type=f32)
    start = 0
    for j in range(heads):
        for ref in (q_ref, k_ref, v_ref, g_ref):
            size = ref.shape[1] // heads
            ref[:, j * size : (j + 1) * size] = joined[:, start : start + size]
            start += size


def projection_grads(cols, joint_all, heads, sizes):
    quota, positions = cols.shape
    wide = joint_all.shape[1]
    return pl.pallas_call(
        functools.partial(projection_kernel, heads),
        grid=(2,),
        in_specs=[
            pl.BlockSpec((quota, positions), lambda c: (0, 0)),
            pl.BlockSpec((positions, wide), lambda c: (c, 0)),
        ],
        out_specs=[pl.BlockSpec((quota, n), lambda c: (0, c)) for n in sizes],
        out_shape=[shaped((quota, 2 * n)) for n in sizes],
        compiler_params=pltpu.CompilerParams(vmem_limit_bytes=56 << 20),
        cost_estimate=pl.CostEstimate(
            flops=4 * quota * positions * wide, bytes_accessed=2 * joint_all.size, transcendentals=0
        ),
    )(cols, joint_all)


QUARTERS = 4


def swap(array):
    return lax.ppermute(array, "dp", [(0, 1), (1, 0)])


def relay(mats, offsets, forward):
    size = lax.axis_size("seq")
    entering = jnp.zeros_like(offsets)
    leaving = offsets
    for step in range(size - 1):
        route = [(step, step + 1)] if forward else [(size - 1 - step, size - 2 - step)]
        got = jnp.stack([lax.ppermute(head, "seq", route) for head in leaving])
        entering = entering + got
        if step < size - 2:
            leaving = jnp.matmul(mats, got, precision=highest) + offsets
    return entering, leaving


def together(*arrays):
    return lax.optimization_barrier(arrays)


def everyone(part):
    return lax.all_gather(part, ("dp", "seq"), axis=0, tiled=True)


def share(rows):
    wide = jnp.broadcast_to(rows[None], (lax.axis_size("head"),) + rows.shape)
    return lax.all_to_all(wide, "head", split_axis=0, concat_axis=0, tiled=True)


def from_others(piece):
    size = lax.axis_size("head")
    return [lax.ppermute(piece(k), "head", [(i, i ^ k) for i in range(size)]) for k in range(1, size)]


def in_group_order(pieces):
    group = lax.axis_index("head")
    stacked = jnp.stack(pieces)
    return jnp.stack(
        [lax.dynamic_index_in_dim(stacked, g ^ group, 0, keepdims=False) for g in range(lax.axis_size("head"))]
    )


def add_by_permutes(vector):
    near, far, across = from_others(lambda k: vector)
    return (vector + near) + (far + across)


def add_parts_by_permutes(parts):
    group = lax.axis_index("head")

    def piece(k):
        return lax.dynamic_index_in_dim(parts, group ^ k, 0, keepdims=False).astype(jnp.bfloat16)

    near, far, across = [got.astype(f32) for got in from_others(piece)]
    return (piece(0).astype(f32) + near) + (far + across)


def add_parts(parts):
    got = lax.all_to_all(parts.astype(jnp.bfloat16), "head", split_axis=0, concat_axis=0, tiled=True)
    return jnp.sum(got.astype(f32), axis=0)


def contract_rows(left, right):
    return lax.dot_general(left, right, (((0,), (0,)), ((), ())), preferred_element_type=f32)


def contract_cols(left, right):
    return lax.dot_general(left, right, (((1,), (1,)), ((), ())), preferred_element_type=f32)


def product(left, right):
    return jnp.dot(left, right, preferred_element_type=f32)


def rms_scale(values, gain):
    return values * lax.rsqrt(jnp.mean(values * values, axis=-1, keepdims=True) + epsilon) * gain


def swiglu(gate_in, up_in):
    return jax.nn.silu(gate_in) * up_in


def on_device(
    activations,
    cotangent,
    lengths,
    query_weight,
    key_weight,
    value_weight,
    gate_weight,
    alpha_weight,
    beta_weight,
    out_weight,
    swiglu_gate,
    swiglu_value,
    swiglu_down,
    mixer_gain,
    feed_gain,
    head_gain,
    decay_rate,
    beta_bias,
):
    bf16 = jnp.bfloat16
    core, stage, group = lax.axis_index("dp"), lax.axis_index("seq"), lax.axis_index("head")
    stages, groups = lax.axis_size("seq"), lax.axis_size("head")
    width = activations.shape[2]
    rows0 = activations.shape[1]
    rows1 = rows0 // QUARTERS
    own0, own1 = rows0 // (2 * groups), rows1 // (2 * groups)
    own = own0 + own1
    quota = width // (2 * stages)
    heads = alpha_weight.shape[1] // 2
    counts = (rows0 // BLOCK, rows1 // BLOCK)
    assert groups == QUARTERS and stages % QUARTERS == 0 and rows1 % BLOCK == 0
    first = core == 0

    def part(array, size, axis, offset=0):
        return lax.dynamic_slice_in_dim(array, offset + core * size, size, axis)

    dk, dv = query_weight.shape[1] // 2, value_weight.shape[1] // 2
    slim = 2 * dk + dv
    mixer_cols = []
    for c in range(2):
        for j in range(c * heads, (c + 1) * heads):
            mixer_cols += [
                query_weight[:, j * dk // heads : (j + 1) * dk // heads],
                key_weight[:, j * dk // heads : (j + 1) * dk // heads],
                value_weight[:, j * dv // heads : (j + 1) * dv // heads],
            ]
    mixer_cols += [alpha_weight, beta_weight]
    mixer_full = everyone(jnp.concatenate(mixer_cols, axis=1).astype(bf16))
    gates_full = everyone(jnp.concatenate([gate_weight, out_weight], axis=1).astype(bf16))
    hidden_units = swiglu_gate.shape[1]
    even = hidden_units // 256 * 256
    odd = hidden_units - even
    assert 0 < odd <= 128
    three = (swiglu_gate, swiglu_value, swiglu_down)
    spare = ((0, 0), (0, 128 - odd))
    feed_full = everyone(
        jnp.concatenate([w[:, :even] for w in three] + [jnp.pad(w[:, even:], spare) for w in three], axis=1).astype(bf16)
    )

    def chip_rows(rows):
        arrived = jnp.zeros((rows1, width), bf16)
        for b in range(QUARTERS):
            route = [(stages + a, stages + QUARTERS * a + b) for a in range(stages // QUARTERS)]
            arrived = arrived + lax.ppermute(rows[b * rows1 : (b + 1) * rows1], ("dp", "seq"), route)
        near0 = lax.ppermute(rows, "dp", [(0, 1)])
        near1 = lax.ppermute(arrived, "dp", [(1, 0)])
        return jnp.concatenate([jnp.where(first, rows, near0), jnp.where(first, near1, arrived)], axis=0)

    inputs = chip_rows(activations[0])
    inputs, late = together(inputs, cotangent[0])
    inputs = inputs.astype(f32)
    spots0 = stage * rows0 + lax.broadcasted_iota(jnp.int32, (rows0, 1), 0)
    spots1 = stage * rows1 + lax.broadcasted_iota(jnp.int32, (rows1, 1), 0)
    mask = jnp.concatenate([spots0 < lengths[0], spots1 < lengths[1]], axis=0).astype(f32)
    masked = (chip_rows(late).astype(f32) * mask).astype(bf16)

    def by_owner(rows):
        wide = rows.shape[1]
        r0 = rows[:rows0].reshape(groups, 2, own0, wide)
        r1 = rows[rows0:].reshape(groups, 2, own1, wide)
        return jnp.concatenate([r0, r1], axis=2).swapaxes(0, 1)

    def in_time(owned):
        wide = owned.shape[3]
        turned = owned.swapaxes(0, 1)
        return jnp.concatenate(
            [turned[:, :, :own0].reshape(rows0, wide), turned[:, :, own0:].reshape(rows1, wide)], axis=0
        )

    def of_core(owned, which):
        return lax.dynamic_index_in_dim(owned, which, 0, keepdims=False)

    def of_group(rows):
        return lax.dynamic_index_in_dim(rows, group, 0, keepdims=False)

    def add_rows(partial):
        owned = by_owner(partial)
        return add_parts_by_permutes(of_core(owned, core) + swap(of_core(owned, 1 - core)))

    def meet_columns(rows):
        return lax.all_to_all(rows, ("dp", "seq"), split_axis=1, concat_axis=0, tiled=True)

    def owned_columns(met, share_rows):
        got = share_rows(met).reshape(groups, 2, stages, own, quota).transpose(2, 0, 1, 3, 4)
        return jnp.concatenate(
            [got[:, :, :, :own0].reshape(stages, rows0, quota), got[:, :, :, own0:].reshape(stages, rows1, quota)], axis=1
        ).reshape(stages * (rows0 + rows1), quota)

    def across_stages(rows):
        wide = jnp.broadcast_to(rows[None], (stages,) + rows.shape)
        met = lax.all_to_all(wide, "seq", split_axis=0, concat_axis=0, tiled=True)
        return met.reshape(stages * rows.shape[0], rows.shape[1])

    def own_columns(rows):
        pieces, positions, piece = rows.shape
        both = []
        for which in (core, 1 - core):
            start = (which * stages + stage) * quota
            both.append(lax.dynamic_slice(rows, (start // piece, 0, start % piece), (1, positions, quota))[0])
        return jnp.concatenate(both, axis=1)

    own_rows = of_group(of_core(by_owner(inputs), core))
    own_mask = of_group(of_core(by_owner(mask), core))
    tokens_masked = of_core(by_owner(masked), core)
    own_masked = of_group(tokens_masked).astype(f32)
    quarter = width // groups
    masked_met = across_stages(
        lax.dynamic_slice_in_dim(tokens_masked.reshape(groups * own, width), group * quarter, quarter, 1)
    )

    factor1 = lax.rsqrt(jnp.mean(inputs * inputs, axis=-1, keepdims=True) + epsilon)
    unit1 = inputs * factor1
    normed = rms_scale(inputs, mixer_gain).astype(bf16)
    normed_cols = owned_columns(meet_columns(of_group(of_core(by_owner(normed), core))), share).T
    mixer_full, masked_met, normed_cols = together(mixer_full, masked_met, normed_cols)
    mixer_w = part(mixer_full, slim, 1)
    gate_w = part(gates_full, dv, 1)
    out_w = part(gates_full, dv, 1, 2 * dv)
    rates_w = mixer_full[:, 2 * slim :]
    proj = product(normed, mixer_w)
    small_pre = product(normed, rates_w)
    gate_pre = product(normed, gate_w)
    alpha_pre = part(small_pre, heads, 1)
    beta_pre = part(small_pre, heads, 1, 2 * heads)
    head0 = (2 * group + core) * heads
    rates = lax.dynamic_slice_in_dim(decay_rate, head0, heads)
    biases = lax.dynamic_slice_in_dim(beta_bias, head0, heads)
    blocks = sum(counts)

    def to_blocks(array):
        return array.T.reshape(heads, blocks, BLOCK)

    def from_blocks(array):
        return array.reshape(heads, blocks * BLOCK).T

    soft = jax.nn.softplus(alpha_pre)
    beta = jax.nn.sigmoid(beta_pre + biases)
    beta_b = to_blocks(beta)
    upto = (
        lax.broadcasted_iota(jnp.int32, (BLOCK, BLOCK), 0) <= lax.broadcasted_iota(jnp.int32, (BLOCK, BLOCK), 1)
    ).astype(f32)
    sums = jnp.matmul(to_blocks(-rates * soft), upto, precision=highest)
    col = jnp.stack([sums, beta_b], axis=-1)
    row = jnp.stack([sums, beta_b], axis=-2)
    solver, scores, w, vt, qt, m, b, mseg, bseg = solve(counts, heads, proj, col, row)
    state_in, unused_carry = relay(mseg, bseg, True)
    state_in, masked_all = together(state_in, share(masked_met))
    gain_row = head_gain[None]
    states, outs, gated = outputs_of(counts, heads, state_in, m, b, qt, scores, vt, gate_pre, gain_row)
    mixed = add_rows(contract_cols(gated, out_w))
    hidden = own_rows + mixed

    normed2, norm2_back = jax.vjp(rms_scale, hidden, feed_gain)
    feed_in = share(
        across_stages(lax.all_to_all(normed2.astype(bf16), "head", split_axis=1, concat_axis=0, tiled=True))
    )
    back_part, feed_part, main_own, main_other, tail_own, tail_other = feed_forward(
        stage[None], feed_in, masked_all, own_columns(feed_in), own_columns(masked_all), feed_full, groups, own
    )
    normed2_grad, main_other, tail_other = together(add_parts(back_part), swap(main_other), swap(tail_other))
    hidden_back, feed_gain_grad = norm2_back(normed2_grad)
    hidden_grad = own_masked + hidden_back
    mixed_own = hidden_grad.astype(bf16)
    mixed_half = share(mixed_own)
    other_half = swap(mixed_half)
    mixed_in = in_time(
        jnp.stack([jnp.where(first, mixed_half, other_half), jnp.where(first, other_half, mixed_half)])
    )

    gated_all = everyone(gated)
    gated_grad = product(mixed_in, out_w)
    mixed_late, unused_rows = together(mixed_own, mixed_in)
    mixed_met = meet_columns(mixed_late)
    gated_grad, gated_all = together(gated_grad, gated_all)
    outs_grad, gate_pre_low, gain_grads, d, dseg = output_grads_of(
        counts, heads, gated_grad, gate_pre, outs, gain_row, qt, m
    )
    dseg, mixed_met = together(dseg, mixed_met)
    later, unused_carry = relay(jnp.swapaxes(mseg, 2, 3), dseg, False)

    half = stages * (rows0 + rows1)
    gate_back = contract_cols(gate_pre_low, gate_w)
    later, gate_back = together(later, gate_back)
    slim_low, joint_low, col_grad, row_grad = input_grads_of(
        counts, heads, proj, col, row, solver, scores, w, vt, m, d, states, outs_grad, gate_pre_low, later
    )
    joint_all = everyone(joint_low)
    slim_low, mixed_met = together(slim_low, mixed_met)
    mixed_pieces = from_others(lambda k: mixed_met)
    sums_grad = col_grad[..., 0] - row_grad[:, :, 0] * beta_b
    decay_back = from_blocks(jnp.matmul(sums_grad, upto.T, precision=highest))
    beta_back = beta * (1.0 - beta) * from_blocks(col_grad[..., 1] + row_grad[:, :, 0])
    rates_grad = -jnp.sum(soft * decay_back, axis=0)
    biases_grad = jnp.sum(beta_back, axis=0)
    alpha_back = -rates * jax.nn.sigmoid(alpha_pre) * decay_back
    small_low = jnp.concatenate([alpha_back, beta_back], axis=1).astype(bf16)
    blank = jnp.zeros((rows0 + rows1, 4 * heads), bf16)
    spread = lax.dynamic_update_slice(blank, small_low[:, :heads], (0, core * heads))
    spread = lax.dynamic_update_slice(spread, small_low[:, heads:], (0, (2 + core) * heads))
    total = gate_back + contract_cols(slim_low, mixer_w) + contract_cols(spread, rates_w)
    normed_grad = add_rows(total)
    mixer_gain_part = jnp.sum(total * unit1, axis=0)
    normed_grad, small_late, mixer_gain_part, feed_part, main_own, main_other, tail_own, tail_other, *mixed_pieces = together(
        normed_grad, small_low, mixer_gain_part, feed_part, main_own, main_other, tail_own, tail_other, mixed_met, *mixed_pieces
    )
    feed = add_parts_by_permutes(feed_part)
    mixed_cols = owned_columns(mixed_met, lambda rows: in_group_order(mixed_pieces))
    outputs_own = (own_mask * (hidden + feed)).astype(bf16)
    out_grad = jnp.concatenate(
        [contract_rows(mixed_cols, gated_all[:half]), contract_rows(mixed_cols, gated_all[half:])], axis=1
    )
    unused_rows, norm1_back = jax.vjp(lambda v: rms_scale(v, mixer_gain), own_rows)
    input_own = (hidden_grad + norm1_back(normed_grad)[0]).astype(bf16)

    main_own, tail_own = main_own + main_other, tail_own + tail_other

    def feed_grad(n):
        pieces = [main_own[(3 * i + n) * 256 : (3 * i + n + 1) * 256] for i in range(even // 256)]
        return jnp.concatenate(pieces + [tail_own[n * 128 : n * 128 + odd]], axis=0)

    feed_gate_grad, feed_value_grad, down_grad = feed_grad(0), feed_grad(1), feed_grad(2)

    small_rows = contract_rows(small_late, normed).reshape(2 * heads, 2 * stages, quota).swapaxes(0, 1)
    total_heads = decay_rate.shape[0]
    none = jnp.zeros((total_heads,), f32)
    vector = jnp.concatenate(
        [
            mixer_gain_part,
            feed_gain_grad,
            jnp.sum(gain_grads, axis=(0, 1)),
            lax.dynamic_update_slice(none, rates_grad, (head0,)),
            lax.dynamic_update_slice(none, biases_grad, (head0,)),
        ]
    )
    mail = jnp.concatenate(
        [
            small_rows.reshape(2 * stages, 2 * heads * quota),
            jnp.broadcast_to(vector[None], (2 * stages, vector.shape[0])),
        ],
        axis=1,
    )
    mail = lax.all_to_all(mail, ("dp", "seq"), split_axis=0, concat_axis=0, tiled=True)
    mail, out_grad = together(mail, out_grad)
    small_rows = jnp.sum(mail[:, : 2 * heads * quota].reshape(2, stages, 2, heads, quota), axis=1)
    alpha_grad = small_rows[:, 0].reshape(2 * heads, quota).T
    beta_grad = small_rows[:, 1].reshape(2 * heads, quota).T
    small = add_by_permutes(jnp.sum(mail[:, 2 * heads * quota :], axis=0))
    joint_all, out_grad = together(joint_all, out_grad)
    query_grad, key_grad, value_grad, gate_grad = projection_grads(normed_cols, joint_all, heads, (dk, dk, dv, dv))

    edges = [width, 2 * width, 2 * width + head_gain.shape[0], 2 * width + head_gain.shape[0] + total_heads]

    def place(rows):
        r0, r1 = rows[:own0], rows[own0:]
        out0 = jnp.concatenate([r0, lax.ppermute(r0, "dp", [(1, 0)])], axis=0)
        pair = jnp.concatenate([lax.ppermute(r1, "dp", [(0, 1)]), r1], axis=0)
        routes = [
            [
                ((stages + QUARTERS * a + b) * groups + k, (stages + a) * groups + b)
                for a in range(stages // QUARTERS)
                for b in range(QUARTERS)
            ]
            for k in range(groups)
        ]
        out1 = jnp.concatenate([lax.ppermute(pair, ("dp", "seq", "head"), route) for route in routes], axis=0)
        return jnp.where(first, out0, out1)[None]

    placed = place(jnp.concatenate([outputs_own, input_own], axis=1))
    return (
        placed[:, :, :width],
        placed[:, :, width:],
        query_grad,
        key_grad,
        value_grad,
        gate_grad,
        alpha_grad,
        beta_grad,
        out_grad,
        feed_gate_grad.T,
        feed_value_grad.T,
        down_grad.T,
        small[: edges[0]],
        small[edges[0] : edges[1]],
        small[edges[1] : edges[2]],
        small[edges[2] : edges[3]],
        small[edges[3] :],
    )


def solution(mesh):
    return jax.shard_map(
        on_device,
        mesh=mesh,
        in_specs=(
            P("dp", "seq", None),
            P("dp", "seq", None),
            P(),
            P(("dp", "seq"), "head"),
            P(("dp", "seq"), "head"),
            P(("dp", "seq"), "head"),
            P(("dp", "seq"), "head"),
            P(("dp", "seq"), "head"),
            P(("dp", "seq"), "head"),
            P(("dp", "seq"), "head"),
            P(("dp", "seq"), "head"),
            P(("dp", "seq"), "head"),
            P(("dp", "seq"), "head"),
            P(),
            P(),
            P(),
            P(),
            P(),
        ),
        out_specs=(
            P("dp", ("seq", "head"), None),
            P("dp", ("seq", "head"), None),
            P(("dp", "seq"), "head"),
            P(("dp", "seq"), "head"),
            P(("dp", "seq"), "head"),
            P(("dp", "seq"), "head"),
            P(("dp", "seq"), "head"),
            P(("dp", "seq"), "head"),
            P(("dp", "seq"), "head"),
            P(("dp", "seq"), "head"),
            P(("dp", "seq"), "head"),
            P(("dp", "seq"), "head"),
            P(),
            P(),
            P(),
            P(),
            P(),
        ),
        check_vma=False,
    )
```

```python
import functools

import jax
import jax.numpy as jnp
from jax import lax
from jax.experimental import pallas as pl
from jax.experimental.pallas import tpu as pltpu
from jax.sharding import PartitionSpec as P

BLOCK = 64
epsilon = 1e-06
highest = lax.Precision.HIGH
f32 = jnp.float32


def mm(left, right, a=1, b=0):
    return lax.dot_general(
        left, right, (((a,), (b,)), ((), ())), precision=highest, preferred_element_type=f32
    )


def mm_nt(left, right):
    return mm(left, right, 1, 1)


def mm_tn(left, right):
    return mm(left, right, 0, 0)


def each(f, *lists):
    return [f(*items) for items in zip(*lists)]


def square_masks():
    rows = lax.broadcasted_iota(jnp.int32, (BLOCK, BLOCK), 0)
    cols = lax.broadcasted_iota(jnp.int32, (BLOCK, BLOCK), 1)
    return rows >= cols, rows > cols, (rows == cols).astype(f32)


def row_factor(values):
    return lax.rsqrt(jnp.sum(values * values, axis=-1, keepdims=True) + epsilon)


def split(values, count):
    return [values[i * BLOCK : (i + 1) * BLOCK] for i in range(count)]


def decays(col_ref, row_ref, count):
    lower, strict, identity = square_masks()
    out = []
    for i in range(count):
        c_col, b_col = col_ref[0, i, :, 0:1], col_ref[0, i, :, 1:2]
        c_row, b_row = row_ref[0, i, 0:1, :], row_ref[0, i, 1:2, :]
        fade = jnp.where(lower, jnp.exp(jnp.where(lower, c_col - c_row, 0.0)), 0.0)
        last = c_col[BLOCK - 1 : BLOCK, :]
        out.append((fade, fade * b_row, jnp.exp(c_col), jnp.exp(last - c_col), b_col, jnp.exp(last)))
    return [list(items) for items in zip(*out)]


def chains(counts):
    start, out = 0, []
    for count in counts:
        out.append(range(start, start + count))
        start += count
    return out


def solve_kernel(counts, q_ref, k_ref, v_ref, col_ref, row_ref, solver_ref, scores_ref, w_ref, vt_ref, qt_ref, m_ref, b_ref, mseg_ref, bseg_ref):
    count = sum(counts)
    lower, strict, identity = square_masks()
    query = q_ref[...]
    query = split(query * row_factor(query), count)
    key = k_ref[...]
    key = split(key * row_factor(key), count)
    value = split(v_ref[...], count)
    fade, ratio, growth, remain, beta, end = decays(col_ref, row_ref, count)
    power = each(lambda k, p: jnp.where(strict, -mm_nt(k, k) * p, 0.0), key, ratio)
    solver = [identity + p for p in power]
    for _ in range((BLOCK - 1).bit_length() - 1):
        power = each(lambda p: mm(p, p), power)
        solver = each(lambda s, p: s + mm(s, p), solver, power)
    scores = each(lambda q, k, p: mm_nt(q, k) * p, query, key, ratio)
    w = each(lambda s, g, k: mm(s, g * k), solver, growth, key)
    vt = each(mm, solver, value)
    qt = each(lambda g, q, a, x: g * q - mm(a, x), growth, query, scores, w)
    weighted = each(lambda k, r, b: k * (r * b), key, remain, beta)
    size = query[0].shape[1]
    wide = (
        lax.broadcasted_iota(jnp.int32, (size, size), 0)
        == lax.broadcasted_iota(jnp.int32, (size, size), 1)
    ).astype(f32)
    m = each(lambda e, k, x: e * wide - mm_tn(k, x), end, weighted, w)
    b = each(mm_tn, weighted, vt)
    for i in range(count):
        solver_ref[0, i] = solver[i]
        scores_ref[0, i] = scores[i]
        w_ref[0, i] = w[i]
        vt_ref[0, i] = vt[i]
        qt_ref[0, i] = qt[i]
        m_ref[0, i] = m[i]
        b_ref[0, i] = b[i]
    for j, chain in enumerate(chains(counts)):
        mseg_ref[0, j] = m[chain[0]]
        bseg_ref[0, j] = b[chain[0]]
        for i in chain[1:]:
            bseg_ref[0, j] = mm(m_ref[0, i], bseg_ref[0, j]) + b_ref[0, i]
            mseg_ref[0, j] = mm(m_ref[0, i], mseg_ref[0, j])


def output_kernel(counts, state_ref, m_ref, b_ref, qt_ref, scores_ref, vt_ref, gate_ref, gain_ref, states_ref, out_ref, gated_ref):
    count = sum(counts)
    states = [None] * count
    for j, chain in enumerate(chains(counts)):
        state = state_ref[0, j]
        for i in chain:
            states[i] = state
            states_ref[0, i] = state
            if i != chain[-1]:
                state = mm(m_ref[0, i], state) + b_ref[0, i]
    gain = gain_ref[...]
    outs = [mm(qt_ref[0, i], states[i]) + mm(scores_ref[0, i], vt_ref[0, i]) for i in range(count)]
    for i in range(count):
        rows = slice(i * BLOCK, (i + 1) * BLOCK)
        out = outs[i]
        gate = gate_ref[rows, :]
        scale = lax.rsqrt(jnp.mean(out * out, axis=-1, keepdims=True) + epsilon)
        out_ref[rows, :] = out
        gated_ref[rows, :] = (out * scale * gain * (gate * jax.nn.sigmoid(gate))).astype(jnp.bfloat16)


def output_grad_kernel(counts, grad_ref, gate_ref, out_ref, gain_ref, qt_ref, m_ref, out_grad_ref, gate_grad_ref, gain_grad_ref, d_ref, dseg_ref):
    count = sum(counts)
    gain = gain_ref[...]
    gain_grad = jnp.zeros_like(gain)
    grads = []
    for i in range(count):
        rows = slice(i * BLOCK, (i + 1) * BLOCK)
        grad, gate, out = grad_ref[rows, :], gate_ref[rows, :], out_ref[rows, :]
        scale = lax.rsqrt(jnp.mean(out * out, axis=-1, keepdims=True) + epsilon)
        unit = out * scale
        sig = jax.nn.sigmoid(gate)
        normed_grad = grad * (gate * sig)
        gate_grad_ref[rows, :] = (grad * (unit * gain) * (sig * (1.0 + gate * (1.0 - sig)))).astype(jnp.bfloat16)
        gain_grad = gain_grad + jnp.sum(normed_grad * unit, axis=0, keepdims=True)
        inner = normed_grad * gain
        out_grad = scale * (inner - unit * jnp.mean(unit * inner, axis=-1, keepdims=True))
        out_grad_ref[rows, :] = out_grad
        grads.append(out_grad)
    gain_grad_ref[0] = gain_grad
    d = [mm_tn(qt_ref[0, i], grads[i]) for i in range(count)]
    for i in range(count):
        d_ref[0, i] = d[i]
    for j, chain in enumerate(chains(counts)):
        dseg_ref[0, j] = d[chain[-1]]
        for i in list(chain)[-2::-1]:
            dseg_ref[0, j] = mm_tn(m_ref[0, i], dseg_ref[0, j]) + d_ref[0, i]


def unit_back(raw, grad):
    factor = row_factor(raw)
    unit = raw * factor
    return factor * (grad - unit * jnp.sum(unit * grad, axis=-1, keepdims=True))


def grads_kernel(counts, q_ref, k_ref, col_ref, row_ref, solver_ref, scores_ref, w_ref, vt_ref, m_ref, d_ref, states_ref, out_grad_ref, gate_ref, later_ref, slim_ref, joint_ref, col_grad_ref, row_grad_ref):
    count = sum(counts)
    span = range(count)
    lower, strict, identity = square_masks()
    raw_q, raw_k = split(q_ref[...], count), split(k_ref[...], count)
    query = [x * row_factor(x) for x in raw_q]
    key = [x * row_factor(x) for x in raw_k]
    fade, ratio, growth, remain, beta, end = decays(col_ref, row_ref, count)
    out_grad = split(out_grad_ref[...], count)
    later = [None] * count
    for j, chain in enumerate(chains(counts)):
        state = later_ref[0, j]
        for i in list(chain)[::-1]:
            later[i] = state
            if i != chain[0]:
                state = mm_tn(m_ref[0, i], state) + d_ref[0, i]
    states = [states_ref[0, i] for i in span]
    update = [vt_ref[0, i] - mm(w_ref[0, i], states[i]) for i in span]
    update_grad = [
        mm_tn(scores_ref[0, i], out_grad[i]) + mm(key[i] * (remain[i] * beta[i]), later[i]) for i in span
    ]
    solved = [mm_tn(solver_ref[0, i], update_grad[i]) for i in span]
    scores_grad = each(mm_nt, out_grad, update)
    inner_grad = each(lambda y, u: jnp.where(strict, -mm_nt(y, u), 0.0), solved, update)
    query_dot = each(mm_nt, query, key)
    keys_dot = each(mm_nt, key, key)
    from_out = each(mm_nt, out_grad, states)
    from_solved = each(mm_nt, solved, states)
    from_update = each(mm_nt, update, later)
    weighted_scores = each(lambda p, x: p * x, ratio, scores_grad)
    weighted_inner = each(lambda p, x: p * x, ratio, inner_grad)
    q_grad = [growth[i] * from_out[i] + mm(weighted_scores[i], key[i]) for i in span]
    k_grad = [
        mm_tn(weighted_scores[i], query[i])
        + (remain[i] * beta[i]) * from_update[i]
        - growth[i] * from_solved[i]
        + mm(weighted_inner[i], key[i])
        + mm_tn(weighted_inner[i], key[i])
        for i in span
    ]
    last_row = (lax.broadcasted_iota(jnp.int32, (BLOCK, 1), 0) == BLOCK - 1).astype(f32)
    for i in span:
        rows = slice(i * BLOCK, (i + 1) * BLOCK)
        start = 0
        for grad in (unit_back(raw_q[i], q_grad[i]), unit_back(raw_k[i], k_grad[i]), solved[i]):
            place = slice(start, start + grad.shape[1])
            start += grad.shape[1]
            slim_ref[rows, place] = grad.astype(jnp.bfloat16)
            joint_ref[rows, place] = grad.astype(jnp.bfloat16)
        joint_ref[rows, start:] = gate_ref[rows, :]
        faded = fade[i] * (scores_grad[i] * query_dot[i] + inner_grad[i] * keys_dot[i])
        b_row = row_ref[0, i, 1:2, :]
        growth_grad = jnp.sum(query[i] * from_out[i] - key[i] * from_solved[i], axis=-1, keepdims=True)
        weight_grad = jnp.sum(key[i] * from_update[i], axis=-1, keepdims=True)
        pulled = remain[i] * beta[i] * weight_grad
        tail = jnp.sum(pulled, axis=0, keepdims=True) + end[i] * jnp.sum(
            jnp.sum(later[i] * states[i], axis=-1, keepdims=True), axis=0, keepdims=True
        )
        c_grad = jnp.sum(faded * b_row, axis=-1, keepdims=True) + growth[i] * growth_grad - pulled + last_row * tail
        col_grad_ref[0, i, :, 0:1] = c_grad
        col_grad_ref[0, i, :, 1:2] = remain[i] * weight_grad
        row_grad_ref[0, i] = jnp.sum(faded, axis=0, keepdims=True)


def whole(shape):
    return pl.BlockSpec((1,) + tuple(shape[1:]), lambda j: (j,) + (0,) * (len(shape) - 1))


def columns(rows, width, first=0, step=1):
    return pl.BlockSpec((rows, width), lambda j: (0, step * j + first))


def shaped(shape, dtype=f32):
    return jax.ShapeDtypeStruct(shape, dtype)


def call(kernel, counts, heads, inputs, outputs, flops):
    moved = sum(x.size * x.dtype.itemsize for x, _ in inputs) + sum(
        x.size * x.dtype.itemsize for x, _ in outputs
    )
    return pl.pallas_call(
        functools.partial(kernel, counts),
        grid=(heads,),
        in_specs=[s for _, s in inputs],
        out_specs=[s for _, s in outputs],
        out_shape=[x for x, _ in outputs],
        compiler_params=pltpu.CompilerParams(vmem_limit_bytes=48 << 20),
        cost_estimate=pl.CostEstimate(flops=flops, bytes_accessed=moved, transcendentals=0),
    )(*[x for x, _ in inputs])


def per_head(heads, *shape, dtype=f32):
    s = (heads,) + shape
    return shaped(s, dtype), whole(s)


def flat(array, width, first=0, step=1):
    return array, columns(array.shape[0], width, first, step)


def stacked(array):
    return array, whole(array.shape)


def solve(counts, heads, proj, col, row):
    n, dk, dv = sum(counts), 128, 256
    return call(
        solve_kernel, counts, heads,
        [flat(proj, dk, 0, 4), flat(proj, dk, 1, 4), flat(proj, dv, 1, 2), stacked(col), stacked(row)],
        [per_head(heads, n, BLOCK, BLOCK), per_head(heads, n, BLOCK, BLOCK), per_head(heads, n, BLOCK, dk),
         per_head(heads, n, BLOCK, dv), per_head(heads, n, BLOCK, dk), per_head(heads, n, dk, dk),
         per_head(heads, n, dk, dv), per_head(heads, len(counts), dk, dk), per_head(heads, len(counts), dk, dv)],
        heads * n * 100_000_000,
    )


def outputs_of(counts, heads, state, m, b, qt, scores, vt, gate_pre, gain):
    n, dk, dv = sum(counts), 128, 256
    rows = gate_pre.shape[0]
    cols = columns(rows, dv)
    return call(
        output_kernel, counts, heads,
        [stacked(state), stacked(m), stacked(b), stacked(qt), stacked(scores), stacked(vt), flat(gate_pre, dv),
         (gain, pl.BlockSpec((1, dv), lambda j: (0, 0)))],
        [per_head(heads, n, dk, dv), (shaped((rows, heads * dv)), cols), (shaped((rows, heads * dv), jnp.bfloat16), cols)],
        heads * n * 50_000_000,
    )


def output_grads_of(counts, heads, grad, gate_pre, outs, gain, qt, m):
    n, dk, dv = sum(counts), 128, 256
    rows = gate_pre.shape[0]
    cols = columns(rows, dv)
    return call(
        output_grad_kernel, counts, heads,
        [flat(grad, dv), flat(gate_pre, dv), flat(outs, dv), (gain, pl.BlockSpec((1, dv), lambda j: (0, 0))), stacked(qt), stacked(m)],
        [(shaped((rows, heads * dv)), cols), (shaped((rows, heads * dv), jnp.bfloat16), cols),
         per_head(heads, 1, dv), per_head(heads, n, dk, dv), per_head(heads, len(counts), dk, dv)],
        heads * n * 50_000_000,
    )


def input_grads_of(counts, heads, proj, col, row, solver, scores, w, vt, m, d, states, out_grad, gate_grad, later):
    n, dk, dv = sum(counts), 128, 256
    rows = proj.shape[0]
    return call(
        grads_kernel, counts, heads,
        [flat(proj, dk, 0, 4), flat(proj, dk, 1, 4), stacked(col), stacked(row), stacked(solver), stacked(scores), stacked(w),
         stacked(vt), stacked(m), stacked(d), stacked(states), flat(out_grad, dv), flat(gate_grad, dv), stacked(later)],
        [(shaped((rows, heads * (2 * dk + dv)), jnp.bfloat16), columns(rows, 2 * dk + dv)),
         (shaped((rows, heads * (2 * dk + 2 * dv)), jnp.bfloat16), columns(rows, 2 * dk + 2 * dv)),
         per_head(heads, n, BLOCK, 2), per_head(heads, n, 1, BLOCK)],
        heads * n * 150_000_000,
    )


def feed_kernel(stage_ref, x_ref, k_ref, xs_ref, ks_ref, w1_ref, w3_ref, w2_ref, t1_ref, t3_ref, t2_ref, back_ref, feed_ref, main_ref, main_other_ref, tail_ref, tail_other_ref, active_s, gate_s, up_s, sums_s):
    step, chunk = pl.program_id(0), pl.program_id(1)
    own, width = sums_s.shape[0], sums_s.shape[1] // 2
    groups, rows_each = back_ref.shape[0], back_ref.shape[1]
    near, piece = x_ref.shape[1] // own, x_ref.shape[2]
    stage = stage_ref[0]
    here = pl.ds(pl.multiple_of(lax.rem(stage, near) * own, own), own)

    @pl.when((step == 0) & (chunk == 0))
    def _():
        sums_s[...] = jnp.zeros_like(sums_s)

    def work(w1, w3, w2, out_refs):
        wide = w1.shape[1]
        gate, up, grad = (
            sum(
                jnp.dot(rows[i], w[i * piece : (i + 1) * piece, :], preferred_element_type=f32)
                for i in range(rows.shape[0])
            )
            for rows, w in ((x_ref, w1), (x_ref, w3), (k_ref, w2))
        )
        sig = jax.nn.sigmoid(gate)
        silu = gate * sig
        active = (silu * up).astype(jnp.bfloat16)
        gate_grad = (grad * up * (sig * (1.0 + gate * (1.0 - sig)))).astype(jnp.bfloat16)
        up_grad = (grad * silu).astype(jnp.bfloat16)
        active_s[:, :wide] = active
        gate_s[:, :wide] = gate_grad
        up_s[:, :wide] = up_grad

        @pl.when(chunk == stage // near)
        def _():
            sums_s[:, width:] += contract_cols(active_s[here, :wide], w2[...])
            sums_s[:, :width] += contract_cols(gate_s[here, :wide], w1[...])
            sums_s[:, :width] += contract_cols(up_s[here, :wide], w3[...])

        parts = (
            contract_rows(gate_grad, xs_ref[...]),
            contract_rows(up_grad, xs_ref[...]),
            contract_rows(active, ks_ref[...]),
        )
        for i, p in enumerate(parts):
            place = slice(i * wide, (i + 1) * wide)
            quota = p.shape[1] // 2

            @pl.when(chunk == 0)
            def _():
                out_refs[0][place, :] = p[:, :quota]
                out_refs[1][place, :] = p[:, quota:]

            @pl.when(chunk > 0)
            def _():
                out_refs[0][place, :] += p[:, :quota]
                out_refs[1][place, :] += p[:, quota:]

    work(w1_ref, w3_ref, w2_ref, (main_ref, main_other_ref))

    @pl.when(step == pl.num_programs(0) - 1)
    def _():
        work(t1_ref, t3_ref, t2_ref, (tail_ref, tail_other_ref))

    @pl.when((step == pl.num_programs(0) - 1) & (chunk == pl.num_programs(1) - 1))
    def _():
        for g in range(groups):
            rows = slice(g * rows_each, (g + 1) * rows_each)
            back_ref[g] = sums_s[rows, :width].astype(jnp.bfloat16)
            feed_ref[g] = sums_s[rows, width:].astype(jnp.bfloat16)


def feed_forward(stage, rows, grads, row_cols, grad_cols, weights, groups, rows_each):
    pieces, positions, piece = rows.shape
    width, own = pieces * piece, groups * rows_each
    picked = row_cols.shape[1]
    tile, rest = 256, 128
    steps = (weights.shape[1] - 3 * rest) // (3 * tile)
    chunk = min(positions, 4 * own)
    first_tail = 3 * steps * tile // rest
    grid = (steps, positions // chunk)
    tokens = pl.BlockSpec((pieces, chunk, piece), lambda i, t, s: (0, t, 0))
    columns_of = pl.BlockSpec((chunk, picked), lambda i, t, s: (t, 0))

    def main_of(n):
        return pl.BlockSpec((width, tile), lambda i, t, s: (0, n * steps + i))

    def tail_of(n):
        return pl.BlockSpec((width, rest), lambda i, t, s: (0, first_tail + n))

    def fixed(*shape):
        return pl.BlockSpec(shape, lambda i, t, s: (0, 0))

    flops = 2 * positions * width * weights.shape[1] + 2 * own * width * weights.shape[1] + 2 * positions * picked * weights.shape[1]
    return pl.pallas_call(
        feed_kernel,
        grid_spec=pltpu.PrefetchScalarGridSpec(
            num_scalar_prefetch=1,
            grid=grid,
            in_specs=[tokens, tokens, columns_of, columns_of, main_of(0), main_of(1), main_of(2), tail_of(0), tail_of(1), tail_of(2)],
            out_specs=[
                pl.BlockSpec((groups, rows_each, width), lambda i, t, s: (0, 0, 0)),
                pl.BlockSpec((groups, rows_each, width), lambda i, t, s: (0, 0, 0)),
                pl.BlockSpec((3 * tile, picked // 2), lambda i, t, s: (i, 0)),
                pl.BlockSpec((3 * tile, picked // 2), lambda i, t, s: (i, 0)),
                fixed(3 * rest, picked // 2),
                fixed(3 * rest, picked // 2),
            ],
            scratch_shapes=[pltpu.VMEM((chunk, tile), jnp.bfloat16)] * 3 + [pltpu.VMEM((own, 2 * width), f32)],
        ),
        out_shape=[
            shaped((groups, rows_each, width), jnp.bfloat16),
            shaped((groups, rows_each, width), jnp.bfloat16),
            shaped((3 * tile * steps, picked // 2)),
            shaped((3 * tile * steps, picked // 2)),
            shaped((3 * rest, picked // 2)),
            shaped((3 * rest, picked // 2)),
        ],
        compiler_params=pltpu.CompilerParams(
            dimension_semantics=("arbitrary", "arbitrary"), vmem_limit_bytes=56 << 20
        ),
        cost_estimate=pl.CostEstimate(
            flops=flops, bytes_accessed=2 * weights.size + 8 * positions * width, transcendentals=0
        ),
    )(stage, rows, grads, row_cols, grad_cols, weights, weights, weights, weights, weights, weights)


def projection_kernel(heads, cols_ref, joint_ref, q_ref, k_ref, v_ref, g_ref):
    joined = jnp.dot(cols_ref[...], joint_ref[...], preferred_element_type=f32)
    start = 0
    for j in range(heads):
        for ref in (q_ref, k_ref, v_ref, g_ref):
            size = ref.shape[1] // heads
            ref[:, j * size : (j + 1) * size] = joined[:, start : start + size]
            start += size


def projection_grads(cols, joint_all, heads, sizes):
    quota, positions = cols.shape
    wide = joint_all.shape[1]
    return pl.pallas_call(
        functools.partial(projection_kernel, heads),
        grid=(2,),
        in_specs=[
            pl.BlockSpec((quota, positions), lambda c: (0, 0)),
            pl.BlockSpec((positions, wide), lambda c: (c, 0)),
        ],
        out_specs=[pl.BlockSpec((quota, n), lambda c: (0, c)) for n in sizes],
        out_shape=[shaped((quota, 2 * n)) for n in sizes],
        compiler_params=pltpu.CompilerParams(vmem_limit_bytes=56 << 20),
        cost_estimate=pl.CostEstimate(
            flops=4 * quota * positions * wide, bytes_accessed=2 * joint_all.size, transcendentals=0
        ),
    )(cols, joint_all)


def pack_kernel(heads, q_ref, k_ref, v_ref, a_ref, b_ref, out_ref):
    start = 0
    for j in range(heads):
        for ref in (q_ref, k_ref, v_ref):
            size = ref.shape[1] // heads
            out_ref[:, start : start + size] = ref[:, j * size : (j + 1) * size].astype(jnp.bfloat16)
            start += size
    out_ref[:, start:] = jnp.concatenate([a_ref[...], b_ref[...]], axis=1).astype(jnp.bfloat16)


def pack_weights(heads, *weights):
    rows, wide = weights[0].shape[0], sum(w.shape[1] for w in weights)
    step = min(rows, 64)
    return pl.pallas_call(
        functools.partial(pack_kernel, heads),
        grid=(rows // step,),
        in_specs=[pl.BlockSpec((step, w.shape[1]), lambda i: (i, 0)) for w in weights],
        out_specs=pl.BlockSpec((step, wide), lambda i: (i, 0)),
        out_shape=shaped((rows, wide), jnp.bfloat16),
        cost_estimate=pl.CostEstimate(flops=rows * wide, bytes_accessed=6 * rows * wide, transcendentals=0),
    )(*weights)


QUARTERS = 4


def swap(array):
    return lax.ppermute(array, "dp", [(0, 1), (1, 0)])


def relay(mats, offsets, forward):
    size = lax.axis_size("seq")
    entering = jnp.zeros_like(offsets)
    leaving = offsets
    for step in range(size - 1):
        route = [(step, step + 1)] if forward else [(size - 1 - step, size - 2 - step)]
        got = jnp.stack([lax.ppermute(head, "seq", route) for head in leaving])
        entering = entering + got
        if step < size - 2:
            leaving = jnp.matmul(mats, got, precision=highest) + offsets
    return entering, leaving


def together(*arrays):
    return lax.optimization_barrier(arrays)


def everyone(part):
    return lax.all_gather(part, ("dp", "seq"), axis=0, tiled=True)


def share(rows):
    wide = jnp.broadcast_to(rows[None], (lax.axis_size("head"),) + rows.shape)
    return lax.all_to_all(wide, "head", split_axis=0, concat_axis=0, tiled=True)


def from_others(piece):
    size = lax.axis_size("head")
    return [lax.ppermute(piece(k), "head", [(i, i ^ k) for i in range(size)]) for k in range(1, size)]


def in_group_order(pieces):
    group = lax.axis_index("head")
    stacked = jnp.stack(pieces)
    return jnp.stack(
        [lax.dynamic_index_in_dim(stacked, g ^ group, 0, keepdims=False) for g in range(lax.axis_size("head"))]
    )


def add_by_permutes(vector):
    near, far, across = from_others(lambda k: vector)
    return (vector + near) + (far + across)


def add_parts_by_permutes(parts):
    group = lax.axis_index("head")

    def piece(k):
        return lax.dynamic_index_in_dim(parts, group ^ k, 0, keepdims=False).astype(jnp.bfloat16)

    near, far, across = [got.astype(f32) for got in from_others(piece)]
    return (piece(0).astype(f32) + near) + (far + across)


def add_parts(parts):
    got = lax.all_to_all(parts.astype(jnp.bfloat16), "head", split_axis=0, concat_axis=0, tiled=True)
    return jnp.sum(got.astype(f32), axis=0)


def contract_rows(left, right):
    return lax.dot_general(left, right, (((0,), (0,)), ((), ())), preferred_element_type=f32)


def contract_cols(left, right):
    return lax.dot_general(left, right, (((1,), (1,)), ((), ())), preferred_element_type=f32)


def product(left, right):
    return jnp.dot(left, right, preferred_element_type=f32)


def rms_scale(values, gain):
    return values * lax.rsqrt(jnp.mean(values * values, axis=-1, keepdims=True) + epsilon) * gain


def swiglu(gate_in, up_in):
    return jax.nn.silu(gate_in) * up_in


def on_device(
    activations,
    cotangent,
    lengths,
    query_weight,
    key_weight,
    value_weight,
    gate_weight,
    alpha_weight,
    beta_weight,
    out_weight,
    swiglu_gate,
    swiglu_value,
    swiglu_down,
    mixer_gain,
    feed_gain,
    head_gain,
    decay_rate,
    beta_bias,
):
    bf16 = jnp.bfloat16
    core, stage, group = lax.axis_index("dp"), lax.axis_index("seq"), lax.axis_index("head")
    stages, groups = lax.axis_size("seq"), lax.axis_size("head")
    width = activations.shape[2]
    rows0 = activations.shape[1]
    rows1 = rows0 // QUARTERS
    own0, own1 = rows0 // (2 * groups), rows1 // (2 * groups)
    own = own0 + own1
    quota = width // (2 * stages)
    heads = alpha_weight.shape[1] // 2
    counts = (rows0 // BLOCK, rows1 // BLOCK)
    assert groups == QUARTERS and stages % QUARTERS == 0 and rows1 % BLOCK == 0
    first = core == 0

    def part(array, size, axis, offset=0):
        return lax.dynamic_slice_in_dim(array, offset + core * size, size, axis)

    dk, dv = query_weight.shape[1] // 2, value_weight.shape[1] // 2
    slim = 2 * dk + dv
    mixer_full = everyone(pack_weights(2 * heads, query_weight, key_weight, value_weight, alpha_weight, beta_weight))
    gates_full = everyone(jnp.concatenate([gate_weight, out_weight], axis=1).astype(bf16))
    hidden_units = swiglu_gate.shape[1]
    even = hidden_units // 256 * 256
    odd = hidden_units - even
    assert 0 < odd <= 128
    three = (swiglu_gate, swiglu_value, swiglu_down)
    spare = ((0, 0), (0, 128 - odd))
    feed_full = everyone(
        jnp.concatenate([w[:, :even] for w in three] + [jnp.pad(w[:, even:], spare) for w in three], axis=1).astype(bf16)
    )

    def chip_rows(rows):
        arrived = jnp.zeros((rows1, width), bf16)
        for b in range(QUARTERS):
            route = [(stages + a, stages + QUARTERS * a + b) for a in range(stages // QUARTERS)]
            arrived = arrived + lax.ppermute(rows[b * rows1 : (b + 1) * rows1], ("dp", "seq"), route)
        near0 = lax.ppermute(rows, "dp", [(0, 1)])
        near1 = lax.ppermute(arrived, "dp", [(1, 0)])
        return jnp.concatenate([jnp.where(first, rows, near0), jnp.where(first, near1, arrived)], axis=0)

    inputs = chip_rows(activations[0])
    inputs, late = together(inputs, cotangent[0])
    inputs = inputs.astype(f32)
    spots0 = stage * rows0 + lax.broadcasted_iota(jnp.int32, (rows0, 1), 0)
    spots1 = stage * rows1 + lax.broadcasted_iota(jnp.int32, (rows1, 1), 0)
    mask = jnp.concatenate([spots0 < lengths[0], spots1 < lengths[1]], axis=0).astype(f32)
    masked = (chip_rows(late).astype(f32) * mask).astype(bf16)

    def by_owner(rows):
        wide = rows.shape[1]
        r0 = rows[:rows0].reshape(groups, 2, own0, wide)
        r1 = rows[rows0:].reshape(groups, 2, own1, wide)
        return jnp.concatenate([r0, r1], axis=2).swapaxes(0, 1)

    def in_time(owned):
        wide = owned.shape[3]
        turned = owned.swapaxes(0, 1)
        return jnp.concatenate(
            [turned[:, :, :own0].reshape(rows0, wide), turned[:, :, own0:].reshape(rows1, wide)], axis=0
        )

    def of_core(owned, which):
        return lax.dynamic_index_in_dim(owned, which, 0, keepdims=False)

    def of_group(rows):
        return lax.dynamic_index_in_dim(rows, group, 0, keepdims=False)

    def add_rows(partial):
        owned = by_owner(partial)
        return add_parts_by_permutes(of_core(owned, core) + swap(of_core(owned, 1 - core)))

    def meet_columns(rows):
        return lax.all_to_all(rows, ("dp", "seq"), split_axis=1, concat_axis=0, tiled=True)

    def owned_columns(met, share_rows):
        got = share_rows(met).reshape(groups, 2, stages, own, quota).transpose(2, 0, 1, 3, 4)
        return jnp.concatenate(
            [got[:, :, :, :own0].reshape(stages, rows0, quota), got[:, :, :, own0:].reshape(stages, rows1, quota)], axis=1
        ).reshape(stages * (rows0 + rows1), quota)

    def across_stages(rows):
        wide = jnp.broadcast_to(rows[None], (stages,) + rows.shape)
        met = lax.all_to_all(wide, "seq", split_axis=0, concat_axis=0, tiled=True)
        return met.reshape(stages * rows.shape[0], rows.shape[1])

    def own_columns(rows):
        pieces, positions, piece = rows.shape
        both = []
        for which in (core, 1 - core):
            start = (which * stages + stage) * quota
            both.append(lax.dynamic_slice(rows, (start // piece, 0, start % piece), (1, positions, quota))[0])
        return jnp.concatenate(both, axis=1)

    own_rows = of_group(of_core(by_owner(inputs), core))
    own_mask = of_group(of_core(by_owner(mask), core))
    tokens_masked = of_core(by_owner(masked), core)
    own_masked = of_group(tokens_masked).astype(f32)
    quarter = width // groups
    masked_met = across_stages(
        lax.dynamic_slice_in_dim(tokens_masked.reshape(groups * own, width), group * quarter, quarter, 1)
    )

    factor1 = lax.rsqrt(jnp.mean(inputs * inputs, axis=-1, keepdims=True) + epsilon)
    unit1 = inputs * factor1
    normed = rms_scale(inputs, mixer_gain).astype(bf16)
    normed_cols = owned_columns(meet_columns(of_group(of_core(by_owner(normed), core))), share).T
    mixer_full, masked_met, normed_cols = together(mixer_full, masked_met, normed_cols)
    mixer_w = part(mixer_full, slim, 1)
    gate_w = part(gates_full, dv, 1)
    out_w = part(gates_full, dv, 1, 2 * dv)
    rates_w = mixer_full[:, 2 * slim :]
    proj = product(normed, mixer_w)
    small_pre = product(normed, rates_w)
    gate_pre = product(normed, gate_w)
    alpha_pre = part(small_pre, heads, 1)
    beta_pre = part(small_pre, heads, 1, 2 * heads)
    head0 = (2 * group + core) * heads
    rates = lax.dynamic_slice_in_dim(decay_rate, head0, heads)
    biases = lax.dynamic_slice_in_dim(beta_bias, head0, heads)
    blocks = sum(counts)

    def to_blocks(array):
        return array.T.reshape(heads, blocks, BLOCK)

    def from_blocks(array):
        return array.reshape(heads, blocks * BLOCK).T

    soft = jax.nn.softplus(alpha_pre)
    beta = jax.nn.sigmoid(beta_pre + biases)
    beta_b = to_blocks(beta)
    upto = (
        lax.broadcasted_iota(jnp.int32, (BLOCK, BLOCK), 0) <= lax.broadcasted_iota(jnp.int32, (BLOCK, BLOCK), 1)
    ).astype(f32)
    sums = jnp.matmul(to_blocks(-rates * soft), upto, precision=highest)
    col = jnp.stack([sums, beta_b], axis=-1)
    row = jnp.stack([sums, beta_b], axis=-2)
    solver, scores, w, vt, qt, m, b, mseg, bseg = solve(counts, heads, proj, col, row)
    state_in, unused_carry = relay(mseg, bseg, True)
    state_in, masked_all = together(state_in, share(masked_met))
    gain_row = head_gain[None]
    states, outs, gated = outputs_of(counts, heads, state_in, m, b, qt, scores, vt, gate_pre, gain_row)
    mixed = add_rows(contract_cols(gated, out_w))
    hidden = own_rows + mixed

    normed2, norm2_back = jax.vjp(rms_scale, hidden, feed_gain)
    feed_in = share(
        across_stages(lax.all_to_all(normed2.astype(bf16), "head", split_axis=1, concat_axis=0, tiled=True))
    )
    back_part, feed_part, main_own, main_other, tail_own, tail_other = feed_forward(
        stage[None], feed_in, masked_all, own_columns(feed_in), own_columns(masked_all), feed_full, groups, own
    )
    normed2_grad, main_other, tail_other = together(add_parts(back_part), swap(main_other), swap(tail_other))
    hidden_back, feed_gain_grad = norm2_back(normed2_grad)
    hidden_grad = own_masked + hidden_back
    mixed_own = hidden_grad.astype(bf16)
    mixed_half = share(mixed_own)
    other_half = swap(mixed_half)
    mixed_in = in_time(
        jnp.stack([jnp.where(first, mixed_half, other_half), jnp.where(first, other_half, mixed_half)])
    )

    gated_all = everyone(gated)
    gated_grad = product(mixed_in, out_w)
    mixed_late, unused_rows = together(mixed_own, mixed_in)
    mixed_met = meet_columns(mixed_late)
    gated_grad, gated_all = together(gated_grad, gated_all)
    outs_grad, gate_pre_low, gain_grads, d, dseg = output_grads_of(
        counts, heads, gated_grad, gate_pre, outs, gain_row, qt, m
    )
    dseg, mixed_met = together(dseg, mixed_met)
    later, unused_carry = relay(jnp.swapaxes(mseg, 2, 3), dseg, False)

    half = stages * (rows0 + rows1)
    gate_back = contract_cols(gate_pre_low, gate_w)
    later, gate_back = together(later, gate_back)
    slim_low, joint_low, col_grad, row_grad = input_grads_of(
        counts, heads, proj, col, row, solver, scores, w, vt, m, d, states, outs_grad, gate_pre_low, later
    )
    joint_all = everyone(joint_low)
    slim_low, mixed_met = together(slim_low, mixed_met)
    mixed_pieces = from_others(lambda k: mixed_met)
    sums_grad = col_grad[..., 0] - row_grad[:, :, 0] * beta_b
    decay_back = from_blocks(jnp.matmul(sums_grad, upto.T, precision=highest))
    beta_back = beta * (1.0 - beta) * from_blocks(col_grad[..., 1] + row_grad[:, :, 0])
    rates_grad = -jnp.sum(soft * decay_back, axis=0)
    biases_grad = jnp.sum(beta_back, axis=0)
    alpha_back = -rates * jax.nn.sigmoid(alpha_pre) * decay_back
    small_low = jnp.concatenate([alpha_back, beta_back], axis=1).astype(bf16)
    blank = jnp.zeros((rows0 + rows1, 4 * heads), bf16)
    spread = lax.dynamic_update_slice(blank, small_low[:, :heads], (0, core * heads))
    spread = lax.dynamic_update_slice(spread, small_low[:, heads:], (0, (2 + core) * heads))
    total = gate_back + contract_cols(slim_low, mixer_w) + contract_cols(spread, rates_w)
    normed_grad = add_rows(total)
    mixer_gain_part = jnp.sum(total * unit1, axis=0)
    normed_grad, small_late, mixer_gain_part, feed_part, main_own, main_other, tail_own, tail_other, *mixed_pieces = together(
        normed_grad, small_low, mixer_gain_part, feed_part, main_own, main_other, tail_own, tail_other, mixed_met, *mixed_pieces
    )
    feed = add_parts_by_permutes(feed_part)
    mixed_cols = owned_columns(mixed_met, lambda rows: in_group_order(mixed_pieces))
    outputs_own = (own_mask * (hidden + feed)).astype(bf16)
    out_grad = jnp.concatenate(
        [contract_rows(mixed_cols, gated_all[:half]), contract_rows(mixed_cols, gated_all[half:])], axis=1
    )
    unused_rows, norm1_back = jax.vjp(lambda v: rms_scale(v, mixer_gain), own_rows)
    input_own = (hidden_grad + norm1_back(normed_grad)[0]).astype(bf16)

    main_own, tail_own = main_own + main_other, tail_own + tail_other

    def feed_grad(n):
        pieces = [main_own[(3 * i + n) * 256 : (3 * i + n + 1) * 256] for i in range(even // 256)]
        return jnp.concatenate(pieces + [tail_own[n * 128 : n * 128 + odd]], axis=0)

    feed_gate_grad, feed_value_grad, down_grad = feed_grad(0), feed_grad(1), feed_grad(2)

    small_rows = contract_rows(small_late, normed).reshape(2 * heads, 2 * stages, quota).swapaxes(0, 1)
    total_heads = decay_rate.shape[0]
    none = jnp.zeros((total_heads,), f32)
    vector = jnp.concatenate(
        [
            mixer_gain_part,
            feed_gain_grad,
            jnp.sum(gain_grads, axis=(0, 1)),
            lax.dynamic_update_slice(none, rates_grad, (head0,)),
            lax.dynamic_update_slice(none, biases_grad, (head0,)),
        ]
    )
    mail = jnp.concatenate(
        [
            small_rows.reshape(2 * stages, 2 * heads * quota),
            jnp.broadcast_to(vector[None], (2 * stages, vector.shape[0])),
        ],
        axis=1,
    )
    mail = lax.all_to_all(mail, ("dp", "seq"), split_axis=0, concat_axis=0, tiled=True)
    mail, out_grad = together(mail, out_grad)
    small_rows = jnp.sum(mail[:, : 2 * heads * quota].reshape(2, stages, 2, heads, quota), axis=1)
    alpha_grad = small_rows[:, 0].reshape(2 * heads, quota).T
    beta_grad = small_rows[:, 1].reshape(2 * heads, quota).T
    small = add_by_permutes(jnp.sum(mail[:, 2 * heads * quota :], axis=0))
    joint_all, out_grad = together(joint_all, out_grad)
    query_grad, key_grad, value_grad, gate_grad = projection_grads(normed_cols, joint_all, heads, (dk, dk, dv, dv))

    edges = [width, 2 * width, 2 * width + head_gain.shape[0], 2 * width + head_gain.shape[0] + total_heads]

    def place(rows):
        r0, r1 = rows[:own0], rows[own0:]
        out0 = jnp.concatenate([r0, lax.ppermute(r0, "dp", [(1, 0)])], axis=0)
        pair = jnp.concatenate([lax.ppermute(r1, "dp", [(0, 1)]), r1], axis=0)
        routes = [
            [
                ((stages + QUARTERS * a + b) * groups + k, (stages + a) * groups + b)
                for a in range(stages // QUARTERS)
                for b in range(QUARTERS)
            ]
            for k in range(groups)
        ]
        out1 = jnp.concatenate([lax.ppermute(pair, ("dp", "seq", "head"), route) for route in routes], axis=0)
        return jnp.where(first, out0, out1)[None]

    placed = place(jnp.concatenate([outputs_own, input_own], axis=1))
    return (
        placed[:, :, :width],
        placed[:, :, width:],
        query_grad,
        key_grad,
        value_grad,
        gate_grad,
        alpha_grad,
        beta_grad,
        out_grad,
        feed_gate_grad.T,
        feed_value_grad.T,
        down_grad.T,
        small[: edges[0]],
        small[edges[0] : edges[1]],
        small[edges[1] : edges[2]],
        small[edges[2] : edges[3]],
        small[edges[3] :],
    )


def solution(mesh):
    return jax.shard_map(
        on_device,
        mesh=mesh,
        in_specs=(
            P("dp", "seq", None),
            P("dp", "seq", None),
            P(),
            P(("dp", "seq"), "head"),
            P(("dp", "seq"), "head"),
            P(("dp", "seq"), "head"),
            P(("dp", "seq"), "head"),
            P(("dp", "seq"), "head"),
            P(("dp", "seq"), "head"),
            P(("dp", "seq"), "head"),
            P(("dp", "seq"), "head"),
            P(("dp", "seq"), "head"),
            P(("dp", "seq"), "head"),
            P(),
            P(),
            P(),
            P(),
            P(),
        ),
        out_specs=(
            P("dp", ("seq", "head"), None),
            P("dp", ("seq", "head"), None),
            P(("dp", "seq"), "head"),
            P(("dp", "seq"), "head"),
            P(("dp", "seq"), "head"),
            P(("dp", "seq"), "head"),
            P(("dp", "seq"), "head"),
            P(("dp", "seq"), "head"),
            P(("dp", "seq"), "head"),
            P(("dp", "seq"), "head"),
            P(("dp", "seq"), "head"),
            P(("dp", "seq"), "head"),
            P(),
            P(),
            P(),
            P(),
            P(),
        ),
        check_vma=False,
    )
```

```python
import functools

import jax
import jax.numpy as jnp
from jax import lax
from jax.experimental import pallas as pl
from jax.experimental.pallas import tpu as pltpu
from jax.sharding import PartitionSpec as P

BLOCK = 64
epsilon = 1e-06
highest = lax.Precision.HIGH
f32 = jnp.float32


def mm(left, right, a=1, b=0):
    return lax.dot_general(
        left, right, (((a,), (b,)), ((), ())), precision=highest, preferred_element_type=f32
    )


def mm_nt(left, right):
    return mm(left, right, 1, 1)


def mm_tn(left, right):
    return mm(left, right, 0, 0)


def each(f, *lists):
    return [f(*items) for items in zip(*lists)]


def square_masks():
    rows = lax.broadcasted_iota(jnp.int32, (BLOCK, BLOCK), 0)
    cols = lax.broadcasted_iota(jnp.int32, (BLOCK, BLOCK), 1)
    return rows >= cols, rows > cols, (rows == cols).astype(f32)


def row_factor(values):
    return lax.rsqrt(jnp.sum(values * values, axis=-1, keepdims=True) + epsilon)


def split(values, count):
    return [values[i * BLOCK : (i + 1) * BLOCK] for i in range(count)]


def decays(col_ref, row_ref, count):
    lower, strict, identity = square_masks()
    out = []
    for i in range(count):
        c_col, b_col = col_ref[0, i, :, 0:1], col_ref[0, i, :, 1:2]
        c_row, b_row = row_ref[0, i, 0:1, :], row_ref[0, i, 1:2, :]
        fade = jnp.where(lower, jnp.exp(jnp.where(lower, c_col - c_row, 0.0)), 0.0)
        last = c_col[BLOCK - 1 : BLOCK, :]
        out.append((fade, fade * b_row, jnp.exp(c_col), jnp.exp(last - c_col), b_col, jnp.exp(last)))
    return [list(items) for items in zip(*out)]


def chains(counts):
    start, out = 0, []
    for count in counts:
        out.append(range(start, start + count))
        start += count
    return out


def solve_kernel(counts, q_ref, k_ref, v_ref, col_ref, row_ref, solver_ref, scores_ref, w_ref, vt_ref, qt_ref, m_ref, b_ref, mseg_ref, bseg_ref):
    count = sum(counts)
    lower, strict, identity = square_masks()
    query = q_ref[...]
    query = split(query * row_factor(query), count)
    key = k_ref[...]
    key = split(key * row_factor(key), count)
    value = split(v_ref[...], count)
    fade, ratio, growth, remain, beta, end = decays(col_ref, row_ref, count)
    power = each(lambda k, p: jnp.where(strict, -mm_nt(k, k) * p, 0.0), key, ratio)
    solver = [identity + p for p in power]
    for _ in range((BLOCK - 1).bit_length() - 1):
        power = each(lambda p: mm(p, p), power)
        solver = each(lambda s, p: s + mm(s, p), solver, power)
    scores = each(lambda q, k, p: mm_nt(q, k) * p, query, key, ratio)
    w = each(lambda s, g, k: mm(s, g * k), solver, growth, key)
    vt = each(mm, solver, value)
    qt = each(lambda g, q, a, x: g * q - mm(a, x), growth, query, scores, w)
    weighted = each(lambda k, r, b: k * (r * b), key, remain, beta)
    size = query[0].shape[1]
    wide = (
        lax.broadcasted_iota(jnp.int32, (size, size), 0)
        == lax.broadcasted_iota(jnp.int32, (size, size), 1)
    ).astype(f32)
    m = each(lambda e, k, x: e * wide - mm_tn(k, x), end, weighted, w)
    b = each(mm_tn, weighted, vt)
    for i in range(count):
        solver_ref[0, i] = solver[i]
        scores_ref[0, i] = scores[i]
        w_ref[0, i] = w[i]
        vt_ref[0, i] = vt[i]
        qt_ref[0, i] = qt[i]
        m_ref[0, i] = m[i]
        b_ref[0, i] = b[i]
    for j, chain in enumerate(chains(counts)):
        mseg_ref[0, j] = m[chain[0]]
        bseg_ref[0, j] = b[chain[0]]
        for i in chain[1:]:
            bseg_ref[0, j] = mm(m_ref[0, i], bseg_ref[0, j]) + b_ref[0, i]
            mseg_ref[0, j] = mm(m_ref[0, i], mseg_ref[0, j])


def output_kernel(counts, state_ref, m_ref, b_ref, qt_ref, scores_ref, vt_ref, gate_ref, gain_ref, states_ref, out_ref, gated_ref):
    count = sum(counts)
    states = [None] * count
    for j, chain in enumerate(chains(counts)):
        state = state_ref[0, j]
        for i in chain:
            states[i] = state
            states_ref[0, i] = state
            if i != chain[-1]:
                state = mm(m_ref[0, i], state) + b_ref[0, i]
    gain = gain_ref[...]
    outs = [mm(qt_ref[0, i], states[i]) + mm(scores_ref[0, i], vt_ref[0, i]) for i in range(count)]
    for i in range(count):
        rows = slice(i * BLOCK, (i + 1) * BLOCK)
        out = outs[i]
        gate = gate_ref[rows, :]
        scale = lax.rsqrt(jnp.mean(out * out, axis=-1, keepdims=True) + epsilon)
        out_ref[rows, :] = out
        gated_ref[rows, :] = (out * scale * gain * (gate * jax.nn.sigmoid(gate))).astype(jnp.bfloat16)


def output_grad_kernel(counts, grad_ref, gate_ref, out_ref, gain_ref, qt_ref, m_ref, out_grad_ref, gate_grad_ref, gain_grad_ref, d_ref, dseg_ref):
    count = sum(counts)
    gain = gain_ref[...]
    gain_grad = jnp.zeros_like(gain)
    grads = []
    for i in range(count):
        rows = slice(i * BLOCK, (i + 1) * BLOCK)
        grad, gate, out = grad_ref[rows, :], gate_ref[rows, :], out_ref[rows, :]
        scale = lax.rsqrt(jnp.mean(out * out, axis=-1, keepdims=True) + epsilon)
        unit = out * scale
        sig = jax.nn.sigmoid(gate)
        normed_grad = grad * (gate * sig)
        gate_grad_ref[rows, :] = (grad * (unit * gain) * (sig * (1.0 + gate * (1.0 - sig)))).astype(jnp.bfloat16)
        gain_grad = gain_grad + jnp.sum(normed_grad * unit, axis=0, keepdims=True)
        inner = normed_grad * gain
        out_grad = scale * (inner - unit * jnp.mean(unit * inner, axis=-1, keepdims=True))
        out_grad_ref[rows, :] = out_grad
        grads.append(out_grad)
    gain_grad_ref[0] = gain_grad
    d = [mm_tn(qt_ref[0, i], grads[i]) for i in range(count)]
    for i in range(count):
        d_ref[0, i] = d[i]
    for j, chain in enumerate(chains(counts)):
        dseg_ref[0, j] = d[chain[-1]]
        for i in list(chain)[-2::-1]:
            dseg_ref[0, j] = mm_tn(m_ref[0, i], dseg_ref[0, j]) + d_ref[0, i]


def unit_back(raw, grad):
    factor = row_factor(raw)
    unit = raw * factor
    return factor * (grad - unit * jnp.sum(unit * grad, axis=-1, keepdims=True))


def grads_kernel(counts, q_ref, k_ref, col_ref, row_ref, solver_ref, scores_ref, w_ref, vt_ref, m_ref, d_ref, states_ref, out_grad_ref, gate_ref, later_ref, slim_ref, joint_ref, col_grad_ref, row_grad_ref):
    count = sum(counts)
    span = range(count)
    lower, strict, identity = square_masks()
    raw_q, raw_k = split(q_ref[...], count), split(k_ref[...], count)
    query = [x * row_factor(x) for x in raw_q]
    key = [x * row_factor(x) for x in raw_k]
    fade, ratio, growth, remain, beta, end = decays(col_ref, row_ref, count)
    out_grad = split(out_grad_ref[...], count)
    later = [None] * count
    for j, chain in enumerate(chains(counts)):
        state = later_ref[0, j]
        for i in list(chain)[::-1]:
            later[i] = state
            if i != chain[0]:
                state = mm_tn(m_ref[0, i], state) + d_ref[0, i]
    states = [states_ref[0, i] for i in span]
    update = [vt_ref[0, i] - mm(w_ref[0, i], states[i]) for i in span]
    update_grad = [
        mm_tn(scores_ref[0, i], out_grad[i]) + mm(key[i] * (remain[i] * beta[i]), later[i]) for i in span
    ]
    solved = [mm_tn(solver_ref[0, i], update_grad[i]) for i in span]
    scores_grad = each(mm_nt, out_grad, update)
    inner_grad = each(lambda y, u: jnp.where(strict, -mm_nt(y, u), 0.0), solved, update)
    query_dot = each(mm_nt, query, key)
    keys_dot = each(mm_nt, key, key)
    from_out = each(mm_nt, out_grad, states)
    from_solved = each(mm_nt, solved, states)
    from_update = each(mm_nt, update, later)
    weighted_scores = each(lambda p, x: p * x, ratio, scores_grad)
    weighted_inner = each(lambda p, x: p * x, ratio, inner_grad)
    q_grad = [growth[i] * from_out[i] + mm(weighted_scores[i], key[i]) for i in span]
    k_grad = [
        mm_tn(weighted_scores[i], query[i])
        + (remain[i] * beta[i]) * from_update[i]
        - growth[i] * from_solved[i]
        + mm(weighted_inner[i], key[i])
        + mm_tn(weighted_inner[i], key[i])
        for i in span
    ]
    last_row = (lax.broadcasted_iota(jnp.int32, (BLOCK, 1), 0) == BLOCK - 1).astype(f32)
    for i in span:
        rows = slice(i * BLOCK, (i + 1) * BLOCK)
        start = 0
        for grad in (unit_back(raw_q[i], q_grad[i]), unit_back(raw_k[i], k_grad[i]), solved[i]):
            place = slice(start, start + grad.shape[1])
            start += grad.shape[1]
            slim_ref[rows, place] = grad.astype(jnp.bfloat16)
            joint_ref[rows, place] = grad.astype(jnp.bfloat16)
        joint_ref[rows, start:] = gate_ref[rows, :]
        faded = fade[i] * (scores_grad[i] * query_dot[i] + inner_grad[i] * keys_dot[i])
        b_row = row_ref[0, i, 1:2, :]
        growth_grad = jnp.sum(query[i] * from_out[i] - key[i] * from_solved[i], axis=-1, keepdims=True)
        weight_grad = jnp.sum(key[i] * from_update[i], axis=-1, keepdims=True)
        pulled = remain[i] * beta[i] * weight_grad
        tail = jnp.sum(pulled, axis=0, keepdims=True) + end[i] * jnp.sum(
            jnp.sum(later[i] * states[i], axis=-1, keepdims=True), axis=0, keepdims=True
        )
        c_grad = jnp.sum(faded * b_row, axis=-1, keepdims=True) + growth[i] * growth_grad - pulled + last_row * tail
        col_grad_ref[0, i, :, 0:1] = c_grad
        col_grad_ref[0, i, :, 1:2] = remain[i] * weight_grad
        row_grad_ref[0, i] = jnp.sum(faded, axis=0, keepdims=True)


def whole(shape):
    return pl.BlockSpec((1,) + tuple(shape[1:]), lambda j: (j,) + (0,) * (len(shape) - 1))


def columns(rows, width, first=0, step=1):
    return pl.BlockSpec((rows, width), lambda j: (0, step * j + first))


def shaped(shape, dtype=f32):
    return jax.ShapeDtypeStruct(shape, dtype)


def call(kernel, counts, heads, inputs, outputs, flops):
    moved = sum(x.size * x.dtype.itemsize for x, _ in inputs) + sum(
        x.size * x.dtype.itemsize for x, _ in outputs
    )
    return pl.pallas_call(
        functools.partial(kernel, counts),
        grid=(heads,),
        in_specs=[s for _, s in inputs],
        out_specs=[s for _, s in outputs],
        out_shape=[x for x, _ in outputs],
        compiler_params=pltpu.CompilerParams(vmem_limit_bytes=48 << 20),
        cost_estimate=pl.CostEstimate(flops=flops, bytes_accessed=moved, transcendentals=0),
    )(*[x for x, _ in inputs])


def per_head(heads, *shape, dtype=f32):
    s = (heads,) + shape
    return shaped(s, dtype), whole(s)


def flat(array, width, first=0, step=1):
    return array, columns(array.shape[0], width, first, step)


def stacked(array):
    return array, whole(array.shape)


def solve(counts, heads, proj, col, row):
    n, dk, dv = sum(counts), 128, 256
    return call(
        solve_kernel, counts, heads,
        [flat(proj, dk, 0, 4), flat(proj, dk, 1, 4), flat(proj, dv, 1, 2), stacked(col), stacked(row)],
        [per_head(heads, n, BLOCK, BLOCK), per_head(heads, n, BLOCK, BLOCK), per_head(heads, n, BLOCK, dk),
         per_head(heads, n, BLOCK, dv), per_head(heads, n, BLOCK, dk), per_head(heads, n, dk, dk),
         per_head(heads, n, dk, dv), per_head(heads, len(counts), dk, dk), per_head(heads, len(counts), dk, dv)],
        heads * n * 100_000_000,
    )


def outputs_of(counts, heads, state, m, b, qt, scores, vt, gate_pre, gain):
    n, dk, dv = sum(counts), 128, 256
    rows = gate_pre.shape[0]
    cols = columns(rows, dv)
    return call(
        output_kernel, counts, heads,
        [stacked(state), stacked(m), stacked(b), stacked(qt), stacked(scores), stacked(vt), flat(gate_pre, dv),
         (gain, pl.BlockSpec((1, dv), lambda j: (0, 0)))],
        [per_head(heads, n, dk, dv), (shaped((rows, heads * dv)), cols), (shaped((rows, heads * dv), jnp.bfloat16), cols)],
        heads * n * 50_000_000,
    )


def output_grads_of(counts, heads, grad, gate_pre, outs, gain, qt, m):
    n, dk, dv = sum(counts), 128, 256
    rows = gate_pre.shape[0]
    cols = columns(rows, dv)
    return call(
        output_grad_kernel, counts, heads,
        [flat(grad, dv), flat(gate_pre, dv), flat(outs, dv), (gain, pl.BlockSpec((1, dv), lambda j: (0, 0))), stacked(qt), stacked(m)],
        [(shaped((rows, heads * dv)), cols), (shaped((rows, heads * dv), jnp.bfloat16), cols),
         per_head(heads, 1, dv), per_head(heads, n, dk, dv), per_head(heads, len(counts), dk, dv)],
        heads * n * 50_000_000,
    )


def input_grads_of(counts, heads, proj, col, row, solver, scores, w, vt, m, d, states, out_grad, gate_grad, later):
    n, dk, dv = sum(counts), 128, 256
    rows = proj.shape[0]
    return call(
        grads_kernel, counts, heads,
        [flat(proj, dk, 0, 4), flat(proj, dk, 1, 4), stacked(col), stacked(row), stacked(solver), stacked(scores), stacked(w),
         stacked(vt), stacked(m), stacked(d), stacked(states), flat(out_grad, dv), flat(gate_grad, dv), stacked(later)],
        [(shaped((rows, heads * (2 * dk + dv)), jnp.bfloat16), columns(rows, 2 * dk + dv)),
         (shaped((rows, heads * (2 * dk + 2 * dv)), jnp.bfloat16), columns(rows, 2 * dk + 2 * dv)),
         per_head(heads, n, BLOCK, 2), per_head(heads, n, 1, BLOCK)],
        heads * n * 150_000_000,
    )


def feed_kernel(stage_ref, x_ref, k_ref, xs_ref, ks_ref, w1_ref, w3_ref, w2_ref, t1_ref, t3_ref, t2_ref, back_ref, feed_ref, main_ref, main_other_ref, tail_ref, tail_other_ref, active_s, gate_s, up_s, sums_s):
    step, chunk = pl.program_id(0), pl.program_id(1)
    own, width = sums_s.shape[0], sums_s.shape[1] // 2
    groups, rows_each = back_ref.shape[0], back_ref.shape[1]
    near, piece = x_ref.shape[1] // own, x_ref.shape[2]
    stage = stage_ref[0]
    here = pl.ds(pl.multiple_of(lax.rem(stage, near) * own, own), own)

    @pl.when((step == 0) & (chunk == 0))
    def _():
        sums_s[...] = jnp.zeros_like(sums_s)

    def work(w1, w3, w2, out_refs):
        wide = w1.shape[1]
        gate, up, grad = (
            sum(
                jnp.dot(rows[i], w[i * piece : (i + 1) * piece, :], preferred_element_type=f32)
                for i in range(rows.shape[0])
            )
            for rows, w in ((x_ref, w1), (x_ref, w3), (k_ref, w2))
        )
        sig = jax.nn.sigmoid(gate)
        silu = gate * sig
        active = (silu * up).astype(jnp.bfloat16)
        gate_grad = (grad * up * (sig * (1.0 + gate * (1.0 - sig)))).astype(jnp.bfloat16)
        up_grad = (grad * silu).astype(jnp.bfloat16)
        active_s[:, :wide] = active
        gate_s[:, :wide] = gate_grad
        up_s[:, :wide] = up_grad

        @pl.when(chunk == stage // near)
        def _():
            sums_s[:, width:] += contract_cols(active_s[here, :wide], w2[...])
            sums_s[:, :width] += contract_cols(gate_s[here, :wide], w1[...])
            sums_s[:, :width] += contract_cols(up_s[here, :wide], w3[...])

        parts = (
            contract_rows(gate_grad, xs_ref[...]),
            contract_rows(up_grad, xs_ref[...]),
            contract_rows(active, ks_ref[...]),
        )
        for i, p in enumerate(parts):
            place = slice(i * wide, (i + 1) * wide)
            quota = p.shape[1] // 2

            @pl.when(chunk == 0)
            def _():
                out_refs[0][place, :] = p[:, :quota]
                out_refs[1][place, :] = p[:, quota:]

            @pl.when(chunk > 0)
            def _():
                out_refs[0][place, :] += p[:, :quota]
                out_refs[1][place, :] += p[:, quota:]

    work(w1_ref, w3_ref, w2_ref, (main_ref, main_other_ref))

    @pl.when(step == pl.num_programs(0) - 1)
    def _():
        work(t1_ref, t3_ref, t2_ref, (tail_ref, tail_other_ref))

    @pl.when((step == pl.num_programs(0) - 1) & (chunk == pl.num_programs(1) - 1))
    def _():
        for g in range(groups):
            rows = slice(g * rows_each, (g + 1) * rows_each)
            back_ref[g] = sums_s[rows, :width].astype(jnp.bfloat16)
            feed_ref[g] = sums_s[rows, width:].astype(jnp.bfloat16)


def feed_forward(stage, rows, grads, row_cols, grad_cols, weights, groups, rows_each):
    pieces, positions, piece = rows.shape
    width, own = pieces * piece, groups * rows_each
    picked = row_cols.shape[1]
    tile, rest = 256, 128
    steps = (weights.shape[1] - 3 * rest) // (3 * tile)
    chunk = min(positions, 4 * own)
    first_tail = 3 * steps * tile // rest
    grid = (steps, positions // chunk)
    tokens = pl.BlockSpec((pieces, chunk, piece), lambda i, t, s: (0, t, 0))
    columns_of = pl.BlockSpec((chunk, picked), lambda i, t, s: (t, 0))

    def main_of(n):
        return pl.BlockSpec((width, tile), lambda i, t, s: (0, n * steps + i))

    def tail_of(n):
        return pl.BlockSpec((width, rest), lambda i, t, s: (0, first_tail + n))

    def fixed(*shape):
        return pl.BlockSpec(shape, lambda i, t, s: (0, 0))

    flops = 2 * positions * width * weights.shape[1] + 2 * own * width * weights.shape[1] + 2 * positions * picked * weights.shape[1]
    return pl.pallas_call(
        feed_kernel,
        grid_spec=pltpu.PrefetchScalarGridSpec(
            num_scalar_prefetch=1,
            grid=grid,
            in_specs=[tokens, tokens, columns_of, columns_of, main_of(0), main_of(1), main_of(2), tail_of(0), tail_of(1), tail_of(2)],
            out_specs=[
                pl.BlockSpec((groups, rows_each, width), lambda i, t, s: (0, 0, 0)),
                pl.BlockSpec((groups, rows_each, width), lambda i, t, s: (0, 0, 0)),
                pl.BlockSpec((3 * tile, picked // 2), lambda i, t, s: (i, 0)),
                pl.BlockSpec((3 * tile, picked // 2), lambda i, t, s: (i, 0)),
                fixed(3 * rest, picked // 2),
                fixed(3 * rest, picked // 2),
            ],
            scratch_shapes=[pltpu.VMEM((chunk, tile), jnp.bfloat16)] * 3 + [pltpu.VMEM((own, 2 * width), f32)],
        ),
        out_shape=[
            shaped((groups, rows_each, width), jnp.bfloat16),
            shaped((groups, rows_each, width), jnp.bfloat16),
            shaped((3 * tile * steps, picked // 2)),
            shaped((3 * tile * steps, picked // 2)),
            shaped((3 * rest, picked // 2)),
            shaped((3 * rest, picked // 2)),
        ],
        compiler_params=pltpu.CompilerParams(
            dimension_semantics=("arbitrary", "arbitrary"), vmem_limit_bytes=56 << 20
        ),
        cost_estimate=pl.CostEstimate(
            flops=flops, bytes_accessed=2 * weights.size + 8 * positions * width, transcendentals=0
        ),
    )(stage, rows, grads, row_cols, grad_cols, weights, weights, weights, weights, weights, weights)


def projection_kernel(heads, cols_ref, joint_ref, q_ref, k_ref, v_ref, g_ref):
    joined = jnp.dot(cols_ref[...], joint_ref[...], preferred_element_type=f32)
    start = 0
    for j in range(heads):
        for ref in (q_ref, k_ref, v_ref, g_ref):
            size = ref.shape[1] // heads
            ref[:, j * size : (j + 1) * size] = joined[:, start : start + size]
            start += size


def projection_grads(cols, joint_all, heads, sizes):
    quota, positions = cols.shape
    wide = joint_all.shape[1]
    return pl.pallas_call(
        functools.partial(projection_kernel, heads),
        grid=(2,),
        in_specs=[
            pl.BlockSpec((quota, positions), lambda c: (0, 0)),
            pl.BlockSpec((positions, wide), lambda c: (c, 0)),
        ],
        out_specs=[pl.BlockSpec((quota, n), lambda c: (0, c)) for n in sizes],
        out_shape=[shaped((quota, 2 * n)) for n in sizes],
        compiler_params=pltpu.CompilerParams(vmem_limit_bytes=56 << 20),
        cost_estimate=pl.CostEstimate(
            flops=4 * quota * positions * wide, bytes_accessed=2 * joint_all.size, transcendentals=0
        ),
    )(cols, joint_all)


QUARTERS = 4


def swap(array):
    return lax.ppermute(array, "dp", [(0, 1), (1, 0)])


def relay(mats, offsets, forward):
    size = lax.axis_size("seq")
    entering = jnp.zeros_like(offsets)
    leaving = offsets
    for step in range(size - 1):
        route = [(step, step + 1)] if forward else [(size - 1 - step, size - 2 - step)]
        got = jnp.stack([lax.ppermute(head, "seq", route) for head in leaving])
        entering = entering + got
        if step < size - 2:
            leaving = jnp.matmul(mats, got, precision=highest) + offsets
    return entering, leaving


def together(*arrays):
    return lax.optimization_barrier(arrays)


def everyone(part):
    return lax.all_gather(part, ("dp", "seq"), axis=0, tiled=True)


def share(rows):
    wide = jnp.broadcast_to(rows[None], (lax.axis_size("head"),) + rows.shape)
    return lax.all_to_all(wide, "head", split_axis=0, concat_axis=0, tiled=True)


def from_others(piece):
    size = lax.axis_size("head")
    return [lax.ppermute(piece(k), "head", [(i, i ^ k) for i in range(size)]) for k in range(1, size)]


def in_group_order(pieces):
    group = lax.axis_index("head")
    stacked = jnp.stack(pieces)
    return jnp.stack(
        [lax.dynamic_index_in_dim(stacked, g ^ group, 0, keepdims=False) for g in range(lax.axis_size("head"))]
    )


def add_by_permutes(vector):
    near, far, across = from_others(lambda k: vector)
    return (vector + near) + (far + across)


def add_parts_by_permutes(parts):
    group = lax.axis_index("head")

    def piece(k):
        return lax.dynamic_index_in_dim(parts, group ^ k, 0, keepdims=False).astype(jnp.bfloat16)

    near, far, across = [got.astype(f32) for got in from_others(piece)]
    return (piece(0).astype(f32) + near) + (far + across)


def add_parts(parts):
    got = lax.all_to_all(parts.astype(jnp.bfloat16), "head", split_axis=0, concat_axis=0, tiled=True)
    return jnp.sum(got.astype(f32), axis=0)


def contract_rows(left, right):
    return lax.dot_general(left, right, (((0,), (0,)), ((), ())), preferred_element_type=f32)


def contract_cols(left, right):
    return lax.dot_general(left, right, (((1,), (1,)), ((), ())), preferred_element_type=f32)


def product(left, right):
    return jnp.dot(left, right, preferred_element_type=f32)


def rms_scale(values, gain):
    return values * lax.rsqrt(jnp.mean(values * values, axis=-1, keepdims=True) + epsilon) * gain


def swiglu(gate_in, up_in):
    return jax.nn.silu(gate_in) * up_in


def on_device(
    activations,
    cotangent,
    lengths,
    query_weight,
    key_weight,
    value_weight,
    gate_weight,
    alpha_weight,
    beta_weight,
    out_weight,
    swiglu_gate,
    swiglu_value,
    swiglu_down,
    mixer_gain,
    feed_gain,
    head_gain,
    decay_rate,
    beta_bias,
):
    bf16 = jnp.bfloat16
    core, stage, group = lax.axis_index("dp"), lax.axis_index("seq"), lax.axis_index("head")
    stages, groups = lax.axis_size("seq"), lax.axis_size("head")
    width = activations.shape[2]
    rows0 = activations.shape[1]
    rows1 = rows0 // QUARTERS
    own0, own1 = rows0 // (2 * groups), rows1 // (2 * groups)
    own = own0 + own1
    quota = width // (2 * stages)
    heads = alpha_weight.shape[1] // 2
    counts = (rows0 // BLOCK, rows1 // BLOCK)
    assert groups == QUARTERS and stages % QUARTERS == 0 and rows1 % BLOCK == 0
    first = core == 0

    def part(array, size, axis, offset=0):
        return lax.dynamic_slice_in_dim(array, offset + core * size, size, axis)

    dk, dv = query_weight.shape[1] // 2, value_weight.shape[1] // 2
    slim = 2 * dk + dv
    mixer_cols = []
    for c in range(2):
        for j in range(c * heads, (c + 1) * heads):
            mixer_cols += [
                query_weight[:, j * dk // heads : (j + 1) * dk // heads],
                key_weight[:, j * dk // heads : (j + 1) * dk // heads],
                value_weight[:, j * dv // heads : (j + 1) * dv // heads],
            ]
    mixer_cols += [alpha_weight, beta_weight]
    mixer_full = everyone(jnp.concatenate(mixer_cols, axis=1).astype(bf16))
    gates_full = everyone(jnp.concatenate([gate_weight, out_weight], axis=1).astype(bf16))
    hidden_units = swiglu_gate.shape[1]
    even = hidden_units // 256 * 256
    odd = hidden_units - even
    assert 0 < odd <= 128
    three = (swiglu_gate, swiglu_value, swiglu_down)
    spare = ((0, 0), (0, 128 - odd))
    feed_full = everyone(
        jnp.concatenate([w[:, :even] for w in three] + [jnp.pad(w[:, even:], spare) for w in three], axis=1).astype(bf16)
    )

    def chip_rows(rows):
        arrived = jnp.zeros((rows1, width), bf16)
        for b in range(QUARTERS):
            route = [(stages + a, stages + QUARTERS * a + b) for a in range(stages // QUARTERS)]
            arrived = arrived + lax.ppermute(rows[b * rows1 : (b + 1) * rows1], ("dp", "seq"), route)
        near0 = lax.ppermute(rows, "dp", [(0, 1)])
        near1 = lax.ppermute(arrived, "dp", [(1, 0)])
        return jnp.concatenate([jnp.where(first, rows, near0), jnp.where(first, near1, arrived)], axis=0)

    inputs = chip_rows(activations[0])
    inputs, late = together(inputs, cotangent[0])
    inputs = inputs.astype(f32)
    spots0 = stage * rows0 + lax.broadcasted_iota(jnp.int32, (rows0, 1), 0)
    spots1 = stage * rows1 + lax.broadcasted_iota(jnp.int32, (rows1, 1), 0)
    mask = jnp.concatenate([spots0 < lengths[0], spots1 < lengths[1]], axis=0).astype(f32)
    masked = (chip_rows(late).astype(f32) * mask).astype(bf16)

    def by_owner(rows):
        wide = rows.shape[1]
        r0 = rows[:rows0].reshape(groups, 2, own0, wide)
        r1 = rows[rows0:].reshape(groups, 2, own1, wide)
        return jnp.concatenate([r0, r1], axis=2).swapaxes(0, 1)

    def in_time(owned):
        wide = owned.shape[3]
        turned = owned.swapaxes(0, 1)
        return jnp.concatenate(
            [turned[:, :, :own0].reshape(rows0, wide), turned[:, :, own0:].reshape(rows1, wide)], axis=0
        )

    def of_core(owned, which):
        return lax.dynamic_index_in_dim(owned, which, 0, keepdims=False)

    def of_group(rows):
        return lax.dynamic_index_in_dim(rows, group, 0, keepdims=False)

    def add_rows(partial):
        owned = by_owner(partial)
        return add_parts_by_permutes(of_core(owned, core) + swap(of_core(owned, 1 - core)))

    def meet_columns(rows):
        return lax.all_to_all(rows, ("dp", "seq"), split_axis=1, concat_axis=0, tiled=True)

    def owned_columns(met, share_rows):
        got = share_rows(met).reshape(groups, 2, stages, own, quota).transpose(2, 0, 1, 3, 4)
        return jnp.concatenate(
            [got[:, :, :, :own0].reshape(stages, rows0, quota), got[:, :, :, own0:].reshape(stages, rows1, quota)], axis=1
        ).reshape(stages * (rows0 + rows1), quota)

    def across_stages(rows):
        wide = jnp.broadcast_to(rows[None], (stages,) + rows.shape)
        met = lax.all_to_all(wide, "seq", split_axis=0, concat_axis=0, tiled=True)
        return met.reshape(stages * rows.shape[0], rows.shape[1])

    def own_columns(rows):
        pieces, positions, piece = rows.shape
        both = []
        for which in (core, 1 - core):
            start = (which * stages + stage) * quota
            both.append(lax.dynamic_slice(rows, (start // piece, 0, start % piece), (1, positions, quota))[0])
        return jnp.concatenate(both, axis=1)

    own_rows = of_group(of_core(by_owner(inputs), core))
    own_mask = of_group(of_core(by_owner(mask), core))
    tokens_masked = of_core(by_owner(masked), core)
    own_masked = of_group(tokens_masked).astype(f32)
    quarter = width // groups
    masked_met = across_stages(
        lax.dynamic_slice_in_dim(tokens_masked.reshape(groups * own, width), group * quarter, quarter, 1)
    )

    factor1 = lax.rsqrt(jnp.mean(inputs * inputs, axis=-1, keepdims=True) + epsilon)
    unit1 = inputs * factor1
    normed = rms_scale(inputs, mixer_gain).astype(bf16)
    normed_cols = owned_columns(meet_columns(of_group(of_core(by_owner(normed), core))), share).T
    mixer_full, masked_met, normed_cols = together(mixer_full, masked_met, normed_cols)
    mixer_w = part(mixer_full, slim, 1)
    gate_w = part(gates_full, dv, 1)
    out_w = part(gates_full, dv, 1, 2 * dv)
    rates_w = mixer_full[:, 2 * slim :]
    proj = product(normed, mixer_w)
    small_pre = product(normed, rates_w)
    gate_pre = product(normed, gate_w)
    alpha_pre = part(small_pre, heads, 1)
    beta_pre = part(small_pre, heads, 1, 2 * heads)
    head0 = (2 * group + core) * heads
    rates = lax.dynamic_slice_in_dim(decay_rate, head0, heads)
    biases = lax.dynamic_slice_in_dim(beta_bias, head0, heads)
    blocks = sum(counts)

    def to_blocks(array):
        return array.T.reshape(heads, blocks, BLOCK)

    def from_blocks(array):
        return array.reshape(heads, blocks * BLOCK).T

    soft = jax.nn.softplus(alpha_pre)
    beta = jax.nn.sigmoid(beta_pre + biases)
    beta_b = to_blocks(beta)
    upto = (
        lax.broadcasted_iota(jnp.int32, (BLOCK, BLOCK), 0) <= lax.broadcasted_iota(jnp.int32, (BLOCK, BLOCK), 1)
    ).astype(f32)
    sums = jnp.matmul(to_blocks(-rates * soft), upto, precision=highest)
    col = jnp.stack([sums, beta_b], axis=-1)
    row = jnp.stack([sums, beta_b], axis=-2)
    solver, scores, w, vt, qt, m, b, mseg, bseg = solve(counts, heads, proj, col, row)
    state_in, unused_carry = relay(mseg, bseg, True)
    state_in, masked_all = together(state_in, share(masked_met))
    gain_row = head_gain[None]
    states, outs, gated = outputs_of(counts, heads, state_in, m, b, qt, scores, vt, gate_pre, gain_row)
    mixed = add_rows(contract_cols(gated, out_w))
    hidden = own_rows + mixed

    normed2, norm2_back = jax.vjp(rms_scale, hidden, feed_gain)
    feed_in = share(
        across_stages(lax.all_to_all(normed2.astype(bf16), "head", split_axis=1, concat_axis=0, tiled=True))
    )
    back_part, feed_part, main_own, main_other, tail_own, tail_other = feed_forward(
        stage[None], feed_in, masked_all, own_columns(feed_in), own_columns(masked_all), feed_full, groups, own
    )
    normed2_grad, main_other, tail_other = together(add_parts_by_permutes(back_part), swap(main_other), swap(tail_other))
    hidden_back, feed_gain_grad = norm2_back(normed2_grad)
    hidden_grad = own_masked + hidden_back
    mixed_own = hidden_grad.astype(bf16)
    mixed_half = share(mixed_own)
    other_half = swap(mixed_half)
    mixed_in = in_time(
        jnp.stack([jnp.where(first, mixed_half, other_half), jnp.where(first, other_half, mixed_half)])
    )

    gated_all = everyone(gated)
    gated_grad = product(mixed_in, out_w)
    mixed_late, unused_rows = together(mixed_own, mixed_in)
    mixed_met = meet_columns(mixed_late)
    gated_grad, gated_all = together(gated_grad, gated_all)
    outs_grad, gate_pre_low, gain_grads, d, dseg = output_grads_of(
        counts, heads, gated_grad, gate_pre, outs, gain_row, qt, m
    )
    dseg, mixed_met = together(dseg, mixed_met)
    later, unused_carry = relay(jnp.swapaxes(mseg, 2, 3), dseg, False)

    half = stages * (rows0 + rows1)
    gate_back = contract_cols(gate_pre_low, gate_w)
    later, gate_back = together(later, gate_back)
    slim_low, joint_low, col_grad, row_grad = input_grads_of(
        counts, heads, proj, col, row, solver, scores, w, vt, m, d, states, outs_grad, gate_pre_low, later
    )
    joint_all = everyone(joint_low)
    slim_low, mixed_met = together(slim_low, mixed_met)
    mixed_pieces = from_others(lambda k: mixed_met)
    sums_grad = col_grad[..., 0] - row_grad[:, :, 0] * beta_b
    decay_back = from_blocks(jnp.matmul(sums_grad, upto.T, precision=highest))
    beta_back = beta * (1.0 - beta) * from_blocks(col_grad[..., 1] + row_grad[:, :, 0])
    rates_grad = -jnp.sum(soft * decay_back, axis=0)
    biases_grad = jnp.sum(beta_back, axis=0)
    alpha_back = -rates * jax.nn.sigmoid(alpha_pre) * decay_back
    small_low = jnp.concatenate([alpha_back, beta_back], axis=1).astype(bf16)
    blank = jnp.zeros((rows0 + rows1, 4 * heads), bf16)
    spread = lax.dynamic_update_slice(blank, small_low[:, :heads], (0, core * heads))
    spread = lax.dynamic_update_slice(spread, small_low[:, heads:], (0, (2 + core) * heads))
    total = gate_back + contract_cols(slim_low, mixer_w) + contract_cols(spread, rates_w)
    normed_grad = add_rows(total)
    mixer_gain_part = jnp.sum(total * unit1, axis=0)
    normed_grad, small_late, mixer_gain_part, feed_part, main_own, main_other, tail_own, tail_other, *mixed_pieces = together(
        normed_grad, small_low, mixer_gain_part, feed_part, main_own, main_other, tail_own, tail_other, mixed_met, *mixed_pieces
    )
    feed = add_parts_by_permutes(feed_part)
    mixed_cols = owned_columns(mixed_met, lambda rows: in_group_order(mixed_pieces))
    outputs_own = (own_mask * (hidden + feed)).astype(bf16)
    out_grad = jnp.concatenate(
        [contract_rows(mixed_cols, gated_all[:half]), contract_rows(mixed_cols, gated_all[half:])], axis=1
    )
    unused_rows, norm1_back = jax.vjp(lambda v: rms_scale(v, mixer_gain), own_rows)
    input_own = (hidden_grad + norm1_back(normed_grad)[0]).astype(bf16)

    main_own, tail_own = main_own + main_other, tail_own + tail_other

    def feed_grad(n):
        pieces = [main_own[(3 * i + n) * 256 : (3 * i + n + 1) * 256] for i in range(even // 256)]
        return jnp.concatenate(pieces + [tail_own[n * 128 : n * 128 + odd]], axis=0)

    feed_gate_grad, feed_value_grad, down_grad = feed_grad(0), feed_grad(1), feed_grad(2)

    small_rows = contract_rows(small_late, normed).reshape(2 * heads, 2 * stages, quota).swapaxes(0, 1)
    total_heads = decay_rate.shape[0]
    none = jnp.zeros((total_heads,), f32)
    vector = jnp.concatenate(
        [
            mixer_gain_part,
            feed_gain_grad,
            jnp.sum(gain_grads, axis=(0, 1)),
            lax.dynamic_update_slice(none, rates_grad, (head0,)),
            lax.dynamic_update_slice(none, biases_grad, (head0,)),
        ]
    )
    mail = jnp.concatenate(
        [
            small_rows.reshape(2 * stages, 2 * heads * quota),
            jnp.broadcast_to(vector[None], (2 * stages, vector.shape[0])),
        ],
        axis=1,
    )
    mail = lax.all_to_all(mail, ("dp", "seq"), split_axis=0, concat_axis=0, tiled=True)
    mail, out_grad = together(mail, out_grad)
    small_rows = jnp.sum(mail[:, : 2 * heads * quota].reshape(2, stages, 2, heads, quota), axis=1)
    alpha_grad = small_rows[:, 0].reshape(2 * heads, quota).T
    beta_grad = small_rows[:, 1].reshape(2 * heads, quota).T
    small = add_by_permutes(jnp.sum(mail[:, 2 * heads * quota :], axis=0))
    joint_all, out_grad = together(joint_all, out_grad)
    query_grad, key_grad, value_grad, gate_grad = projection_grads(normed_cols, joint_all, heads, (dk, dk, dv, dv))

    edges = [width, 2 * width, 2 * width + head_gain.shape[0], 2 * width + head_gain.shape[0] + total_heads]

    def place(rows):
        r0, r1 = rows[:own0], rows[own0:]
        out0 = jnp.concatenate([r0, lax.ppermute(r0, "dp", [(1, 0)])], axis=0)
        pair = jnp.concatenate([lax.ppermute(r1, "dp", [(0, 1)]), r1], axis=0)
        routes = [
            [
                ((stages + QUARTERS * a + b) * groups + k, (stages + a) * groups + b)
                for a in range(stages // QUARTERS)
                for b in range(QUARTERS)
            ]
            for k in range(groups)
        ]
        out1 = jnp.concatenate([lax.ppermute(pair, ("dp", "seq", "head"), route) for route in routes], axis=0)
        return jnp.where(first, out0, out1)[None]

    placed = place(jnp.concatenate([outputs_own, input_own], axis=1))
    return (
        placed[:, :, :width],
        placed[:, :, width:],
        query_grad,
        key_grad,
        value_grad,
        gate_grad,
        alpha_grad,
        beta_grad,
        out_grad,
        feed_gate_grad.T,
        feed_value_grad.T,
        down_grad.T,
        small[: edges[0]],
        small[edges[0] : edges[1]],
        small[edges[1] : edges[2]],
        small[edges[2] : edges[3]],
        small[edges[3] :],
    )


def solution(mesh):
    return jax.shard_map(
        on_device,
        mesh=mesh,
        in_specs=(
            P("dp", "seq", None),
            P("dp", "seq", None),
            P(),
            P(("dp", "seq"), "head"),
            P(("dp", "seq"), "head"),
            P(("dp", "seq"), "head"),
            P(("dp", "seq"), "head"),
            P(("dp", "seq"), "head"),
            P(("dp", "seq"), "head"),
            P(("dp", "seq"), "head"),
            P(("dp", "seq"), "head"),
            P(("dp", "seq"), "head"),
            P(("dp", "seq"), "head"),
            P(),
            P(),
            P(),
            P(),
            P(),
        ),
        out_specs=(
            P("dp", ("seq", "head"), None),
            P("dp", ("seq", "head"), None),
            P(("dp", "seq"), "head"),
            P(("dp", "seq"), "head"),
            P(("dp", "seq"), "head"),
            P(("dp", "seq"), "head"),
            P(("dp", "seq"), "head"),
            P(("dp", "seq"), "head"),
            P(("dp", "seq"), "head"),
            P(("dp", "seq"), "head"),
            P(("dp", "seq"), "head"),
            P(("dp", "seq"), "head"),
            P(),
            P(),
            P(),
            P(),
            P(),
        ),
        check_vma=False,
    )
```
